32 devices in a mesh: ctx: 8 (over z, y), fsdp: 4 (over x, core).
Axes of the slice: x: 2, y: 2, z: 4, core: 2. Of those that a mesh axis runs over, the one named last changes fastest.
Arguments:
- inputs: bfloat16 [16, 1024, 768], P('fsdp', 'ctx'), may hold values from -6 to 6
- query_weight: bfloat16 [768, 3072], P('fsdp'), may hold values from -0.21875 to 0.21875
- kv_weight: bfloat16 [768, 1536], P('fsdp'), may hold values from -0.21875 to 0.21875
- out_weight: bfloat16 [768, 768], P('fsdp'), may hold values from -3 to 3
- up_weight: bfloat16 [768, 3072], P('fsdp'), may hold values from -0.21875 to 0.21875
- down_weight: bfloat16 [3072, 768], P('fsdp'), may hold values from -0.109375 to 0.109375
- query_bias: bfloat16 [3072], P('fsdp'), may hold values from -4 to 4
- value_bias: bfloat16 [768], P('fsdp'), may hold values from -6 to 6
- out_bias: bfloat16 [768], P('fsdp'), may hold values from -4 to 4
- up_bias: bfloat16 [3072], P('fsdp'), may hold values from -4 to 4
- down_bias: bfloat16 [768], P('fsdp'), may hold values from -4 to 4
- norm1_gain: bfloat16 [768], P('fsdp'), may hold values from 0.5 to 1.5
- norm1_shift: bfloat16 [768], P('fsdp'), may hold values from -3 to 3
- norm2_gain: bfloat16 [768], P('fsdp'), may hold values from 0.5 to 1.5
- norm2_shift: bfloat16 [768], P('fsdp'), may hold values from -3 to 3
- types: int32 [16, 1024], P('fsdp'), may hold values 0 or 1
- lengths: int32 [16, 4], P('fsdp'), may hold values from 1 to 960, 1024 in all within a row
- cotangent: bfloat16 [16, 1024, 768], P('fsdp', 'ctx'), may hold values from -6 to 6
Outputs:
- output: bfloat16 [16, 1024, 768], P('fsdp', 'ctx')
- input_grad: bfloat16 [16, 1024, 768], P('fsdp', 'ctx')
- query_weight_grad: float32 [768, 3072], P('fsdp')
- kv_weight_grad: float32 [768, 1536], P('fsdp')
- out_weight_grad: float32 [768, 768], P('fsdp')
- up_weight_grad: float32 [768, 3072], P('fsdp')
- down_weight_grad: float32 [3072, 768], P('fsdp')
- query_bias_grad: float32 [3072], P('fsdp')
- value_bias_grad: float32 [768], P('fsdp')
- out_bias_grad: float32 [768], P('fsdp')
- up_bias_grad: float32 [3072], P('fsdp')
- down_bias_grad: float32 [768], P('fsdp')
- norm1_gain_grad: float32 [768], P('fsdp')
- norm1_shift_grad: float32 [768], P('fsdp')
- norm2_gain_grad: float32 [768], P('fsdp')
- norm2_shift_grad: float32 [768], P('fsdp')
The draws below stay inside these ranges and needn't reach their ends.
Inputs may be any that keep to these rules, and one draw needn't show every extreme that they name: Each row holds the lengths of 4 documents packed in order into one sequence of 1024 tokens; they sum to 1024, and the largest is exactly 960.
All inputs are finite; a program needn't handle non-finite values. No bound on the sum of `types` on one device may be relied on, other than what follows from the above.
Results may differ from the reference program's by a relative error of at most 0.023.
Values may be sent and summed in bfloat16 or wider, within the bound.
No kernel may reach another device: no remote copies, remote signals or barrier semaphores. Data moves between devices by JAX's collectives and lax.ppermute only.
A program may use at most 256 MiB of HBM per device.

```python
import math
import jax
import jax.numpy as jnp
import numpy as np
from jax import lax

D = 768
HEADS = 12
HEAD_DIM = 64
FF = 3072
CTX_TOK = 128
DOCS = 4
L = 1024
ROWS = 16


def with_ends(values, key, low, high):
    spot = [jax.random.randint(jax.random.fold_in(key, axis), (), 0, length) for axis, length in enumerate(values.shape)]
    main_axis = values.shape.index(max(values.shape))
    beside = spot[:main_axis] + [(spot[main_axis] + 1) % values.shape[main_axis]] + spot[main_axis + 1:]
    return values.at[tuple(spot)].set(low).at[tuple(beside)].set(high)


def levels(stream_key, shape, pieces, least, high):
    def one(position, shards_of):
        steps = jax.random.uniform(jax.random.fold_in(jax.random.fold_in(stream_key, 6), position), (shards_of,), jnp.float32, least / len(pieces), high / len(pieces))
        return jnp.repeat(jnp.exp(steps), shape[position] // shards_of).reshape((-1,) + (1,) * (len(shape) - position - 1))

    gain = one(*pieces[0])
    for cut in pieces[1:]:
        gain = gain * one(*cut)
    return gain


def profile(count, total, reach, slope):
    loads = [(1 << 20) // math.isqrt(grade ** slope) + 1 for grade in range(2, count + 1)]
    spare, counts = total - reach - (count - 1), [1] * (count - 1)
    while spare > 0:
        candidates = [i for i in range(count - 1) if counts[i] < reach]
        mass, budget = sum([loads[i] for i in candidates]), spare
        for i in candidates:
            extra = min(reach - counts[i], max(1, budget * loads[i] // mass), spare)
            counts[i] = counts[i] + extra
            spare = spare - extra
    return np.array([reach] + counts)


def ragged_sizes(own_key, amount, total, reach, lean):
    if amount == 2:
        one = jax.random.randint(own_key, (), max(1, total - reach), min(reach, total - 1) + 1)
        return jnp.stack([one, total - one])
    sizes = jnp.asarray(profile(amount, total, reach, lean), jnp.int32)
    couples = (amount - 1) // 2
    donor, sink = sizes[1:1 + 2 * couples:2], sizes[2:2 + 2 * couples:2]
    margin = jnp.minimum(donor - 1, reach - sink)
    moved = jax.random.randint(jax.random.fold_in(own_key, 1), (couples,), 0, 1 << 20) % (margin + 1)
    sizes = sizes.at[1:1 + 2 * couples:2].set(donor - moved).at[2:2 + 2 * couples:2].set(sink + moved)
    return sizes[jax.random.permutation(jax.random.fold_in(own_key, 2), amount)]


def scatter_about(key, dims, spread, limit, cuts=(), kind=jnp.bfloat16):
    level = levels(key, dims, cuts, -0.22, 0.18) if cuts else 1.0
    values = jax.random.normal(key, dims, jnp.float32) * spread * level
    return jnp.minimum(jnp.maximum(values, -limit), limit).astype(kind)


def setup_inputs(seed: int = 0) -> dict:
    key_of = jax.random.split(jax.random.key(seed), 19)
    inputs = scatter_about(key_of[0], (ROWS, L, D), 1.0, 6.0, ((0, 4), (1, 8)))
    query_weight = scatter_about(key_of[1], (D, 4 * D), D ** -0.5, 0.21875, ((0, 4),))
    kv_weight = scatter_about(key_of[2], (D, 2 * D), D ** -0.5, 0.21875, ((0, 4),))
    out_weight = scatter_about(key_of[3], (D, D), 4 ** -0.5, 3.0, ((0, 4),))
    up_weight = scatter_about(key_of[4], (D, FF), D ** -0.5, 0.21875, ((0, 4),))
    down_weight = scatter_about(key_of[5], (FF, D), FF ** -0.5, 0.109375, ((0, 4),))
    query_bias = scatter_about(key_of[6], (4 * D,), 0.3, 4.0, ((0, 4),))
    value_bias = scatter_about(key_of[7], (D,), 0.5, 6.0, ((0, 4),))
    out_bias = scatter_about(key_of[8], (D,), 0.3, 4.0, ((0, 4),))
    up_bias = scatter_about(key_of[9], (FF,), 0.3, 4.0, ((0, 4),))
    down_bias = scatter_about(key_of[10], (D,), 0.3, 4.0, ((0, 4),))
    norm1_gain = jnp.clip(1.0 + 0.1 * jax.random.normal(key_of[11], (D,), jnp.float32), 0.5, 1.5).astype(jnp.bfloat16)
    norm1_shift = scatter_about(key_of[12], (D,), 0.2, 3.0, ((0, 4),))
    norm2_gain = jnp.clip(1.0 + 0.1 * jax.random.normal(key_of[13], (D,), jnp.float32), 0.5, 1.5).astype(jnp.bfloat16)
    norm2_shift = scatter_about(key_of[14], (D,), 0.2, 3.0, ((0, 4),))
    types = with_ends((jax.random.randint(key_of[15], (ROWS, L), 0, 4) < 1).astype(jnp.int32), jax.random.fold_in(key_of[15], 1), 0, 1)
    lengths = jax.vmap(lambda own: ragged_sizes(own, DOCS, L, L - CTX_TOK // 2, 0))(jax.random.split(key_of[16], ROWS)).reshape((ROWS, DOCS)).astype(jnp.int32)
    cotangent = scatter_about(key_of[17], (ROWS, L, D), 1.0, 6.0, ((0, 4), (1, 8)))
    return dict(inputs=inputs, query_weight=query_weight, kv_weight=kv_weight, out_weight=out_weight, up_weight=up_weight, down_weight=down_weight, query_bias=query_bias, value_bias=value_bias, out_bias=out_bias, up_bias=up_bias, down_bias=down_bias, norm1_gain=norm1_gain, norm1_shift=norm1_shift, norm2_gain=norm2_gain, norm2_shift=norm2_shift, types=types, lengths=lengths, cotangent=cotangent)


@jax.custom_vjp
def reduced_precision(v):
    return lax.optimization_barrier(v.astype(jnp.bfloat16)).astype(jnp.float32)

@jax.custom_vjp
def low_back(v):
    return v

def low_keep(v):
    return (reduced_precision(v), None)

def low_pass(kept, grad):
    return (grad,)

def back_keep(v):
    return (v, None)

def back_low(kept, grad):
    return (reduced_precision(grad),)
reduced_precision.defvjp(low_keep, low_pass)
low_back.defvjp(back_keep, back_low)
TOP_PRECISION = lax.Precision.HIGHEST
EPSILON = 1e-05
MASKED = -1e+30

def normalize(values, gain_vec, shift_vec):
    center = values - lax.optimization_barrier(jnp.mean(values, axis=-1, keepdims=True))
    variance = lax.optimization_barrier(jnp.mean(center * center, axis=-1, keepdims=True))
    return center * lax.rsqrt(variance + EPSILON) * gain_vec + shift_vec

def segments(lengths):
    doc_ends = jnp.cumsum(lengths, axis=-1).astype(jnp.int32)
    positions = jnp.arange(L, dtype=jnp.int32)
    return lax.optimization_barrier(jnp.sum((positions[None, :, None] >= doc_ends[:, None, :]).astype(jnp.int32), axis=-1))

def project(values, weight_mat):
    return jnp.einsum('bld,de->ble', values, weight_mat, precision=TOP_PRECISION)

def layer_block(inputs, query_weight, kv_weight, out_weight, up_weight, down_weight, query_bias, value_bias, out_bias, up_bias, down_bias, gain_one, shift_one, gain_two, shift_two, entity, seg_ids):
    blocks = inputs.shape[0]
    is_entity = (entity > 0)[..., None]
    query_all = project(inputs, query_weight) + query_bias
    query_word = low_back(reduced_precision(jnp.where(is_entity, query_all[..., 2 * D:3 * D], query_all[..., :D])))
    query_ent = low_back(reduced_precision(jnp.where(is_entity, query_all[..., 3 * D:], query_all[..., D:2 * D])))
    key_val = project(inputs, kv_weight)
    key_rows = low_back(reduced_precision(key_val[..., :D]))
    val_rows = low_back(reduced_precision(key_val[..., D:] + value_bias))
    key_entity = (entity > 0)[:, None, :]
    same_doc = seg_ids[:, :, None] == seg_ids[:, None, :]
    score_scale = HEAD_DIM ** (-0.5)

    def per_head(head_data):
        word_query_head, entity_query_head, key_head_rows, value_head_rows = head_data
        word_score_matrix = jnp.einsum('urs,uas->ura', word_query_head, key_head_rows, precision=TOP_PRECISION)
        entity_score_matrix = jnp.einsum('urs,uas->ura', entity_query_head, key_head_rows, precision=TOP_PRECISION)
        scores = low_back(score_scale * jnp.where(key_entity, entity_score_matrix, word_score_matrix))
        scores = jnp.where(same_doc, scores, MASKED)
        row_top = lax.optimization_barrier(jnp.max(scores, axis=-1, keepdims=True))
        weights = jnp.exp(scores - row_top)
        attention_probs = weights / lax.optimization_barrier(jnp.sum(weights, axis=-1, keepdims=True))
        return jnp.einsum('psn,png->psg', reduced_precision(attention_probs), value_head_rows, precision=TOP_PRECISION)

    def split_heads(values):
        return jnp.transpose(values.reshape(blocks, L, HEADS, HEAD_DIM), (2, 0, 1, 3))
    mixed_heads = lax.map(jax.checkpoint(per_head), (split_heads(query_word), split_heads(query_ent), split_heads(key_rows), split_heads(val_rows)))
    attended = low_back(reduced_precision(jnp.transpose(mixed_heads, (1, 2, 0, 3)).reshape(blocks, L, D)))
    attn_out = low_back(project(attended, out_weight) + out_bias)
    hidden = normalize(inputs + attn_out, gain_one, shift_one)
    up_proj = low_back(project(reduced_precision(hidden), up_weight) + up_bias)
    act_low = reduced_precision(jax.nn.gelu(up_proj, approximate=False))
    ffn_out = low_back(project(act_low, down_weight) + down_bias)
    return normalize(hidden + ffn_out, gain_two, shift_two)

def reference(inputs, query_weight, kv_weight, out_weight, up_weight, down_weight, query_bias, value_bias, out_bias, up_bias, down_bias, norm1_gain, norm1_shift, norm2_gain, norm2_shift, types, lengths, cotangent):
    params = tuple((param.astype(jnp.float32) for param in (query_weight, kv_weight, out_weight, up_weight, down_weight, query_bias, value_bias, out_bias, up_bias, down_bias, norm1_gain, norm1_shift, norm2_gain, norm2_shift)))
    halves = ROWS // 2
    scan_data = (inputs.astype(jnp.float32).reshape(halves, 2, L, D), types.reshape(halves, 2, L), lengths.reshape(halves, 2, DOCS), cotangent.astype(jnp.float32).reshape(halves, 2, L, D))

    def scan_step(grad_totals, block_data):
        block_in, block_types, block_lengths, block_cot = block_data
        seg_ids = segments(block_lengths)

        def forward(values_in, *weights_in):
            return layer_block(values_in, *weights_in, block_types, seg_ids)
        result, pull_back = jax.vjp(forward, block_in, *params)
        grads = pull_back(block_cot)
        new_totals = tuple((grad_sum + grad_new for grad_sum, grad_new in zip(grad_totals, grads[1:])))
        return (new_totals, (result.astype(jnp.bfloat16), grads[0].astype(jnp.bfloat16)))
    zero_totals = tuple((jnp.zeros_like(param) for param in params))
    grad_totals, (results, input_grads) = lax.scan(scan_step, zero_totals, scan_data)
    return (results.reshape(ROWS, L, D), input_grads.reshape(ROWS, L, D), grad_totals[0], grad_totals[1], grad_totals[2], grad_totals[3], grad_totals[4], grad_totals[5], grad_totals[6], grad_totals[7], grad_totals[8], grad_totals[9], grad_totals[10], grad_totals[11], grad_totals[12], grad_totals[13])
```

```python
import functools

import jax
import jax.numpy as jnp
from jax import lax
from jax.experimental import pallas as pl
from jax.experimental.pallas import tpu as pltpu
from jax.sharding import Mesh
from jax.sharding import PartitionSpec as P

HEADS = 12
EPSILON = 1e-05
BLOCKED = -1e30
BF = jnp.bfloat16
F32 = jnp.float32
LANES = 128
CHUNK = 16


def matmul(left_mat, right_mat):
    return jnp.dot(left_mat, right_mat, preferred_element_type=F32)


def rows_inner(left_mat, right_mat):
    return lax.dot_general(left_mat, right_mat, (((0,), (0,)), ((), ())), preferred_element_type=F32)


def times_transposed(left_mat, right_mat):
    return lax.dot_general(left_mat, right_mat, (((1,), (1,)), ((), ())), preferred_element_type=F32)


def normalize(values, gain_vec, shift_vec):
    center = values - jnp.mean(values, axis=-1, keepdims=True)
    scale_inv = lax.rsqrt(jnp.mean(center * center, axis=-1, keepdims=True) + EPSILON)
    normed = center * scale_inv
    return (normed * gain_vec + shift_vec, normed, scale_inv)


def normalize_back(grad_in, normed, scale_inv, gain_vec):
    scaled = grad_in * gain_vec
    inner_part = (
        scaled
        - jnp.mean(scaled, axis=-1, keepdims=True)
        - normed * jnp.mean(scaled * normed, axis=-1, keepdims=True)
    )
    return (inner_part * scale_inv, jnp.sum(grad_in * normed, axis=0), jnp.sum(grad_in, axis=0))


def column_sum(values):
    return jnp.sum(values.astype(F32), axis=0)


def forward_kernel(
    heads, hd, rows_ref, w_ref, bias_ref, ent_ref, qseg_ref, kseg_ref,
    att_ref, wts_ref, inv_ref, qcat_ref, kcat_ref, vneg_ref,
    kaug_s, vaug_s, score_s,
):
    step = pl.program_id(0)
    span = heads * hd
    full = rows_ref.shape[0]
    block = att_ref.shape[0]
    scale = hd ** (-0.5)

    @pl.when(step == 0)
    def _():
        kaug_s[:, :, LANES:] = jnp.broadcast_to(kseg_ref[...][None], (heads, full, LANES))
        lane = lax.broadcasted_iota(jnp.int32, (block, LANES - hd), 1)
        one_col = jnp.where(lane == 0, 1.0, 0.0).astype(BF)
        neg_col = jnp.where(lane < 2, -1.0, 0.0).astype(BF)

        def project(piece, carry):
            at = pl.ds(pl.multiple_of(piece * block, block), block)
            rows = rows_ref[at, :]
            ent = ent_ref[at, :hd]
            wide = ent_ref[at, :1] > 0
            word = (1 - ent).astype(BF)

            def part(index):
                cols = slice(index * span, (index + 1) * span)
                return jnp.dot(rows, w_ref[:, cols], preferred_element_type=F32) + bias_ref[:, cols]

            q_word = (jnp.where(wide, part(2), part(0))).astype(BF) * BF(scale)
            q_ent = (jnp.where(wide, part(3), part(1))).astype(BF) * BF(scale)
            keys = part(4).astype(BF)
            vals = part(5).astype(BF)
            for h in range(heads):
                cut = slice(h * hd, (h + 1) * hd)
                qcat_ref[h, at, :] = jnp.concatenate([q_word[:, cut], q_ent[:, cut]], axis=1)
                k_pair = jnp.concatenate([keys[:, cut] * word, keys[:, cut] * ent], axis=1)
                kcat_ref[h, at, :] = k_pair
                kaug_s[h, at, :LANES] = k_pair
                vneg_ref[h, at, :] = jnp.concatenate([vals[:, cut], neg_col], axis=1)
                vaug_s[h, at, :] = jnp.concatenate([vals[:, cut], one_col], axis=1)
            return carry

        lax.fori_loop(0, full // block, project, 0)

    here = pl.ds(pl.multiple_of(step * block, block), block)
    q_seg = qseg_ref[here, :]
    lane = lax.broadcasted_iota(jnp.int32, (block, LANES), 1)
    inv_all = jnp.zeros((block, LANES), F32)
    mixed = []
    for h in range(heads):
        q_aug = jnp.concatenate([qcat_ref[h, here, :], q_seg], axis=1)
        score_s[h % 2] = lax.dot_general(
            q_aug, kaug_s[h], (((1,), (1,)), ((), ())), preferred_element_type=F32
        )
        for r in range(0, block, CHUNK):
            s = score_s[h % 2, r : r + CHUNK, :]
            top = jnp.max(s, axis=1, keepdims=True)
            wts_ref[h, r : r + CHUNK, :] = jnp.exp(s - top).astype(BF)
        out = jnp.dot(wts_ref[h], vaug_s[h], preferred_element_type=F32)
        inv = 1.0 / out[:, hd : hd + 1]
        inv_all = jnp.where(lane == h, inv, inv_all)
        mixed.append((out[:, :hd] * inv).astype(BF))
    att_ref[...] = jnp.concatenate(mixed, axis=1)
    inv_ref[...] = inv_all


def attention_forward(rows, w_sel, bias_sel, ent, qseg, kseg, heads, hd):
    full, width = rows.shape
    block = min(256, full)
    span = heads * hd
    steps = full // block
    whole = lambda *dims: pl.BlockSpec(dims, lambda i: (0,) * len(dims))
    return pl.pallas_call(
        functools.partial(forward_kernel, heads, hd),
        grid=(steps,),
        in_specs=[
            whole(full, width),
            whole(width, 6 * span),
            whole(1, 6 * span),
            whole(full, LANES),
            whole(full, LANES),
            whole(full, LANES),
        ],
        out_specs=[
            pl.BlockSpec((block, span), lambda i: (i, 0)),
            pl.BlockSpec((heads, block, full), lambda i: (0, i, 0)),
            pl.BlockSpec((block, LANES), lambda i: (i, 0)),
            whole(heads, full, 2 * hd),
            whole(heads, full, 2 * hd),
            whole(heads, full, LANES),
        ],
        out_shape=[
            jax.ShapeDtypeStruct((full, span), BF),
            jax.ShapeDtypeStruct((heads, full, full), BF),
            jax.ShapeDtypeStruct((full, LANES), F32),
            jax.ShapeDtypeStruct((heads, full, 2 * hd), BF),
            jax.ShapeDtypeStruct((heads, full, 2 * hd), BF),
            jax.ShapeDtypeStruct((heads, full, LANES), BF),
        ],
        scratch_shapes=[
            pltpu.VMEM((heads, full, 2 * LANES), BF),
            pltpu.VMEM((heads, full, LANES), BF),
            pltpu.VMEM((2, block, full), F32),
        ],
        compiler_params=pltpu.CompilerParams(vmem_limit_bytes=60 << 20),
        cost_estimate=pl.CostEstimate(
            flops=2 * full * width * 6 * span + 8 * heads * full * full * LANES,
            bytes_accessed=2 * heads * full * full + 10 * full * width,
            transcendentals=heads * full * full,
        ),
        name="attention_forward",
    )(rows, w_sel, bias_sel, ent, qseg, kseg)


def backward_kernel(
    heads, hd, go_ref, att_ref, inv_ref, wts_ref, qcat_ref, kcat_ref, vneg_ref, ent_ref, entb_ref,
    gq_ref, gkv_ref, gscore_s, low_s, gk_s, gv_s,
):
    step = pl.program_id(0)
    span = heads * hd
    block = go_ref.shape[0]
    full = kcat_ref.shape[1]
    scale = hd ** (-0.5)
    lane = lax.broadcasted_iota(jnp.int32, (block, LANES - hd), 1)
    is_ent = entb_ref[:, :1] > 0
    g_word, g_ent = [], []
    for h in range(heads):
        cut = slice(h * hd, (h + 1) * hd)
        g_low = (go_ref[:, cut].astype(F32) * inv_ref[:, h : h + 1]).astype(BF)
        delta = jnp.sum(g_low.astype(F32) * att_ref[:, cut].astype(F32), axis=1, keepdims=True)
        d_hi = delta.astype(BF)
        d_lo = (delta - d_hi.astype(F32)).astype(BF)
        extra = jnp.where(
            lane == 0, d_hi.astype(F32), jnp.where(lane == 1, d_lo.astype(F32), 0.0)
        ).astype(BF)
        g_aug = jnp.concatenate([g_low, extra], axis=1)
        gscore_s[h % 2] = lax.dot_general(
            g_aug, vneg_ref[h], (((1,), (1,)), ((), ())), preferred_element_type=F32
        )
        for r in range(0, block, CHUNK):
            low_s[h % 2, r : r + CHUNK, :] = (
                wts_ref[h, r : r + CHUNK, :].astype(F32) * gscore_s[h % 2, r : r + CHUNK, :]
            ).astype(BF)
        g_q = jnp.dot(low_s[h % 2], kcat_ref[h], preferred_element_type=F32) * scale
        g_word.append(g_q[:, :hd])
        g_ent.append(g_q[:, hd:])
        g_k = lax.dot_general(
            qcat_ref[h], low_s[h % 2], (((0,), (0,)), ((), ())), preferred_element_type=F32
        )
        g_v = lax.dot_general(
            g_low, wts_ref[h], (((0,), (0,)), ((), ())), preferred_element_type=F32
        )

        @pl.when(step == 0)
        def _(h=h, g_k=g_k, g_v=g_v):
            gk_s[h] = g_k
            gv_s[h] = g_v

        @pl.when(step > 0)
        def _(h=h, g_k=g_k, g_v=g_v):
            gk_s[h] += g_k
            gv_s[h] += g_v

    g_word = jnp.concatenate(g_word, axis=1)
    g_ent = jnp.concatenate(g_ent, axis=1)
    gq_ref[:, :span] = jnp.where(is_ent, 0.0, g_word).astype(BF)
    gq_ref[:, span : 2 * span] = jnp.where(is_ent, 0.0, g_ent).astype(BF)
    gq_ref[:, 2 * span : 3 * span] = jnp.where(is_ent, g_word, 0.0).astype(BF)
    gq_ref[:, 3 * span :] = jnp.where(is_ent, g_ent, 0.0).astype(BF)

    @pl.when(step == pl.num_programs(0) - 1)
    def _():
        def close(piece, carry):
            at = pl.ds(pl.multiple_of(piece * block, block), block)
            pick = ent_ref[at, :1] > 0
            g_keys, g_vals = [], []
            for h in range(heads):
                both = gk_s[h, :, at].T
                g_keys.append(jnp.where(pick, both[:, hd:], both[:, :hd]))
                g_vals.append(gv_s[h, :, at].T)
            gkv_ref[at, :span] = jnp.concatenate(g_keys, axis=1).astype(BF)
            gkv_ref[at, span:] = jnp.concatenate(g_vals, axis=1).astype(BF)
            return carry

        lax.fori_loop(0, full // block, close, 0)


def attention_backward(g_out, att, inv, wts, qcat, kcat, vneg, ent, heads, hd):
    full, span = att.shape
    block = min(256, full)
    whole = lambda *dims: pl.BlockSpec(dims, lambda i: (0,) * len(dims))
    by_rows = lambda width: pl.BlockSpec((block, width), lambda i: (i, 0))
    by_head = lambda width: pl.BlockSpec((heads, block, width), lambda i: (0, i, 0))
    return pl.pallas_call(
        functools.partial(backward_kernel, heads, hd),
        grid=(full // block,),
        in_specs=[
            by_rows(span),
            by_rows(span),
            by_rows(LANES),
            by_head(full),
            by_head(2 * hd),
            whole(heads, full, 2 * hd),
            whole(heads, full, LANES),
            whole(full, LANES),
            by_rows(LANES),
        ],
        out_specs=[by_rows(4 * span), whole(full, 2 * span)],
        out_shape=[
            jax.ShapeDtypeStruct((full, 4 * span), BF),
            jax.ShapeDtypeStruct((full, 2 * span), BF),
        ],
        scratch_shapes=[
            pltpu.VMEM((2, block, full), F32),
            pltpu.VMEM((2, block, full), BF),
            pltpu.VMEM((heads, 2 * hd, full), F32),
            pltpu.VMEM((heads, hd, full), F32),
        ],
        compiler_params=pltpu.CompilerParams(vmem_limit_bytes=60 << 20),
        cost_estimate=pl.CostEstimate(
            flops=16 * heads * full * full * LANES,
            bytes_accessed=2 * heads * full * full + 20 * full * span,
            transcendentals=0,
        ),
        name="attention_backward",
    )(g_out, att, inv, wts, qcat, kcat, vneg, ent, ent)


def layer(
    half, per_row, inputs, query_weight, kv_weight, out_weight, up_weight, down_weight,
    query_bias, value_bias, out_bias, up_bias, down_bias,
    norm1_gain, norm1_shift, norm2_gain, norm2_shift, types, lengths, cotangent,
):
    rows_here, span, width = inputs.shape
    head_dim = width // HEADS
    full = types.shape[1]
    members = 2 * per_row
    heads = HEADS // members
    cols = heads * head_dim
    row_count = lax.axis_size("row")
    outer = lax.axis_size("outer")
    core = lax.axis_index("core")
    group = lax.axis_index("group")
    member = group * 2 + core
    row_id = lax.axis_index("row")
    own = row_count * (span // 2)

    def swap(values):
        return lax.ppermute(values, "core", [(0, 1), (1, 0)])

    def in_order(index, mine, other):
        return jnp.stack([jnp.where(index == 0, mine, other), jnp.where(index == 0, other, mine)])

    def gather_outer(values):
        if outer == 2:
            other = lax.ppermute(values, "outer", [(0, 1), (1, 0)])
            return in_order(lax.axis_index("outer"), values, other)
        return lax.all_gather(values, "outer", axis=0, tiled=False)

    def gather_members(values):
        pair = in_order(core, values, swap(values))
        if per_row == 1:
            return pair
        spread = lax.all_gather(pair, "group", axis=0, tiled=False)
        return spread.reshape((members,) + values.shape)

    def exchange_members(values):
        if per_row == 1:
            mine = lax.dynamic_index_in_dim(values, core, 0, keepdims=False)
            away = lax.dynamic_index_in_dim(values, 1 - core, 0, keepdims=False)
            return in_order(core, mine, swap(away))
        return lax.all_to_all(values, ("group", "core"), 0, 0, tiled=True)

    def take(values, index, axis):
        return lax.dynamic_index_in_dim(values, index, axis, keepdims=False)

    def to_row(values):
        pieces = values.reshape(rows_here, 2, span // 2, width)
        other = swap(take(pieces, 1 - core, 1))
        both = in_order(core, take(pieces, core, 1), other).reshape(row_count, span // 2, width)
        return lax.all_to_all(both, "row", 0, 0, tiled=True).reshape(own, width)

    def from_row(values):
        back = lax.all_to_all(values.reshape(row_count, span // 2, width), "row", 0, 0, tiled=True)
        back = back.reshape(2, rows_here, span // 2, width)
        other = swap(take(back, 1 - core, 0))
        both = in_order(core, take(back, core, 0), other)
        return both.transpose(1, 0, 2, 3).reshape(rows_here, span, width)

    own_rows = to_row(inputs)
    all_rows = gather_members(own_rows).reshape(full, width)

    tags = jnp.concatenate([types, lengths], axis=1)
    tags = in_order(core, tags, swap(tags)).reshape(row_count, -1)
    tags = take(tags, row_id, 0)
    types_row, lengths_row = tags[:full], tags[full:]

    def by_member(values):
        return values.reshape(row_count, per_row, 2, span // 2).transpose(1, 2, 0, 3).reshape(full)

    entity = by_member(types_row) > 0
    positions = by_member(lax.iota(jnp.int32, full))
    docs = lengths_row.shape[0]
    ends = [jnp.sum(lengths_row[: d + 1]) for d in range(docs)]
    seg = sum((positions >= end).astype(jnp.int32) for end in ends)
    lanes = lax.broadcasted_iota(jnp.int32, (full, LANES), 1)
    same = lanes == seg[:, None]
    qseg = jnp.where(same, 1.0, 0.0).astype(BF)
    kseg = jnp.where(same | (lanes >= docs), 0.0, BLOCKED).astype(BF)
    ent = jnp.broadcast_to(jnp.where(entity, 1.0, 0.0).astype(BF)[:, None], (full, LANES))

    shard = query_weight.shape[0]
    cut = jnp.concatenate([query_weight, kv_weight], axis=1).reshape(shard, 6, members, cols)
    away = take(cut, group * 2 + 1 - core, 2).reshape(shard, 6 * cols)
    mine = take(cut, member, 2).reshape(shard, 6 * cols)
    w_sel = gather_outer(in_order(core, mine, swap(away))).reshape(width, 6 * cols)

    vectors = (
        query_bias, value_bias, out_bias, up_bias, down_bias,
        norm1_gain, norm1_shift, norm2_gain, norm2_shift,
    )
    sizes = [v.shape[0] for v in vectors]
    packed = jnp.concatenate(vectors)
    packed = lax.all_gather(packed, ("outer", "core"), axis=0, tiled=False)
    offsets = [sum(sizes[:i]) for i in range(len(sizes) + 1)]
    (b_query, b_value, b_out, b_up, b_down, g_one, s_one, g_two, s_two) = (
        packed[:, a:b].reshape(-1).astype(F32) for a, b in zip(offsets[:-1], offsets[1:])
    )
    b_six = jnp.concatenate([b_query, jnp.zeros((width,), F32), b_value])
    b_sel = take(b_six.reshape(6, members, cols), member, 1).reshape(1, 6 * cols)

    att, inv_stored, wts = None, None, None
    att, wts, inv_stored, qcat, kcat, vneg = attention_forward(
        all_rows, w_sel, b_sel, ent, qseg, kseg, heads, head_dim
    )

    def fetch(values):
        return gather_outer(in_order(core, values, swap(values))).reshape(-1, values.shape[1])

    w_out, w_up, w_down = fetch(out_weight), fetch(up_weight), fetch(down_weight)

    def heads_to_tokens(values):
        got = exchange_members(values.reshape(members, own, cols))
        return got.transpose(1, 0, 2).reshape(own, width)

    def tokens_to_heads(values):
        parts = values.reshape(own, members, cols).transpose(1, 0, 2)
        return exchange_members(parts).reshape(full, cols)

    attended = heads_to_tokens(att)
    attn_out = matmul(attended, w_out) + b_out
    hidden, normed_one, inv_one = normalize(own_rows.astype(F32) + attn_out, g_one, s_one)
    hidden_low = hidden.astype(BF)
    up_proj = matmul(hidden_low, w_up) + b_up
    gelu_out, gelu_pull = jax.vjp(lambda v: jax.nn.gelu(v, approximate=False), up_proj)
    act_low = gelu_out.astype(BF)
    ffn_out = matmul(act_low, w_down) + b_down
    result, normed_two, inv_two = normalize(hidden + ffn_out, g_two, s_two)
    output = from_row(result.astype(BF))

    cot = to_row(cotangent).astype(F32)
    grad_y2, grad_g2, grad_s2 = normalize_back(cot, normed_two, inv_two, g_two)
    grad_ffn = grad_y2.astype(BF)
    grad_act = times_transposed(grad_ffn, w_down)
    grad_up = gelu_pull(grad_act)[0].astype(BF)
    grad_hidden = grad_y2 + times_transposed(grad_up, w_up)
    grad_y1, grad_g1, grad_s1 = normalize_back(grad_hidden, normed_one, inv_one, g_one)
    grad_attn = grad_y1.astype(BF)
    grad_attended = times_transposed(grad_attn, w_out).astype(BF)

    def pick_rows(left, core_index, outer_index):
        parts = left.reshape(left.shape[0], outer, 2, -1)
        if outer_index is None:
            return take(parts, core_index, 2).reshape(left.shape[0], -1)
        return take(take(parts, core_index, 2), outer_index, 1)

    def reduce_outer(partial):
        if outer == 2:
            me = lax.axis_index("outer")
            other = lax.ppermute(take(partial, 1 - me, 0).astype(BF), "outer", [(0, 1), (1, 0)])
            return take(partial, me, 0).astype(F32) + other.astype(F32)
        return lax.psum_scatter(partial.astype(BF), "outer", scatter_dimension=0, tiled=False).astype(F32)

    def shard_grad(left, right):
        away = rows_inner(pick_rows(left, 1 - core, None), right).astype(BF)
        mine = rows_inner(pick_rows(left, core, None), right)
        pair = mine + swap(away).astype(F32)
        part = reduce_outer(pair.reshape(outer, -1, right.shape[1]))
        return lax.psum(part.astype(BF), ("row", "group")).astype(F32)

    g_w_down = shard_grad(act_low, grad_ffn)
    g_w_up = shard_grad(hidden_low, grad_up)
    g_w_out = shard_grad(attended, grad_attn)

    gq, gkv = attention_backward(
        tokens_to_heads(grad_attended), att, inv_stored, wts, qcat, kcat, vneg, ent, heads, head_dim
    )
    g_six = jnp.concatenate([gq, gkv], axis=1)
    g_sel = reduce_outer(rows_inner(all_rows, g_six).reshape(outer, -1, 6 * cols))
    g_sel = lax.psum(g_sel.astype(BF), "row").reshape(2, shard, 6, cols)
    got = in_order(core, take(g_sel, core, 0), swap(take(g_sel, 1 - core, 0)))
    if per_row > 1:
        got = lax.all_gather(got, "group", axis=0, tiled=False)
    got = got.reshape(members, shard, 6, cols).transpose(1, 2, 0, 3).reshape(shard, 6 * width)
    g_w_query = got[:, : 4 * width].astype(F32)
    g_w_kv = got[:, 4 * width :].astype(F32)

    part_in = times_transposed(g_six, w_sel)
    got_in = exchange_members(part_in.astype(BF).reshape(members, own, width))
    grad_in = grad_y1 + jnp.sum(got_in.astype(F32), axis=0)
    input_grad = from_row(grad_in.astype(BF))

    six_sum = column_sum(g_six).reshape(6, 1, cols)
    spot = lax.broadcasted_iota(jnp.int32, (1, members, 1), 1) == member
    six_sum = jnp.where(spot, six_sum, 0.0).reshape(6, width)
    small = [
        six_sum[:4].reshape(-1), six_sum[5], column_sum(grad_attn), column_sum(grad_up),
        column_sum(grad_ffn), grad_g1, grad_s1, grad_g2, grad_s2,
    ]
    total = lax.psum(jnp.concatenate(small), ("row", "group", "outer", "core"))
    me = lax.axis_index("outer") * 2 + core
    pieces, at = [], 0
    for size in sizes:
        whole_size = size * outer * 2
        pieces.append(lax.dynamic_slice_in_dim(total[at : at + whole_size], me * size, size))
        at += whole_size
    return (output, input_grad, g_w_query, g_w_kv, g_w_out, g_w_up, g_w_down, *pieces)


def solution(mesh):
    def step(*args):
        ctx, fsdp = mesh.shape["ctx"], mesh.shape["fsdp"]
        row_count = args[0].shape[0] // (fsdp // 2)
        per_row = ctx // row_count
        fine = Mesh(
            mesh.devices.reshape(row_count, per_row, fsdp // 2, 2), ("row", "group", "outer", "core")
        )
        tokens = P(("outer", "core"), ("row", "group"), None)
        mat, vec = P(("outer", "core"), None), P(("outer", "core"))
        in_specs = (tokens, *[mat] * 5, *[vec] * 9, mat, mat, tokens)
        out_specs = (tokens, tokens, *[mat] * 5, *[vec] * 9)
        body = functools.partial(layer, None, per_row)
        return jax.shard_map(
            body, mesh=fine, in_specs=in_specs, out_specs=out_specs, check_vma=False
        )(*args)

    return step
```

```python
import functools

import jax
import jax.numpy as jnp
from jax import lax
from jax.experimental import pallas as pl
from jax.experimental.pallas import tpu as pltpu
from jax.sharding import Mesh
from jax.sharding import PartitionSpec as P

HEADS = 12
EPSILON = 1e-05
BLOCKED = -1e30
BF = jnp.bfloat16
F32 = jnp.float32
LANES = 128
CHUNK = 16


def matmul(left_mat, right_mat):
    return jnp.dot(left_mat, right_mat, preferred_element_type=F32)


def rows_inner(left_mat, right_mat):
    return lax.dot_general(left_mat, right_mat, (((0,), (0,)), ((), ())), preferred_element_type=F32)


def times_transposed(left_mat, right_mat):
    return lax.dot_general(left_mat, right_mat, (((1,), (1,)), ((), ())), preferred_element_type=F32)


def normalize(values, gain_vec, shift_vec):
    center = values - jnp.mean(values, axis=-1, keepdims=True)
    scale_inv = lax.rsqrt(jnp.mean(center * center, axis=-1, keepdims=True) + EPSILON)
    normed = center * scale_inv
    return (normed * gain_vec + shift_vec, normed, scale_inv)


def normalize_back(grad_in, normed, scale_inv, gain_vec):
    scaled = grad_in * gain_vec
    inner_part = (
        scaled
        - jnp.mean(scaled, axis=-1, keepdims=True)
        - normed * jnp.mean(scaled * normed, axis=-1, keepdims=True)
    )
    return (inner_part * scale_inv, jnp.sum(grad_in * normed, axis=0), jnp.sum(grad_in, axis=0))


def column_sum(values):
    return jnp.sum(values.astype(F32), axis=0)


def forward_kernel(
    heads, hd, rows_ref, w_ref, bias_ref, ent_ref, qseg_ref, kseg_ref,
    att_ref, wts_ref, inv_ref, qcat_ref, kcat_ref, vneg_ref,
    kaug_s, vaug_s, score_s,
):
    step = pl.program_id(0)
    span = heads * hd
    full = rows_ref.shape[0]
    block = att_ref.shape[0]
    scale = hd ** (-0.5)

    @pl.when(step == 0)
    def _():
        kaug_s[:, :, LANES:] = jnp.broadcast_to(kseg_ref[...][None], (heads, full, LANES))
        lane = lax.broadcasted_iota(jnp.int32, (block, LANES - hd), 1)
        one_col = jnp.where(lane == 0, 1.0, 0.0).astype(BF)
        neg_col = jnp.where(lane < 2, -1.0, 0.0).astype(BF)

        def project(piece, carry):
            at = pl.ds(pl.multiple_of(piece * block, block), block)
            rows = rows_ref[at, :]
            ent = ent_ref[at, :hd]
            wide = ent_ref[at, :1] > 0
            word = (1 - ent).astype(BF)

            def part(index):
                cols = slice(index * span, (index + 1) * span)
                return jnp.dot(rows, w_ref[:, cols], preferred_element_type=F32) + bias_ref[:, cols]

            q_word = (jnp.where(wide, part(2), part(0))).astype(BF) * BF(scale)
            q_ent = (jnp.where(wide, part(3), part(1))).astype(BF) * BF(scale)
            keys = part(4).astype(BF)
            vals = part(5).astype(BF)
            for h in range(heads):
                cut = slice(h * hd, (h + 1) * hd)
                qcat_ref[h, at, :] = jnp.concatenate([q_word[:, cut], q_ent[:, cut]], axis=1)
                k_pair = jnp.concatenate([keys[:, cut] * word, keys[:, cut] * ent], axis=1)
                kcat_ref[h, at, :] = k_pair
                kaug_s[h, at, :LANES] = k_pair
                vneg_ref[h, at, :] = jnp.concatenate([vals[:, cut], neg_col], axis=1)
                vaug_s[h, at, :] = jnp.concatenate([vals[:, cut], one_col], axis=1)
            return carry

        lax.fori_loop(0, full // block, project, 0)

    here = pl.ds(pl.multiple_of(step * block, block), block)
    q_seg = qseg_ref[here, :]
    lane = lax.broadcasted_iota(jnp.int32, (block, LANES), 1)
    inv_all = jnp.zeros((block, LANES), F32)
    mixed = []
    for h in range(heads):
        q_aug = jnp.concatenate([qcat_ref[h, here, :], q_seg], axis=1)
        score_s[h % 2] = lax.dot_general(
            q_aug, kaug_s[h], (((1,), (1,)), ((), ())), preferred_element_type=F32
        )
        for r in range(0, block, CHUNK):
            s = score_s[h % 2, r : r + CHUNK, :]
            top = jnp.max(s, axis=1, keepdims=True)
            wts_ref[h, r : r + CHUNK, :] = jnp.exp(s - top).astype(BF)
        out = jnp.dot(wts_ref[h], vaug_s[h], preferred_element_type=F32)
        inv = 1.0 / out[:, hd : hd + 1]
        inv_all = jnp.where(lane == h, inv, inv_all)
        mixed.append((out[:, :hd] * inv).astype(BF))
    att_ref[...] = jnp.concatenate(mixed, axis=1)
    inv_ref[...] = inv_all


def attention_forward(rows, w_sel, bias_sel, ent, qseg, kseg, heads, hd):
    full, width = rows.shape
    block = min(256, full)
    span = heads * hd
    steps = full // block
    whole = lambda *dims: pl.BlockSpec(dims, lambda i: (0,) * len(dims))
    return pl.pallas_call(
        functools.partial(forward_kernel, heads, hd),
        grid=(steps,),
        in_specs=[
            whole(full, width),
            whole(width, 6 * span),
            whole(1, 6 * span),
            whole(full, LANES),
            whole(full, LANES),
            whole(full, LANES),
        ],
        out_specs=[
            pl.BlockSpec((block, span), lambda i: (i, 0)),
            pl.BlockSpec((heads, block, full), lambda i: (0, i, 0)),
            pl.BlockSpec((block, LANES), lambda i: (i, 0)),
            whole(heads, full, 2 * hd),
            whole(heads, full, 2 * hd),
            whole(heads, full, LANES),
        ],
        out_shape=[
            jax.ShapeDtypeStruct((full, span), BF),
            jax.ShapeDtypeStruct((heads, full, full), BF),
            jax.ShapeDtypeStruct((full, LANES), F32),
            jax.ShapeDtypeStruct((heads, full, 2 * hd), BF),
            jax.ShapeDtypeStruct((heads, full, 2 * hd), BF),
            jax.ShapeDtypeStruct((heads, full, LANES), BF),
        ],
        scratch_shapes=[
            pltpu.VMEM((heads, full, 2 * LANES), BF),
            pltpu.VMEM((heads, full, LANES), BF),
            pltpu.VMEM((2, block, full), F32),
        ],
        compiler_params=pltpu.CompilerParams(vmem_limit_bytes=60 << 20),
        cost_estimate=pl.CostEstimate(
            flops=2 * full * width * 6 * span + 8 * heads * full * full * LANES,
            bytes_accessed=2 * heads * full * full + 10 * full * width,
            transcendentals=heads * full * full,
        ),
        name="attention_forward",
    )(rows, w_sel, bias_sel, ent, qseg, kseg)


def backward_kernel(
    heads, hd, go_ref, att_ref, inv_ref, wts_ref, qcat_ref, kcat_ref, vneg_ref, ent_ref, entb_ref,
    gq_ref, gkv_ref, gscore_s, low_s, gk_s, gv_s,
):
    step = pl.program_id(0)
    span = heads * hd
    block = go_ref.shape[0]
    full = kcat_ref.shape[1]
    scale = hd ** (-0.5)
    lane = lax.broadcasted_iota(jnp.int32, (block, LANES - hd), 1)
    is_ent = entb_ref[:, :1] > 0
    g_word, g_ent = [], []
    for h in range(heads):
        cut = slice(h * hd, (h + 1) * hd)
        g_low = (go_ref[:, cut].astype(F32) * inv_ref[:, h : h + 1]).astype(BF)
        delta = jnp.sum(g_low.astype(F32) * att_ref[:, cut].astype(F32), axis=1, keepdims=True)
        d_hi = delta.astype(BF)
        d_lo = (delta - d_hi.astype(F32)).astype(BF)
        extra = jnp.where(
            lane == 0, d_hi.astype(F32), jnp.where(lane == 1, d_lo.astype(F32), 0.0)
        ).astype(BF)
        g_aug = jnp.concatenate([g_low, extra], axis=1)
        gscore_s[h % 2] = lax.dot_general(
            g_aug, vneg_ref[h], (((1,), (1,)), ((), ())), preferred_element_type=F32
        )
        for r in range(0, block, CHUNK):
            low_s[h % 2, r : r + CHUNK, :] = (
                wts_ref[h, r : r + CHUNK, :].astype(F32) * gscore_s[h % 2, r : r + CHUNK, :]
            ).astype(BF)
        g_q = jnp.dot(low_s[h % 2], kcat_ref[h], preferred_element_type=F32) * scale
        g_word.append(g_q[:, :hd])
        g_ent.append(g_q[:, hd:])
        g_k = lax.dot_general(
            qcat_ref[h], low_s[h % 2], (((0,), (0,)), ((), ())), preferred_element_type=F32
        )
        g_v = lax.dot_general(
            g_low, wts_ref[h], (((0,), (0,)), ((), ())), preferred_element_type=F32
        )

        @pl.when(step == 0)
        def _(h=h, g_k=g_k, g_v=g_v):
            gk_s[h] = g_k
            gv_s[h] = g_v

        @pl.when(step > 0)
        def _(h=h, g_k=g_k, g_v=g_v):
            gk_s[h] += g_k
            gv_s[h] += g_v

    g_word = jnp.concatenate(g_word, axis=1)
    g_ent = jnp.concatenate(g_ent, axis=1)
    gq_ref[:, :span] = jnp.where(is_ent, 0.0, g_word).astype(BF)
    gq_ref[:, span : 2 * span] = jnp.where(is_ent, 0.0, g_ent).astype(BF)
    gq_ref[:, 2 * span : 3 * span] = jnp.where(is_ent, g_word, 0.0).astype(BF)
    gq_ref[:, 3 * span :] = jnp.where(is_ent, g_ent, 0.0).astype(BF)

    @pl.when(step == pl.num_programs(0) - 1)
    def _():
        def close(piece, carry):
            at = pl.ds(pl.multiple_of(piece * block, block), block)
            pick = ent_ref[at, :1] > 0
            g_keys, g_vals = [], []
            for h in range(heads):
                both = gk_s[h, :, at].T
                g_keys.append(jnp.where(pick, both[:, hd:], both[:, :hd]))
                g_vals.append(gv_s[h, :, at].T)
            gkv_ref[at, :span] = jnp.concatenate(g_keys, axis=1).astype(BF)
            gkv_ref[at, span:] = jnp.concatenate(g_vals, axis=1).astype(BF)
            return carry

        lax.fori_loop(0, full // block, close, 0)


def attention_backward(g_out, att, inv, wts, qcat, kcat, vneg, ent, heads, hd):
    full, span = att.shape
    block = min(256, full)
    whole = lambda *dims: pl.BlockSpec(dims, lambda i: (0,) * len(dims))
    by_rows = lambda width: pl.BlockSpec((block, width), lambda i: (i, 0))
    by_head = lambda width: pl.BlockSpec((heads, block, width), lambda i: (0, i, 0))
    return pl.pallas_call(
        functools.partial(backward_kernel, heads, hd),
        grid=(full // block,),
        in_specs=[
            by_rows(span),
            by_rows(span),
            by_rows(LANES),
            by_head(full),
            by_head(2 * hd),
            whole(heads, full, 2 * hd),
            whole(heads, full, LANES),
            whole(full, LANES),
            by_rows(LANES),
        ],
        out_specs=[by_rows(4 * span), whole(full, 2 * span)],
        out_shape=[
            jax.ShapeDtypeStruct((full, 4 * span), BF),
            jax.ShapeDtypeStruct((full, 2 * span), BF),
        ],
        scratch_shapes=[
            pltpu.VMEM((2, block, full), F32),
            pltpu.VMEM((2, block, full), BF),
            pltpu.VMEM((heads, 2 * hd, full), F32),
            pltpu.VMEM((heads, hd, full), F32),
        ],
        compiler_params=pltpu.CompilerParams(vmem_limit_bytes=60 << 20),
        cost_estimate=pl.CostEstimate(
            flops=16 * heads * full * full * LANES,
            bytes_accessed=2 * heads * full * full + 20 * full * span,
            transcendentals=0,
        ),
        name="attention_backward",
    )(g_out, att, inv, wts, qcat, kcat, vneg, ent, ent)


def layer(
    half, per_row, inputs, query_weight, kv_weight, out_weight, up_weight, down_weight,
    query_bias, value_bias, out_bias, up_bias, down_bias,
    norm1_gain, norm1_shift, norm2_gain, norm2_shift, types, lengths, cotangent,
):
    rows_here, span, width = inputs.shape
    head_dim = width // HEADS
    full = types.shape[1]
    members = 2 * per_row
    heads = HEADS // members
    cols = heads * head_dim
    row_count = lax.axis_size("row")
    outer = lax.axis_size("outer")
    core = lax.axis_index("core")
    group = lax.axis_index("group")
    member = group * 2 + core
    row_id = lax.axis_index("row")
    own = row_count * (span // 2)

    def swap(values):
        return lax.ppermute(values, "core", [(0, 1), (1, 0)])

    def in_order(index, mine, other):
        return jnp.stack([jnp.where(index == 0, mine, other), jnp.where(index == 0, other, mine)])

    def gather_outer(values):
        if outer == 2:
            other = lax.ppermute(values, "outer", [(0, 1), (1, 0)])
            return in_order(lax.axis_index("outer"), values, other)
        return lax.all_gather(values, "outer", axis=0, tiled=False)

    def gather_members(values):
        pair = in_order(core, values, swap(values))
        if per_row == 1:
            return pair
        spread = lax.all_gather(pair, "group", axis=0, tiled=False)
        return spread.reshape((members,) + values.shape)

    def exchange_members(values):
        if per_row == 1:
            mine = lax.dynamic_index_in_dim(values, core, 0, keepdims=False)
            away = lax.dynamic_index_in_dim(values, 1 - core, 0, keepdims=False)
            return in_order(core, mine, swap(away))
        return lax.all_to_all(values, ("group", "core"), 0, 0, tiled=True)

    def take(values, index, axis):
        return lax.dynamic_index_in_dim(values, index, axis, keepdims=False)

    def to_row(values):
        pieces = values.reshape(rows_here, 2, span // 2, width)
        other = swap(take(pieces, 1 - core, 1))
        both = in_order(core, take(pieces, core, 1), other).reshape(row_count, span // 2, width)
        return lax.all_to_all(both, "row", 0, 0, tiled=True).reshape(own, width)

    def from_row(values):
        back = lax.all_to_all(values.reshape(row_count, span // 2, width), "row", 0, 0, tiled=True)
        back = back.reshape(2, rows_here, span // 2, width)
        other = swap(take(back, 1 - core, 0))
        both = in_order(core, take(back, core, 0), other)
        return both.transpose(1, 0, 2, 3).reshape(rows_here, span, width)

    own_rows = to_row(inputs)
    all_rows = gather_members(own_rows).reshape(full, width)

    tags = jnp.concatenate([types, lengths], axis=1)
    tags = in_order(core, tags, swap(tags)).reshape(row_count, -1)
    tags = take(tags, row_id, 0)
    types_row, lengths_row = tags[:full], tags[full:]

    def by_member(values):
        return values.reshape(row_count, per_row, 2, span // 2).transpose(1, 2, 0, 3).reshape(full)

    entity = by_member(types_row) > 0
    positions = by_member(lax.iota(jnp.int32, full))
    docs = lengths_row.shape[0]
    ends = [jnp.sum(lengths_row[: d + 1]) for d in range(docs)]
    seg = sum((positions >= end).astype(jnp.int32) for end in ends)
    lanes = lax.broadcasted_iota(jnp.int32, (full, LANES), 1)
    same = lanes == seg[:, None]
    qseg = jnp.where(same, 1.0, 0.0).astype(BF)
    kseg = jnp.where(same | (lanes >= docs), 0.0, BLOCKED).astype(BF)
    ent = jnp.broadcast_to(jnp.where(entity, 1.0, 0.0).astype(BF)[:, None], (full, LANES))

    shard = query_weight.shape[0]
    cut = jnp.concatenate([query_weight, kv_weight], axis=1).reshape(shard, 6, members, cols)
    away = take(cut, group * 2 + 1 - core, 2).reshape(shard, 6 * cols)
    mine = take(cut, member, 2).reshape(shard, 6 * cols)
    w_sel = gather_outer(in_order(core, mine, swap(away))).reshape(width, 6 * cols)

    vectors = (
        query_bias, value_bias, out_bias, up_bias, down_bias,
        norm1_gain, norm1_shift, norm2_gain, norm2_shift,
    )
    sizes = [v.shape[0] for v in vectors]
    packed = jnp.concatenate(vectors)
    packed = lax.all_gather(packed, ("outer", "core"), axis=0, tiled=False)
    offsets = [sum(sizes[:i]) for i in range(len(sizes) + 1)]
    (b_query, b_value, b_out, b_up, b_down, g_one, s_one, g_two, s_two) = (
        packed[:, a:b].reshape(-1).astype(F32) for a, b in zip(offsets[:-1], offsets[1:])
    )
    b_six = jnp.concatenate([b_query, jnp.zeros((width,), F32), b_value])
    b_sel = take(b_six.reshape(6, members, cols), member, 1).reshape(1, 6 * cols)

    att, inv_stored, wts = None, None, None
    att, wts, inv_stored, qcat, kcat, vneg = attention_forward(
        all_rows, w_sel, b_sel, ent, qseg, kseg, heads, head_dim
    )

    def fetch(values):
        return gather_outer(in_order(core, values, swap(values))).reshape(-1, values.shape[1])

    w_out, w_up, w_down = fetch(out_weight), fetch(up_weight), fetch(down_weight)

    def heads_to_tokens(values):
        got = exchange_members(values.reshape(members, own, cols))
        return got.transpose(1, 0, 2).reshape(own, width)

    def tokens_to_heads(values):
        parts = values.reshape(own, members, cols).transpose(1, 0, 2)
        return exchange_members(parts).reshape(full, cols)

    attended = heads_to_tokens(att)
    attn_out = matmul(attended, w_out) + b_out
    hidden, normed_one, inv_one = normalize(own_rows.astype(F32) + attn_out, g_one, s_one)
    hidden_low = hidden.astype(BF)
    up_proj = matmul(hidden_low, w_up) + b_up
    gelu_out, gelu_pull = jax.vjp(lambda v: jax.nn.gelu(v, approximate=False), up_proj)
    act_low = gelu_out.astype(BF)
    ffn_out = matmul(act_low, w_down) + b_down
    result, normed_two, inv_two = normalize(hidden + ffn_out, g_two, s_two)
    output = from_row(result.astype(BF))

    cot = to_row(cotangent).astype(F32)
    grad_y2, grad_g2, grad_s2 = normalize_back(cot, normed_two, inv_two, g_two)
    grad_ffn = grad_y2.astype(BF)
    grad_act = times_transposed(grad_ffn, w_down)
    grad_up = gelu_pull(grad_act)[0].astype(BF)
    grad_hidden = grad_y2 + times_transposed(grad_up, w_up)
    grad_y1, grad_g1, grad_s1 = normalize_back(grad_hidden, normed_one, inv_one, g_one)
    grad_attn = grad_y1.astype(BF)
    grad_attended = times_transposed(grad_attn, w_out).astype(BF)

    def pick_rows(left, core_index, outer_index):
        parts = left.reshape(left.shape[0], outer, 2, -1)
        if outer_index is None:
            return take(parts, core_index, 2).reshape(left.shape[0], -1)
        return take(take(parts, core_index, 2), outer_index, 1)

    def reduce_outer(partial):
        if outer == 2:
            me = lax.axis_index("outer")
            other = lax.ppermute(take(partial, 1 - me, 0).astype(BF), "outer", [(0, 1), (1, 0)])
            return take(partial, me, 0).astype(F32) + other.astype(F32)
        return lax.psum_scatter(partial.astype(BF), "outer", scatter_dimension=0, tiled=False).astype(F32)

    def shard_grad(left, right):
        away = rows_inner(pick_rows(left, 1 - core, None), right).astype(BF)
        mine = rows_inner(pick_rows(left, core, None), right)
        pair = mine + swap(away).astype(F32)
        part = reduce_outer(pair.reshape(outer, -1, right.shape[1]))
        return lax.psum(part.astype(BF), ("row", "group")).astype(F32)

    g_w_down = shard_grad(act_low, grad_ffn)
    g_w_up = shard_grad(hidden_low, grad_up)
    g_w_out = shard_grad(attended, grad_attn)

    gq, gkv = attention_backward(
        tokens_to_heads(grad_attended), att, inv_stored, wts, qcat, kcat, vneg, ent, heads, head_dim
    )
    g_six = jnp.concatenate([gq, gkv], axis=1)
    g_sel = reduce_outer(rows_inner(all_rows, g_six).reshape(outer, -1, 6 * cols))
    g_sel = lax.psum(g_sel.astype(BF), "row").reshape(2, shard, 6, cols)
    got = in_order(core, take(g_sel, core, 0), swap(take(g_sel, 1 - core, 0)))
    if per_row > 1:
        got = lax.all_gather(got, "group", axis=0, tiled=False)
    got = got.reshape(members, shard, 6, cols).transpose(1, 2, 0, 3).reshape(shard, 6 * width)
    g_w_query = got[:, : 4 * width].astype(F32)
    g_w_kv = got[:, 4 * width :].astype(F32)

    part_in = times_transposed(g_six, w_sel)
    got_in = exchange_members(part_in.astype(BF).reshape(members, own, width))
    grad_in = grad_y1 + jnp.sum(got_in.astype(F32), axis=0)
    input_grad = from_row(grad_in.astype(BF))

    six_sum = column_sum(g_six).reshape(6, 1, cols)
    spot = lax.broadcasted_iota(jnp.int32, (1, members, 1), 1) == member
    six_sum = jnp.where(spot, six_sum, 0.0).reshape(6, width)
    small = [
        six_sum[:4].reshape(-1), six_sum[5], column_sum(grad_attn), column_sum(grad_up),
        column_sum(grad_ffn), grad_g1, grad_s1, grad_g2, grad_s2,
    ]
    total = lax.psum(jnp.concatenate(small), ("row", "group", "outer", "core"))
    me = lax.axis_index("outer") * 2 + core
    pieces, at = [], 0
    for size in sizes:
        whole_size = size * outer * 2
        pieces.append(lax.dynamic_slice_in_dim(total[at : at + whole_size], me * size, size))
        at += whole_size
    return (output, input_grad, g_w_query, g_w_kv, g_w_out, g_w_up, g_w_down, *pieces)


def project_kernel(
    heads, hd, query_rows, kv_rows, at_ref, own_ref, other_ref, bias_ref, ent_ref, *refs
):
    n_query, n_kv = len(query_rows), len(kv_rows)
    query_refs, kv_refs = refs[:n_query], refs[n_query : n_query + n_kv]
    qcat_ref, kcat_ref, vaug_ref, w_ref, sems = refs[n_query + n_kv :]
    span = heads * hd
    half, width = own_ref.shape
    block = min(256, half)
    scale = hd ** (-0.5)
    core = at_ref[0]
    made = []
    for i, (ref, rows) in enumerate(zip(query_refs + kv_refs, query_rows + kv_rows)):
        first, blocks = (0, 4) if i < n_query else (4, 2)
        to = pl.ds(pl.multiple_of(at_ref[1 + i], 16), rows)
        for b in range(blocks):
            here = pl.ds(pl.multiple_of(b * width + core * span, LANES), span)
            cols = slice((first + b) * span, (first + b + 1) * span)
            copy = pltpu.make_async_copy(ref.at[:, here], w_ref.at[to, cols], sems.at[len(made)])
            copy.start()
            made.append(copy)
    lane = lax.broadcasted_iota(jnp.int32, (block, LANES - hd), 1)
    tail = jnp.where(lane < 2, -1.0, jnp.where(lane == 2, 1.0, 0.0)).astype(BF)
    for copy in made:
        copy.wait()
    for side, rows_ref in enumerate((own_ref, other_ref)):

        def project(piece, carry, side=side, rows_ref=rows_ref):
            rows = rows_ref[pl.ds(pl.multiple_of(piece * block, block), block), :]
            at = pl.ds(pl.multiple_of(side * half + piece * block, block), block)
            ent = ent_ref[at, :hd]
            wide = ent_ref[at, :1] > 0
            word = (1 - ent).astype(BF)

            def part(index):
                cols = slice(index * span, (index + 1) * span)
                return jnp.dot(rows, w_ref[:, cols], preferred_element_type=F32) + bias_ref[:, cols]

            q_word = (jnp.where(wide, part(2), part(0))).astype(BF) * BF(scale)
            q_ent = (jnp.where(wide, part(3), part(1))).astype(BF) * BF(scale)
            keys = part(4).astype(BF)
            vals = part(5).astype(BF)
            for h in range(heads):
                cut = slice(h * hd, (h + 1) * hd)
                qcat_ref[h, at, :] = jnp.concatenate([q_word[:, cut], q_ent[:, cut]], axis=1)
                kcat_ref[h, at, :] = jnp.concatenate([keys[:, cut] * word, keys[:, cut] * ent], axis=1)
                vaug_ref[h, at, :] = jnp.concatenate([vals[:, cut], tail], axis=1)
            return carry

        lax.fori_loop(0, half // block, project, 0)


def row_project(at, own, other, bias, ent, query_pieces, kv_pieces, heads, hd):
    half, width = own.shape
    full = 2 * half
    span = heads * hd
    vmem = pl.BlockSpec(memory_space=pltpu.VMEM)
    anywhere = pl.BlockSpec(memory_space=pl.ANY)
    query_rows = tuple(p.shape[0] for p in query_pieces)
    kv_rows = tuple(p.shape[0] for p in kv_pieces)
    return pl.pallas_call(
        functools.partial(project_kernel, heads, hd, query_rows, kv_rows),
        in_specs=[pl.BlockSpec(memory_space=pltpu.SMEM)]
        + [vmem] * 4
        + [anywhere] * (len(query_pieces) + len(kv_pieces)),
        out_specs=[vmem] * 4,
        out_shape=[
            jax.ShapeDtypeStruct((heads, full, 2 * hd), BF),
            jax.ShapeDtypeStruct((heads, full, 2 * hd), BF),
            jax.ShapeDtypeStruct((heads, full, LANES), BF),
            jax.ShapeDtypeStruct((width, 6 * span), BF),
        ],
        scratch_shapes=[pltpu.SemaphoreType.DMA((4 * len(query_pieces) + 2 * len(kv_pieces),))],
        compiler_params=pltpu.CompilerParams(vmem_limit_bytes=60 << 20),
        cost_estimate=pl.CostEstimate(
            flops=2 * full * width * 6 * span, bytes_accessed=18 * full * width, transcendentals=0
        ),
        name="row_project",
    )(at, own, other, bias, ent, *query_pieces, *kv_pieces)


def attend_kernel(
    heads, hd, qcat_ref, qseg_ref, kcat_ref, kseg_ref, vaug_ref, keep_ref, send_ref, wts_ref, inv_ref, score_s
):
    step = pl.program_id(0)
    block = keep_ref.shape[0]
    q_seg = qseg_ref[...]
    lane = lax.broadcasted_iota(jnp.int32, (block, LANES), 1)
    inv_all = jnp.zeros((block, LANES), F32)
    mixed = []
    for h in range(heads):
        q_aug = jnp.concatenate([qcat_ref[h], q_seg], axis=1)
        k_aug = jnp.concatenate([kcat_ref[h], kseg_ref[...]], axis=1)
        score_s[h % 2] = lax.dot_general(
            q_aug, k_aug, (((1,), (1,)), ((), ())), preferred_element_type=F32
        )
        for r in range(0, block, CHUNK):
            s = score_s[h % 2, r : r + CHUNK, :]
            top = jnp.max(s, axis=1, keepdims=True)
            wts_ref[h, r : r + CHUNK, :] = jnp.exp(s - top).astype(BF)
        out = jnp.dot(wts_ref[h], vaug_ref[h], preferred_element_type=F32)
        inv = 1.0 / out[:, hd + 2 : hd + 3]
        inv_all = jnp.where(lane == h, inv, inv_all)
        mixed.append((out[:, :hd] * inv).astype(BF))
    mixed = jnp.concatenate(mixed, axis=1)
    inv_ref[...] = inv_all
    late = pl.num_programs(0) // 2

    @pl.when(step < late)
    def _():
        send_ref[...] = mixed

    @pl.when(step >= late)
    def _():
        keep_ref[...] = mixed


def row_attend(qcat, kcat, vaug, qseg, kseg, heads, hd):
    full = qcat.shape[1]
    half = full // 2
    block = min(256, half)
    span = heads * hd
    first = half // block
    whole = lambda *dims: pl.BlockSpec(dims, lambda i: (0,) * len(dims))
    turn = lambda i: jnp.where(i < first, i + first, i - first)
    return pl.pallas_call(
        functools.partial(attend_kernel, heads, hd),
        grid=(full // block,),
        in_specs=[
            pl.BlockSpec((heads, block, 2 * hd), lambda i: (0, turn(i), 0)),
            pl.BlockSpec((block, LANES), lambda i: (turn(i), 0)),
            whole(heads, full, 2 * hd),
            whole(full, LANES),
            whole(heads, full, LANES),
        ],
        out_specs=[
            pl.BlockSpec((block, span), lambda i: (jnp.maximum(i - first, 0), 0)),
            pl.BlockSpec((block, span), lambda i: (jnp.minimum(i, first - 1), 0)),
            pl.BlockSpec((heads, block, full), lambda i: (0, turn(i), 0)),
            pl.BlockSpec((block, LANES), lambda i: (turn(i), 0)),
        ],
        out_shape=[
            jax.ShapeDtypeStruct((half, span), BF),
            jax.ShapeDtypeStruct((half, span), BF),
            jax.ShapeDtypeStruct((heads, full, full), BF),
            jax.ShapeDtypeStruct((full, LANES), F32),
        ],
        scratch_shapes=[pltpu.VMEM((2, block, full), F32)],
        compiler_params=pltpu.CompilerParams(vmem_limit_bytes=60 << 20),
        cost_estimate=pl.CostEstimate(
            flops=8 * heads * full * full * LANES,
            bytes_accessed=2 * heads * full * full + 4 * full * LANES * heads,
            transcendentals=heads * full * full,
        ),
        name="row_attend",
    )(qcat, qseg, kcat, kseg, vaug)


def token_kernel(
    out_rows, up_rows, down_rows, at_ref, own_ref, mine_ref, theirs_ref, cot_ref, vec_ref, *refs
):
    groups = (out_rows, up_rows, down_rows)
    sets, at = [], 0
    for rows in groups:
        sets.append(refs[at : at + len(rows)])
        at += len(rows)
    (
        result_ref, gy1_ref, gmine_ref, gtheirs_ref, act_ref, hlow_ref, gffn_ref, gup_ref, gattn_ref,
        small_ref, wout_s, wup_s, wdown_s, acc_s, hid_s, norm_s, inv_s, slope_s, gy2_s, tmp_s, sum_s, sems,
    ) = refs[at:]
    total, width = own_ref.shape
    ff = wup_s.shape[1]
    parts = ff // width
    span = mine_ref.shape[1]
    core = at_ref[0]
    made, slot = [], 0
    for rows, piece_refs, dst in zip(groups, sets, (wout_s, wup_s, wdown_s)):
        batch = []
        for n, ref in zip(rows, piece_refs):
            to = pl.ds(pl.multiple_of(at_ref[1 + slot], 16), n)
            copy = pltpu.make_async_copy(ref, dst.at[to, :], sems.at[slot])
            copy.start()
            batch.append(copy)
            slot += 1
        made.append(batch)

    def wait(index):
        for copy in made[index]:
            copy.wait()

    def row(index):
        return vec_ref[index : index + 1, :]

    rows_at = lambda i, n: pl.ds(pl.multiple_of(i * n, n), n)
    chunk = 16
    mine_rows = pl.ds(pl.multiple_of(core * span, LANES), span)
    other_rows = pl.ds(pl.multiple_of((1 - core) * span, LANES), span)
    sum_s[...] = jnp.zeros_like(sum_s)
    wait(0)
    acc_s[...] = jnp.dot(mine_ref[...], wout_s[mine_rows, :], preferred_element_type=F32)
    acc_s[...] += jnp.dot(theirs_ref[...], wout_s[other_rows, :], preferred_element_type=F32)

    def first_norm(i, carry):
        at = rows_at(i, chunk)
        y = own_ref[at, :].astype(F32) + (acc_s[at, :] + row(4))
        center = y - jnp.mean(y, axis=1, keepdims=True)
        inv = lax.rsqrt(jnp.mean(center * center, axis=1, keepdims=True) + EPSILON)
        normed = center * inv
        hidden = normed * row(6) + row(7)
        norm_s[at, :] = normed
        inv_s[at, :] = jnp.broadcast_to(inv, (chunk, LANES))
        hid_s[at, :] = hidden
        hlow_ref[at, :] = hidden.astype(BF)
        return carry

    lax.fori_loop(0, total // chunk, first_norm, 0, unroll=4)
    wait(1)
    for c in range(parts):
        cols = slice(c * width, (c + 1) * width)
        tmp_s[c % 2] = jnp.dot(hlow_ref[...], wup_s[:, cols], preferred_element_type=F32)
        for r in range(0, total, chunk):
            x = tmp_s[c % 2, r : r + chunk, :] + row(c)
            cdf = 0.5 + 0.5 * lax.erf(x * (0.5**0.5))
            act_ref[r : r + chunk, cols] = (x * cdf).astype(BF)
            slope_s[r : r + chunk, cols] = cdf + x * (jnp.exp(-0.5 * x * x) * (0.15915494309189535**0.5))
    wait(2)
    acc_s[...] = jnp.dot(act_ref[...], wdown_s[...], preferred_element_type=F32)

    def second_norm(i, carry):
        at = rows_at(i, chunk)
        y = hid_s[at, :] + (acc_s[at, :] + row(5))
        center = y - jnp.mean(y, axis=1, keepdims=True)
        inv = lax.rsqrt(jnp.mean(center * center, axis=1, keepdims=True) + EPSILON)
        normed = center * inv
        result_ref[at, :] = (normed * row(8) + row(9)).astype(BF)
        cot = cot_ref[at, :].astype(F32)
        sum_s[2] += cot * normed
        sum_s[3] += cot
        scaled = cot * row(8)
        g = inv * (
            scaled
            - jnp.mean(scaled, axis=1, keepdims=True)
            - normed * jnp.mean(scaled * normed, axis=1, keepdims=True)
        )
        gy2_s[at, :] = g
        gffn_ref[at, :] = g.astype(BF)
        return carry

    lax.fori_loop(0, total // chunk, second_norm, 0, unroll=2)
    ones = jnp.ones((8, total), BF)
    for c in range(parts):
        cols = slice(c * width, (c + 1) * width)
        tmp_s[c % 2] = lax.dot_general(
            gffn_ref[...], wdown_s[cols, :], (((1,), (1,)), ((), ())), preferred_element_type=F32
        )
        for r in range(0, total, chunk):
            gup_ref[r : r + chunk, cols] = (
                tmp_s[c % 2, r : r + chunk, :] * slope_s[r : r + chunk, cols]
            ).astype(BF)
        small_ref[c : c + 1, :] = jnp.dot(ones, gup_ref[:, cols], preferred_element_type=F32)[:1]
    acc_s[...] = lax.dot_general(
        gup_ref[...], wup_s[...], (((1,), (1,)), ((), ())), preferred_element_type=F32
    )

    def first_back(i, carry):
        at = rows_at(i, chunk)
        g_in = gy2_s[at, :] + acc_s[at, :]
        normed = norm_s[at, :]
        sum_s[0] += g_in * normed
        sum_s[1] += g_in
        scaled = g_in * row(6)
        g = inv_s[at, :1] * (
            scaled
            - jnp.mean(scaled, axis=1, keepdims=True)
            - normed * jnp.mean(scaled * normed, axis=1, keepdims=True)
        )
        gy1_ref[at, :] = g
        gattn_ref[at, :] = g.astype(BF)
        return carry

    lax.fori_loop(0, total // chunk, first_back, 0, unroll=2)
    gmine_ref[...] = lax.dot_general(
        gattn_ref[...], wout_s[mine_rows, :], (((1,), (1,)), ((), ())), preferred_element_type=F32
    ).astype(BF)
    gtheirs_ref[...] = lax.dot_general(
        gattn_ref[...], wout_s[other_rows, :], (((1,), (1,)), ((), ())), preferred_element_type=F32
    ).astype(BF)
    small_ref[4:5, :] = jnp.dot(ones, gattn_ref[...], preferred_element_type=F32)[:1]
    small_ref[5:6, :] = jnp.dot(ones, gffn_ref[...], preferred_element_type=F32)[:1]
    for i in range(4):
        small_ref[6 + i : 7 + i, :] = jnp.sum(sum_s[i], axis=0, keepdims=True)
    small_ref[10:, :] = jnp.zeros((small_ref.shape[0] - 10, width), F32)


def token_block(at, own, mine, theirs, cot, vec, out_pieces, up_pieces, down_pieces):
    total, width = own.shape
    span = mine.shape[1]
    ff = up_pieces[0].shape[1]
    vmem = pl.BlockSpec(memory_space=pltpu.VMEM)
    pieces = [*out_pieces, *up_pieces, *down_pieces]
    shapes = [
        ((total, width), BF), ((total, width), F32), ((total, span), BF), ((total, span), BF),
        ((total, ff), BF), ((total, width), BF), ((total, width), BF), ((total, ff), BF),
        ((total, width), BF), ((16, width), F32),
    ]
    rows = lambda group: tuple(p.shape[0] for p in group)
    return pl.pallas_call(
        functools.partial(token_kernel, rows(out_pieces), rows(up_pieces), rows(down_pieces)),
        in_specs=[pl.BlockSpec(memory_space=pltpu.SMEM)]
        + [vmem] * 5
        + [pl.BlockSpec(memory_space=pl.ANY)] * len(pieces),
        out_specs=[vmem] * len(shapes),
        out_shape=[jax.ShapeDtypeStruct(s, d) for s, d in shapes],
        scratch_shapes=[
            pltpu.VMEM((width, width), BF),
            pltpu.VMEM((width, ff), BF),
            pltpu.VMEM((ff, width), BF),
            pltpu.VMEM((total, width), F32),
            pltpu.VMEM((total, width), F32),
            pltpu.VMEM((total, width), F32),
            pltpu.VMEM((total, LANES), F32),
            pltpu.VMEM((total, ff), F32),
            pltpu.VMEM((total, width), F32),
            pltpu.VMEM((2, total, width), F32),
            pltpu.VMEM((4, 16, width), F32),
            pltpu.SemaphoreType.DMA((len(pieces),)),
        ],
        compiler_params=pltpu.CompilerParams(vmem_limit_bytes=60 << 20),
        cost_estimate=pl.CostEstimate(
            flops=2 * total * width * (4 * ff + 2 * width),
            bytes_accessed=4 * width * ff + 6 * total * ff,
            transcendentals=2 * total * ff,
        ),
        name="token_block",
    )(at, own, mine, theirs, cot, vec, *pieces)


def weight_kernel(
    at_ref, mine_ref, theirs_ref, hlow_ref, act_ref, gffn_ref, gup_ref, gattn_ref,
    up_send, rest_send, up_keep, rest_keep, hid_t, att_t,
):
    total, width = hlow_ref.shape
    span = mine_ref.shape[1]
    ff = act_ref.shape[1]
    core = at_ref[0]
    n, wide = width // 4, ff // 4
    hid_t[...] = hlow_ref[...].T
    att_t[pl.ds(pl.multiple_of(core * span, LANES), span), :] = mine_ref[...].T
    att_t[pl.ds(pl.multiple_of((1 - core) * span, LANES), span), :] = theirs_ref[...].T
    for which, up_ref, rest_ref in ((1 - core, up_send, rest_send), (core, up_keep, rest_keep)):
        for outer in range(2):
            shard = 2 * outer + which
            rows = pl.ds(pl.multiple_of(shard * n, 16), n)
            left = hid_t[rows, :]
            for i in range(8):
                up_ref[outer, i] = jnp.dot(
                    left, gup_ref[:, i * span : (i + 1) * span], preferred_element_type=F32
                ).astype(BF)
            left = act_ref[:, pl.ds(pl.multiple_of(shard * wide, LANES), wide)]
            down = lax.dot_general(left, gffn_ref[...], (((0,), (0,)), ((), ())), preferred_element_type=F32)
            out = jnp.dot(att_t[rows, :], gattn_ref[...], preferred_element_type=F32)
            for i in range(8):
                r, c = i // 2, i % 2
                cols = slice(c * span, (c + 1) * span)
                rest_ref[outer, i, : wide // 4, :] = down[r * wide // 4 : (r + 1) * wide // 4, cols].astype(BF)
                rest_ref[outer, i, wide // 4 :, :] = out[r * n // 4 : (r + 1) * n // 4, cols].astype(BF)


def weight_grads(at, mine, theirs, hlow, act, gffn, gup, gattn):
    total, width = hlow.shape
    span = mine.shape[1]
    ff = act.shape[1]
    vmem = pl.BlockSpec(memory_space=pltpu.VMEM)
    shapes = [(2, 8, width // 4, ff // 8), (2, 8, ff // 16 + width // 16, span)] * 2
    return pl.pallas_call(
        weight_kernel,
        in_specs=[pl.BlockSpec(memory_space=pltpu.SMEM)] + [vmem] * 7,
        out_specs=[vmem] * 4,
        out_shape=[jax.ShapeDtypeStruct(s, BF) for s in shapes],
        scratch_shapes=[pltpu.VMEM((width, total), BF), pltpu.VMEM((width, total), BF)],
        compiler_params=pltpu.CompilerParams(vmem_limit_bytes=60 << 20),
        cost_estimate=pl.CostEstimate(
            flops=2 * total * width * (2 * ff + width),
            bytes_accessed=4 * width * ff + 6 * total * ff,
            transcendentals=0,
        ),
        name="weight_grads",
    )(at, mine, theirs, hlow, act, gffn, gup, gattn)


def row_backward_kernel(
    heads, hd, first_head, gmine_ref, gother_ref, keep_ref, send_ref, inv_ref, wts_ref, qcat_ref, kcat_ref,
    vaug_ref, ent_ref, entb_ref, *refs,
):
    gq_ref, gkv_ref, gscore_s, low_s, gk_s, gv_s = refs[-6:]
    step = pl.program_id(0)
    block = gmine_ref.shape[0]
    full = kcat_ref.shape[1]
    scale = hd ** (-0.5)
    lane = lax.broadcasted_iota(jnp.int32, (block, LANES - hd), 1)
    is_ent = entb_ref[:, :1] > 0
    early = step < pl.num_programs(0) // 2
    g_all = jnp.where(early, gmine_ref[...], gother_ref[...])
    att_all = jnp.where(early, keep_ref[...], send_ref[...])
    g_word, g_ent = [], []
    for h in range(heads):
        cut = slice(h * hd, (h + 1) * hd)
        g_low = (g_all[:, cut].astype(F32) * inv_ref[:, first_head + h : first_head + h + 1]).astype(BF)
        delta = jnp.sum(g_low.astype(F32) * att_all[:, cut].astype(F32), axis=1, keepdims=True)
        d_hi = delta.astype(BF)
        d_lo = (delta - d_hi.astype(F32)).astype(BF)
        extra = jnp.where(
            lane == 0, d_hi.astype(F32), jnp.where(lane == 1, d_lo.astype(F32), 0.0)
        ).astype(BF)
        g_aug = jnp.concatenate([g_low, extra], axis=1)
        gscore_s[h % 2] = lax.dot_general(
            g_aug, vaug_ref[h], (((1,), (1,)), ((), ())), preferred_element_type=F32
        )
        for r in range(0, block, CHUNK):
            low_s[h % 2, r : r + CHUNK, :] = (
                wts_ref[h, r : r + CHUNK, :].astype(F32) * gscore_s[h % 2, r : r + CHUNK, :]
            ).astype(BF)
        g_q = jnp.dot(low_s[h % 2], kcat_ref[h], preferred_element_type=F32) * scale
        g_word.append(g_q[:, :hd])
        g_ent.append(g_q[:, hd:])
        g_k = lax.dot_general(
            qcat_ref[h], low_s[h % 2], (((0,), (0,)), ((), ())), preferred_element_type=F32
        )
        g_v = lax.dot_general(
            g_low, wts_ref[h], (((0,), (0,)), ((), ())), preferred_element_type=F32
        )

        @pl.when(step == 0)
        def _(h=h, g_k=g_k, g_v=g_v):
            gk_s[h] = g_k
            gv_s[h] = g_v

        @pl.when(step > 0)
        def _(h=h, g_k=g_k, g_v=g_v):
            gk_s[h] += g_k
            gv_s[h] += g_v

    g_word = jnp.concatenate(g_word, axis=1)
    g_ent = jnp.concatenate(g_ent, axis=1)
    gq_ref[0] = jnp.where(is_ent, 0.0, g_word).astype(BF)
    gq_ref[1] = jnp.where(is_ent, 0.0, g_ent).astype(BF)
    gq_ref[2] = jnp.where(is_ent, g_word, 0.0).astype(BF)
    gq_ref[3] = jnp.where(is_ent, g_ent, 0.0).astype(BF)

    @pl.when(step == pl.num_programs(0) - 1)
    def _():
        def close(piece, carry):
            at = pl.ds(pl.multiple_of(piece * block, block), block)
            pick = ent_ref[at, :1] > 0
            g_keys, g_vals = [], []
            for h in range(heads):
                both = gk_s[h, :, at].T
                g_keys.append(jnp.where(pick, both[:, hd:], both[:, :hd]))
                g_vals.append(gv_s[h, :, at].T)
            gkv_ref[0, at, :] = jnp.concatenate(g_keys, axis=1).astype(BF)
            gkv_ref[1, at, :] = jnp.concatenate(g_vals, axis=1).astype(BF)
            return carry

        lax.fori_loop(0, full // block, close, 0)


def row_backward(first_head, heads, grads, gmine, gother, keep, send, inv, wts, qcat, kcat, vaug, ent, hd):
    half, all_cols = keep.shape
    full = 2 * half
    block = min(256, half)
    first = half // block
    cols = heads * hd
    g, c = first_head // heads, first_head * hd // cols
    by_rows = pl.BlockSpec((block, LANES), lambda i: (i, 0))
    by_head = lambda width: pl.BlockSpec((heads, block, width), lambda i: (g, i, 0))
    of_head = lambda width: pl.BlockSpec((heads, full, width), lambda i: (g, 0, 0))
    low = pl.BlockSpec((block, cols), lambda i: (jnp.minimum(i, first - 1), c))
    high = pl.BlockSpec((block, cols), lambda i: (jnp.maximum(i - first, 0), c))
    given = [] if grads is None else list(grads)
    return pl.pallas_call(
        functools.partial(row_backward_kernel, heads, hd, first_head),
        grid=(full // block,),
        in_specs=[
            low, high, low, high,
            by_rows,
            by_head(full),
            by_head(2 * hd),
            of_head(2 * hd),
            of_head(LANES),
            pl.BlockSpec((full, LANES), lambda i: (0, 0)),
            by_rows,
        ]
        + [pl.BlockSpec(memory_space=pl.ANY)] * len(given),
        out_specs=[
            pl.BlockSpec((4, block, cols), lambda i: (0, i, c)),
            pl.BlockSpec((2, full, cols), lambda i: (0, 0, c)),
        ],
        out_shape=[
            jax.ShapeDtypeStruct((4, full, all_cols), BF),
            jax.ShapeDtypeStruct((2, full, all_cols), BF),
        ],
        scratch_shapes=[
            pltpu.VMEM((2, block, full), F32),
            pltpu.VMEM((2, block, full), BF),
            pltpu.VMEM((heads, 2 * hd, full), F32),
            pltpu.VMEM((heads, hd, full), F32),
        ],
        input_output_aliases={11 + i: i for i in range(len(given))},
        compiler_params=pltpu.CompilerParams(vmem_limit_bytes=60 << 20),
        cost_estimate=pl.CostEstimate(
            flops=16 * heads * full * full * LANES,
            bytes_accessed=2 * heads * full * full + 20 * full * cols,
            transcendentals=0,
        ),
        name="row_backward",
    )(gmine, gother, keep, send, inv, wts, qcat, kcat, vaug, ent, ent, *given)


def project_back_kernel(
    at_ref, own_ref, other_ref, gq_ref, gkv_ref, w_ref, gy1_ref,
    send1, send2, keep1, keep2, mine_ref, away_ref, sum_ref, rows_t,
):
    half, width = own_ref.shape
    span = gkv_ref.shape[2]
    outer, near = at_ref[0], at_ref[1]
    rows_t[:, :half] = own_ref[...].T
    rows_t[:, half:] = other_ref[...].T

    def grads(b):
        return gq_ref.at[b] if b < 4 else gkv_ref.at[b - 4]

    n = width // 16
    for which, out_ref in ((1 - outer, send1), (outer, keep1)):
        left = rows_t[pl.ds(pl.multiple_of(which * 8 * n, 16), 8 * n), :]
        for b in range(3):
            piece = jnp.dot(left, grads(b)[...], preferred_element_type=F32)
            out_ref[:, b] = piece.reshape(8, n, span).astype(BF)
    for which, out_ref in ((1 - near, send2), (near, keep2)):
        for o in range(2):
            left = rows_t[pl.ds(pl.multiple_of(o * 8 * n + which * 4 * n, 16), 4 * n), :]
            for b in range(3):
                piece = jnp.dot(left, grads(3 + b)[...], preferred_element_type=F32)
                out_ref[o, :, b] = piece.reshape(4, n, span).astype(BF)

    def back(at):
        total = None
        for b in range(6):
            part = lax.dot_general(
                grads(b)[at, :], w_ref[:, b * span : (b + 1) * span], (((1,), (1,)), ((), ())),
                preferred_element_type=F32,
            )
            total = part if total is None else total + part
        return total

    away_ref[...] = back(slice(half, 2 * half)).astype(BF)
    mine_ref[...] = gy1_ref[...] + back(slice(0, half))
    ones = jnp.ones((8, 2 * half), BF)
    for b in range(6):
        sum_ref[b : b + 1, :] = jnp.dot(ones, grads(b)[...], preferred_element_type=F32)[:1]
    sum_ref[6:, :] = jnp.zeros((2, span), F32)


def project_back(at, own, other, gq, gkv, w, gy1):
    half, width = own.shape
    span = gkv.shape[2]
    n = width // 16
    vmem = pl.BlockSpec(memory_space=pltpu.VMEM)
    one, two = ((8, 3, n, span), BF), ((2, 4, 3, n, span), BF)
    shapes = [one, two, one, two, ((half, width), F32), ((half, width), BF), ((8, span), F32)]
    return pl.pallas_call(
        project_back_kernel,
        in_specs=[pl.BlockSpec(memory_space=pltpu.SMEM)] + [vmem] * 6,
        out_specs=[vmem] * 7,
        out_shape=[jax.ShapeDtypeStruct(s, d) for s, d in shapes],
        scratch_shapes=[pltpu.VMEM((width, 2 * half), BF)],
        compiler_params=pltpu.CompilerParams(vmem_limit_bytes=60 << 20),
        cost_estimate=pl.CostEstimate(
            flops=8 * half * width * 6 * span, bytes_accessed=20 * half * width, transcendentals=0
        ),
        name="project_back",
    )(at, own, other, gq, gkv, w, gy1)


def row_layer(
    inputs, query_weight, kv_weight, out_weight, up_weight, down_weight,
    query_bias, value_bias, out_bias, up_bias, down_bias,
    norm1_gain, norm1_shift, norm2_gain, norm2_shift, types, lengths, cotangent,
):
    rows_here, span, width = inputs.shape
    hd = width // HEADS
    full = types.shape[1]
    heads = HEADS // 2
    cols = heads * hd
    row_count = lax.axis_size("row")
    core, outer, row_id = (lax.axis_index(n) for n in ("core", "outer", "row"))
    place = [row_id // bit % 2 for bit in (1, 2, 4)]
    near = place[0]
    own_count = full // 2
    both_ways = [(0, 1), (1, 0)]

    def after(values, *others):
        return lax.optimization_barrier((values, *others))[0]

    def swap(values):
        return lax.ppermute(values, "core", both_ways)

    def cross(values):
        return lax.ppermute(values, "outer", both_ways)

    def pair_up(values, bit):
        return lax.ppermute(values, "row", [(i, i ^ bit) for i in range(row_count)])

    def in_order(index, mine, other, axis=0):
        first, second = jnp.where(index == 0, mine, other), jnp.where(index == 0, other, mine)
        return jnp.stack([first, second], axis=axis)

    def take(values, index, axis=0):
        return lax.dynamic_index_in_dim(values, index, axis, keepdims=False)

    def halves_of_rows(values):
        pieces = values.reshape(rows_here, 2, span // 2, width)
        other = swap(take(pieces, 1 - core, 1))
        return in_order(core, take(pieces, core, 1), other).reshape(row_count, span // 2, width)

    def over_rows(values):
        return lax.all_to_all(values, "row", 0, 0, tiled=True)

    def rows_whole(back):
        back = back.reshape(2, rows_here, span // 2, width)
        other = swap(take(back, 1 - core))
        both = in_order(core, take(back, core), other)
        return both.transpose(1, 0, 2, 3).reshape(rows_here, span, width)

    shard = query_weight.shape[0]
    wide = down_weight.shape[0]

    def near_half(values):
        return take(values.reshape(2, values.shape[0] // 2, values.shape[1]), near)

    f_own, f_core = 2 * outer + core, 2 * outer + 1 - core
    f_cross, f_both = 2 * (1 - outer) + core, 2 * (1 - outer) + 1 - core

    q_got = cross(near_half(query_weight))
    to_rows = halves_of_rows(inputs)
    own_rows = over_rows(to_rows).reshape(own_count, width)
    types, lengths, query_bias, cotangent, query_own, kv_own = lax.optimization_barrier(
        (types, lengths, query_bias, cotangent, query_weight, kv_weight, to_rows)
    )[:6]
    q_core, kv_core = swap(query_own), swap(kv_own)
    kv_got = cross(after(kv_weight, q_got))
    cot_halves = halves_of_rows(cotangent)
    q_passed = pair_up(q_got, 1)
    q_got2, q_passed2, kv_got2 = swap(q_got), swap(q_passed), swap(kv_got)
    other_rows = swap(own_rows)
    query_pieces = [query_weight, q_core, q_got, q_passed, q_got2, q_passed2]
    kv_pieces = [kv_weight, kv_core, kv_got, kv_got2]
    part = shard // 2
    query_at = [
        f_own * shard, f_core * shard,
        f_cross * shard + near * part, f_cross * shard + (1 - near) * part,
        f_both * shard + near * part, f_both * shard + (1 - near) * part,
    ]
    kv_at = [f_own * shard, f_core * shard, f_cross * shard, f_both * shard]
    at_qkv = jnp.stack([core, *query_at, *kv_at]).astype(jnp.int32)

    tags = jnp.concatenate([types, lengths], axis=1)
    tags = take(in_order(core, tags, swap(tags)).reshape(row_count, -1), row_id)
    types_row, lengths_row = tags[:full], tags[full:]

    def by_member(values):
        two = values.reshape(row_count, 2, span // 2).transpose(1, 0, 2)
        return jnp.concatenate([take(two, core), take(two, 1 - core)], axis=0).reshape(full)

    entity = by_member(types_row) > 0
    positions = by_member(lax.iota(jnp.int32, full))
    docs = lengths_row.shape[0]
    ends = [jnp.sum(lengths_row[: d + 1]) for d in range(docs)]
    seg = sum((positions >= end).astype(jnp.int32) for end in ends)
    lanes = lax.broadcasted_iota(jnp.int32, (full, LANES), 1)
    same = lanes == seg[:, None]
    qseg = jnp.where(same, 1.0, 0.0).astype(BF)
    kseg = jnp.where(same | (lanes >= docs), 0.0, BLOCKED).astype(BF)
    ent = jnp.broadcast_to(jnp.where(entity, 1.0, 0.0).astype(BF)[:, None], (full, LANES))

    vectors = (
        query_bias, value_bias, out_bias, up_bias, down_bias,
        norm1_gain, norm1_shift, norm2_gain, norm2_shift,
    )
    packed = jnp.concatenate([v.reshape(-1, shard) for v in vectors], axis=0)
    packed = in_order(outer, packed, cross(packed))
    packed = in_order(core, packed, swap(packed)).transpose(1, 0, 2, 3).reshape(4, -1, shard)

    def joined(first, count):
        return packed[:, first : first + count].reshape(-1, width).astype(F32)

    b_query, b_value = joined(0, 4), joined(4, 1)
    vec = jnp.concatenate(
        [joined(6, 4), joined(5, 1), joined(10, 1), joined(11, 1), joined(12, 1), joined(13, 1), joined(14, 1)]
    )
    b_six = jnp.concatenate([b_query, jnp.zeros((1, width), F32), b_value]).reshape(6, 2, cols)
    b_sel = take(b_six, core, 1).reshape(1, 6 * cols)

    qcat, kcat, vaug, w_sel = row_project(
        at_qkv, own_rows, other_rows, b_sel, ent, query_pieces, kv_pieces, heads, hd
    )

    low_rows = down_weight[: wide // 2]
    u_got = cross(after(near_half(up_weight), kv_got))
    d_got = cross(after(near_half(low_rows), kv_got))
    late_out, late_up, late_down = lax.optimization_barrier((out_weight, up_weight, down_weight, kv_got))[:3]
    o_core, u_core, d_core = swap(late_out), swap(late_up), swap(late_down)
    u_mid, d_mid, m_out, m_down = lax.optimization_barrier((u_got, d_got, out_weight, down_weight, kcat))[:4]
    u_passed, d_passed = pair_up(u_mid, 1), pair_up(d_mid, 1)
    o_got, t_got = cross(m_out), cross(m_down[wide // 2 :])
    u_got2, d_got2 = swap(u_mid), swap(d_mid)
    keep, send, wts, inv = row_attend(qcat, kcat, vaug, qseg, kseg, heads, hd)
    theirs = swap(send)
    u_passed2, d_passed2, o_got2, t_got2 = (
        swap(v) for v in lax.optimization_barrier((u_passed, d_passed, o_got, t_got, keep))[:4]
    )
    out_pieces = [out_weight, o_core, o_got, o_got2]
    out_at = [f * shard for f in (f_own, f_core, f_cross, f_both)]
    up_pieces = [up_weight, u_core, u_got, u_passed, u_got2, u_passed2]
    down_pieces = [down_weight, d_core, d_got, d_passed, t_got, d_got2, d_passed2, t_got2]
    quarter = wide // 4
    down_at = [
        f_own * wide, f_core * wide,
        f_cross * wide + near * quarter, f_cross * wide + (1 - near) * quarter, f_cross * wide + 2 * quarter,
        f_both * wide + near * quarter, f_both * wide + (1 - near) * quarter, f_both * wide + 2 * quarter,
    ]
    at_rest = jnp.stack([core, *out_at, *query_at, *down_at]).astype(jnp.int32)

    cot = over_rows(after(cot_halves, own_rows)).reshape(own_count, width)
    (
        result, gy1, gmine, gtheirs, act, hlow, gffn, gup, gattn, small
    ) = token_block(at_rest, own_rows, keep, theirs, cot, vec, out_pieces, up_pieces, down_pieces)
    gother = swap(gtheirs)
    at_core = core.astype(jnp.int32).reshape(1)
    up_send, rest_send, up_keep, rest_keep = weight_grads(
        at_core, keep, theirs, hlow, act, gffn, gup, gattn
    )
    output_rows = over_rows(after(result, gother).reshape(row_count, span // 2, width))

    def add(a, b):
        return (a.astype(F32) + b.astype(F32)).astype(BF)

    index_of = {"outer": outer, "y": place[0], "z": place[1], "far": place[2]}

    def send_over(values, name):
        return cross(values) if name == "outer" else pair_up(values, {"y": 1, "z": 2, "far": 4}[name])

    bits = (2, 2, 2)
    state, token = {}, [gother]

    def begin(name, mine, other, left):
        state[name] = (mine, other, left, None)

    def reduce(name, axis):
        mine, other, left, _ = state[name]
        mine, other = lax.optimization_barrier((mine, other, token[0]))[:2]
        at = left.index(axis)
        away, mine = (
            add(take(mine, i, at), take(other, i, at)) for i in (1 - index_of[axis], index_of[axis])
        )
        token[0] = away
        state[name] = (mine, send_over(away, axis), [a for a in left if a != axis], None)

    def gather(name, axis):
        total = settle(name)
        token[0] = total
        have = state[name][3] or []
        state[name] = (total, send_over(total, axis), None, [*have, axis])

    def settle(name):
        mine, other, left, have = state[name]
        mine, other = lax.optimization_barrier((mine, other, token[0]))[:2]
        if left is not None:
            assert not left
            return add(mine, other)
        now = [a for a in ("y", "z", "far") if a in have]
        return in_order(index_of[have[-1]], mine, other, axis=now.index(have[-1]))

    every = ["outer", "y", "z", "far"]

    def pieces_of(values, *lead):
        return values.reshape(*lead, *values.shape[-2:])

    begin("up", pieces_of(up_keep, 2, *bits), pieces_of(swap(up_send), 2, *bits), every)
    begin("rest", pieces_of(rest_keep, 2, *bits), pieces_of(swap(rest_send), 2, *bits), every)
    gq, gkv = row_backward(
        4, 2, None, gmine, gother, keep, send, inv, wts, qcat, kcat, vaug, ent, hd
    )
    token[0] = gkv
    reduce("up", "outer")
    reduce("rest", "y")
    gq, gkv, _ = lax.optimization_barrier((gq, gkv, token[0]))
    gq, gkv = row_backward(
        0, 4, (gq, gkv), gmine, gother, keep, send, inv, wts, qcat, kcat, vaug, ent, hd
    )
    token[0] = gkv
    reduce("up", "y")
    output = rows_whole(after(output_rows, gkv))
    gq, gkv, _ = lax.optimization_barrier((gq, gkv, token[0]))
    at_back = jnp.stack([outer, near]).astype(jnp.int32)
    send1, send2, keep1, keep2, in_mine, in_away, six_sum = project_back(
        at_back, own_rows, other_rows, gq, gkv, w_sel, gy1
    )
    n = width // 16
    begin("one", keep1.reshape(*bits, 3 * n, cols), cross(send1).reshape(*bits, 3 * n, cols), every[1:])
    begin(
        "two",
        keep2.reshape(2, *bits[1:], 3 * n, cols),
        pair_up(send2, 1).reshape(2, *bits[1:], 3 * n, cols),
        ["outer", "z", "far"],
    )
    grad_in = (in_mine + swap(in_away).astype(F32)).astype(BF)
    token[0] = grad_in
    input_rows = over_rows(grad_in.reshape(row_count, span // 2, width))
    reduce("up", "z")
    reduce("rest", "outer")

    spot = lax.broadcasted_iota(jnp.int32, (1, 2, 1), 1) == core
    wide_sum = jnp.where(spot, six_sum[:6].reshape(6, 1, cols), 0.0).reshape(6, width)
    each = jnp.concatenate([small[4:10], wide_sum[5:]], axis=0).reshape(7, 4, shard).transpose(1, 0, 2)
    small = jnp.concatenate(
        [small[:4].reshape(4, 4, shard), wide_sum[:4].reshape(4, 4, shard), each, jnp.zeros_like(each[:, :1])], axis=1
    )
    small = jnp.broadcast_to(small[None], (row_count, 4, 16, shard)).reshape(-1, 16, shard)
    small = lax.all_to_all(
        after(small, token[0]), ("row", "group", "outer", "core"), 0, 0, tiled=True
    )

    reduce("one", "y")
    reduce("two", "outer")
    reduce("up", "far")
    reduce("one", "z")
    reduce("two", "z")
    reduce("rest", "z")
    small = jnp.sum(after(small, token[0]), axis=0)
    gather("up", "far")
    reduce("one", "far")
    reduce("two", "far")
    input_grad = rows_whole(after(input_rows, token[0]))
    gather("up", "z")
    gather("one", "far")
    gather("two", "far")
    reduce("rest", "far")
    gather("up", "y")
    gather("one", "z")
    gather("two", "z")
    gather("rest", "far")
    gather("one", "y")
    gather("rest", "z")
    gather("two", "y")
    up_total = settle("up")
    gather("rest", "y")
    first_total, second_total, rest_total = settle("one"), settle("two"), settle("rest")

    def both_cores(total):
        parts = total.reshape(2, 4, 3, -1, cols)
        halves = in_order(core, take(parts, core), swap(take(parts, 1 - core)))
        return halves.transpose(1, 3, 2, 0, 4).reshape(shard, 3 * width).astype(F32)

    one, two = both_cores(first_total), both_cores(second_total)
    g_query = jnp.concatenate([one, two[:, :width]], axis=1)
    g_kv = two[:, width:]
    g_up = up_total.reshape(8, shard, -1).transpose(1, 0, 2).reshape(shard, -1).astype(F32)
    rest_total = rest_total.reshape(4, 2, -1, cols)
    n = wide // 4
    g_down = rest_total[:, :, :n].transpose(0, 2, 1, 3).reshape(wide, width).astype(F32)
    g_out = rest_total[:, :, n:].transpose(0, 2, 1, 3).reshape(shard, width).astype(F32)

    return (
        output, input_grad, g_query, g_kv, g_out, g_up, g_down,
        small[4:8].reshape(-1), small[14], small[8], small[:4].reshape(-1), *(small[i] for i in range(9, 14)),
    )


def solution(mesh):
    def step(*args):
        ctx, fsdp = mesh.shape["ctx"], mesh.shape["fsdp"]
        row_count = args[0].shape[0] // (fsdp // 2)
        per_row = ctx // row_count
        fine = Mesh(
            mesh.devices.reshape(row_count, per_row, fsdp // 2, 2), ("row", "group", "outer", "core")
        )
        tokens = P(("outer", "core"), ("row", "group"), None)
        mat, vec = P(("outer", "core"), None), P(("outer", "core"))
        in_specs = (tokens, *[mat] * 5, *[vec] * 9, mat, mat, tokens)
        out_specs = (tokens, tokens, *[mat] * 5, *[vec] * 9)
        quarter = args[0].shape[2] // 4
        fits = per_row == 1 and fsdp == 4 and row_count == 8 and args[0].shape[2] % (2 * LANES) == 0 and quarter % 32 == 0
        body = row_layer if fits else functools.partial(layer, None, per_row)
        return jax.shard_map(
            body, mesh=fine, in_specs=in_specs, out_specs=out_specs, check_vma=False
        )(*args)

    return step
```

```python
import functools

import jax
import jax.numpy as jnp
from jax import lax
from jax.experimental import pallas as pl
from jax.experimental.pallas import tpu as pltpu
from jax.sharding import Mesh
from jax.sharding import PartitionSpec as P

HEADS = 12
EPSILON = 1e-05
BLOCKED = -1e30
BF = jnp.bfloat16
F32 = jnp.float32
LANES = 128
CHUNK = 16


def matmul(left_mat, right_mat):
    return jnp.dot(left_mat, right_mat, preferred_element_type=F32)


def rows_inner(left_mat, right_mat):
    return lax.dot_general(left_mat, right_mat, (((0,), (0,)), ((), ())), preferred_element_type=F32)


def times_transposed(left_mat, right_mat):
    return lax.dot_general(left_mat, right_mat, (((1,), (1,)), ((), ())), preferred_element_type=F32)


def normalize(values, gain_vec, shift_vec):
    center = values - jnp.mean(values, axis=-1, keepdims=True)
    scale_inv = lax.rsqrt(jnp.mean(center * center, axis=-1, keepdims=True) + EPSILON)
    normed = center * scale_inv
    return (normed * gain_vec + shift_vec, normed, scale_inv)


def normalize_back(grad_in, normed, scale_inv, gain_vec):
    scaled = grad_in * gain_vec
    inner_part = (
        scaled
        - jnp.mean(scaled, axis=-1, keepdims=True)
        - normed * jnp.mean(scaled * normed, axis=-1, keepdims=True)
    )
    return (inner_part * scale_inv, jnp.sum(grad_in * normed, axis=0), jnp.sum(grad_in, axis=0))


def column_sum(values):
    return jnp.sum(values.astype(F32), axis=0)


def forward_kernel(
    heads, hd, rows_ref, w_ref, bias_ref, ent_ref, qseg_ref, kseg_ref,
    att_ref, wts_ref, inv_ref, qcat_ref, kcat_ref, vneg_ref,
    kaug_s, vaug_s, score_s,
):
    step = pl.program_id(0)
    span = heads * hd
    full = rows_ref.shape[0]
    block = att_ref.shape[0]
    scale = hd ** (-0.5)

    @pl.when(step == 0)
    def _():
        kaug_s[:, :, LANES:] = jnp.broadcast_to(kseg_ref[...][None], (heads, full, LANES))
        lane = lax.broadcasted_iota(jnp.int32, (block, LANES - hd), 1)
        one_col = jnp.where(lane == 0, 1.0, 0.0).astype(BF)
        neg_col = jnp.where(lane < 2, -1.0, 0.0).astype(BF)

        def project(piece, carry):
            at = pl.ds(pl.multiple_of(piece * block, block), block)
            rows = rows_ref[at, :]
            ent = ent_ref[at, :hd]
            wide = ent_ref[at, :1] > 0
            word = (1 - ent).astype(BF)

            def part(index):
                cols = slice(index * span, (index + 1) * span)
                return jnp.dot(rows, w_ref[:, cols], preferred_element_type=F32) + bias_ref[:, cols]

            q_word = (jnp.where(wide, part(2), part(0))).astype(BF) * BF(scale)
            q_ent = (jnp.where(wide, part(3), part(1))).astype(BF) * BF(scale)
            keys = part(4).astype(BF)
            vals = part(5).astype(BF)
            for h in range(heads):
                cut = slice(h * hd, (h + 1) * hd)
                qcat_ref[h, at, :] = jnp.concatenate([q_word[:, cut], q_ent[:, cut]], axis=1)
                k_pair = jnp.concatenate([keys[:, cut] * word, keys[:, cut] * ent], axis=1)
                kcat_ref[h, at, :] = k_pair
                kaug_s[h, at, :LANES] = k_pair
                vneg_ref[h, at, :] = jnp.concatenate([vals[:, cut], neg_col], axis=1)
                vaug_s[h, at, :] = jnp.concatenate([vals[:, cut], one_col], axis=1)
            return carry

        lax.fori_loop(0, full // block, project, 0)

    here = pl.ds(pl.multiple_of(step * block, block), block)
    q_seg = qseg_ref[here, :]
    lane = lax.broadcasted_iota(jnp.int32, (block, LANES), 1)
    inv_all = jnp.zeros((block, LANES), F32)
    mixed = []
    for h in range(heads):
        q_aug = jnp.concatenate([qcat_ref[h, here, :], q_seg], axis=1)
        score_s[h % 2] = lax.dot_general(
            q_aug, kaug_s[h], (((1,), (1,)), ((), ())), preferred_element_type=F32
        )
        for r in range(0, block, CHUNK):
            s = score_s[h % 2, r : r + CHUNK, :]
            top = jnp.max(s, axis=1, keepdims=True)
            wts_ref[h, r : r + CHUNK, :] = jnp.exp(s - top).astype(BF)
        out = jnp.dot(wts_ref[h], vaug_s[h], preferred_element_type=F32)
        inv = 1.0 / out[:, hd : hd + 1]
        inv_all = jnp.where(lane == h, inv, inv_all)
        mixed.append((out[:, :hd] * inv).astype(BF))
    att_ref[...] = jnp.concatenate(mixed, axis=1)
    inv_ref[...] = inv_all


def attention_forward(rows, w_sel, bias_sel, ent, qseg, kseg, heads, hd):
    full, width = rows.shape
    block = min(256, full)
    span = heads * hd
    steps = full // block
    whole = lambda *dims: pl.BlockSpec(dims, lambda i: (0,) * len(dims))
    return pl.pallas_call(
        functools.partial(forward_kernel, heads, hd),
        grid=(steps,),
        in_specs=[
            whole(full, width),
            whole(width, 6 * span),
            whole(1, 6 * span),
            whole(full, LANES),
            whole(full, LANES),
            whole(full, LANES),
        ],
        out_specs=[
            pl.BlockSpec((block, span), lambda i: (i, 0)),
            pl.BlockSpec((heads, block, full), lambda i: (0, i, 0)),
            pl.BlockSpec((block, LANES), lambda i: (i, 0)),
            whole(heads, full, 2 * hd),
            whole(heads, full, 2 * hd),
            whole(heads, full, LANES),
        ],
        out_shape=[
            jax.ShapeDtypeStruct((full, span), BF),
            jax.ShapeDtypeStruct((heads, full, full), BF),
            jax.ShapeDtypeStruct((full, LANES), F32),
            jax.ShapeDtypeStruct((heads, full, 2 * hd), BF),
            jax.ShapeDtypeStruct((heads, full, 2 * hd), BF),
            jax.ShapeDtypeStruct((heads, full, LANES), BF),
        ],
        scratch_shapes=[
            pltpu.VMEM((heads, full, 2 * LANES), BF),
            pltpu.VMEM((heads, full, LANES), BF),
            pltpu.VMEM((2, block, full), F32),
        ],
        compiler_params=pltpu.CompilerParams(vmem_limit_bytes=60 << 20),
        cost_estimate=pl.CostEstimate(
            flops=2 * full * width * 6 * span + 8 * heads * full * full * LANES,
            bytes_accessed=2 * heads * full * full + 10 * full * width,
            transcendentals=heads * full * full,
        ),
        name="attention_forward",
    )(rows, w_sel, bias_sel, ent, qseg, kseg)


def backward_kernel(
    heads, hd, go_ref, att_ref, inv_ref, wts_ref, qcat_ref, kcat_ref, vneg_ref, ent_ref, entb_ref,
    gq_ref, gkv_ref, gscore_s, low_s, gk_s, gv_s,
):
    step = pl.program_id(0)
    span = heads * hd
    block = go_ref.shape[0]
    full = kcat_ref.shape[1]
    scale = hd ** (-0.5)
    lane = lax.broadcasted_iota(jnp.int32, (block, LANES - hd), 1)
    is_ent = entb_ref[:, :1] > 0
    g_word, g_ent = [], []
    for h in range(heads):
        cut = slice(h * hd, (h + 1) * hd)
        g_low = (go_ref[:, cut].astype(F32) * inv_ref[:, h : h + 1]).astype(BF)
        delta = jnp.sum(g_low.astype(F32) * att_ref[:, cut].astype(F32), axis=1, keepdims=True)
        d_hi = delta.astype(BF)
        d_lo = (delta - d_hi.astype(F32)).astype(BF)
        extra = jnp.where(
            lane == 0, d_hi.astype(F32), jnp.where(lane == 1, d_lo.astype(F32), 0.0)
        ).astype(BF)
        g_aug = jnp.concatenate([g_low, extra], axis=1)
        gscore_s[h % 2] = lax.dot_general(
            g_aug, vneg_ref[h], (((1,), (1,)), ((), ())), preferred_element_type=F32
        )
        for r in range(0, block, CHUNK):
            low_s[h % 2, r : r + CHUNK, :] = (
                wts_ref[h, r : r + CHUNK, :].astype(F32) * gscore_s[h % 2, r : r + CHUNK, :]
            ).astype(BF)
        g_q = jnp.dot(low_s[h % 2], kcat_ref[h], preferred_element_type=F32) * scale
        g_word.append(g_q[:, :hd])
        g_ent.append(g_q[:, hd:])
        g_k = lax.dot_general(
            qcat_ref[h], low_s[h % 2], (((0,), (0,)), ((), ())), preferred_element_type=F32
        )
        g_v = lax.dot_general(
            g_low, wts_ref[h], (((0,), (0,)), ((), ())), preferred_element_type=F32
        )

        @pl.when(step == 0)
        def _(h=h, g_k=g_k, g_v=g_v):
            gk_s[h] = g_k
            gv_s[h] = g_v

        @pl.when(step > 0)
        def _(h=h, g_k=g_k, g_v=g_v):
            gk_s[h] += g_k
            gv_s[h] += g_v

    g_word = jnp.concatenate(g_word, axis=1)
    g_ent = jnp.concatenate(g_ent, axis=1)
    gq_ref[:, :span] = jnp.where(is_ent, 0.0, g_word).astype(BF)
    gq_ref[:, span : 2 * span] = jnp.where(is_ent, 0.0, g_ent).astype(BF)
    gq_ref[:, 2 * span : 3 * span] = jnp.where(is_ent, g_word, 0.0).astype(BF)
    gq_ref[:, 3 * span :] = jnp.where(is_ent, g_ent, 0.0).astype(BF)

    @pl.when(step == pl.num_programs(0) - 1)
    def _():
        def close(piece, carry):
            at = pl.ds(pl.multiple_of(piece * block, block), block)
            pick = ent_ref[at, :1] > 0
            g_keys, g_vals = [], []
            for h in range(heads):
                both = gk_s[h, :, at].T
                g_keys.append(jnp.where(pick, both[:, hd:], both[:, :hd]))
                g_vals.append(gv_s[h, :, at].T)
            gkv_ref[at, :span] = jnp.concatenate(g_keys, axis=1).astype(BF)
            gkv_ref[at, span:] = jnp.concatenate(g_vals, axis=1).astype(BF)
            return carry

        lax.fori_loop(0, full // block, close, 0)


def attention_backward(g_out, att, inv, wts, qcat, kcat, vneg, ent, heads, hd):
    full, span = att.shape
    block = min(256, full)
    whole = lambda *dims: pl.BlockSpec(dims, lambda i: (0,) * len(dims))
    by_rows = lambda width: pl.BlockSpec((block, width), lambda i: (i, 0))
    by_head = lambda width: pl.BlockSpec((heads, block, width), lambda i: (0, i, 0))
    return pl.pallas_call(
        functools.partial(backward_kernel, heads, hd),
        grid=(full // block,),
        in_specs=[
            by_rows(span),
            by_rows(span),
            by_rows(LANES),
            by_head(full),
            by_head(2 * hd),
            whole(heads, full, 2 * hd),
            whole(heads, full, LANES),
            whole(full, LANES),
            by_rows(LANES),
        ],
        out_specs=[by_rows(4 * span), whole(full, 2 * span)],
        out_shape=[
            jax.ShapeDtypeStruct((full, 4 * span), BF),
            jax.ShapeDtypeStruct((full, 2 * span), BF),
        ],
        scratch_shapes=[
            pltpu.VMEM((2, block, full), F32),
            pltpu.VMEM((2, block, full), BF),
            pltpu.VMEM((heads, 2 * hd, full), F32),
            pltpu.VMEM((heads, hd, full), F32),
        ],
        compiler_params=pltpu.CompilerParams(vmem_limit_bytes=60 << 20),
        cost_estimate=pl.CostEstimate(
            flops=16 * heads * full * full * LANES,
            bytes_accessed=2 * heads * full * full + 20 * full * span,
            transcendentals=0,
        ),
        name="attention_backward",
    )(g_out, att, inv, wts, qcat, kcat, vneg, ent, ent)


def layer(
    half, per_row, inputs, query_weight, kv_weight, out_weight, up_weight, down_weight,
    query_bias, value_bias, out_bias, up_bias, down_bias,
    norm1_gain, norm1_shift, norm2_gain, norm2_shift, types, lengths, cotangent,
):
    rows_here, span, width = inputs.shape
    head_dim = width // HEADS
    full = types.shape[1]
    members = 2 * per_row
    heads = HEADS // members
    cols = heads * head_dim
    row_count = lax.axis_size("row")
    outer = lax.axis_size("outer")
    core = lax.axis_index("core")
    group = lax.axis_index("group")
    member = group * 2 + core
    row_id = lax.axis_index("row")
    own = row_count * (span // 2)

    def swap(values):
        return lax.ppermute(values, "core", [(0, 1), (1, 0)])

    def in_order(index, mine, other):
        return jnp.stack([jnp.where(index == 0, mine, other), jnp.where(index == 0, other, mine)])

    def gather_outer(values):
        if outer == 2:
            other = lax.ppermute(values, "outer", [(0, 1), (1, 0)])
            return in_order(lax.axis_index("outer"), values, other)
        return lax.all_gather(values, "outer", axis=0, tiled=False)

    def gather_members(values):
        pair = in_order(core, values, swap(values))
        if per_row == 1:
            return pair
        spread = lax.all_gather(pair, "group", axis=0, tiled=False)
        return spread.reshape((members,) + values.shape)

    def exchange_members(values):
        if per_row == 1:
            mine = lax.dynamic_index_in_dim(values, core, 0, keepdims=False)
            away = lax.dynamic_index_in_dim(values, 1 - core, 0, keepdims=False)
            return in_order(core, mine, swap(away))
        return lax.all_to_all(values, ("group", "core"), 0, 0, tiled=True)

    def take(values, index, axis):
        return lax.dynamic_index_in_dim(values, index, axis, keepdims=False)

    def to_row(values):
        pieces = values.reshape(rows_here, 2, span // 2, width)
        other = swap(take(pieces, 1 - core, 1))
        both = in_order(core, take(pieces, core, 1), other).reshape(row_count, span // 2, width)
        return lax.all_to_all(both, "row", 0, 0, tiled=True).reshape(own, width)

    def from_row(values):
        back = lax.all_to_all(values.reshape(row_count, span // 2, width), "row", 0, 0, tiled=True)
        back = back.reshape(2, rows_here, span // 2, width)
        other = swap(take(back, 1 - core, 0))
        both = in_order(core, take(back, core, 0), other)
        return both.transpose(1, 0, 2, 3).reshape(rows_here, span, width)

    own_rows = to_row(inputs)
    all_rows = gather_members(own_rows).reshape(full, width)

    tags = jnp.concatenate([types, lengths], axis=1)
    tags = in_order(core, tags, swap(tags)).reshape(row_count, -1)
    tags = take(tags, row_id, 0)
    types_row, lengths_row = tags[:full], tags[full:]

    def by_member(values):
        return values.reshape(row_count, per_row, 2, span // 2).transpose(1, 2, 0, 3).reshape(full)

    entity = by_member(types_row) > 0
    positions = by_member(lax.iota(jnp.int32, full))
    docs = lengths_row.shape[0]
    ends = [jnp.sum(lengths_row[: d + 1]) for d in range(docs)]
    seg = sum((positions >= end).astype(jnp.int32) for end in ends)
    lanes = lax.broadcasted_iota(jnp.int32, (full, LANES), 1)
    same = lanes == seg[:, None]
    qseg = jnp.where(same, 1.0, 0.0).astype(BF)
    kseg = jnp.where(same | (lanes >= docs), 0.0, BLOCKED).astype(BF)
    ent = jnp.broadcast_to(jnp.where(entity, 1.0, 0.0).astype(BF)[:, None], (full, LANES))

    shard = query_weight.shape[0]
    cut = jnp.concatenate([query_weight, kv_weight], axis=1).reshape(shard, 6, members, cols)
    away = take(cut, group * 2 + 1 - core, 2).reshape(shard, 6 * cols)
    mine = take(cut, member, 2).reshape(shard, 6 * cols)
    w_sel = gather_outer(in_order(core, mine, swap(away))).reshape(width, 6 * cols)

    vectors = (
        query_bias, value_bias, out_bias, up_bias, down_bias,
        norm1_gain, norm1_shift, norm2_gain, norm2_shift,
    )
    sizes = [v.shape[0] for v in vectors]
    packed = jnp.concatenate(vectors)
    packed = lax.all_gather(packed, ("outer", "core"), axis=0, tiled=False)
    offsets = [sum(sizes[:i]) for i in range(len(sizes) + 1)]
    (b_query, b_value, b_out, b_up, b_down, g_one, s_one, g_two, s_two) = (
        packed[:, a:b].reshape(-1).astype(F32) for a, b in zip(offsets[:-1], offsets[1:])
    )
    b_six = jnp.concatenate([b_query, jnp.zeros((width,), F32), b_value])
    b_sel = take(b_six.reshape(6, members, cols), member, 1).reshape(1, 6 * cols)

    att, inv_stored, wts = None, None, None
    att, wts, inv_stored, qcat, kcat, vneg = attention_forward(
        all_rows, w_sel, b_sel, ent, qseg, kseg, heads, head_dim
    )

    def fetch(values):
        return gather_outer(in_order(core, values, swap(values))).reshape(-1, values.shape[1])

    w_out, w_up, w_down = fetch(out_weight), fetch(up_weight), fetch(down_weight)

    def heads_to_tokens(values):
        got = exchange_members(values.reshape(members, own, cols))
        return got.transpose(1, 0, 2).reshape(own, width)

    def tokens_to_heads(values):
        parts = values.reshape(own, members, cols).transpose(1, 0, 2)
        return exchange_members(parts).reshape(full, cols)

    attended = heads_to_tokens(att)
    attn_out = matmul(attended, w_out) + b_out
    hidden, normed_one, inv_one = normalize(own_rows.astype(F32) + attn_out, g_one, s_one)
    hidden_low = hidden.astype(BF)
    up_proj = matmul(hidden_low, w_up) + b_up
    gelu_out, gelu_pull = jax.vjp(lambda v: jax.nn.gelu(v, approximate=False), up_proj)
    act_low = gelu_out.astype(BF)
    ffn_out = matmul(act_low, w_down) + b_down
    result, normed_two, inv_two = normalize(hidden + ffn_out, g_two, s_two)
    output = from_row(result.astype(BF))

    cot = to_row(cotangent).astype(F32)
    grad_y2, grad_g2, grad_s2 = normalize_back(cot, normed_two, inv_two, g_two)
    grad_ffn = grad_y2.astype(BF)
    grad_act = times_transposed(grad_ffn, w_down)
    grad_up = gelu_pull(grad_act)[0].astype(BF)
    grad_hidden = grad_y2 + times_transposed(grad_up, w_up)
    grad_y1, grad_g1, grad_s1 = normalize_back(grad_hidden, normed_one, inv_one, g_one)
    grad_attn = grad_y1.astype(BF)
    grad_attended = times_transposed(grad_attn, w_out).astype(BF)

    def pick_rows(left, core_index, outer_index):
        parts = left.reshape(left.shape[0], outer, 2, -1)
        if outer_index is None:
            return take(parts, core_index, 2).reshape(left.shape[0], -1)
        return take(take(parts, core_index, 2), outer_index, 1)

    def reduce_outer(partial):
        if outer == 2:
            me = lax.axis_index("outer")
            other = lax.ppermute(take(partial, 1 - me, 0).astype(BF), "outer", [(0, 1), (1, 0)])
            return take(partial, me, 0).astype(F32) + other.astype(F32)
        return lax.psum_scatter(partial.astype(BF), "outer", scatter_dimension=0, tiled=False).astype(F32)

    def shard_grad(left, right):
        away = rows_inner(pick_rows(left, 1 - core, None), right).astype(BF)
        mine = rows_inner(pick_rows(left, core, None), right)
        pair = mine + swap(away).astype(F32)
        part = reduce_outer(pair.reshape(outer, -1, right.shape[1]))
        return lax.psum(part.astype(BF), ("row", "group")).astype(F32)

    g_w_down = shard_grad(act_low, grad_ffn)
    g_w_up = shard_grad(hidden_low, grad_up)
    g_w_out = shard_grad(attended, grad_attn)

    gq, gkv = attention_backward(
        tokens_to_heads(grad_attended), att, inv_stored, wts, qcat, kcat, vneg, ent, heads, head_dim
    )
    g_six = jnp.concatenate([gq, gkv], axis=1)
    g_sel = reduce_outer(rows_inner(all_rows, g_six).reshape(outer, -1, 6 * cols))
    g_sel = lax.psum(g_sel.astype(BF), "row").reshape(2, shard, 6, cols)
    got = in_order(core, take(g_sel, core, 0), swap(take(g_sel, 1 - core, 0)))
    if per_row > 1:
        got = lax.all_gather(got, "group", axis=0, tiled=False)
    got = got.reshape(members, shard, 6, cols).transpose(1, 2, 0, 3).reshape(shard, 6 * width)
    g_w_query = got[:, : 4 * width].astype(F32)
    g_w_kv = got[:, 4 * width :].astype(F32)

    part_in = times_transposed(g_six, w_sel)
    got_in = exchange_members(part_in.astype(BF).reshape(members, own, width))
    grad_in = grad_y1 + jnp.sum(got_in.astype(F32), axis=0)
    input_grad = from_row(grad_in.astype(BF))

    six_sum = column_sum(g_six).reshape(6, 1, cols)
    spot = lax.broadcasted_iota(jnp.int32, (1, members, 1), 1) == member
    six_sum = jnp.where(spot, six_sum, 0.0).reshape(6, width)
    small = [
        six_sum[:4].reshape(-1), six_sum[5], column_sum(grad_attn), column_sum(grad_up),
        column_sum(grad_ffn), grad_g1, grad_s1, grad_g2, grad_s2,
    ]
    total = lax.psum(jnp.concatenate(small), ("row", "group", "outer", "core"))
    me = lax.axis_index("outer") * 2 + core
    pieces, at = [], 0
    for size in sizes:
        whole_size = size * outer * 2
        pieces.append(lax.dynamic_slice_in_dim(total[at : at + whole_size], me * size, size))
        at += whole_size
    return (output, input_grad, g_w_query, g_w_kv, g_w_out, g_w_up, g_w_down, *pieces)


def project_kernel(
    heads, hd, query_rows, kv_rows, at_ref, own_ref, other_ref, bias_ref, ent_ref, *refs
):
    n_query, n_kv = len(query_rows), len(kv_rows)
    query_refs, kv_refs = refs[:n_query], refs[n_query : n_query + n_kv]
    qcat_ref, kcat_ref, vaug_ref, w_ref, sems = refs[n_query + n_kv :]
    span = heads * hd
    half, width = own_ref.shape
    block = min(256, half)
    scale = hd ** (-0.5)
    core = at_ref[0]
    made = []
    for i, (ref, rows) in enumerate(zip(query_refs + kv_refs, query_rows + kv_rows)):
        first, blocks = (0, 4) if i < n_query else (4, 2)
        to = pl.ds(pl.multiple_of(at_ref[1 + i], 16), rows)
        for b in range(blocks):
            here = pl.ds(pl.multiple_of(b * width + core * span, LANES), span)
            cols = slice((first + b) * span, (first + b + 1) * span)
            copy = pltpu.make_async_copy(ref.at[:, here], w_ref.at[to, cols], sems.at[len(made)])
            copy.start()
            made.append(copy)
    lane = lax.broadcasted_iota(jnp.int32, (block, LANES - hd), 1)
    tail = jnp.where(lane < 2, -1.0, jnp.where(lane == 2, 1.0, 0.0)).astype(BF)
    for copy in made:
        copy.wait()
    for side, rows_ref in enumerate((own_ref, other_ref)):

        def project(piece, carry, side=side, rows_ref=rows_ref):
            rows = rows_ref[pl.ds(pl.multiple_of(piece * block, block), block), :]
            at = pl.ds(pl.multiple_of(side * half + piece * block, block), block)
            ent = ent_ref[at, :hd]
            wide = ent_ref[at, :1] > 0
            word = (1 - ent).astype(BF)

            def part(index):
                cols = slice(index * span, (index + 1) * span)
                return jnp.dot(rows, w_ref[:, cols], preferred_element_type=F32) + bias_ref[:, cols]

            q_word = (jnp.where(wide, part(2), part(0))).astype(BF) * BF(scale)
            q_ent = (jnp.where(wide, part(3), part(1))).astype(BF) * BF(scale)
            keys = part(4).astype(BF)
            vals = part(5).astype(BF)
            for h in range(heads):
                cut = slice(h * hd, (h + 1) * hd)
                qcat_ref[h, at, :] = jnp.concatenate([q_word[:, cut], q_ent[:, cut]], axis=1)
                kcat_ref[h, at, :] = jnp.concatenate([keys[:, cut] * word, keys[:, cut] * ent], axis=1)
                vaug_ref[h, at, :] = jnp.concatenate([vals[:, cut], tail], axis=1)
            return carry

        lax.fori_loop(0, half // block, project, 0)


def row_project(at, own, other, bias, ent, query_pieces, kv_pieces, heads, hd):
    half, width = own.shape
    full = 2 * half
    span = heads * hd
    vmem = pl.BlockSpec(memory_space=pltpu.VMEM)
    anywhere = pl.BlockSpec(memory_space=pl.ANY)
    query_rows = tuple(p.shape[0] for p in query_pieces)
    kv_rows = tuple(p.shape[0] for p in kv_pieces)
    return pl.pallas_call(
        functools.partial(project_kernel, heads, hd, query_rows, kv_rows),
        in_specs=[pl.BlockSpec(memory_space=pltpu.SMEM)]
        + [vmem] * 4
        + [anywhere] * (len(query_pieces) + len(kv_pieces)),
        out_specs=[vmem] * 4,
        out_shape=[
            jax.ShapeDtypeStruct((heads, full, 2 * hd), BF),
            jax.ShapeDtypeStruct((heads, full, 2 * hd), BF),
            jax.ShapeDtypeStruct((heads, full, LANES), BF),
            jax.ShapeDtypeStruct((width, 6 * span), BF),
        ],
        scratch_shapes=[pltpu.SemaphoreType.DMA((4 * len(query_pieces) + 2 * len(kv_pieces),))],
        compiler_params=pltpu.CompilerParams(vmem_limit_bytes=60 << 20),
        cost_estimate=pl.CostEstimate(
            flops=2 * full * width * 6 * span, bytes_accessed=18 * full * width, transcendentals=0
        ),
        name="row_project",
    )(at, own, other, bias, ent, *query_pieces, *kv_pieces)


def attend_kernel(
    heads, hd, qcat_ref, qseg_ref, kcat_ref, kseg_ref, vaug_ref, keep_ref, send_ref, wts_ref, inv_ref, score_s
):
    step = pl.program_id(0)
    block = keep_ref.shape[0]
    q_seg = qseg_ref[...]
    lane = lax.broadcasted_iota(jnp.int32, (block, LANES), 1)
    inv_all = jnp.zeros((block, LANES), F32)
    mixed = []
    for h in range(heads):
        q_aug = jnp.concatenate([qcat_ref[h], q_seg], axis=1)
        k_aug = jnp.concatenate([kcat_ref[h], kseg_ref[...]], axis=1)
        score_s[h % 2] = lax.dot_general(
            q_aug, k_aug, (((1,), (1,)), ((), ())), preferred_element_type=F32
        )
        for r in range(0, block, CHUNK):
            s = score_s[h % 2, r : r + CHUNK, :]
            top = jnp.max(s, axis=1, keepdims=True)
            wts_ref[h, r : r + CHUNK, :] = jnp.exp(s - top).astype(BF)
        out = jnp.dot(wts_ref[h], vaug_ref[h], preferred_element_type=F32)
        inv = 1.0 / out[:, hd + 2 : hd + 3]
        inv_all = jnp.where(lane == h, inv, inv_all)
        mixed.append((out[:, :hd] * inv).astype(BF))
    mixed = jnp.concatenate(mixed, axis=1)
    inv_ref[...] = inv_all
    late = pl.num_programs(0) // 2

    @pl.when(step < late)
    def _():
        send_ref[...] = mixed

    @pl.when(step >= late)
    def _():
        keep_ref[...] = mixed


def row_attend(qcat, kcat, vaug, qseg, kseg, heads, hd):
    full = qcat.shape[1]
    half = full // 2
    block = min(256, half)
    span = heads * hd
    first = half // block
    whole = lambda *dims: pl.BlockSpec(dims, lambda i: (0,) * len(dims))
    turn = lambda i: jnp.where(i < first, i + first, i - first)
    return pl.pallas_call(
        functools.partial(attend_kernel, heads, hd),
        grid=(full // block,),
        in_specs=[
            pl.BlockSpec((heads, block, 2 * hd), lambda i: (0, turn(i), 0)),
            pl.BlockSpec((block, LANES), lambda i: (turn(i), 0)),
            whole(heads, full, 2 * hd),
            whole(full, LANES),
            whole(heads, full, LANES),
        ],
        out_specs=[
            pl.BlockSpec((block, span), lambda i: (jnp.maximum(i - first, 0), 0)),
            pl.BlockSpec((block, span), lambda i: (jnp.minimum(i, first - 1), 0)),
            pl.BlockSpec((heads, block, full), lambda i: (0, turn(i), 0)),
            pl.BlockSpec((block, LANES), lambda i: (turn(i), 0)),
        ],
        out_shape=[
            jax.ShapeDtypeStruct((half, span), BF),
            jax.ShapeDtypeStruct((half, span), BF),
            jax.ShapeDtypeStruct((heads, full, full), BF),
            jax.ShapeDtypeStruct((full, LANES), F32),
        ],
        scratch_shapes=[pltpu.VMEM((2, block, full), F32)],
        compiler_params=pltpu.CompilerParams(vmem_limit_bytes=60 << 20),
        cost_estimate=pl.CostEstimate(
            flops=8 * heads * full * full * LANES,
            bytes_accessed=2 * heads * full * full + 4 * full * LANES * heads,
            transcendentals=heads * full * full,
        ),
        name="row_attend",
    )(qcat, qseg, kcat, kseg, vaug)


def token_kernel(
    out_rows, up_rows, down_rows, at_ref, own_ref, mine_ref, theirs_ref, cot_ref, vec_ref, *refs
):
    groups = (out_rows, up_rows, down_rows)
    sets, at = [], 0
    for rows in groups:
        sets.append(refs[at : at + len(rows)])
        at += len(rows)
    (
        result_ref, gy1_ref, gmine_ref, gtheirs_ref, act_ref, hlow_ref, gffn_ref, gup_ref, gattn_ref,
        small_ref, wout_s, wup_s, wdown_s, acc_s, hid_s, norm_s, inv_s, slope_s, gy2_s, tmp_s, sum_s, sems,
    ) = refs[at:]
    total, width = own_ref.shape
    ff = wup_s.shape[1]
    parts = ff // width
    span = mine_ref.shape[1]
    core = at_ref[0]
    made, slot = [], 0
    for rows, piece_refs, dst in zip(groups, sets, (wout_s, wup_s, wdown_s)):
        batch = []
        for n, ref in zip(rows, piece_refs):
            to = pl.ds(pl.multiple_of(at_ref[1 + slot], 16), n)
            copy = pltpu.make_async_copy(ref, dst.at[to, :], sems.at[slot])
            copy.start()
            batch.append(copy)
            slot += 1
        made.append(batch)

    def wait(index):
        for copy in made[index]:
            copy.wait()

    def row(index):
        return vec_ref[index : index + 1, :]

    rows_at = lambda i, n: pl.ds(pl.multiple_of(i * n, n), n)
    chunk = 16
    mine_rows = pl.ds(pl.multiple_of(core * span, LANES), span)
    other_rows = pl.ds(pl.multiple_of((1 - core) * span, LANES), span)
    sum_s[...] = jnp.zeros_like(sum_s)
    wait(0)
    acc_s[...] = jnp.dot(mine_ref[...], wout_s[mine_rows, :], preferred_element_type=F32)
    acc_s[...] += jnp.dot(theirs_ref[...], wout_s[other_rows, :], preferred_element_type=F32)

    def first_norm(i, carry):
        at = rows_at(i, chunk)
        y = own_ref[at, :].astype(F32) + (acc_s[at, :] + row(4))
        center = y - jnp.mean(y, axis=1, keepdims=True)
        inv = lax.rsqrt(jnp.mean(center * center, axis=1, keepdims=True) + EPSILON)
        normed = center * inv
        hidden = normed * row(6) + row(7)
        norm_s[at, :] = normed
        inv_s[at, :] = jnp.broadcast_to(inv, (chunk, LANES))
        hid_s[at, :] = hidden
        hlow_ref[at, :] = hidden.astype(BF)
        return carry

    lax.fori_loop(0, total // chunk, first_norm, 0, unroll=4)
    wait(1)
    for c in range(parts):
        cols = slice(c * width, (c + 1) * width)
        tmp_s[c % 2] = jnp.dot(hlow_ref[...], wup_s[:, cols], preferred_element_type=F32)
        for r in range(0, total, chunk):
            x = tmp_s[c % 2, r : r + chunk, :] + row(c)
            cdf = 0.5 + 0.5 * lax.erf(x * (0.5**0.5))
            act_ref[r : r + chunk, cols] = (x * cdf).astype(BF)
            slope_s[r : r + chunk, cols] = cdf + x * (jnp.exp(-0.5 * x * x) * (0.15915494309189535**0.5))
    wait(2)
    acc_s[...] = jnp.dot(act_ref[...], wdown_s[...], preferred_element_type=F32)

    def second_norm(i, carry):
        at = rows_at(i, chunk)
        y = hid_s[at, :] + (acc_s[at, :] + row(5))
        center = y - jnp.mean(y, axis=1, keepdims=True)
        inv = lax.rsqrt(jnp.mean(center * center, axis=1, keepdims=True) + EPSILON)
        normed = center * inv
        result_ref[at, :] = (normed * row(8) + row(9)).astype(BF)
        cot = cot_ref[at, :].astype(F32)
        sum_s[2] += cot * normed
        sum_s[3] += cot
        scaled = cot * row(8)
        g = inv * (
            scaled
            - jnp.mean(scaled, axis=1, keepdims=True)
            - normed * jnp.mean(scaled * normed, axis=1, keepdims=True)
        )
        gy2_s[at, :] = g
        gffn_ref[at, :] = g.astype(BF)
        return carry

    lax.fori_loop(0, total // chunk, second_norm, 0, unroll=2)
    ones = jnp.ones((8, total), BF)
    for c in range(parts):
        cols = slice(c * width, (c + 1) * width)
        tmp_s[c % 2] = lax.dot_general(
            gffn_ref[...], wdown_s[cols, :], (((1,), (1,)), ((), ())), preferred_element_type=F32
        )
        for r in range(0, total, chunk):
            gup_ref[r : r + chunk, cols] = (
                tmp_s[c % 2, r : r + chunk, :] * slope_s[r : r + chunk, cols]
            ).astype(BF)
        small_ref[c : c + 1, :] = jnp.dot(ones, gup_ref[:, cols], preferred_element_type=F32)[:1]
    acc_s[...] = lax.dot_general(
        gup_ref[...], wup_s[...], (((1,), (1,)), ((), ())), preferred_element_type=F32
    )

    def first_back(i, carry):
        at = rows_at(i, chunk)
        g_in = gy2_s[at, :] + acc_s[at, :]
        normed = norm_s[at, :]
        sum_s[0] += g_in * normed
        sum_s[1] += g_in
        scaled = g_in * row(6)
        g = inv_s[at, :1] * (
            scaled
            - jnp.mean(scaled, axis=1, keepdims=True)
            - normed * jnp.mean(scaled * normed, axis=1, keepdims=True)
        )
        gy1_ref[at, :] = g
        gattn_ref[at, :] = g.astype(BF)
        return carry

    lax.fori_loop(0, total // chunk, first_back, 0, unroll=2)
    gmine_ref[...] = lax.dot_general(
        gattn_ref[...], wout_s[mine_rows, :], (((1,), (1,)), ((), ())), preferred_element_type=F32
    ).astype(BF)
    gtheirs_ref[...] = lax.dot_general(
        gattn_ref[...], wout_s[other_rows, :], (((1,), (1,)), ((), ())), preferred_element_type=F32
    ).astype(BF)
    small_ref[4:5, :] = jnp.dot(ones, gattn_ref[...], preferred_element_type=F32)[:1]
    small_ref[5:6, :] = jnp.dot(ones, gffn_ref[...], preferred_element_type=F32)[:1]
    for i in range(4):
        small_ref[6 + i : 7 + i, :] = jnp.sum(sum_s[i], axis=0, keepdims=True)
    small_ref[10:, :] = jnp.zeros((small_ref.shape[0] - 10, width), F32)


def token_block(at, own, mine, theirs, cot, vec, out_pieces, up_pieces, down_pieces):
    total, width = own.shape
    span = mine.shape[1]
    ff = up_pieces[0].shape[1]
    vmem = pl.BlockSpec(memory_space=pltpu.VMEM)
    pieces = [*out_pieces, *up_pieces, *down_pieces]
    shapes = [
        ((total, width), BF), ((total, width), F32), ((total, span), BF), ((total, span), BF),
        ((total, ff), BF), ((total, width), BF), ((total, width), BF), ((total, ff), BF),
        ((total, width), BF), ((16, width), F32),
    ]
    rows = lambda group: tuple(p.shape[0] for p in group)
    return pl.pallas_call(
        functools.partial(token_kernel, rows(out_pieces), rows(up_pieces), rows(down_pieces)),
        in_specs=[pl.BlockSpec(memory_space=pltpu.SMEM)]
        + [vmem] * 5
        + [pl.BlockSpec(memory_space=pl.ANY)] * len(pieces),
        out_specs=[vmem] * len(shapes),
        out_shape=[jax.ShapeDtypeStruct(s, d) for s, d in shapes],
        scratch_shapes=[
            pltpu.VMEM((width, width), BF),
            pltpu.VMEM((width, ff), BF),
            pltpu.VMEM((ff, width), BF),
            pltpu.VMEM((total, width), F32),
            pltpu.VMEM((total, width), F32),
            pltpu.VMEM((total, width), F32),
            pltpu.VMEM((total, LANES), F32),
            pltpu.VMEM((total, ff), F32),
            pltpu.VMEM((total, width), F32),
            pltpu.VMEM((2, total, width), F32),
            pltpu.VMEM((4, 16, width), F32),
            pltpu.SemaphoreType.DMA((len(pieces),)),
        ],
        compiler_params=pltpu.CompilerParams(vmem_limit_bytes=60 << 20),
        cost_estimate=pl.CostEstimate(
            flops=2 * total * width * (4 * ff + 2 * width),
            bytes_accessed=4 * width * ff + 6 * total * ff,
            transcendentals=2 * total * ff,
        ),
        name="token_block",
    )(at, own, mine, theirs, cot, vec, *pieces)


def turned(core, outer, near, z):
    pick = lambda a, b: jnp.where(core == 0, a, b)
    return pick(outer, near), pick(z, outer), pick(near, z)


def up_grad_kernel(at_ref, hlow_ref, gup_ref, send_ref, keep_ref, hid_t):
    width = hlow_ref.shape[1]
    n, span = width // 4, gup_ref.shape[1] // 8
    core = at_ref[0]
    hid_t[...] = hlow_ref[...].T
    for which, out_ref in ((1 - core, send_ref), (core, keep_ref)):
        for outer in range(2):
            left = hid_t[pl.ds(pl.multiple_of((2 * outer + which) * n, 16), n), :]
            for i in range(8):
                out_ref[(*turned(which, outer, i // 4, i // 2 % 2), i % 2)] = jnp.dot(
                    left, gup_ref[:, i * span : (i + 1) * span], preferred_element_type=F32
                ).astype(BF)


def up_grad(at, hlow, gup):
    total, width = hlow.shape
    ff = gup.shape[1]
    vmem = pl.BlockSpec(memory_space=pltpu.VMEM)
    return pl.pallas_call(
        up_grad_kernel,
        in_specs=[pl.BlockSpec(memory_space=pltpu.SMEM), vmem, vmem],
        out_specs=[vmem] * 2,
        out_shape=[jax.ShapeDtypeStruct((2, 2, 2, 2, width // 4, ff // 8), BF)] * 2,
        scratch_shapes=[pltpu.VMEM((width, total), BF)],
        compiler_params=pltpu.CompilerParams(vmem_limit_bytes=60 << 20),
        cost_estimate=pl.CostEstimate(
            flops=2 * total * width * ff, bytes_accessed=2 * width * ff + 2 * total * ff, transcendentals=0
        ),
        name="up_grad",
    )(at, hlow, gup)


def rest_grad_kernel(
    at_ref, mine_ref, theirs_ref, act_ref, gffn_ref, gattn_ref, send_ref, keep_ref, att_t
):
    width = gffn_ref.shape[1]
    span = mine_ref.shape[1]
    core = at_ref[0]
    n, wide = width // 4, act_ref.shape[1] // 4
    att_t[pl.ds(pl.multiple_of(core * span, LANES), span), :] = mine_ref[...].T
    att_t[pl.ds(pl.multiple_of((1 - core) * span, LANES), span), :] = theirs_ref[...].T
    for which, rest_ref in ((1 - core, send_ref), (core, keep_ref)):
        for outer in range(2):
            shard = 2 * outer + which
            left = act_ref[:, pl.ds(pl.multiple_of(shard * wide, LANES), wide)]
            down = lax.dot_general(left, gffn_ref[...], (((0,), (0,)), ((), ())), preferred_element_type=F32)
            rows = pl.ds(pl.multiple_of(shard * n, 16), n)
            out = jnp.dot(att_t[rows, :], gattn_ref[...], preferred_element_type=F32)
            for i in range(8):
                r, c = i // 2, i % 2
                cols = slice(c * span, (c + 1) * span)
                at = (*turned(which, outer, i // 4, i // 2 % 2), i % 2)
                rest_ref[(*at, slice(0, wide // 4))] = down[r * wide // 4 : (r + 1) * wide // 4, cols].astype(BF)
                rest_ref[(*at, slice(wide // 4, None))] = out[r * n // 4 : (r + 1) * n // 4, cols].astype(BF)


def rest_grad(at, mine, theirs, act, gffn, gattn):
    total, width = gffn.shape
    span = mine.shape[1]
    ff = act.shape[1]
    vmem = pl.BlockSpec(memory_space=pltpu.VMEM)
    return pl.pallas_call(
        rest_grad_kernel,
        in_specs=[pl.BlockSpec(memory_space=pltpu.SMEM)] + [vmem] * 5,
        out_specs=[vmem] * 2,
        out_shape=[jax.ShapeDtypeStruct((2, 2, 2, 2, ff // 16 + width // 16, span), BF)] * 2,
        scratch_shapes=[pltpu.VMEM((width, total), BF)],
        compiler_params=pltpu.CompilerParams(vmem_limit_bytes=60 << 20),
        cost_estimate=pl.CostEstimate(
            flops=2 * total * width * (ff + width),
            bytes_accessed=2 * width * ff + 2 * total * ff,
            transcendentals=0,
        ),
        name="rest_grad",
    )(at, mine, theirs, act, gffn, gattn)


def row_backward_kernel(
    heads, hd, first_head, gmine_ref, gother_ref, keep_ref, send_ref, inv_ref, wts_ref, qcat_ref, kcat_ref,
    vaug_ref, ent_ref, entb_ref, *refs,
):
    gq_ref, gkv_ref, gscore_s, low_s, gk_s, gv_s = refs[-6:]
    step = pl.program_id(0)
    block = gmine_ref.shape[0]
    full = kcat_ref.shape[1]
    scale = hd ** (-0.5)
    lane = lax.broadcasted_iota(jnp.int32, (block, LANES - hd), 1)
    is_ent = entb_ref[:, :1] > 0
    early = step < pl.num_programs(0) // 2
    g_all = jnp.where(early, gmine_ref[...], gother_ref[...])
    att_all = jnp.where(early, keep_ref[...], send_ref[...])
    g_word, g_ent = [], []
    for h in range(heads):
        cut = slice(h * hd, (h + 1) * hd)
        g_low = (g_all[:, cut].astype(F32) * inv_ref[:, first_head + h : first_head + h + 1]).astype(BF)
        delta = jnp.sum(g_low.astype(F32) * att_all[:, cut].astype(F32), axis=1, keepdims=True)
        d_hi = delta.astype(BF)
        d_lo = (delta - d_hi.astype(F32)).astype(BF)
        extra = jnp.where(
            lane == 0, d_hi.astype(F32), jnp.where(lane == 1, d_lo.astype(F32), 0.0)
        ).astype(BF)
        g_aug = jnp.concatenate([g_low, extra], axis=1)
        gscore_s[h % 2] = lax.dot_general(
            g_aug, vaug_ref[h], (((1,), (1,)), ((), ())), preferred_element_type=F32
        )
        for r in range(0, block, CHUNK):
            low_s[h % 2, r : r + CHUNK, :] = (
                wts_ref[h, r : r + CHUNK, :].astype(F32) * gscore_s[h % 2, r : r + CHUNK, :]
            ).astype(BF)
        g_q = jnp.dot(low_s[h % 2], kcat_ref[h], preferred_element_type=F32) * scale
        g_word.append(g_q[:, :hd])
        g_ent.append(g_q[:, hd:])
        g_k = lax.dot_general(
            qcat_ref[h], low_s[h % 2], (((0,), (0,)), ((), ())), preferred_element_type=F32
        )
        g_v = lax.dot_general(
            g_low, wts_ref[h], (((0,), (0,)), ((), ())), preferred_element_type=F32
        )

        @pl.when(step == 0)
        def _(h=h, g_k=g_k, g_v=g_v):
            gk_s[h] = g_k
            gv_s[h] = g_v

        @pl.when(step > 0)
        def _(h=h, g_k=g_k, g_v=g_v):
            gk_s[h] += g_k
            gv_s[h] += g_v

    g_word = jnp.concatenate(g_word, axis=1)
    g_ent = jnp.concatenate(g_ent, axis=1)
    gq_ref[0] = jnp.where(is_ent, 0.0, g_word).astype(BF)
    gq_ref[1] = jnp.where(is_ent, 0.0, g_ent).astype(BF)
    gq_ref[2] = jnp.where(is_ent, g_word, 0.0).astype(BF)
    gq_ref[3] = jnp.where(is_ent, g_ent, 0.0).astype(BF)

    @pl.when(step == pl.num_programs(0) - 1)
    def _():
        def close(piece, carry):
            at = pl.ds(pl.multiple_of(piece * block, block), block)
            pick = ent_ref[at, :1] > 0
            g_keys, g_vals = [], []
            for h in range(heads):
                both = gk_s[h, :, at].T
                g_keys.append(jnp.where(pick, both[:, hd:], both[:, :hd]))
                g_vals.append(gv_s[h, :, at].T)
            gkv_ref[0, at, :] = jnp.concatenate(g_keys, axis=1).astype(BF)
            gkv_ref[1, at, :] = jnp.concatenate(g_vals, axis=1).astype(BF)
            return carry

        lax.fori_loop(0, full // block, close, 0)


def row_backward(first_head, heads, grads, gmine, gother, keep, send, inv, wts, qcat, kcat, vaug, ent, hd):
    half, all_cols = keep.shape
    full = 2 * half
    block = min(256, half)
    first = half // block
    cols = heads * hd
    g, c = first_head // heads, first_head * hd // cols
    by_rows = pl.BlockSpec((block, LANES), lambda i: (i, 0))
    by_head = lambda width: pl.BlockSpec((heads, block, width), lambda i: (g, i, 0))
    of_head = lambda width: pl.BlockSpec((heads, full, width), lambda i: (g, 0, 0))
    low = pl.BlockSpec((block, cols), lambda i: (jnp.minimum(i, first - 1), c))
    high = pl.BlockSpec((block, cols), lambda i: (jnp.maximum(i - first, 0), c))
    given = [] if grads is None else list(grads)
    return pl.pallas_call(
        functools.partial(row_backward_kernel, heads, hd, first_head),
        grid=(full // block,),
        in_specs=[
            low, high, low, high,
            by_rows,
            by_head(full),
            by_head(2 * hd),
            of_head(2 * hd),
            of_head(LANES),
            pl.BlockSpec((full, LANES), lambda i: (0, 0)),
            by_rows,
        ]
        + [pl.BlockSpec(memory_space=pl.ANY)] * len(given),
        out_specs=[
            pl.BlockSpec((4, block, cols), lambda i: (0, i, c)),
            pl.BlockSpec((2, full, cols), lambda i: (0, 0, c)),
        ],
        out_shape=[
            jax.ShapeDtypeStruct((4, full, all_cols), BF),
            jax.ShapeDtypeStruct((2, full, all_cols), BF),
        ],
        scratch_shapes=[
            pltpu.VMEM((2, block, full), F32),
            pltpu.VMEM((2, block, full), BF),
            pltpu.VMEM((heads, 2 * hd, full), F32),
            pltpu.VMEM((heads, hd, full), F32),
        ],
        input_output_aliases={11 + i: i for i in range(len(given))},
        compiler_params=pltpu.CompilerParams(vmem_limit_bytes=60 << 20),
        cost_estimate=pl.CostEstimate(
            flops=16 * heads * full * full * LANES,
            bytes_accessed=2 * heads * full * full + 20 * full * cols,
            transcendentals=0,
        ),
        name="row_backward",
    )(gmine, gother, keep, send, inv, wts, qcat, kcat, vaug, ent, ent, *given)


def qkv_grad_kernel(at_ref, own_ref, other_ref, gq_ref, gkv_ref, send_ref, keep_ref, rows_t):
    half, width = own_ref.shape
    n = width // 16
    span = gq_ref.shape[2]
    core, index = at_ref[0], at_ref[1]
    rows_t[:, :half] = own_ref[...].T
    rows_t[:, half:] = other_ref[...].T

    def write(out_ref, at, start, count):
        left = rows_t[pl.ds(pl.multiple_of(start, 16), count * n), :]
        for b in range(6):
            right = gq_ref[b] if b < 4 else gkv_ref[b - 4]
            piece = jnp.dot(left, right, preferred_element_type=F32).astype(BF)
            for p in range(count):
                out_ref[(*at(p), b)] = piece[p * n : (p + 1) * n, :]

    for which, out_ref in ((1 - index, send_ref), (index, keep_ref)):

        @pl.when(core == 0)
        def _(which=which, out_ref=out_ref):
            write(out_ref, lambda p: (p // 2 % 2, p // 4, p % 2), which * 8 * n, 8)

        @pl.when(core == 1)
        def _(which=which, out_ref=out_ref):
            for o in range(2):
                write(out_ref, lambda p, o=o: (o, p // 2, p % 2), o * 8 * n + which * 4 * n, 4)


def qkv_grad(at, own, other, gq, gkv):
    half, width = own.shape
    span = gkv.shape[2]
    n = width // 16
    vmem = pl.BlockSpec(memory_space=pltpu.VMEM)
    return pl.pallas_call(
        qkv_grad_kernel,
        in_specs=[pl.BlockSpec(memory_space=pltpu.SMEM)] + [vmem] * 4,
        out_specs=[vmem] * 2,
        out_shape=[jax.ShapeDtypeStruct((2, 2, 2, 6, n, span), BF)] * 2,
        scratch_shapes=[pltpu.VMEM((width, 2 * half), BF)],
        compiler_params=pltpu.CompilerParams(vmem_limit_bytes=60 << 20),
        cost_estimate=pl.CostEstimate(
            flops=24 * half * width * span, bytes_accessed=32 * half * span, transcendentals=0
        ),
        name="qkv_grad",
    )(at, own, other, gq, gkv)


def add_halves_kernel(at_ref, *refs):
    del at_ref
    away_ref, mine_ref = refs[-2:]
    count = (len(refs) - 2) // 4
    for out_ref, first in ((away_ref, 0), (mine_ref, 2)):
        at = 0
        for p in range(count):
            a, b = refs[4 * p + first], refs[4 * p + first + 1]
            rows = a.shape[2]
            out_ref[0, at : at + rows, :] = (a[0, 0].astype(F32) + b[0, 0].astype(F32)).astype(BF)
            at += rows


def add_halves(index, pairs):
    pieces, cols = pairs[0][0].shape[1], pairs[0][0].shape[3]
    height = sum(a.shape[2] for a, _ in pairs)
    specs, arrays = [], []
    for a, b in pairs:
        for other in (True, False):
            pick = (lambda i, at: (1 - at[0], i, 0, 0)) if other else (lambda i, at: (at[0], i, 0, 0))
            specs += [pl.BlockSpec((1, 1, *a.shape[2:]), pick)] * 2
            arrays += [a, b]
    out = pl.BlockSpec((1, height, cols), lambda i, at: (i, 0, 0))
    return pl.pallas_call(
        add_halves_kernel,
        grid_spec=pltpu.PrefetchScalarGridSpec(
            num_scalar_prefetch=1, grid=(pieces,), in_specs=specs, out_specs=[out, out]
        ),
        out_shape=[jax.ShapeDtypeStruct((pieces, height, cols), BF)] * 2,
        compiler_params=pltpu.CompilerParams(vmem_limit_bytes=60 << 20),
        cost_estimate=pl.CostEstimate(
            flops=2 * pieces * height * cols, bytes_accessed=12 * pieces * height * cols, transcendentals=0
        ),
        name="add_halves",
    )(index, *arrays)


def input_grad_kernel(gq_ref, gkv_ref, w_ref, gy1_ref, mine_ref, away_ref, sum_ref):
    half = gy1_ref.shape[0]
    span = gkv_ref.shape[2]

    def grads(b):
        return gq_ref.at[b] if b < 4 else gkv_ref.at[b - 4]

    def back(at):
        total = None
        for b in range(6):
            part = lax.dot_general(
                grads(b)[at, :], w_ref[:, b * span : (b + 1) * span], (((1,), (1,)), ((), ())),
                preferred_element_type=F32,
            )
            total = part if total is None else total + part
        return total

    away_ref[...] = back(slice(half, 2 * half)).astype(BF)
    mine_ref[...] = gy1_ref[...] + back(slice(0, half))
    ones = jnp.ones((8, 2 * half), BF)
    for b in range(6):
        sum_ref[b : b + 1, :] = jnp.dot(ones, grads(b)[...], preferred_element_type=F32)[:1]
    sum_ref[6:, :] = jnp.zeros((2, span), F32)


def row_input_grad(gq, gkv, w, gy1):
    half, width = gy1.shape
    span = gkv.shape[2]
    vmem = pl.BlockSpec(memory_space=pltpu.VMEM)
    shapes = [((half, width), F32), ((half, width), BF), ((8, span), F32)]
    return pl.pallas_call(
        input_grad_kernel,
        in_specs=[vmem] * 4,
        out_specs=[vmem] * 3,
        out_shape=[jax.ShapeDtypeStruct(s, d) for s, d in shapes],
        compiler_params=pltpu.CompilerParams(vmem_limit_bytes=60 << 20),
        cost_estimate=pl.CostEstimate(
            flops=4 * half * width * 6 * span, bytes_accessed=20 * half * width, transcendentals=0
        ),
        name="row_input_grad",
    )(gq, gkv, w, gy1)


def lay_rest_kernel(at_ref, mine_ref, other_ref, up_ref, down_ref, out_ref):
    span = mine_ref.shape[2]
    k, n, m = up_ref.shape[0], down_ref.shape[0] // 4, out_ref.shape[0] // 4
    core, index = at_ref[0], at_ref[1]
    for a, ref in ((index, mine_ref), (1 - index, other_ref)):
        for b in range(2):
            pair = jnp.where(core == 0, b * 2 + a, a * 2 + b)
            for far in range(2):
                j = b * 2 + far
                cols = pl.ds(pl.multiple_of((pair * 2 + far) * span, LANES), span)
                up_ref[:, cols] = ref[j, :k, :].astype(F32)
                cols = slice(far * span, (far + 1) * span)
                down_ref[pl.ds(pl.multiple_of(pair * n, 8), n), cols] = ref[j, k : k + n, :].astype(F32)
                out_ref[pl.ds(pl.multiple_of(pair * m, 8), m), cols] = ref[j, k + n :, :].astype(F32)


def lay_qkv_kernel(at_ref, keep_ref, got_ref, query_ref, kv_ref):
    n, span = keep_ref.shape[2:]
    for half, src in ((at_ref[0], keep_ref), (1 - at_ref[0], got_ref)):
        for b in range(6):
            ref, i = (query_ref, b) if b < 4 else (kv_ref, b - 4)
            cols = pl.ds(pl.multiple_of(i * 2 * span + half * span, LANES), span)
            for j in range(4):
                ref[j * n : (j + 1) * n, cols] = src[j, b].astype(F32)


def lay(kernel, name, at, arrays, shapes):
    vmem = pl.BlockSpec(memory_space=pltpu.VMEM)
    return pl.pallas_call(
        kernel,
        in_specs=[pl.BlockSpec(memory_space=pltpu.SMEM)] + [vmem] * len(arrays),
        out_specs=[vmem] * len(shapes),
        out_shape=[jax.ShapeDtypeStruct(s, F32) for s in shapes],
        compiler_params=pltpu.CompilerParams(vmem_limit_bytes=60 << 20),
        cost_estimate=pl.CostEstimate(
            flops=0, bytes_accessed=6 * sum(a.size for a in arrays), transcendentals=0
        ),
        name=name,
    )(at, *arrays)


def row_layer(
    inputs, query_weight, kv_weight, out_weight, up_weight, down_weight,
    query_bias, value_bias, out_bias, up_bias, down_bias,
    norm1_gain, norm1_shift, norm2_gain, norm2_shift, types, lengths, cotangent,
):
    rows_here, span, width = inputs.shape
    hd = width // HEADS
    full = types.shape[1]
    heads = HEADS // 2
    cols = heads * hd
    row_count = lax.axis_size("row")
    core, outer, row_id = (lax.axis_index(n) for n in ("core", "outer", "row"))
    place = [row_id // bit % 2 for bit in (1, 2, 4)]
    near = place[0]
    own_count = full // 2
    both_ways = [(0, 1), (1, 0)]

    def after(values, *others):
        return lax.optimization_barrier((values, *others))[0]

    def swap(values):
        return lax.ppermute(values, "core", both_ways)

    def cross(values):
        return lax.ppermute(values, "outer", both_ways)

    def pair_up(values, bit):
        return lax.ppermute(values, "row", [(i, i ^ bit) for i in range(row_count)])

    def in_order(index, mine, other, axis=0):
        first, second = jnp.where(index == 0, mine, other), jnp.where(index == 0, other, mine)
        return jnp.stack([first, second], axis=axis)

    def take(values, index, axis=0):
        return lax.dynamic_index_in_dim(values, index, axis, keepdims=False)

    def halves_of_rows(values):
        pieces = values.reshape(rows_here, 2, span // 2, width)
        other = swap(take(pieces, 1 - core, 1))
        return in_order(core, take(pieces, core, 1), other).reshape(row_count, span // 2, width)

    def over_rows(values):
        return lax.all_to_all(values, "row", 0, 0, tiled=True)

    shard = query_weight.shape[0]
    wide = down_weight.shape[0]

    def near_half(values):
        return take(values.reshape(2, values.shape[0] // 2, values.shape[1]), near)

    f_own, f_core = 2 * outer + core, 2 * outer + 1 - core
    f_cross, f_both = 2 * (1 - outer) + core, 2 * (1 - outer) + 1 - core

    q_got = cross(near_half(query_weight))
    to_rows = halves_of_rows(inputs)
    own_rows = over_rows(to_rows).reshape(own_count, width)
    query_own, kv_own, types, lengths, query_bias = lax.optimization_barrier(
        (query_weight, kv_weight, types, lengths, query_bias, to_rows)
    )[:5]
    q_core, kv_core = swap(query_own), swap(kv_own)
    q_passed, kv_got = pair_up(q_got, 1), cross(after(kv_weight, q_got))
    q_got2 = swap(after(q_got, q_core, kv_core))
    own_rows, q_passed = lax.optimization_barrier((own_rows, q_passed))
    other_rows = swap(own_rows)
    q_passed2, kv_got2 = swap(q_passed), swap(kv_got)
    cot_halves = halves_of_rows(after(cotangent, own_rows))
    query_pieces = [query_weight, q_core, q_got, q_passed, q_got2, q_passed2]
    kv_pieces = [kv_weight, kv_core, kv_got, kv_got2]
    part = shard // 2
    query_at = [
        f_own * shard, f_core * shard,
        f_cross * shard + near * part, f_cross * shard + (1 - near) * part,
        f_both * shard + near * part, f_both * shard + (1 - near) * part,
    ]
    kv_at = [f_own * shard, f_core * shard, f_cross * shard, f_both * shard]
    at_qkv = jnp.stack([core, *query_at, *kv_at]).astype(jnp.int32)

    tags = jnp.concatenate([types, lengths], axis=1)
    tags_other = after(swap(tags), q_passed)
    tags = take(in_order(core, tags, tags_other).reshape(row_count, -1), row_id)
    types_row, lengths_row = tags[:full], tags[full:]

    def by_member(values):
        two = values.reshape(row_count, 2, span // 2).transpose(1, 0, 2)
        return jnp.concatenate([take(two, core), take(two, 1 - core)], axis=0).reshape(full)

    entity = by_member(types_row) > 0
    positions = by_member(lax.iota(jnp.int32, full))
    docs = lengths_row.shape[0]
    ends = [jnp.sum(lengths_row[: d + 1]) for d in range(docs)]
    seg = sum((positions >= end).astype(jnp.int32) for end in ends)
    lanes = lax.broadcasted_iota(jnp.int32, (full, LANES), 1)
    same = lanes == seg[:, None]
    qseg = jnp.where(same, 1.0, 0.0).astype(BF)
    kseg = jnp.where(same | (lanes >= docs), 0.0, BLOCKED).astype(BF)
    ent = jnp.broadcast_to(jnp.where(entity, 1.0, 0.0).astype(BF)[:, None], (full, LANES))

    vectors = (
        query_bias, value_bias, out_bias, up_bias, down_bias,
        norm1_gain, norm1_shift, norm2_gain, norm2_shift,
    )
    packed = jnp.concatenate([v.reshape(-1, shard) for v in vectors], axis=0)
    packed = in_order(outer, packed, cross(packed))
    packed = in_order(core, packed, swap(packed)).transpose(1, 0, 2, 3).reshape(4, -1, shard)

    def joined(first, count):
        return packed[:, first : first + count].reshape(-1, width).astype(F32)

    b_query, b_value = joined(0, 4), joined(4, 1)
    vec = jnp.concatenate(
        [joined(6, 4), joined(5, 1), joined(10, 1), joined(11, 1), joined(12, 1), joined(13, 1), joined(14, 1)]
    )
    b_six = jnp.concatenate([b_query, jnp.zeros((1, width), F32), b_value]).reshape(6, 2, cols)
    b_sel = take(b_six, core, 1).reshape(1, 6 * cols)

    qcat, kcat, vaug, w_sel = row_project(
        at_qkv, own_rows, other_rows, b_sel, ent, query_pieces, kv_pieces, heads, hd
    )

    low_rows = down_weight[: wide // 2]
    u_got = cross(after(near_half(up_weight), kv_got))
    d_got = cross(after(near_half(low_rows), kv_got))
    late_out, late_up, late_down = lax.optimization_barrier((out_weight, up_weight, down_weight, kv_got2))[:3]
    o_core, u_core, d_core = swap(late_out), swap(late_up), swap(late_down)
    u_mid, d_mid, m_out, m_down, o_core, u_core, d_core = lax.optimization_barrier(
        (u_got, d_got, out_weight, down_weight, o_core, u_core, d_core, kcat)
    )[:7]
    u_passed, d_passed = pair_up(u_mid, 1), pair_up(d_mid, 1)
    o_got, t_got = cross(m_out), cross(m_down[wide // 2 :])
    u_got2, d_got2 = swap(u_mid), swap(d_mid)
    cot = over_rows(after(cot_halves, other_rows)).reshape(own_count, width)
    keep, send, wts, inv = row_attend(qcat, kcat, vaug, qseg, kseg, heads, hd)
    theirs = swap(send)
    u_passed2, d_passed2, o_got2, t_got2 = (
        swap(v) for v in lax.optimization_barrier((u_passed, d_passed, o_got, t_got, keep))[:4]
    )
    out_pieces = [out_weight, o_core, o_got, o_got2]
    out_at = [f * shard for f in (f_own, f_core, f_cross, f_both)]
    up_pieces = [up_weight, u_core, u_got, u_passed, u_got2, u_passed2]
    down_pieces = [down_weight, d_core, d_got, d_passed, t_got, d_got2, d_passed2, t_got2]
    quarter = wide // 4
    down_at = [
        f_own * wide, f_core * wide,
        f_cross * wide + near * quarter, f_cross * wide + (1 - near) * quarter, f_cross * wide + 2 * quarter,
        f_both * wide + near * quarter, f_both * wide + (1 - near) * quarter, f_both * wide + 2 * quarter,
    ]
    at_rest = jnp.stack([core, *out_at, *query_at, *down_at]).astype(jnp.int32)

    (
        result, gy1, gmine, gtheirs, act, hlow, gffn, gup, gattn, small
    ) = token_block(at_rest, own_rows, keep, theirs, cot, vec, out_pieces, up_pieces, down_pieces)
    gother = swap(gtheirs)
    at_core = core.astype(jnp.int32).reshape(1)
    at_near = near.astype(jnp.int32).reshape(1)
    rest_send, rest_keep = rest_grad(at_core, keep, theirs, act, gffn, gattn)
    hlow, gup, gother, rest_send = lax.optimization_barrier((hlow, gup, gother, rest_send))
    up_send, up_keep = up_grad(at_core, hlow, gup)

    def add(*arrays):
        return functools.reduce(jnp.add, [v.astype(F32) for v in arrays]).astype(BF)

    def by_core(a, b):
        return jnp.where(core == 0, a, b)

    stages = {"s1": ("outer", "y"), "s2": ("z", "outer"), "s3": ("y", "z"), "far": ("far", "far"), "g1": ("z", "y")}
    index_on = {"outer": outer, "y": near, "z": place[1], "far": place[2]}
    index_of = {name: by_core(index_on[a], index_on[b]) for name, (a, b) in stages.items()}
    every = ("row", "outer", "core")

    def pairs_of(stage):
        found = []
        for r in range(row_count):
            for o in range(2):
                for c in range(2):
                    axis = stages[stage][c]
                    to = (r, 1 - o) if axis == "outer" else (r ^ {"y": 1, "z": 2, "far": 4}[axis], o)
                    found.append(((r * 2 + o) * 2 + c, (to[0] * 2 + to[1]) * 2 + c))
        return found

    def send_over(values, stage):
        return lax.ppermute(values, every, pairs_of(stage))

    token = [gother]

    def in_turn(*arrays):
        return lax.optimization_barrier((*arrays, token[0]))[: len(arrays)]

    def halve(state, axis):
        mine, other = in_turn(*state)
        away, mine = (
            add(take(mine, i), take(other, i)) for i in (1 - index_of[axis], index_of[axis])
        )
        token[0] = away
        return mine, send_over(away, axis)

    def start_spread(state, axis):
        total = add(*in_turn(*state))
        token[0] = total
        return total, send_over(total, axis)

    def spread(state, have, axis):
        total = in_order(index_of[have], *in_turn(*state))
        token[0] = total
        return total, send_over(total, axis)

    state = [
        (v.reshape(2, 8, *v.shape[4:]), swap(w).reshape(2, 8, *v.shape[4:]))
        for v, w in ((up_keep, up_send), (rest_keep, rest_send))
    ]
    away, mine = add_halves(index_of["s1"].astype(jnp.int32).reshape(1), state)
    bits = (2, 2, 2)
    rest = (mine.reshape(*bits, *mine.shape[1:]), send_over(away, "s1").reshape(*bits, *mine.shape[1:]))
    gmine, _ = lax.optimization_barrier((gmine, away))
    gq, gkv = row_backward(
        0, heads, None, gmine, gother, keep, send, inv, wts, qcat, kcat, vaug, ent, hd
    )
    n = width // 16
    token[0] = gkv
    rest = halve(rest, "s2")
    at_first = jnp.stack([core, index_of["s1"]]).astype(jnp.int32)
    q_send, q_keep = qkv_grad(at_first, own_rows, after(other_rows, token[0]), gq, gkv)
    six = (q_keep.reshape(*bits, 6 * n, cols), send_over(q_send, "s1").reshape(*bits, 6 * n, cols))
    in_mine, in_away, six_sum = row_input_grad(gq, gkv, after(w_sel, q_send), gy1)
    in_other = swap(in_away)
    token[0] = in_away
    rest = halve(rest, "s3")
    in_mine, in_other = in_turn(in_mine, in_other)
    grad_in = (in_mine + in_other.astype(F32)).astype(BF)
    both_out = jnp.stack([v.reshape(row_count, span // 2, width) for v in (result, grad_in)], axis=1)
    token[0] = both_out
    both_out = over_rows(both_out)
    six = halve(six, "s2")
    rest = halve(rest, "far")

    spot = lax.broadcasted_iota(jnp.int32, (1, 2, 1), 1) == core
    wide_sum = jnp.where(spot, six_sum[:6].reshape(6, 1, cols), 0.0).reshape(6, width)
    each = jnp.concatenate([small[4:10], wide_sum[5:]], axis=0).reshape(7, 4, shard).transpose(1, 0, 2)
    small = jnp.concatenate(
        [small[:4].reshape(4, 4, shard), wide_sum[:4].reshape(4, 4, shard), each, jnp.zeros_like(each[:, :1])], axis=1
    )
    small = jnp.broadcast_to(small[None], (row_count, 4, 16, shard)).reshape(-1, 16, shard)
    small = lax.all_to_all(small, ("row", "group", "outer", "core"), 0, 0, tiled=True)

    six = halve(six, "s3")
    rest = start_spread(rest, "far")
    six = halve(six, "far")
    both_out = in_turn(both_out)[0]
    token[0] = both_out
    rest = spread(rest, "far", "s3")
    six = start_spread(six, "far")
    rest = spread(rest, "s3", "g1")
    small = jnp.sum(in_turn(small)[0], axis=0)
    token[0] = small
    six = spread(six, "far", "s3")
    both_out = both_out.reshape(2, rows_here, 2, span // 2, width)
    halves = in_order(core, take(both_out, core), swap(take(both_out, 1 - core)))
    output, input_grad = (
        halves[:, :, i].transpose(1, 0, 2, 3).reshape(rows_here, span, width) for i in range(2)
    )
    six = spread(six, "s3", "g1")
    at_last = jnp.stack([core, index_of["g1"]]).astype(jnp.int32)
    g_up, g_down, g_out = lay(
        lay_rest_kernel, "lay_rest", at_last, [v.reshape(4, *v.shape[2:]) for v in in_turn(*rest)],
        [up_weight.shape, down_weight.shape, out_weight.shape],
    )
    token[0] = g_out
    six = in_order(index_of["g1"], *in_turn(*six))
    away, kept = by_core(six[:, 1], six[0]), by_core(six[:, 0], six[1])
    parts = [v.reshape(4, 6, n, cols) for v in (kept, swap(away))]
    g_query, g_kv = lay(
        lay_qkv_kernel, "lay_qkv", at_core, parts, [query_weight.shape, kv_weight.shape]
    )
    return (
        output, input_grad, g_query, g_kv, g_out, g_up, g_down,
        small[4:8].reshape(-1), small[14], small[8], small[:4].reshape(-1), *(small[i] for i in range(9, 14)),
    )


def solution(mesh):
    def step(*args):
        ctx, fsdp = mesh.shape["ctx"], mesh.shape["fsdp"]
        row_count = args[0].shape[0] // (fsdp // 2)
        per_row = ctx // row_count
        fine = Mesh(
            mesh.devices.reshape(row_count, per_row, fsdp // 2, 2), ("row", "group", "outer", "core")
        )
        tokens = P(("outer", "core"), ("row", "group"), None)
        mat, vec = P(("outer", "core"), None), P(("outer", "core"))
        in_specs = (tokens, *[mat] * 5, *[vec] * 9, mat, mat, tokens)
        out_specs = (tokens, tokens, *[mat] * 5, *[vec] * 9)
        quarter = args[0].shape[2] // 4
        fits = per_row == 1 and fsdp == 4 and row_count == 8 and args[0].shape[2] % (2 * LANES) == 0 and quarter % 32 == 0
        body = row_layer if fits else functools.partial(layer, None, per_row)
        return jax.shard_map(
            body, mesh=fine, in_specs=in_specs, out_specs=out_specs, check_vma=False
        )(*args)

    return step
```

```python
import functools

import jax
import jax.numpy as jnp
from jax import lax
from jax.experimental import pallas as pl
from jax.experimental.pallas import tpu as pltpu
from jax.sharding import Mesh
from jax.sharding import PartitionSpec as P

HEADS = 12
EPSILON = 1e-05
BLOCKED = -1e30
BF = jnp.bfloat16
F32 = jnp.float32
LANES = 128
CHUNK = 16


def matmul(left_mat, right_mat):
    return jnp.dot(left_mat, right_mat, preferred_element_type=F32)


def rows_inner(left_mat, right_mat):
    return lax.dot_general(left_mat, right_mat, (((0,), (0,)), ((), ())), preferred_element_type=F32)


def times_transposed(left_mat, right_mat):
    return lax.dot_general(left_mat, right_mat, (((1,), (1,)), ((), ())), preferred_element_type=F32)


def normalize(values, gain_vec, shift_vec):
    center = values - jnp.mean(values, axis=-1, keepdims=True)
    scale_inv = lax.rsqrt(jnp.mean(center * center, axis=-1, keepdims=True) + EPSILON)
    normed = center * scale_inv
    return (normed * gain_vec + shift_vec, normed, scale_inv)


def normalize_back(grad_in, normed, scale_inv, gain_vec):
    scaled = grad_in * gain_vec
    inner_part = (
        scaled
        - jnp.mean(scaled, axis=-1, keepdims=True)
        - normed * jnp.mean(scaled * normed, axis=-1, keepdims=True)
    )
    return (inner_part * scale_inv, jnp.sum(grad_in * normed, axis=0), jnp.sum(grad_in, axis=0))


def column_sum(values):
    return jnp.sum(values.astype(F32), axis=0)


def forward_kernel(
    heads, hd, rows_ref, w_ref, bias_ref, ent_ref, qseg_ref, kseg_ref,
    att_ref, wts_ref, inv_ref, qcat_ref, kcat_ref, vneg_ref,
    kaug_s, vaug_s, score_s,
):
    step = pl.program_id(0)
    span = heads * hd
    full = rows_ref.shape[0]
    block = att_ref.shape[0]
    scale = hd ** (-0.5)

    @pl.when(step == 0)
    def _():
        kaug_s[:, :, LANES:] = jnp.broadcast_to(kseg_ref[...][None], (heads, full, LANES))
        lane = lax.broadcasted_iota(jnp.int32, (block, LANES - hd), 1)
        one_col = jnp.where(lane == 0, 1.0, 0.0).astype(BF)
        neg_col = jnp.where(lane < 2, -1.0, 0.0).astype(BF)

        def project(piece, carry):
            at = pl.ds(pl.multiple_of(piece * block, block), block)
            rows = rows_ref[at, :]
            ent = ent_ref[at, :hd]
            wide = ent_ref[at, :1] > 0
            word = (1 - ent).astype(BF)

            def part(index):
                cols = slice(index * span, (index + 1) * span)
                return jnp.dot(rows, w_ref[:, cols], preferred_element_type=F32) + bias_ref[:, cols]

            q_word = (jnp.where(wide, part(2), part(0))).astype(BF) * BF(scale)
            q_ent = (jnp.where(wide, part(3), part(1))).astype(BF) * BF(scale)
            keys = part(4).astype(BF)
            vals = part(5).astype(BF)
            for h in range(heads):
                cut = slice(h * hd, (h + 1) * hd)
                qcat_ref[h, at, :] = jnp.concatenate([q_word[:, cut], q_ent[:, cut]], axis=1)
                k_pair = jnp.concatenate([keys[:, cut] * word, keys[:, cut] * ent], axis=1)
                kcat_ref[h, at, :] = k_pair
                kaug_s[h, at, :LANES] = k_pair
                vneg_ref[h, at, :] = jnp.concatenate([vals[:, cut], neg_col], axis=1)
                vaug_s[h, at, :] = jnp.concatenate([vals[:, cut], one_col], axis=1)
            return carry

        lax.fori_loop(0, full // block, project, 0)

    here = pl.ds(pl.multiple_of(step * block, block), block)
    q_seg = qseg_ref[here, :]
    lane = lax.broadcasted_iota(jnp.int32, (block, LANES), 1)
    inv_all = jnp.zeros((block, LANES), F32)
    mixed = []
    for h in range(heads):
        q_aug = jnp.concatenate([qcat_ref[h, here, :], q_seg], axis=1)
        score_s[h % 2] = lax.dot_general(
            q_aug, kaug_s[h], (((1,), (1,)), ((), ())), preferred_element_type=F32
        )
        for r in range(0, block, CHUNK):
            s = score_s[h % 2, r : r + CHUNK, :]
            top = jnp.max(s, axis=1, keepdims=True)
            wts_ref[h, r : r + CHUNK, :] = jnp.exp(s - top).astype(BF)
        out = jnp.dot(wts_ref[h], vaug_s[h], preferred_element_type=F32)
        inv = 1.0 / out[:, hd : hd + 1]
        inv_all = jnp.where(lane == h, inv, inv_all)
        mixed.append((out[:, :hd] * inv).astype(BF))
    att_ref[...] = jnp.concatenate(mixed, axis=1)
    inv_ref[...] = inv_all


def attention_forward(rows, w_sel, bias_sel, ent, qseg, kseg, heads, hd):
    full, width = rows.shape
    block = min(256, full)
    span = heads * hd
    steps = full // block
    whole = lambda *dims: pl.BlockSpec(dims, lambda i: (0,) * len(dims))
    return pl.pallas_call(
        functools.partial(forward_kernel, heads, hd),
        grid=(steps,),
        in_specs=[
            whole(full, width),
            whole(width, 6 * span),
            whole(1, 6 * span),
            whole(full, LANES),
            whole(full, LANES),
            whole(full, LANES),
        ],
        out_specs=[
            pl.BlockSpec((block, span), lambda i: (i, 0)),
            pl.BlockSpec((heads, block, full), lambda i: (0, i, 0)),
            pl.BlockSpec((block, LANES), lambda i: (i, 0)),
            whole(heads, full, 2 * hd),
            whole(heads, full, 2 * hd),
            whole(heads, full, LANES),
        ],
        out_shape=[
            jax.ShapeDtypeStruct((full, span), BF),
            jax.ShapeDtypeStruct((heads, full, full), BF),
            jax.ShapeDtypeStruct((full, LANES), F32),
            jax.ShapeDtypeStruct((heads, full, 2 * hd), BF),
            jax.ShapeDtypeStruct((heads, full, 2 * hd), BF),
            jax.ShapeDtypeStruct((heads, full, LANES), BF),
        ],
        scratch_shapes=[
            pltpu.VMEM((heads, full, 2 * LANES), BF),
            pltpu.VMEM((heads, full, LANES), BF),
            pltpu.VMEM((2, block, full), F32),
        ],
        compiler_params=pltpu.CompilerParams(vmem_limit_bytes=60 << 20),
        cost_estimate=pl.CostEstimate(
            flops=2 * full * width * 6 * span + 8 * heads * full * full * LANES,
            bytes_accessed=2 * heads * full * full + 10 * full * width,
            transcendentals=heads * full * full,
        ),
        name="attention_forward",
    )(rows, w_sel, bias_sel, ent, qseg, kseg)


def backward_kernel(
    heads, hd, go_ref, att_ref, inv_ref, wts_ref, qcat_ref, kcat_ref, vneg_ref, ent_ref, entb_ref,
    gq_ref, gkv_ref, gscore_s, low_s, gk_s, gv_s,
):
    step = pl.program_id(0)
    span = heads * hd
    block = go_ref.shape[0]
    full = kcat_ref.shape[1]
    scale = hd ** (-0.5)
    lane = lax.broadcasted_iota(jnp.int32, (block, LANES - hd), 1)
    is_ent = entb_ref[:, :1] > 0
    g_word, g_ent = [], []
    for h in range(heads):
        cut = slice(h * hd, (h + 1) * hd)
        g_low = (go_ref[:, cut].astype(F32) * inv_ref[:, h : h + 1]).astype(BF)
        delta = jnp.sum(g_low.astype(F32) * att_ref[:, cut].astype(F32), axis=1, keepdims=True)
        d_hi = delta.astype(BF)
        d_lo = (delta - d_hi.astype(F32)).astype(BF)
        extra = jnp.where(
            lane == 0, d_hi.astype(F32), jnp.where(lane == 1, d_lo.astype(F32), 0.0)
        ).astype(BF)
        g_aug = jnp.concatenate([g_low, extra], axis=1)
        gscore_s[h % 2] = lax.dot_general(
            g_aug, vneg_ref[h], (((1,), (1,)), ((), ())), preferred_element_type=F32
        )
        for r in range(0, block, CHUNK):
            low_s[h % 2, r : r + CHUNK, :] = (
                wts_ref[h, r : r + CHUNK, :].astype(F32) * gscore_s[h % 2, r : r + CHUNK, :]
            ).astype(BF)
        g_q = jnp.dot(low_s[h % 2], kcat_ref[h], preferred_element_type=F32) * scale
        g_word.append(g_q[:, :hd])
        g_ent.append(g_q[:, hd:])
        g_k = lax.dot_general(
            qcat_ref[h], low_s[h % 2], (((0,), (0,)), ((), ())), preferred_element_type=F32
        )
        g_v = lax.dot_general(
            g_low, wts_ref[h], (((0,), (0,)), ((), ())), preferred_element_type=F32
        )

        @pl.when(step == 0)
        def _(h=h, g_k=g_k, g_v=g_v):
            gk_s[h] = g_k
            gv_s[h] = g_v

        @pl.when(step > 0)
        def _(h=h, g_k=g_k, g_v=g_v):
            gk_s[h] += g_k
            gv_s[h] += g_v

    g_word = jnp.concatenate(g_word, axis=1)
    g_ent = jnp.concatenate(g_ent, axis=1)
    gq_ref[:, :span] = jnp.where(is_ent, 0.0, g_word).astype(BF)
    gq_ref[:, span : 2 * span] = jnp.where(is_ent, 0.0, g_ent).astype(BF)
    gq_ref[:, 2 * span : 3 * span] = jnp.where(is_ent, g_word, 0.0).astype(BF)
    gq_ref[:, 3 * span :] = jnp.where(is_ent, g_ent, 0.0).astype(BF)

    @pl.when(step == pl.num_programs(0) - 1)
    def _():
        def close(piece, carry):
            at = pl.ds(pl.multiple_of(piece * block, block), block)
            pick = ent_ref[at, :1] > 0
            g_keys, g_vals = [], []
            for h in range(heads):
                both = gk_s[h, :, at].T
                g_keys.append(jnp.where(pick, both[:, hd:], both[:, :hd]))
                g_vals.append(gv_s[h, :, at].T)
            gkv_ref[at, :span] = jnp.concatenate(g_keys, axis=1).astype(BF)
            gkv_ref[at, span:] = jnp.concatenate(g_vals, axis=1).astype(BF)
            return carry

        lax.fori_loop(0, full // block, close, 0)


def attention_backward(g_out, att, inv, wts, qcat, kcat, vneg, ent, heads, hd):
    full, span = att.shape
    block = min(256, full)
    whole = lambda *dims: pl.BlockSpec(dims, lambda i: (0,) * len(dims))
    by_rows = lambda width: pl.BlockSpec((block, width), lambda i: (i, 0))
    by_head = lambda width: pl.BlockSpec((heads, block, width), lambda i: (0, i, 0))
    return pl.pallas_call(
        functools.partial(backward_kernel, heads, hd),
        grid=(full // block,),
        in_specs=[
            by_rows(span),
            by_rows(span),
            by_rows(LANES),
            by_head(full),
            by_head(2 * hd),
            whole(heads, full, 2 * hd),
            whole(heads, full, LANES),
            whole(full, LANES),
            by_rows(LANES),
        ],
        out_specs=[by_rows(4 * span), whole(full, 2 * span)],
        out_shape=[
            jax.ShapeDtypeStruct((full, 4 * span), BF),
            jax.ShapeDtypeStruct((full, 2 * span), BF),
        ],
        scratch_shapes=[
            pltpu.VMEM((2, block, full), F32),
            pltpu.VMEM((2, block, full), BF),
            pltpu.VMEM((heads, 2 * hd, full), F32),
            pltpu.VMEM((heads, hd, full), F32),
        ],
        compiler_params=pltpu.CompilerParams(vmem_limit_bytes=60 << 20),
        cost_estimate=pl.CostEstimate(
            flops=16 * heads * full * full * LANES,
            bytes_accessed=2 * heads * full * full + 20 * full * span,
            transcendentals=0,
        ),
        name="attention_backward",
    )(g_out, att, inv, wts, qcat, kcat, vneg, ent, ent)


def layer(
    half, per_row, inputs, query_weight, kv_weight, out_weight, up_weight, down_weight,
    query_bias, value_bias, out_bias, up_bias, down_bias,
    norm1_gain, norm1_shift, norm2_gain, norm2_shift, types, lengths, cotangent,
):
    rows_here, span, width = inputs.shape
    head_dim = width // HEADS
    full = types.shape[1]
    members = 2 * per_row
    heads = HEADS // members
    cols = heads * head_dim
    row_count = lax.axis_size("row")
    outer = lax.axis_size("outer")
    core = lax.axis_index("core")
    group = lax.axis_index("group")
    member = group * 2 + core
    row_id = lax.axis_index("row")
    own = row_count * (span // 2)

    def swap(values):
        return lax.ppermute(values, "core", [(0, 1), (1, 0)])

    def in_order(index, mine, other):
        return jnp.stack([jnp.where(index == 0, mine, other), jnp.where(index == 0, other, mine)])

    def gather_outer(values):
        if outer == 2:
            other = lax.ppermute(values, "outer", [(0, 1), (1, 0)])
            return in_order(lax.axis_index("outer"), values, other)
        return lax.all_gather(values, "outer", axis=0, tiled=False)

    def gather_members(values):
        pair = in_order(core, values, swap(values))
        if per_row == 1:
            return pair
        spread = lax.all_gather(pair, "group", axis=0, tiled=False)
        return spread.reshape((members,) + values.shape)

    def exchange_members(values):
        if per_row == 1:
            mine = lax.dynamic_index_in_dim(values, core, 0, keepdims=False)
            away = lax.dynamic_index_in_dim(values, 1 - core, 0, keepdims=False)
            return in_order(core, mine, swap(away))
        return lax.all_to_all(values, ("group", "core"), 0, 0, tiled=True)

    def take(values, index, axis):
        return lax.dynamic_index_in_dim(values, index, axis, keepdims=False)

    def to_row(values):
        pieces = values.reshape(rows_here, 2, span // 2, width)
        other = swap(take(pieces, 1 - core, 1))
        both = in_order(core, take(pieces, core, 1), other).reshape(row_count, span // 2, width)
        return lax.all_to_all(both, "row", 0, 0, tiled=True).reshape(own, width)

    def from_row(values):
        back = lax.all_to_all(values.reshape(row_count, span // 2, width), "row", 0, 0, tiled=True)
        back = back.reshape(2, rows_here, span // 2, width)
        other = swap(take(back, 1 - core, 0))
        both = in_order(core, take(back, core, 0), other)
        return both.transpose(1, 0, 2, 3).reshape(rows_here, span, width)

    own_rows = to_row(inputs)
    all_rows = gather_members(own_rows).reshape(full, width)

    tags = jnp.concatenate([types, lengths], axis=1)
    tags = in_order(core, tags, swap(tags)).reshape(row_count, -1)
    tags = take(tags, row_id, 0)
    types_row, lengths_row = tags[:full], tags[full:]

    def by_member(values):
        return values.reshape(row_count, per_row, 2, span // 2).transpose(1, 2, 0, 3).reshape(full)

    entity = by_member(types_row) > 0
    positions = by_member(lax.iota(jnp.int32, full))
    docs = lengths_row.shape[0]
    ends = [jnp.sum(lengths_row[: d + 1]) for d in range(docs)]
    seg = sum((positions >= end).astype(jnp.int32) for end in ends)
    lanes = lax.broadcasted_iota(jnp.int32, (full, LANES), 1)
    same = lanes == seg[:, None]
    qseg = jnp.where(same, 1.0, 0.0).astype(BF)
    kseg = jnp.where(same | (lanes >= docs), 0.0, BLOCKED).astype(BF)
    ent = jnp.broadcast_to(jnp.where(entity, 1.0, 0.0).astype(BF)[:, None], (full, LANES))

    shard = query_weight.shape[0]
    cut = jnp.concatenate([query_weight, kv_weight], axis=1).reshape(shard, 6, members, cols)
    away = take(cut, group * 2 + 1 - core, 2).reshape(shard, 6 * cols)
    mine = take(cut, member, 2).reshape(shard, 6 * cols)
    w_sel = gather_outer(in_order(core, mine, swap(away))).reshape(width, 6 * cols)

    vectors = (
        query_bias, value_bias, out_bias, up_bias, down_bias,
        norm1_gain, norm1_shift, norm2_gain, norm2_shift,
    )
    sizes = [v.shape[0] for v in vectors]
    packed = jnp.concatenate(vectors)
    packed = lax.all_gather(packed, ("outer", "core"), axis=0, tiled=False)
    offsets = [sum(sizes[:i]) for i in range(len(sizes) + 1)]
    (b_query, b_value, b_out, b_up, b_down, g_one, s_one, g_two, s_two) = (
        packed[:, a:b].reshape(-1).astype(F32) for a, b in zip(offsets[:-1], offsets[1:])
    )
    b_six = jnp.concatenate([b_query, jnp.zeros((width,), F32), b_value])
    b_sel = take(b_six.reshape(6, members, cols), member, 1).reshape(1, 6 * cols)

    att, inv_stored, wts = None, None, None
    att, wts, inv_stored, qcat, kcat, vneg = attention_forward(
        all_rows, w_sel, b_sel, ent, qseg, kseg, heads, head_dim
    )

    def fetch(values):
        return gather_outer(in_order(core, values, swap(values))).reshape(-1, values.shape[1])

    w_out, w_up, w_down = fetch(out_weight), fetch(up_weight), fetch(down_weight)

    def heads_to_tokens(values):
        got = exchange_members(values.reshape(members, own, cols))
        return got.transpose(1, 0, 2).reshape(own, width)

    def tokens_to_heads(values):
        parts = values.reshape(own, members, cols).transpose(1, 0, 2)
        return exchange_members(parts).reshape(full, cols)

    attended = heads_to_tokens(att)
    attn_out = matmul(attended, w_out) + b_out
    hidden, normed_one, inv_one = normalize(own_rows.astype(F32) + attn_out, g_one, s_one)
    hidden_low = hidden.astype(BF)
    up_proj = matmul(hidden_low, w_up) + b_up
    gelu_out, gelu_pull = jax.vjp(lambda v: jax.nn.gelu(v, approximate=False), up_proj)
    act_low = gelu_out.astype(BF)
    ffn_out = matmul(act_low, w_down) + b_down
    result, normed_two, inv_two = normalize(hidden + ffn_out, g_two, s_two)
    output = from_row(result.astype(BF))

    cot = to_row(cotangent).astype(F32)
    grad_y2, grad_g2, grad_s2 = normalize_back(cot, normed_two, inv_two, g_two)
    grad_ffn = grad_y2.astype(BF)
    grad_act = times_transposed(grad_ffn, w_down)
    grad_up = gelu_pull(grad_act)[0].astype(BF)
    grad_hidden = grad_y2 + times_transposed(grad_up, w_up)
    grad_y1, grad_g1, grad_s1 = normalize_back(grad_hidden, normed_one, inv_one, g_one)
    grad_attn = grad_y1.astype(BF)
    grad_attended = times_transposed(grad_attn, w_out).astype(BF)

    def pick_rows(left, core_index, outer_index):
        parts = left.reshape(left.shape[0], outer, 2, -1)
        if outer_index is None:
            return take(parts, core_index, 2).reshape(left.shape[0], -1)
        return take(take(parts, core_index, 2), outer_index, 1)

    def reduce_outer(partial):
        if outer == 2:
            me = lax.axis_index("outer")
            other = lax.ppermute(take(partial, 1 - me, 0).astype(BF), "outer", [(0, 1), (1, 0)])
            return take(partial, me, 0).astype(F32) + other.astype(F32)
        return lax.psum_scatter(partial.astype(BF), "outer", scatter_dimension=0, tiled=False).astype(F32)

    def shard_grad(left, right):
        away = rows_inner(pick_rows(left, 1 - core, None), right).astype(BF)
        mine = rows_inner(pick_rows(left, core, None), right)
        pair = mine + swap(away).astype(F32)
        part = reduce_outer(pair.reshape(outer, -1, right.shape[1]))
        return lax.psum(part.astype(BF), ("row", "group")).astype(F32)

    g_w_down = shard_grad(act_low, grad_ffn)
    g_w_up = shard_grad(hidden_low, grad_up)
    g_w_out = shard_grad(attended, grad_attn)

    gq, gkv = attention_backward(
        tokens_to_heads(grad_attended), att, inv_stored, wts, qcat, kcat, vneg, ent, heads, head_dim
    )
    g_six = jnp.concatenate([gq, gkv], axis=1)
    g_sel = reduce_outer(rows_inner(all_rows, g_six).reshape(outer, -1, 6 * cols))
    g_sel = lax.psum(g_sel.astype(BF), "row").reshape(2, shard, 6, cols)
    got = in_order(core, take(g_sel, core, 0), swap(take(g_sel, 1 - core, 0)))
    if per_row > 1:
        got = lax.all_gather(got, "group", axis=0, tiled=False)
    got = got.reshape(members, shard, 6, cols).transpose(1, 2, 0, 3).reshape(shard, 6 * width)
    g_w_query = got[:, : 4 * width].astype(F32)
    g_w_kv = got[:, 4 * width :].astype(F32)

    part_in = times_transposed(g_six, w_sel)
    got_in = exchange_members(part_in.astype(BF).reshape(members, own, width))
    grad_in = grad_y1 + jnp.sum(got_in.astype(F32), axis=0)
    input_grad = from_row(grad_in.astype(BF))

    six_sum = column_sum(g_six).reshape(6, 1, cols)
    spot = lax.broadcasted_iota(jnp.int32, (1, members, 1), 1) == member
    six_sum = jnp.where(spot, six_sum, 0.0).reshape(6, width)
    small = [
        six_sum[:4].reshape(-1), six_sum[5], column_sum(grad_attn), column_sum(grad_up),
        column_sum(grad_ffn), grad_g1, grad_s1, grad_g2, grad_s2,
    ]
    total = lax.psum(jnp.concatenate(small), ("row", "group", "outer", "core"))
    me = lax.axis_index("outer") * 2 + core
    pieces, at = [], 0
    for size in sizes:
        whole_size = size * outer * 2
        pieces.append(lax.dynamic_slice_in_dim(total[at : at + whole_size], me * size, size))
        at += whole_size
    return (output, input_grad, g_w_query, g_w_kv, g_w_out, g_w_up, g_w_down, *pieces)


def project_kernel(
    heads, hd, query_rows, kv_rows, at_ref, ends_ref, own_ref, other_ref, vec_ref, types_ref, *refs
):
    n_query, n_kv = len(query_rows), len(kv_rows)
    query_refs, kv_refs = refs[:n_query], refs[n_query : n_query + n_kv]
    qcat_ref, kcat_ref, vaug_ref, w_ref, ent_ref, qseg_ref, kseg_ref, kinds_s, bias_s, sems = refs[n_query + n_kv :]
    span = heads * hd
    half, width = own_ref.shape
    block = min(256, half)
    scale = hd ** (-0.5)
    core = at_ref[0]
    made = []
    for i, (ref, rows) in enumerate(zip(query_refs + kv_refs, query_rows + kv_rows)):
        first, blocks = (0, 4) if i < n_query else (4, 2)
        to = pl.ds(pl.multiple_of(at_ref[1 + i], 16), rows)
        for b in range(blocks):
            here = pl.ds(pl.multiple_of(b * width + core * span, LANES), span)
            cols = slice((first + b) * span, (first + b + 1) * span)
            copy = pltpu.make_async_copy(ref.at[:, here], w_ref.at[to, cols], sems.at[len(made)])
            copy.start()
            made.append(copy)
    row = lambda c, o, r: vec_ref[c, o, r : r + 1, :].astype(F32)
    for b in range(4):
        pair = [jnp.where(core == 0, row(b % 2, b // 2, i), row(b % 2, b // 2, 2 + i)) for i in range(2)]
        bias_s[:, b * span : (b + 1) * span] = jnp.concatenate(pair, axis=1)
    bias_s[:, 4 * span : 5 * span] = jnp.zeros((1, span), F32)
    bias_s[:, 5 * span :] = jnp.concatenate([row(i, core, 4) for i in range(2)], axis=1)
    chunks, wide = types_ref.shape
    part = wide // 2
    kinds_s[:, :chunks] = jnp.where(types_ref[...] > 0, 1.0, 0.0).T
    for side in range(2):
        kind = core if side == 0 else 1 - core
        column = kinds_s[pl.ds(pl.multiple_of(kind * part, part), part), :]
        for chunk in range(chunks):
            at = side * half + chunk * part
            ent_ref[at : at + part, :] = jnp.broadcast_to(column[:, chunk : chunk + 1], (part, LANES)).astype(BF)
            place = chunk * wide + kind * part + lax.broadcasted_iota(jnp.int32, (part, LANES), 0)
            lanes = lax.broadcasted_iota(jnp.int32, (part, LANES), 1)
            seg = sum((place >= ends_ref[d]).astype(jnp.int32) for d in range(ends_ref.shape[0]))
            same = lanes == seg
            qseg_ref[at : at + part, :] = jnp.where(same, 1.0, 0.0).astype(BF)
            kseg_ref[at : at + part, :] = jnp.where(same | (lanes >= ends_ref.shape[0]), 0.0, BLOCKED).astype(BF)
    lane = lax.broadcasted_iota(jnp.int32, (block, LANES - hd), 1)
    tail = jnp.where(lane < 2, -1.0, jnp.where(lane == 2, 1.0, 0.0)).astype(BF)
    for copy in made:
        copy.wait()
    for side, rows_ref in enumerate((own_ref, other_ref)):

        def project(piece, carry, side=side, rows_ref=rows_ref):
            rows = rows_ref[pl.ds(pl.multiple_of(piece * block, block), block), :]
            at = pl.ds(pl.multiple_of(side * half + piece * block, block), block)
            ent = ent_ref[at, :hd]
            wide = ent_ref[at, :1] > 0
            word = (1 - ent).astype(BF)

            def part(index):
                cols = slice(index * span, (index + 1) * span)
                return jnp.dot(rows, w_ref[:, cols], preferred_element_type=F32) + bias_s[:, cols]

            q_word = (jnp.where(wide, part(2), part(0))).astype(BF) * BF(scale)
            q_ent = (jnp.where(wide, part(3), part(1))).astype(BF) * BF(scale)
            keys = part(4).astype(BF)
            vals = part(5).astype(BF)
            for h in range(heads):
                cut = slice(h * hd, (h + 1) * hd)
                qcat_ref[h, at, :] = jnp.concatenate([q_word[:, cut], q_ent[:, cut]], axis=1)
                kcat_ref[h, at, :] = jnp.concatenate([keys[:, cut] * word, keys[:, cut] * ent], axis=1)
                vaug_ref[h, at, :] = jnp.concatenate([vals[:, cut], tail], axis=1)
            return carry

        lax.fori_loop(0, half // block, project, 0)


def row_project(at, ends, own, other, vec, types, query_pieces, kv_pieces, heads, hd):
    half, width = own.shape
    full = 2 * half
    span = heads * hd
    vmem = pl.BlockSpec(memory_space=pltpu.VMEM)
    smem = pl.BlockSpec(memory_space=pltpu.SMEM)
    anywhere = pl.BlockSpec(memory_space=pl.ANY)
    query_rows = tuple(p.shape[0] for p in query_pieces)
    kv_rows = tuple(p.shape[0] for p in kv_pieces)
    shapes = [
        (heads, full, 2 * hd), (heads, full, 2 * hd), (heads, full, LANES), (width, 6 * span),
        (full, LANES), (full, LANES), (full, LANES),
    ]
    return pl.pallas_call(
        functools.partial(project_kernel, heads, hd, query_rows, kv_rows),
        in_specs=[smem, smem] + [vmem] * 4 + [anywhere] * (len(query_pieces) + len(kv_pieces)),
        out_specs=[vmem] * len(shapes),
        out_shape=[jax.ShapeDtypeStruct(s, BF) for s in shapes],
        scratch_shapes=[
            pltpu.VMEM((types.shape[1], LANES), F32),
            pltpu.VMEM((1, 6 * span), F32),
            pltpu.SemaphoreType.DMA((4 * len(query_pieces) + 2 * len(kv_pieces),)),
        ],
        compiler_params=pltpu.CompilerParams(vmem_limit_bytes=60 << 20),
        cost_estimate=pl.CostEstimate(
            flops=2 * full * width * 6 * span, bytes_accessed=18 * full * width, transcendentals=0
        ),
        name="row_project",
    )(at, ends, own, other, vec, types, *query_pieces, *kv_pieces)


def attend_kernel(
    heads, hd, qcat_ref, qseg_ref, kcat_ref, kseg_ref, vaug_ref, keep_ref, send_ref, wts_ref, inv_ref, score_s
):
    step = pl.program_id(0)
    block = keep_ref.shape[0]
    q_seg = qseg_ref[...]
    lane = lax.broadcasted_iota(jnp.int32, (block, LANES), 1)
    inv_all = jnp.zeros((block, LANES), F32)
    mixed = []
    for h in range(heads):
        q_aug = jnp.concatenate([qcat_ref[h], q_seg], axis=1)
        k_aug = jnp.concatenate([kcat_ref[h], kseg_ref[...]], axis=1)
        score_s[h % 2] = lax.dot_general(
            q_aug, k_aug, (((1,), (1,)), ((), ())), preferred_element_type=F32
        )
        for r in range(0, block, CHUNK):
            s = score_s[h % 2, r : r + CHUNK, :]
            top = jnp.max(s, axis=1, keepdims=True)
            wts_ref[h, r : r + CHUNK, :] = jnp.exp(s - top).astype(BF)
        out = jnp.dot(wts_ref[h], vaug_ref[h], preferred_element_type=F32)
        inv = 1.0 / out[:, hd + 2 : hd + 3]
        inv_all = jnp.where(lane == h, inv, inv_all)
        mixed.append((out[:, :hd] * inv).astype(BF))
    mixed = jnp.concatenate(mixed, axis=1)
    inv_ref[...] = inv_all
    late = pl.num_programs(0) // 2

    @pl.when(step < late)
    def _():
        send_ref[...] = mixed

    @pl.when(step >= late)
    def _():
        keep_ref[...] = mixed


def row_attend(qcat, kcat, vaug, qseg, kseg, heads, hd):
    full = qcat.shape[1]
    half = full // 2
    block = min(256, half)
    span = heads * hd
    first = half // block
    whole = lambda *dims: pl.BlockSpec(dims, lambda i: (0,) * len(dims))
    turn = lambda i: jnp.where(i < first, i + first, i - first)
    return pl.pallas_call(
        functools.partial(attend_kernel, heads, hd),
        grid=(full // block,),
        in_specs=[
            pl.BlockSpec((heads, block, 2 * hd), lambda i: (0, turn(i), 0)),
            pl.BlockSpec((block, LANES), lambda i: (turn(i), 0)),
            whole(heads, full, 2 * hd),
            whole(full, LANES),
            whole(heads, full, LANES),
        ],
        out_specs=[
            pl.BlockSpec((block, span), lambda i: (jnp.maximum(i - first, 0), 0)),
            pl.BlockSpec((block, span), lambda i: (jnp.minimum(i, first - 1), 0)),
            pl.BlockSpec((heads, block, full), lambda i: (0, turn(i), 0)),
            pl.BlockSpec((block, LANES), lambda i: (turn(i), 0)),
        ],
        out_shape=[
            jax.ShapeDtypeStruct((half, span), BF),
            jax.ShapeDtypeStruct((half, span), BF),
            jax.ShapeDtypeStruct((heads, full, full), BF),
            jax.ShapeDtypeStruct((full, LANES), F32),
        ],
        scratch_shapes=[pltpu.VMEM((2, block, full), F32)],
        compiler_params=pltpu.CompilerParams(vmem_limit_bytes=60 << 20),
        cost_estimate=pl.CostEstimate(
            flops=8 * heads * full * full * LANES,
            bytes_accessed=2 * heads * full * full + 4 * full * LANES * heads,
            transcendentals=heads * full * full,
        ),
        name="row_attend",
    )(qcat, qseg, kcat, kseg, vaug)


def token_kernel(
    out_rows, up_rows, down_rows, at_ref, own_ref, mine_ref, theirs_ref, cot_ref, vec_ref, *refs
):
    groups = (out_rows, up_rows, down_rows)
    sets, at = [], 0
    for rows in groups:
        sets.append(refs[at : at + len(rows)])
        at += len(rows)
    (
        result_ref, gy1_ref, gmine_ref, gtheirs_ref, act_ref, hlow_ref, gffn_ref, gup_ref, gattn_ref,
        small_ref, wout_s, wup_s, wdown_s, acc_s, hid_s, norm_s, inv_s, slope_s, gy2_s, tmp_s, sum_s, vec_s, sems,
    ) = refs[at:]
    total, width = own_ref.shape
    ff = wup_s.shape[1]
    parts = ff // width
    span = mine_ref.shape[1]
    core = at_ref[0]
    made, slot = [], 0
    for rows, piece_refs, dst in zip(groups, sets, (wout_s, wup_s, wdown_s)):
        batch = []
        for n, ref in zip(rows, piece_refs):
            to = pl.ds(pl.multiple_of(at_ref[1 + slot], 16), n)
            copy = pltpu.make_async_copy(ref, dst.at[to, :], sems.at[slot])
            copy.start()
            batch.append(copy)
            slot += 1
        made.append(batch)

    def wait(index):
        for copy in made[index]:
            copy.wait()

    def whole_vector(r):
        return jnp.concatenate([vec_ref[f % 2, f // 2, r : r + 1, :] for f in range(4)], axis=1).astype(F32)

    for c in range(parts):
        up_bias = [vec_ref[c % 2, c // 2, 6 + i : 7 + i, :] for i in range(4)]
        vec_s[c : c + 1, :] = jnp.concatenate(up_bias, axis=1).astype(F32)
    for i, r in enumerate((5, 10, 11, 12, 13, 14)):
        vec_s[4 + i : 5 + i, :] = whole_vector(r)

    def row(index):
        return vec_s[index : index + 1, :]

    rows_at = lambda i, n: pl.ds(pl.multiple_of(i * n, n), n)
    chunk = 16
    mine_rows = pl.ds(pl.multiple_of(core * span, LANES), span)
    other_rows = pl.ds(pl.multiple_of((1 - core) * span, LANES), span)
    sum_s[...] = jnp.zeros_like(sum_s)
    wait(0)
    acc_s[...] = jnp.dot(mine_ref[...], wout_s[mine_rows, :], preferred_element_type=F32)
    acc_s[...] += jnp.dot(theirs_ref[...], wout_s[other_rows, :], preferred_element_type=F32)

    def first_norm(i, carry):
        at = rows_at(i, chunk)
        y = own_ref[at, :].astype(F32) + (acc_s[at, :] + row(4))
        center = y - jnp.mean(y, axis=1, keepdims=True)
        inv = lax.rsqrt(jnp.mean(center * center, axis=1, keepdims=True) + EPSILON)
        normed = center * inv
        hidden = normed * row(6) + row(7)
        norm_s[at, :] = normed
        inv_s[at, :] = jnp.broadcast_to(inv, (chunk, LANES))
        hid_s[at, :] = hidden
        hlow_ref[at, :] = hidden.astype(BF)
        return carry

    lax.fori_loop(0, total // chunk, first_norm, 0, unroll=4)
    wait(1)
    for c in range(parts):
        cols = slice(c * width, (c + 1) * width)
        tmp_s[c % 2] = jnp.dot(hlow_ref[...], wup_s[:, cols], preferred_element_type=F32)
        for r in range(0, total, chunk):
            x = tmp_s[c % 2, r : r + chunk, :] + row(c)
            cdf = 0.5 + 0.5 * lax.erf(x * (0.5**0.5))
            act_ref[r : r + chunk, cols] = (x * cdf).astype(BF)
            slope_s[r : r + chunk, cols] = cdf + x * (jnp.exp(-0.5 * x * x) * (0.15915494309189535**0.5))
    wait(2)
    acc_s[...] = jnp.dot(act_ref[...], wdown_s[...], preferred_element_type=F32)

    def second_norm(i, carry):
        at = rows_at(i, chunk)
        y = hid_s[at, :] + (acc_s[at, :] + row(5))
        center = y - jnp.mean(y, axis=1, keepdims=True)
        inv = lax.rsqrt(jnp.mean(center * center, axis=1, keepdims=True) + EPSILON)
        normed = center * inv
        result_ref[at, :] = (normed * row(8) + row(9)).astype(BF)
        cot = cot_ref[at, :].astype(F32)
        sum_s[2] += cot * normed
        sum_s[3] += cot
        scaled = cot * row(8)
        g = inv * (
            scaled
            - jnp.mean(scaled, axis=1, keepdims=True)
            - normed * jnp.mean(scaled * normed, axis=1, keepdims=True)
        )
        gy2_s[at, :] = g
        gffn_ref[at, :] = g.astype(BF)
        return carry

    lax.fori_loop(0, total // chunk, second_norm, 0, unroll=2)
    ones = jnp.ones((8, total), BF)
    ups = []
    for c in range(parts):
        cols = slice(c * width, (c + 1) * width)
        tmp_s[c % 2] = lax.dot_general(
            gffn_ref[...], wdown_s[cols, :], (((1,), (1,)), ((), ())), preferred_element_type=F32
        )
        for r in range(0, total, chunk):
            gup_ref[r : r + chunk, cols] = (
                tmp_s[c % 2, r : r + chunk, :] * slope_s[r : r + chunk, cols]
            ).astype(BF)
        ups.append(jnp.dot(ones, gup_ref[:, cols], preferred_element_type=F32)[:1])
    acc_s[...] = lax.dot_general(
        gup_ref[...], wup_s[...], (((1,), (1,)), ((), ())), preferred_element_type=F32
    )

    def first_back(i, carry):
        at = rows_at(i, chunk)
        g_in = gy2_s[at, :] + acc_s[at, :]
        normed = norm_s[at, :]
        sum_s[0] += g_in * normed
        sum_s[1] += g_in
        scaled = g_in * row(6)
        g = inv_s[at, :1] * (
            scaled
            - jnp.mean(scaled, axis=1, keepdims=True)
            - normed * jnp.mean(scaled * normed, axis=1, keepdims=True)
        )
        gy1_ref[at, :] = g
        gattn_ref[at, :] = g.astype(BF)
        return carry

    lax.fori_loop(0, total // chunk, first_back, 0, unroll=2)
    gmine_ref[...] = lax.dot_general(
        gattn_ref[...], wout_s[mine_rows, :], (((1,), (1,)), ((), ())), preferred_element_type=F32
    ).astype(BF)
    gtheirs_ref[...] = lax.dot_general(
        gattn_ref[...], wout_s[other_rows, :], (((1,), (1,)), ((), ())), preferred_element_type=F32
    ).astype(BF)
    sums = [jnp.dot(ones, ref[...], preferred_element_type=F32)[:1] for ref in (gattn_ref, gffn_ref)]
    sums += [jnp.sum(sum_s[i], axis=0, keepdims=True) for i in range(4)]
    n = width // 4
    half = width // 2
    for shard in range(4):
        at = 8 * shard
        cut = slice(shard * n, (shard + 1) * n)
        for i in range(2):
            small_ref[at + i : at + i + 1, :] = ups[shard][:, i * half : (i + 1) * half]
        for i in range(3):
            small_ref[at + 2 + i : at + 3 + i, :] = jnp.concatenate(
                [sums[2 * i][:, cut], sums[2 * i + 1][:, cut]], axis=1
            )
        small_ref[at + 5 : at + 8, :] = jnp.zeros((3, half), F32)


def token_block(at, own, mine, theirs, cot, vec, out_pieces, up_pieces, down_pieces):
    total, width = own.shape
    span = mine.shape[1]
    ff = up_pieces[0].shape[1]
    vmem = pl.BlockSpec(memory_space=pltpu.VMEM)
    pieces = [*out_pieces, *up_pieces, *down_pieces]
    shapes = [
        ((total, width), BF), ((total, width), F32), ((total, span), BF), ((total, span), BF),
        ((total, ff), BF), ((total, width), BF), ((total, width), BF), ((total, ff), BF),
        ((total, width), BF), ((32, width // 2), F32),
    ]
    rows = lambda group: tuple(p.shape[0] for p in group)
    return pl.pallas_call(
        functools.partial(token_kernel, rows(out_pieces), rows(up_pieces), rows(down_pieces)),
        in_specs=[pl.BlockSpec(memory_space=pltpu.SMEM)]
        + [vmem] * 5
        + [pl.BlockSpec(memory_space=pl.ANY)] * len(pieces),
        out_specs=[vmem] * len(shapes),
        out_shape=[jax.ShapeDtypeStruct(s, d) for s, d in shapes],
        scratch_shapes=[
            pltpu.VMEM((width, width), BF),
            pltpu.VMEM((width, ff), BF),
            pltpu.VMEM((ff, width), BF),
            pltpu.VMEM((total, width), F32),
            pltpu.VMEM((total, width), F32),
            pltpu.VMEM((total, width), F32),
            pltpu.VMEM((total, LANES), F32),
            pltpu.VMEM((total, ff), F32),
            pltpu.VMEM((total, width), F32),
            pltpu.VMEM((2, total, width), F32),
            pltpu.VMEM((4, 16, width), F32),
            pltpu.VMEM((16, width), F32),
            pltpu.SemaphoreType.DMA((len(pieces),)),
        ],
        compiler_params=pltpu.CompilerParams(vmem_limit_bytes=60 << 20),
        cost_estimate=pl.CostEstimate(
            flops=2 * total * width * (4 * ff + 2 * width),
            bytes_accessed=4 * width * ff + 6 * total * ff,
            transcendentals=2 * total * ff,
        ),
        name="token_block",
    )(at, own, mine, theirs, cot, vec, *pieces)


def turned(core, outer, near, z):
    pick = lambda a, b: jnp.where(core == 0, a, b)
    return pick(outer, near), pick(z, outer), pick(near, z)


def place_of(owner, index, relative, b, c):
    first = index if relative else 1 - index
    return (first, c, b) if owner == 0 else (b, first, c)


def up_pieces(owner, index, n, span, hid_t, gup_ref, emit):
    for relative in range(2):
        for b in range(2):
            for c in range(2):
                outer, near, z = place_of(owner, index, relative, b, c)
                left = hid_t[pl.ds(pl.multiple_of((2 * outer + owner) * n, 16), n), :]
                for far in range(2):
                    cols = pl.ds(pl.multiple_of((near * 4 + z * 2 + far) * span, LANES), span)
                    emit((relative, b, c, far), jnp.dot(left, gup_ref[:, cols], preferred_element_type=F32))


def rest_pieces(owner, index, n, wide, span, att_t, act_ref, gffn_ref, gattn_ref, small_ref, emit):
    half = wide // 2
    for relative in range(2):
        for b in range(2):
            outer = place_of(owner, index, relative, b, 0)[0]
            shard = 2 * outer + owner
            small = small_ref[pl.ds(pl.multiple_of(shard * 8, 8), 8), :]
            for c in range(2):
                _, near, z = place_of(owner, index, relative, b, c)
                cols = pl.ds(pl.multiple_of(shard * wide + near * half, LANES), half)
                if owner == 0:
                    if b:
                        continue
                    rows, marks = act_ref[:, cols], [((relative, zz, c), zz) for zz in range(2)]
                else:
                    if c:
                        continue
                    rows, marks = act_ref[:, cols], [((relative, b, zz), zz) for zz in range(2)]
                down = lax.dot_general(rows, gffn_ref[...], (((0,), (0,)), ((), ())), preferred_element_type=F32)
                for mark, zz in marks:
                    at = pl.ds(pl.multiple_of(shard * n + (near * 2 + zz) * (n // 4), 16), n // 4)
                    out = jnp.dot(att_t[at, :], gattn_ref[...], preferred_element_type=F32)
                    for far in range(2):
                        cut = slice(far * span, (far + 1) * span)
                        head = (near == 0) if zz == 0 and far == 0 else False
                        emit(
                            (*mark, far),
                            down[zz * half // 2 : (zz + 1) * half // 2, cut],
                            out[:, cut],
                            jnp.where(head, small, 0.0),
                        )


def up_send_kernel(at_ref, hlow_ref, gup_ref, send_ref, hid_t):
    width = hlow_ref.shape[1]
    n, span = width // 4, gup_ref.shape[1] // 8
    hid_t[...] = hlow_ref[...].T

    def emit(at, value):
        send_ref[at] = value.astype(BF)

    for owner in range(2):

        @pl.when(at_ref[0] == 1 - owner)
        def _(owner=owner):
            up_pieces(owner, at_ref[1 + owner], n, span, hid_t, gup_ref, emit)


def fill_att(at_ref, mine_ref, theirs_ref, att_t):
    span = mine_ref.shape[1]
    core = at_ref[0]
    att_t[pl.ds(pl.multiple_of(core * span, LANES), span), :] = mine_ref[...].T
    att_t[pl.ds(pl.multiple_of((1 - core) * span, LANES), span), :] = theirs_ref[...].T


def rest_send_kernel(at_ref, mine_ref, theirs_ref, act_ref, gffn_ref, gattn_ref, small_ref, send_ref, att_t):
    width = gffn_ref.shape[1]
    n, wide, span = width // 4, act_ref.shape[1] // 4, mine_ref.shape[1]
    fill_att(at_ref, mine_ref, theirs_ref, att_t)

    def emit(at, down, out, small):
        send_ref[(*at, slice(0, wide // 4))] = down.astype(BF)
        send_ref[(*at, slice(wide // 4, wide // 4 + n // 4))] = out.astype(BF)
        send_ref[(*at, slice(wide // 4 + n // 4, None))] = small.astype(BF)

    for owner in range(2):

        @pl.when(at_ref[0] == 1 - owner)
        def _(owner=owner):
            rest_pieces(
                owner, at_ref[1 + owner], n, wide, span, att_t, act_ref, gffn_ref, gattn_ref, small_ref, emit
            )


def keep_kernel(
    at_ref, mine_ref, theirs_ref, hlow_ref, act_ref, gffn_ref, gup_ref, gattn_ref, small_ref, up_ref, rest_ref,
    away_ref, kept_ref, hid_t, att_t,
):
    width = gffn_ref.shape[1]
    n, wide, span = width // 4, act_ref.shape[1] // 4, mine_ref.shape[1]
    m = n + wide // 4
    hid_t[...] = hlow_ref[...].T
    fill_att(at_ref, mine_ref, theirs_ref, att_t)

    def put(at, rows, value, got_ref, got):
        out_ref = kept_ref if at[0] else away_ref
        out_ref[(*at[1:], rows)] = (value + got_ref[(*at, got)].astype(F32)).astype(BF)

    def emit_up(at, value):
        put(at, slice(0, n), value, up_ref, slice(None))

    def emit(at, down, out, small):
        put(at, slice(n, m), down, rest_ref, slice(0, wide // 4))
        put(at, slice(m, m + n // 4), out, rest_ref, slice(wide // 4, wide // 4 + n // 4))
        put(at, slice(m + n // 4, None), small, rest_ref, slice(wide // 4 + n // 4, None))

    for owner in range(2):

        @pl.when(at_ref[0] == owner)
        def _(owner=owner):
            index = at_ref[1 + owner]
            up_pieces(owner, index, n, span, hid_t, gup_ref, emit_up)
            rest_pieces(owner, index, n, wide, span, att_t, act_ref, gffn_ref, gattn_ref, small_ref, emit)


def grads_call(kernel, name, at, arrays, shapes, transposed, flops):
    vmem = pl.BlockSpec(memory_space=pltpu.VMEM)
    return pl.pallas_call(
        kernel,
        in_specs=[pl.BlockSpec(memory_space=pltpu.SMEM)] + [vmem] * len(arrays),
        out_specs=[vmem] * len(shapes),
        out_shape=[jax.ShapeDtypeStruct(s, BF) for s in shapes],
        scratch_shapes=[pltpu.VMEM(t, BF) for t in transposed],
        compiler_params=pltpu.CompilerParams(vmem_limit_bytes=60 << 20),
        cost_estimate=pl.CostEstimate(
            flops=flops, bytes_accessed=2 * sum(a.size for a in arrays), transcendentals=0
        ),
        name=name,
    )(at, *arrays)


def row_backward_kernel(
    heads, hd, first_head, gmine_ref, gother_ref, keep_ref, send_ref, inv_ref, wts_ref, qcat_ref, kcat_ref,
    vaug_ref, ent_ref, entb_ref, *refs,
):
    gq_ref, gkv_ref, gscore_s, low_s, gk_s, gv_s = refs[-6:]
    step = pl.program_id(0)
    block = gmine_ref.shape[0]
    full = kcat_ref.shape[1]
    scale = hd ** (-0.5)
    lane = lax.broadcasted_iota(jnp.int32, (block, LANES - hd), 1)
    is_ent = entb_ref[:, :1] > 0
    early = step < pl.num_programs(0) // 2
    g_all = jnp.where(early, gmine_ref[...], gother_ref[...])
    att_all = jnp.where(early, keep_ref[...], send_ref[...])
    g_word, g_ent = [], []
    for h in range(heads):
        cut = slice(h * hd, (h + 1) * hd)
        g_low = (g_all[:, cut].astype(F32) * inv_ref[:, first_head + h : first_head + h + 1]).astype(BF)
        delta = jnp.sum(g_low.astype(F32) * att_all[:, cut].astype(F32), axis=1, keepdims=True)
        d_hi = delta.astype(BF)
        d_lo = (delta - d_hi.astype(F32)).astype(BF)
        extra = jnp.where(
            lane == 0, d_hi.astype(F32), jnp.where(lane == 1, d_lo.astype(F32), 0.0)
        ).astype(BF)
        g_aug = jnp.concatenate([g_low, extra], axis=1)
        gscore_s[h % 2] = lax.dot_general(
            g_aug, vaug_ref[h], (((1,), (1,)), ((), ())), preferred_element_type=F32
        )
        for r in range(0, block, CHUNK):
            low_s[h % 2, r : r + CHUNK, :] = (
                wts_ref[h, r : r + CHUNK, :].astype(F32) * gscore_s[h % 2, r : r + CHUNK, :]
            ).astype(BF)
        g_q = jnp.dot(low_s[h % 2], kcat_ref[h], preferred_element_type=F32) * scale
        g_word.append(g_q[:, :hd])
        g_ent.append(g_q[:, hd:])
        g_k = lax.dot_general(
            qcat_ref[h], low_s[h % 2], (((0,), (0,)), ((), ())), preferred_element_type=F32
        )
        g_v = lax.dot_general(
            g_low, wts_ref[h], (((0,), (0,)), ((), ())), preferred_element_type=F32
        )

        @pl.when(step == 0)
        def _(h=h, g_k=g_k, g_v=g_v):
            gk_s[h] = g_k
            gv_s[h] = g_v

        @pl.when(step > 0)
        def _(h=h, g_k=g_k, g_v=g_v):
            gk_s[h] += g_k
            gv_s[h] += g_v

    g_word = jnp.concatenate(g_word, axis=1)
    g_ent = jnp.concatenate(g_ent, axis=1)
    gq_ref[0] = jnp.where(is_ent, 0.0, g_word).astype(BF)
    gq_ref[1] = jnp.where(is_ent, 0.0, g_ent).astype(BF)
    gq_ref[2] = jnp.where(is_ent, g_word, 0.0).astype(BF)
    gq_ref[3] = jnp.where(is_ent, g_ent, 0.0).astype(BF)

    @pl.when(step == pl.num_programs(0) - 1)
    def _():
        def close(piece, carry):
            at = pl.ds(pl.multiple_of(piece * block, block), block)
            pick = ent_ref[at, :1] > 0
            g_keys, g_vals = [], []
            for h in range(heads):
                both = gk_s[h, :, at].T
                g_keys.append(jnp.where(pick, both[:, hd:], both[:, :hd]))
                g_vals.append(gv_s[h, :, at].T)
            gkv_ref[0, at, :] = jnp.concatenate(g_keys, axis=1).astype(BF)
            gkv_ref[1, at, :] = jnp.concatenate(g_vals, axis=1).astype(BF)
            return carry

        lax.fori_loop(0, full // block, close, 0)


def row_backward(first_head, heads, grads, gmine, gother, keep, send, inv, wts, qcat, kcat, vaug, ent, hd):
    half, all_cols = keep.shape
    full = 2 * half
    block = min(256, half)
    first = half // block
    cols = heads * hd
    g, c = first_head // heads, first_head * hd // cols
    by_rows = pl.BlockSpec((block, LANES), lambda i: (i, 0))
    by_head = lambda width: pl.BlockSpec((heads, block, width), lambda i: (g, i, 0))
    of_head = lambda width: pl.BlockSpec((heads, full, width), lambda i: (g, 0, 0))
    low = pl.BlockSpec((block, cols), lambda i: (jnp.minimum(i, first - 1), c))
    high = pl.BlockSpec((block, cols), lambda i: (jnp.maximum(i - first, 0), c))
    given = [] if grads is None else list(grads)
    return pl.pallas_call(
        functools.partial(row_backward_kernel, heads, hd, first_head),
        grid=(full // block,),
        in_specs=[
            low, high, low, high,
            by_rows,
            by_head(full),
            by_head(2 * hd),
            of_head(2 * hd),
            of_head(LANES),
            pl.BlockSpec((full, LANES), lambda i: (0, 0)),
            by_rows,
        ]
        + [pl.BlockSpec(memory_space=pl.ANY)] * len(given),
        out_specs=[
            pl.BlockSpec((4, block, cols), lambda i: (0, i, c)),
            pl.BlockSpec((2, full, cols), lambda i: (0, 0, c)),
        ],
        out_shape=[
            jax.ShapeDtypeStruct((4, full, all_cols), BF),
            jax.ShapeDtypeStruct((2, full, all_cols), BF),
        ],
        scratch_shapes=[
            pltpu.VMEM((2, block, full), F32),
            pltpu.VMEM((2, block, full), BF),
            pltpu.VMEM((heads, 2 * hd, full), F32),
            pltpu.VMEM((heads, hd, full), F32),
        ],
        input_output_aliases={11 + i: i for i in range(len(given))},
        compiler_params=pltpu.CompilerParams(vmem_limit_bytes=60 << 20),
        cost_estimate=pl.CostEstimate(
            flops=16 * heads * full * full * LANES,
            bytes_accessed=2 * heads * full * full + 20 * full * cols,
            transcendentals=0,
        ),
        name="row_backward",
    )(gmine, gother, keep, send, inv, wts, qcat, kcat, vaug, ent, ent, *given)


def qkv_grad_kernel(at_ref, own_ref, other_ref, gq_ref, gkv_ref, send_ref, keep_ref, rows_t):
    half, width = own_ref.shape
    n = width // 16
    span = gq_ref.shape[2]
    core, index = at_ref[0], at_ref[1]
    rows_t[:, :half] = own_ref[...].T
    rows_t[:, half:] = other_ref[...].T

    def write(out_ref, at, start, count):
        left = rows_t[pl.ds(pl.multiple_of(start, 16), count * n), :]
        for b in range(6):
            right = gq_ref[b] if b < 4 else gkv_ref[b - 4]
            piece = jnp.dot(left, right, preferred_element_type=F32).astype(BF)
            for p in range(count):
                out_ref[(*at(p), slice(b * n, (b + 1) * n))] = piece[p * n : (p + 1) * n, :]

    ones = jnp.ones((8, 2 * half), BF)
    sums = [
        jnp.dot(ones, gq_ref[b] if b < 4 else gkv_ref[b - 4], preferred_element_type=F32)[:1] for b in range(6)
    ]

    def write_sums(out_ref, at, outer, near, on_core):
        query = jnp.where(outer == 0, jnp.where(near == 0, sums[0], sums[1]), jnp.where(near == 0, sums[2], sums[3]))
        value = jnp.where(outer == on_core, sums[5], 0.0)
        rows = jnp.concatenate([query, value, jnp.zeros((6, span), F32)], axis=0)
        out_ref[(*at, slice(6 * n, None))] = rows.astype(BF)

    for which, out_ref in ((1 - index, send_ref), (index, keep_ref)):

        @pl.when(core == 0)
        def _(which=which, out_ref=out_ref):
            write(out_ref, lambda p: (p // 2 % 2, p // 4, p % 2), which * 8 * n, 8)
            for p in range(8):
                at = (p // 2 % 2, p // 4, p % 2)
                write_sums(out_ref, at, which, p // 4, 0)

        @pl.when(core == 1)
        def _(which=which, out_ref=out_ref):
            for o in range(2):
                write(out_ref, lambda p, o=o: (o, p // 2, p % 2), o * 8 * n + which * 4 * n, 4)
                for p in range(4):
                    write_sums(out_ref, (o, p // 2, p % 2), o, which, 1)


def qkv_grad(at, own, other, gq, gkv):
    half, width = own.shape
    span = gkv.shape[2]
    n = width // 16
    vmem = pl.BlockSpec(memory_space=pltpu.VMEM)
    return pl.pallas_call(
        qkv_grad_kernel,
        in_specs=[pl.BlockSpec(memory_space=pltpu.SMEM)] + [vmem] * 4,
        out_specs=[vmem] * 2,
        out_shape=[jax.ShapeDtypeStruct((2, 2, 2, 6 * n + 8, span), BF)] * 2,
        scratch_shapes=[pltpu.VMEM((width, 2 * half), BF)],
        compiler_params=pltpu.CompilerParams(vmem_limit_bytes=60 << 20),
        cost_estimate=pl.CostEstimate(
            flops=24 * half * width * span, bytes_accessed=32 * half * span, transcendentals=0
        ),
        name="qkv_grad",
    )(at, own, other, gq, gkv)


def input_grad_kernel(gq_ref, gkv_ref, w_ref, gy1_ref, mine_ref, away_ref):
    half = gy1_ref.shape[0]
    span = gkv_ref.shape[2]

    def grads(b):
        return gq_ref.at[b] if b < 4 else gkv_ref.at[b - 4]

    def back(at):
        total = None
        for b in range(6):
            part = lax.dot_general(
                grads(b)[at, :], w_ref[:, b * span : (b + 1) * span], (((1,), (1,)), ((), ())),
                preferred_element_type=F32,
            )
            total = part if total is None else total + part
        return total

    away_ref[...] = back(slice(half, 2 * half)).astype(BF)
    mine_ref[...] = gy1_ref[...] + back(slice(0, half))


def row_input_grad(gq, gkv, w, gy1):
    half, width = gy1.shape
    span = gkv.shape[2]
    vmem = pl.BlockSpec(memory_space=pltpu.VMEM)
    shapes = [((half, width), F32), ((half, width), BF)]
    return pl.pallas_call(
        input_grad_kernel,
        in_specs=[vmem] * 4,
        out_specs=[vmem] * 2,
        out_shape=[jax.ShapeDtypeStruct(s, d) for s, d in shapes],
        compiler_params=pltpu.CompilerParams(vmem_limit_bytes=60 << 20),
        cost_estimate=pl.CostEstimate(
            flops=4 * half * width * 6 * span, bytes_accessed=20 * half * width, transcendentals=0
        ),
        name="row_input_grad",
    )(gq, gkv, w, gy1)


def lay_rest_kernel(at_ref, mine_ref, other_ref, up_ref, down_ref, out_ref, small_ref):
    span = mine_ref.shape[2]
    k, n, m = up_ref.shape[0], down_ref.shape[0] // 4, out_ref.shape[0] // 4
    core, index = at_ref[0], at_ref[1]
    last = slice(k + n + m, None)
    small_ref[...] = jnp.where(index == 0, mine_ref[0, last, :].astype(F32), other_ref[0, last, :].astype(F32))
    for a, ref in ((index, mine_ref), (1 - index, other_ref)):
        for b in range(2):
            pair = jnp.where(core == 0, b * 2 + a, a * 2 + b)
            for far in range(2):
                j = b * 2 + far
                cols = pl.ds(pl.multiple_of((pair * 2 + far) * span, LANES), span)
                up_ref[:, cols] = ref[j, :k, :].astype(F32)
                cols = slice(far * span, (far + 1) * span)
                down_ref[pl.ds(pl.multiple_of(pair * n, 8), n), cols] = ref[j, k : k + n, :].astype(F32)
                out_ref[pl.ds(pl.multiple_of(pair * m, 8), m), cols] = ref[j, k + n : k + n + m, :].astype(F32)


def lay_qkv_kernel(at_ref, keep_ref, got_ref, query_ref, kv_ref, small_ref):
    span = keep_ref.shape[2]
    n = (keep_ref.shape[1] - 8) // 6
    last = slice(6 * n, None)
    for half, src in ((at_ref[0], keep_ref), (1 - at_ref[0], got_ref)):
        small_ref[half] = src[0, last, :].astype(F32)
        for b in range(6):
            ref, i = (query_ref, b) if b < 4 else (kv_ref, b - 4)
            cols = pl.ds(pl.multiple_of(i * 2 * span + half * span, LANES), span)
            for j in range(4):
                ref[j * n : (j + 1) * n, cols] = src[j, b * n : (b + 1) * n, :].astype(F32)


def lay(kernel, name, at, arrays, shapes):
    vmem = pl.BlockSpec(memory_space=pltpu.VMEM)
    return pl.pallas_call(
        kernel,
        in_specs=[pl.BlockSpec(memory_space=pltpu.SMEM)] + [vmem] * len(arrays),
        out_specs=[vmem] * len(shapes),
        out_shape=[jax.ShapeDtypeStruct(s, F32) for s in shapes],
        compiler_params=pltpu.CompilerParams(vmem_limit_bytes=60 << 20),
        cost_estimate=pl.CostEstimate(
            flops=0, bytes_accessed=6 * sum(a.size for a in arrays), transcendentals=0
        ),
        name=name,
    )(at, *arrays)


def row_layer(
    inputs, query_weight, kv_weight, out_weight, up_weight, down_weight,
    query_bias, value_bias, out_bias, up_bias, down_bias,
    norm1_gain, norm1_shift, norm2_gain, norm2_shift, types, lengths, cotangent,
):
    rows_here, span, width = inputs.shape
    hd = width // HEADS
    full = types.shape[1]
    heads = HEADS // 2
    cols = heads * hd
    row_count = lax.axis_size("row")
    core, outer, row_id = (lax.axis_index(n) for n in ("core", "outer", "row"))
    place = [row_id // bit % 2 for bit in (1, 2, 4)]
    near = place[0]
    own_count = full // 2
    both_ways = [(0, 1), (1, 0)]

    def after(values, *others):
        return lax.optimization_barrier((values, *others))[0]

    def swap(values):
        return lax.ppermute(values, "core", both_ways)

    def cross(values):
        return lax.ppermute(values, "outer", both_ways)

    def pair_up(values, bit):
        return lax.ppermute(values, "row", [(i, i ^ bit) for i in range(row_count)])

    def in_order(index, mine, other, axis=0):
        first, second = jnp.where(index == 0, mine, other), jnp.where(index == 0, other, mine)
        return jnp.stack([first, second], axis=axis)

    def take(values, index, axis=0):
        return lax.dynamic_index_in_dim(values, index, axis, keepdims=False)

    def halves_of_rows(values):
        pieces = values.reshape(rows_here, 2, span // 2, width)
        other = swap(take(pieces, 1 - core, 1))
        return in_order(core, take(pieces, core, 1), other).reshape(row_count, span // 2, width)

    def over_rows(values):
        return lax.all_to_all(values, "row", 0, 0, tiled=True)

    def rows_whole(back):
        back = back.reshape(2, rows_here, span // 2, width)
        other = swap(take(back, 1 - core))
        both = in_order(core, take(back, core), other)
        return both.transpose(1, 0, 2, 3).reshape(rows_here, span, width)

    shard = query_weight.shape[0]
    wide = down_weight.shape[0]

    def near_half(values):
        return take(values.reshape(2, values.shape[0] // 2, values.shape[1]), near)

    f_own, f_core = 2 * outer + core, 2 * outer + 1 - core
    f_cross, f_both = 2 * (1 - outer) + core, 2 * (1 - outer) + 1 - core

    q_got = cross(near_half(query_weight))
    to_rows = halves_of_rows(inputs)
    own_rows = over_rows(to_rows).reshape(own_count, width)
    query_own, kv_own, types, lengths, query_bias = lax.optimization_barrier(
        (query_weight, kv_weight, types, lengths, query_bias, to_rows)
    )[:5]
    q_core, kv_core = swap(query_own), swap(kv_own)
    q_passed, kv_got = pair_up(q_got, 1), cross(after(kv_weight, q_got))
    q_got2 = swap(after(q_got, q_core, kv_core))
    own_rows, q_passed = lax.optimization_barrier((own_rows, q_passed))
    other_rows = swap(own_rows)
    q_passed2, kv_got2 = swap(q_passed), swap(kv_got)
    cot_halves = halves_of_rows(after(cotangent, own_rows))
    query_pieces = [query_weight, q_core, q_got, q_passed, q_got2, q_passed2]
    kv_pieces = [kv_weight, kv_core, kv_got, kv_got2]
    part = shard // 2
    query_at = [
        f_own * shard, f_core * shard,
        f_cross * shard + near * part, f_cross * shard + (1 - near) * part,
        f_both * shard + near * part, f_both * shard + (1 - near) * part,
    ]
    kv_at = [f_own * shard, f_core * shard, f_cross * shard, f_both * shard]
    at_qkv = jnp.stack([core, *query_at, *kv_at]).astype(jnp.int32)

    tags = jnp.concatenate([types, lengths], axis=1)
    tags_other = after(swap(tags), q_got2)
    tags = take(in_order(core, tags, tags_other).reshape(row_count, -1), row_id)
    types_row, lengths_row = tags[:full].reshape(row_count, span), tags[full:]
    docs = lengths_row.shape[0]
    ends = jnp.sum(jnp.where(jnp.arange(docs)[:, None] >= jnp.arange(docs)[None], lengths_row[None], 0), axis=1)

    vectors = (
        query_bias, value_bias, out_bias, up_bias, down_bias,
        norm1_gain, norm1_shift, norm2_gain, norm2_shift,
    )
    packed = jnp.concatenate(vectors)
    packed = in_order(outer, packed, cross(packed))
    vec = in_order(core, packed, swap(packed)).reshape(2, 2, -1, shard)

    qcat, kcat, vaug, w_sel, ent, qseg, kseg = row_project(
        at_qkv, ends, own_rows, other_rows, vec, types_row, query_pieces, kv_pieces, heads, hd
    )

    low_rows = down_weight[: wide // 2]
    u_got = cross(after(near_half(up_weight), kv_got))
    d_got = cross(after(near_half(low_rows), kv_got))
    late_out, late_up, late_down = lax.optimization_barrier((out_weight, up_weight, down_weight, kv_got2))[:3]
    o_core, u_core, d_core = swap(late_out), swap(late_up), swap(late_down)
    u_mid, d_mid, m_out, m_down, o_core, u_core, d_core = lax.optimization_barrier(
        (u_got, d_got, out_weight, down_weight, o_core, u_core, d_core, kcat)
    )[:7]
    u_passed, d_passed = pair_up(u_mid, 1), pair_up(d_mid, 1)
    o_got, t_got = cross(m_out), cross(m_down[wide // 2 :])
    u_got2, d_got2 = swap(u_mid), swap(d_mid)
    cot = over_rows(after(cot_halves, other_rows)).reshape(own_count, width)
    keep, send, wts, inv = row_attend(qcat, kcat, vaug, qseg, kseg, heads, hd)
    theirs = swap(send)
    u_passed2, d_passed2, o_got2, t_got2 = (
        swap(v) for v in lax.optimization_barrier((u_passed, d_passed, o_got, t_got, keep))[:4]
    )
    out_pieces = [out_weight, o_core, o_got, o_got2]
    out_at = [f * shard for f in (f_own, f_core, f_cross, f_both)]
    up_pieces = [up_weight, u_core, u_got, u_passed, u_got2, u_passed2]
    down_pieces = [down_weight, d_core, d_got, d_passed, t_got, d_got2, d_passed2, t_got2]
    quarter = wide // 4
    down_at = [
        f_own * wide, f_core * wide,
        f_cross * wide + near * quarter, f_cross * wide + (1 - near) * quarter, f_cross * wide + 2 * quarter,
        f_both * wide + near * quarter, f_both * wide + (1 - near) * quarter, f_both * wide + 2 * quarter,
    ]
    at_rest = jnp.stack([core, *out_at, *query_at, *down_at]).astype(jnp.int32)

    (
        result, gy1, gmine, gtheirs, act, hlow, gffn, gup, gattn, small
    ) = token_block(at_rest, own_rows, keep, theirs, cot, vec, out_pieces, up_pieces, down_pieces)
    gother = swap(gtheirs)
    at_core = core.astype(jnp.int32).reshape(1)
    at_near = near.astype(jnp.int32).reshape(1)
    at_grads = jnp.stack([core, outer, near]).astype(jnp.int32)
    m, ff = width // 16, up_weight.shape[1]
    bits = (2, 2, 2)
    tall = (2, *bits, ff // 16 + m + 8, cols)
    (rest_send,) = grads_call(
        rest_send_kernel, "rest_send", at_grads, [keep, theirs, act, gffn, gattn, small], [tall],
        [(width, own_count)], own_count * width * (ff + width),
    )
    hlow, gup, gother, rest_send = lax.optimization_barrier((hlow, gup, gother, rest_send))
    (up_send,) = grads_call(
        up_send_kernel, "up_send", at_grads, [hlow, gup], [(2, *bits, shard, cols)],
        [(width, own_count)], own_count * width * ff,
    )

    def add(*arrays):
        return functools.reduce(jnp.add, [v.astype(F32) for v in arrays]).astype(BF)

    def by_core(a, b):
        return jnp.where(core == 0, a, b)

    stages = {
        "s1": ("outer", "y"), "s2": ("z", "outer"), "s3": ("y", "z"), "far": ("far", "far"), "g1": ("z", "y"),
        "t1": ("z", "y"), "t2": ("y", "z"), "t3": ("far", "far"),
    }
    index_on = {"outer": outer, "y": near, "z": place[1], "far": place[2]}
    index_of = {name: by_core(index_on[a], index_on[b]) for name, (a, b) in stages.items()}
    every = ("row", "outer", "core")

    def pairs_of(stage):
        found = []
        for r in range(row_count):
            for o in range(2):
                for c in range(2):
                    axis = stages[stage][c]
                    to = (r, 1 - o) if axis == "outer" else (r ^ {"y": 1, "z": 2, "far": 4}[axis], o)
                    found.append(((r * 2 + o) * 2 + c, (to[0] * 2 + to[1]) * 2 + c))
        return found

    def send_over(values, stage):
        return lax.ppermute(values, every, pairs_of(stage))

    axis_at = {"far": 0, "z": 1, "y": 2}

    def trade(values, stage):
        away, mine = (
            by_core(*(take(values, i, axis_at[axis]) for axis in stages[stage]))
            for i in (1 - index_of[stage], index_of[stage])
        )
        token[0] = away
        return mine, send_over(away, stage)

    def traded(state, stage):
        mine, other = in_turn(*state)
        token[0] = other
        return by_core(*(in_order(index_of[stage], mine, other, axis_at[axis]) for axis in stages[stage]))

    def by_rows(values):
        return values.reshape(2, 2, 2, span // 2, width)

    token = [gother]

    def in_turn(*arrays):
        return lax.optimization_barrier((*arrays, token[0]))[: len(arrays)]

    def halve(state, axis):
        mine, other = in_turn(*state)
        away, mine = (
            add(take(mine, i), take(other, i)) for i in (1 - index_of[axis], index_of[axis])
        )
        token[0] = away
        return mine, send_over(away, axis)

    def start_spread(state, axis):
        total = add(*in_turn(*state))
        token[0] = total
        return total, send_over(total, axis)

    def spread(state, have, axis):
        total = in_order(index_of[have], *in_turn(*state))
        token[0] = total
        return total, send_over(total, axis)

    out_rows = trade(by_rows(result), "t1")
    away, mine = grads_call(
        keep_kernel, "keep_grads", at_grads,
        [keep, theirs, hlow, act, gffn, gup, gattn, small, swap(up_send), swap(rest_send)],
        [(*bits, shard + tall[-2], cols)] * 2, [(width, own_count)] * 2, own_count * width * (2 * ff + width),
    )
    rest = (mine, send_over(away, "s1"))
    token[0] = away
    out_rows = trade(traded(out_rows, "t1"), "t2")
    gmine, _ = lax.optimization_barrier((gmine, token[0]))
    gq, gkv = row_backward(
        0, heads, None, gmine, gother, keep, send, inv, wts, qcat, kcat, vaug, ent, hd
    )
    n = width // 16
    token[0] = gkv
    out_rows = trade(traded(out_rows, "t2"), "t3")
    rest = halve(rest, "s2")
    at_first = jnp.stack([core, index_of["s1"]]).astype(jnp.int32)
    q_send, q_keep = qkv_grad(at_first, own_rows, after(other_rows, token[0]), gq, gkv)
    six = (q_keep, send_over(q_send, "s1"))
    token[0] = q_send
    out_rows = traded(out_rows, "t3")
    in_mine, in_away = row_input_grad(gq, gkv, after(w_sel, token[0]), gy1)
    in_other = swap(in_away)
    token[0] = in_away
    rest = halve(rest, "s3")
    in_mine, in_other = in_turn(in_mine, in_other)
    grad_in = (in_mine + in_other.astype(F32)).astype(BF)
    in_rows = trade(by_rows(grad_in), "t3")
    six = halve(six, "s2")
    rest = halve(rest, "far")
    in_rows = trade(traded(in_rows, "t3"), "t1")
    six = halve(six, "s3")
    rest = start_spread(rest, "far")
    six = halve(six, "far")
    in_rows = trade(traded(in_rows, "t1"), "t2")
    rest = spread(rest, "far", "s3")
    six = start_spread(six, "far")
    rest = spread(rest, "s3", "g1")
    six = spread(six, "far", "s3")
    in_rows = traded(in_rows, "t2")
    output, input_grad = rows_whole(out_rows), rows_whole(in_rows)
    six = spread(six, "s3", "g1")
    at_last = jnp.stack([core, index_of["g1"]]).astype(jnp.int32)
    g_up, g_down, g_out, small = lay(
        lay_rest_kernel, "lay_rest", at_last, [v.reshape(4, *v.shape[2:]) for v in in_turn(*rest)],
        [up_weight.shape, down_weight.shape, out_weight.shape, (8, cols)],
    )
    token[0] = g_out
    six = in_order(index_of["g1"], *in_turn(*six))
    away, kept = by_core(six[:, 1], six[0]), by_core(six[:, 0], six[1])
    parts = [v.reshape(4, *v.shape[2:]) for v in (kept, swap(away))]
    g_query, g_kv, halves = lay(
        lay_qkv_kernel, "lay_qkv", at_core, parts, [query_weight.shape, kv_weight.shape, (2, 8, cols)]
    )
    pairs = small[2:5].reshape(6, shard)
    value = take(halves[:, 1].sum(axis=0).reshape(2, shard), core)
    return (
        output, input_grad, g_query, g_kv, g_out, g_up, g_down,
        halves[:, 0].reshape(-1), value, pairs[0], small[:2].reshape(-1), *(pairs[i] for i in range(1, 6)),
    )


def solution(mesh):
    def step(*args):
        ctx, fsdp = mesh.shape["ctx"], mesh.shape["fsdp"]
        row_count = args[0].shape[0] // (fsdp // 2)
        per_row = ctx // row_count
        fine = Mesh(
            mesh.devices.reshape(row_count, per_row, fsdp // 2, 2), ("row", "group", "outer", "core")
        )
        tokens = P(("outer", "core"), ("row", "group"), None)
        mat, vec = P(("outer", "core"), None), P(("outer", "core"))
        in_specs = (tokens, *[mat] * 5, *[vec] * 9, mat, mat, tokens)
        out_specs = (tokens, tokens, *[mat] * 5, *[vec] * 9)
        quarter = args[0].shape[2] // 4
        fits = per_row == 1 and fsdp == 4 and row_count == 8 and args[0].shape[2] % (2 * LANES) == 0 and quarter % 32 == 0
        body = row_layer if fits else functools.partial(layer, None, per_row)
        return jax.shard_map(
            body, mesh=fine, in_specs=in_specs, out_specs=out_specs, check_vma=False
        )(*args)

    return step
```

```python
import functools

import jax
import jax.numpy as jnp
from jax import lax
from jax.experimental import pallas as pl
from jax.experimental.pallas import tpu as pltpu
from jax.sharding import Mesh
from jax.sharding import PartitionSpec as P

HEADS = 12
EPSILON = 1e-05
BLOCKED = -1e30
BF = jnp.bfloat16
F32 = jnp.float32
LANES = 128
CHUNK = 16


def matmul(left_mat, right_mat):
    return jnp.dot(left_mat, right_mat, preferred_element_type=F32)


def rows_inner(left_mat, right_mat):
    return lax.dot_general(left_mat, right_mat, (((0,), (0,)), ((), ())), preferred_element_type=F32)


def times_transposed(left_mat, right_mat):
    return lax.dot_general(left_mat, right_mat, (((1,), (1,)), ((), ())), preferred_element_type=F32)


def normalize(values, gain_vec, shift_vec):
    center = values - jnp.mean(values, axis=-1, keepdims=True)
    scale_inv = lax.rsqrt(jnp.mean(center * center, axis=-1, keepdims=True) + EPSILON)
    normed = center * scale_inv
    return (normed * gain_vec + shift_vec, normed, scale_inv)


def normalize_back(grad_in, normed, scale_inv, gain_vec):
    scaled = grad_in * gain_vec
    inner_part = (
        scaled
        - jnp.mean(scaled, axis=-1, keepdims=True)
        - normed * jnp.mean(scaled * normed, axis=-1, keepdims=True)
    )
    return (inner_part * scale_inv, jnp.sum(grad_in * normed, axis=0), jnp.sum(grad_in, axis=0))


def column_sum(values):
    return jnp.sum(values.astype(F32), axis=0)


def forward_kernel(
    heads, hd, rows_ref, w_ref, bias_ref, ent_ref, qseg_ref, kseg_ref,
    att_ref, wts_ref, inv_ref, qcat_ref, kcat_ref, vneg_ref,
    kaug_s, vaug_s, score_s,
):
    step = pl.program_id(0)
    span = heads * hd
    full = rows_ref.shape[0]
    block = att_ref.shape[0]
    scale = hd ** (-0.5)

    @pl.when(step == 0)
    def _():
        kaug_s[:, :, LANES:] = jnp.broadcast_to(kseg_ref[...][None], (heads, full, LANES))
        lane = lax.broadcasted_iota(jnp.int32, (block, LANES - hd), 1)
        one_col = jnp.where(lane == 0, 1.0, 0.0).astype(BF)
        neg_col = jnp.where(lane < 2, -1.0, 0.0).astype(BF)

        def project(piece, carry):
            at = pl.ds(pl.multiple_of(piece * block, block), block)
            rows = rows_ref[at, :]
            ent = ent_ref[at, :hd]
            wide = ent_ref[at, :1] > 0
            word = (1 - ent).astype(BF)

            def part(index):
                cols = slice(index * span, (index + 1) * span)
                return jnp.dot(rows, w_ref[:, cols], preferred_element_type=F32) + bias_ref[:, cols]

            q_word = (jnp.where(wide, part(2), part(0))).astype(BF) * BF(scale)
            q_ent = (jnp.where(wide, part(3), part(1))).astype(BF) * BF(scale)
            keys = part(4).astype(BF)
            vals = part(5).astype(BF)
            for h in range(heads):
                cut = slice(h * hd, (h + 1) * hd)
                qcat_ref[h, at, :] = jnp.concatenate([q_word[:, cut], q_ent[:, cut]], axis=1)
                k_pair = jnp.concatenate([keys[:, cut] * word, keys[:, cut] * ent], axis=1)
                kcat_ref[h, at, :] = k_pair
                kaug_s[h, at, :LANES] = k_pair
                vneg_ref[h, at, :] = jnp.concatenate([vals[:, cut], neg_col], axis=1)
                vaug_s[h, at, :] = jnp.concatenate([vals[:, cut], one_col], axis=1)
            return carry

        lax.fori_loop(0, full // block, project, 0)

    here = pl.ds(pl.multiple_of(step * block, block), block)
    q_seg = qseg_ref[here, :]
    lane = lax.broadcasted_iota(jnp.int32, (block, LANES), 1)
    inv_all = jnp.zeros((block, LANES), F32)
    mixed = []
    for h in range(heads):
        q_aug = jnp.concatenate([qcat_ref[h, here, :], q_seg], axis=1)
        score_s[h % 2] = lax.dot_general(
            q_aug, kaug_s[h], (((1,), (1,)), ((), ())), preferred_element_type=F32
        )
        for r in range(0, block, CHUNK):
            s = score_s[h % 2, r : r + CHUNK, :]
            top = jnp.max(s, axis=1, keepdims=True)
            wts_ref[h, r : r + CHUNK, :] = jnp.exp(s - top).astype(BF)
        out = jnp.dot(wts_ref[h], vaug_s[h], preferred_element_type=F32)
        inv = 1.0 / out[:, hd : hd + 1]
        inv_all = jnp.where(lane == h, inv, inv_all)
        mixed.append((out[:, :hd] * inv).astype(BF))
    att_ref[...] = jnp.concatenate(mixed, axis=1)
    inv_ref[...] = inv_all


def attention_forward(rows, w_sel, bias_sel, ent, qseg, kseg, heads, hd):
    full, width = rows.shape
    block = min(256, full)
    span = heads * hd
    steps = full // block
    whole = lambda *dims: pl.BlockSpec(dims, lambda i: (0,) * len(dims))
    return pl.pallas_call(
        functools.partial(forward_kernel, heads, hd),
        grid=(steps,),
        in_specs=[
            whole(full, width),
            whole(width, 6 * span),
            whole(1, 6 * span),
            whole(full, LANES),
            whole(full, LANES),
            whole(full, LANES),
        ],
        out_specs=[
            pl.BlockSpec((block, span), lambda i: (i, 0)),
            pl.BlockSpec((heads, block, full), lambda i: (0, i, 0)),
            pl.BlockSpec((block, LANES), lambda i: (i, 0)),
            whole(heads, full, 2 * hd),
            whole(heads, full, 2 * hd),
            whole(heads, full, LANES),
        ],
        out_shape=[
            jax.ShapeDtypeStruct((full, span), BF),
            jax.ShapeDtypeStruct((heads, full, full), BF),
            jax.ShapeDtypeStruct((full, LANES), F32),
            jax.ShapeDtypeStruct((heads, full, 2 * hd), BF),
            jax.ShapeDtypeStruct((heads, full, 2 * hd), BF),
            jax.ShapeDtypeStruct((heads, full, LANES), BF),
        ],
        scratch_shapes=[
            pltpu.VMEM((heads, full, 2 * LANES), BF),
            pltpu.VMEM((heads, full, LANES), BF),
            pltpu.VMEM((2, block, full), F32),
        ],
        compiler_params=pltpu.CompilerParams(vmem_limit_bytes=60 << 20),
        cost_estimate=pl.CostEstimate(
            flops=2 * full * width * 6 * span + 8 * heads * full * full * LANES,
            bytes_accessed=2 * heads * full * full + 10 * full * width,
            transcendentals=heads * full * full,
        ),
        name="attention_forward",
    )(rows, w_sel, bias_sel, ent, qseg, kseg)


def backward_kernel(
    heads, hd, go_ref, att_ref, inv_ref, wts_ref, qcat_ref, kcat_ref, vneg_ref, ent_ref, entb_ref,
    gq_ref, gkv_ref, gscore_s, low_s, gk_s, gv_s,
):
    step = pl.program_id(0)
    span = heads * hd
    block = go_ref.shape[0]
    full = kcat_ref.shape[1]
    scale = hd ** (-0.5)
    lane = lax.broadcasted_iota(jnp.int32, (block, LANES - hd), 1)
    is_ent = entb_ref[:, :1] > 0
    g_word, g_ent = [], []
    for h in range(heads):
        cut = slice(h * hd, (h + 1) * hd)
        g_low = (go_ref[:, cut].astype(F32) * inv_ref[:, h : h + 1]).astype(BF)
        delta = jnp.sum(g_low.astype(F32) * att_ref[:, cut].astype(F32), axis=1, keepdims=True)
        d_hi = delta.astype(BF)
        d_lo = (delta - d_hi.astype(F32)).astype(BF)
        extra = jnp.where(
            lane == 0, d_hi.astype(F32), jnp.where(lane == 1, d_lo.astype(F32), 0.0)
        ).astype(BF)
        g_aug = jnp.concatenate([g_low, extra], axis=1)
        gscore_s[h % 2] = lax.dot_general(
            g_aug, vneg_ref[h], (((1,), (1,)), ((), ())), preferred_element_type=F32
        )
        for r in range(0, block, CHUNK):
            low_s[h % 2, r : r + CHUNK, :] = (
                wts_ref[h, r : r + CHUNK, :].astype(F32) * gscore_s[h % 2, r : r + CHUNK, :]
            ).astype(BF)
        g_q = jnp.dot(low_s[h % 2], kcat_ref[h], preferred_element_type=F32) * scale
        g_word.append(g_q[:, :hd])
        g_ent.append(g_q[:, hd:])
        g_k = lax.dot_general(
            qcat_ref[h], low_s[h % 2], (((0,), (0,)), ((), ())), preferred_element_type=F32
        )
        g_v = lax.dot_general(
            g_low, wts_ref[h], (((0,), (0,)), ((), ())), preferred_element_type=F32
        )

        @pl.when(step == 0)
        def _(h=h, g_k=g_k, g_v=g_v):
            gk_s[h] = g_k
            gv_s[h] = g_v

        @pl.when(step > 0)
        def _(h=h, g_k=g_k, g_v=g_v):
            gk_s[h] += g_k
            gv_s[h] += g_v

    g_word = jnp.concatenate(g_word, axis=1)
    g_ent = jnp.concatenate(g_ent, axis=1)
    gq_ref[:, :span] = jnp.where(is_ent, 0.0, g_word).astype(BF)
    gq_ref[:, span : 2 * span] = jnp.where(is_ent, 0.0, g_ent).astype(BF)
    gq_ref[:, 2 * span : 3 * span] = jnp.where(is_ent, g_word, 0.0).astype(BF)
    gq_ref[:, 3 * span :] = jnp.where(is_ent, g_ent, 0.0).astype(BF)

    @pl.when(step == pl.num_programs(0) - 1)
    def _():
        def close(piece, carry):
            at = pl.ds(pl.multiple_of(piece * block, block), block)
            pick = ent_ref[at, :1] > 0
            g_keys, g_vals = [], []
            for h in range(heads):
                both = gk_s[h, :, at].T
                g_keys.append(jnp.where(pick, both[:, hd:], both[:, :hd]))
                g_vals.append(gv_s[h, :, at].T)
            gkv_ref[at, :span] = jnp.concatenate(g_keys, axis=1).astype(BF)
            gkv_ref[at, span:] = jnp.concatenate(g_vals, axis=1).astype(BF)
            return carry

        lax.fori_loop(0, full // block, close, 0)


def attention_backward(g_out, att, inv, wts, qcat, kcat, vneg, ent, heads, hd):
    full, span = att.shape
    block = min(256, full)
    whole = lambda *dims: pl.BlockSpec(dims, lambda i: (0,) * len(dims))
    by_rows = lambda width: pl.BlockSpec((block, width), lambda i: (i, 0))
    by_head = lambda width: pl.BlockSpec((heads, block, width), lambda i: (0, i, 0))
    return pl.pallas_call(
        functools.partial(backward_kernel, heads, hd),
        grid=(full // block,),
        in_specs=[
            by_rows(span),
            by_rows(span),
            by_rows(LANES),
            by_head(full),
            by_head(2 * hd),
            whole(heads, full, 2 * hd),
            whole(heads, full, LANES),
            whole(full, LANES),
            by_rows(LANES),
        ],
        out_specs=[by_rows(4 * span), whole(full, 2 * span)],
        out_shape=[
            jax.ShapeDtypeStruct((full, 4 * span), BF),
            jax.ShapeDtypeStruct((full, 2 * span), BF),
        ],
        scratch_shapes=[
            pltpu.VMEM((2, block, full), F32),
            pltpu.VMEM((2, block, full), BF),
            pltpu.VMEM((heads, 2 * hd, full), F32),
            pltpu.VMEM((heads, hd, full), F32),
        ],
        compiler_params=pltpu.CompilerParams(vmem_limit_bytes=60 << 20),
        cost_estimate=pl.CostEstimate(
            flops=16 * heads * full * full * LANES,
            bytes_accessed=2 * heads * full * full + 20 * full * span,
            transcendentals=0,
        ),
        name="attention_backward",
    )(g_out, att, inv, wts, qcat, kcat, vneg, ent, ent)


def layer(
    half, per_row, inputs, query_weight, kv_weight, out_weight, up_weight, down_weight,
    query_bias, value_bias, out_bias, up_bias, down_bias,
    norm1_gain, norm1_shift, norm2_gain, norm2_shift, types, lengths, cotangent,
):
    rows_here, span, width = inputs.shape
    head_dim = width // HEADS
    full = types.shape[1]
    members = 2 * per_row
    heads = HEADS // members
    cols = heads * head_dim
    row_count = lax.axis_size("row")
    outer = lax.axis_size("outer")
    core = lax.axis_index("core")
    group = lax.axis_index("group")
    member = group * 2 + core
    row_id = lax.axis_index("row")
    own = row_count * (span // 2)

    def swap(values):
        return lax.ppermute(values, "core", [(0, 1), (1, 0)])

    def in_order(index, mine, other):
        return jnp.stack([jnp.where(index == 0, mine, other), jnp.where(index == 0, other, mine)])

    def gather_outer(values):
        if outer == 2:
            other = lax.ppermute(values, "outer", [(0, 1), (1, 0)])
            return in_order(lax.axis_index("outer"), values, other)
        return lax.all_gather(values, "outer", axis=0, tiled=False)

    def gather_members(values):
        pair = in_order(core, values, swap(values))
        if per_row == 1:
            return pair
        spread = lax.all_gather(pair, "group", axis=0, tiled=False)
        return spread.reshape((members,) + values.shape)

    def exchange_members(values):
        if per_row == 1:
            mine = lax.dynamic_index_in_dim(values, core, 0, keepdims=False)
            away = lax.dynamic_index_in_dim(values, 1 - core, 0, keepdims=False)
            return in_order(core, mine, swap(away))
        return lax.all_to_all(values, ("group", "core"), 0, 0, tiled=True)

    def take(values, index, axis):
        return lax.dynamic_index_in_dim(values, index, axis, keepdims=False)

    def to_row(values):
        pieces = values.reshape(rows_here, 2, span // 2, width)
        other = swap(take(pieces, 1 - core, 1))
        both = in_order(core, take(pieces, core, 1), other).reshape(row_count, span // 2, width)
        return lax.all_to_all(both, "row", 0, 0, tiled=True).reshape(own, width)

    def from_row(values):
        back = lax.all_to_all(values.reshape(row_count, span // 2, width), "row", 0, 0, tiled=True)
        back = back.reshape(2, rows_here, span // 2, width)
        other = swap(take(back, 1 - core, 0))
        both = in_order(core, take(back, core, 0), other)
        return both.transpose(1, 0, 2, 3).reshape(rows_here, span, width)

    own_rows = to_row(inputs)
    all_rows = gather_members(own_rows).reshape(full, width)

    tags = jnp.concatenate([types, lengths], axis=1)
    tags = in_order(core, tags, swap(tags)).reshape(row_count, -1)
    tags = take(tags, row_id, 0)
    types_row, lengths_row = tags[:full], tags[full:]

    def by_member(values):
        return values.reshape(row_count, per_row, 2, span // 2).transpose(1, 2, 0, 3).reshape(full)

    entity = by_member(types_row) > 0
    positions = by_member(lax.iota(jnp.int32, full))
    docs = lengths_row.shape[0]
    ends = [jnp.sum(lengths_row[: d + 1]) for d in range(docs)]
    seg = sum((positions >= end).astype(jnp.int32) for end in ends)
    lanes = lax.broadcasted_iota(jnp.int32, (full, LANES), 1)
    same = lanes == seg[:, None]
    qseg = jnp.where(same, 1.0, 0.0).astype(BF)
    kseg = jnp.where(same | (lanes >= docs), 0.0, BLOCKED).astype(BF)
    ent = jnp.broadcast_to(jnp.where(entity, 1.0, 0.0).astype(BF)[:, None], (full, LANES))

    shard = query_weight.shape[0]
    cut = jnp.concatenate([query_weight, kv_weight], axis=1).reshape(shard, 6, members, cols)
    away = take(cut, group * 2 + 1 - core, 2).reshape(shard, 6 * cols)
    mine = take(cut, member, 2).reshape(shard, 6 * cols)
    w_sel = gather_outer(in_order(core, mine, swap(away))).reshape(width, 6 * cols)

    vectors = (
        query_bias, value_bias, out_bias, up_bias, down_bias,
        norm1_gain, norm1_shift, norm2_gain, norm2_shift,
    )
    sizes = [v.shape[0] for v in vectors]
    packed = jnp.concatenate(vectors)
    packed = lax.all_gather(packed, ("outer", "core"), axis=0, tiled=False)
    offsets = [sum(sizes[:i]) for i in range(len(sizes) + 1)]
    (b_query, b_value, b_out, b_up, b_down, g_one, s_one, g_two, s_two) = (
        packed[:, a:b].reshape(-1).astype(F32) for a, b in zip(offsets[:-1], offsets[1:])
    )
    b_six = jnp.concatenate([b_query, jnp.zeros((width,), F32), b_value])
    b_sel = take(b_six.reshape(6, members, cols), member, 1).reshape(1, 6 * cols)

    att, inv_stored, wts = None, None, None
    att, wts, inv_stored, qcat, kcat, vneg = attention_forward(
        all_rows, w_sel, b_sel, ent, qseg, kseg, heads, head_dim
    )

    def fetch(values):
        return gather_outer(in_order(core, values, swap(values))).reshape(-1, values.shape[1])

    w_out, w_up, w_down = fetch(out_weight), fetch(up_weight), fetch(down_weight)

    def heads_to_tokens(values):
        got = exchange_members(values.reshape(members, own, cols))
        return got.transpose(1, 0, 2).reshape(own, width)

    def tokens_to_heads(values):
        parts = values.reshape(own, members, cols).transpose(1, 0, 2)
        return exchange_members(parts).reshape(full, cols)

    attended = heads_to_tokens(att)
    attn_out = matmul(attended, w_out) + b_out
    hidden, normed_one, inv_one = normalize(own_rows.astype(F32) + attn_out, g_one, s_one)
    hidden_low = hidden.astype(BF)
    up_proj = matmul(hidden_low, w_up) + b_up
    gelu_out, gelu_pull = jax.vjp(lambda v: jax.nn.gelu(v, approximate=False), up_proj)
    act_low = gelu_out.astype(BF)
    ffn_out = matmul(act_low, w_down) + b_down
    result, normed_two, inv_two = normalize(hidden + ffn_out, g_two, s_two)
    output = from_row(result.astype(BF))

    cot = to_row(cotangent).astype(F32)
    grad_y2, grad_g2, grad_s2 = normalize_back(cot, normed_two, inv_two, g_two)
    grad_ffn = grad_y2.astype(BF)
    grad_act = times_transposed(grad_ffn, w_down)
    grad_up = gelu_pull(grad_act)[0].astype(BF)
    grad_hidden = grad_y2 + times_transposed(grad_up, w_up)
    grad_y1, grad_g1, grad_s1 = normalize_back(grad_hidden, normed_one, inv_one, g_one)
    grad_attn = grad_y1.astype(BF)
    grad_attended = times_transposed(grad_attn, w_out).astype(BF)

    def pick_rows(left, core_index, outer_index):
        parts = left.reshape(left.shape[0], outer, 2, -1)
        if outer_index is None:
            return take(parts, core_index, 2).reshape(left.shape[0], -1)
        return take(take(parts, core_index, 2), outer_index, 1)

    def reduce_outer(partial):
        if outer == 2:
            me = lax.axis_index("outer")
            other = lax.ppermute(take(partial, 1 - me, 0).astype(BF), "outer", [(0, 1), (1, 0)])
            return take(partial, me, 0).astype(F32) + other.astype(F32)
        return lax.psum_scatter(partial.astype(BF), "outer", scatter_dimension=0, tiled=False).astype(F32)

    def shard_grad(left, right):
        away = rows_inner(pick_rows(left, 1 - core, None), right).astype(BF)
        mine = rows_inner(pick_rows(left, core, None), right)
        pair = mine + swap(away).astype(F32)
        part = reduce_outer(pair.reshape(outer, -1, right.shape[1]))
        return lax.psum(part.astype(BF), ("row", "group")).astype(F32)

    g_w_down = shard_grad(act_low, grad_ffn)
    g_w_up = shard_grad(hidden_low, grad_up)
    g_w_out = shard_grad(attended, grad_attn)

    gq, gkv = attention_backward(
        tokens_to_heads(grad_attended), att, inv_stored, wts, qcat, kcat, vneg, ent, heads, head_dim
    )
    g_six = jnp.concatenate([gq, gkv], axis=1)
    g_sel = reduce_outer(rows_inner(all_rows, g_six).reshape(outer, -1, 6 * cols))
    g_sel = lax.psum(g_sel.astype(BF), "row").reshape(2, shard, 6, cols)
    got = in_order(core, take(g_sel, core, 0), swap(take(g_sel, 1 - core, 0)))
    if per_row > 1:
        got = lax.all_gather(got, "group", axis=0, tiled=False)
    got = got.reshape(members, shard, 6, cols).transpose(1, 2, 0, 3).reshape(shard, 6 * width)
    g_w_query = got[:, : 4 * width].astype(F32)
    g_w_kv = got[:, 4 * width :].astype(F32)

    part_in = times_transposed(g_six, w_sel)
    got_in = exchange_members(part_in.astype(BF).reshape(members, own, width))
    grad_in = grad_y1 + jnp.sum(got_in.astype(F32), axis=0)
    input_grad = from_row(grad_in.astype(BF))

    six_sum = column_sum(g_six).reshape(6, 1, cols)
    spot = lax.broadcasted_iota(jnp.int32, (1, members, 1), 1) == member
    six_sum = jnp.where(spot, six_sum, 0.0).reshape(6, width)
    small = [
        six_sum[:4].reshape(-1), six_sum[5], column_sum(grad_attn), column_sum(grad_up),
        column_sum(grad_ffn), grad_g1, grad_s1, grad_g2, grad_s2,
    ]
    total = lax.psum(jnp.concatenate(small), ("row", "group", "outer", "core"))
    me = lax.axis_index("outer") * 2 + core
    pieces, at = [], 0
    for size in sizes:
        whole_size = size * outer * 2
        pieces.append(lax.dynamic_slice_in_dim(total[at : at + whole_size], me * size, size))
        at += whole_size
    return (output, input_grad, g_w_query, g_w_kv, g_w_out, g_w_up, g_w_down, *pieces)


def project_kernel(
    heads, hd, query_rows, kv_rows, at_ref, ends_ref, own_ref, other_ref, vec_ref, types_ref, *refs
):
    n_query, n_kv = len(query_rows), len(kv_rows)
    query_refs, kv_refs = refs[:n_query], refs[n_query : n_query + n_kv]
    qcat_ref, kcat_ref, vaug_ref, w_ref, ent_ref, qseg_ref, kseg_ref, kinds_s, bias_s, sems = refs[n_query + n_kv :]
    span = heads * hd
    half, width = own_ref.shape
    block = min(256, half)
    scale = hd ** (-0.5)
    core = at_ref[0]
    made = []
    for i, (ref, rows) in enumerate(zip(query_refs + kv_refs, query_rows + kv_rows)):
        first, blocks = (0, 4) if i < n_query else (4, 2)
        to = pl.ds(pl.multiple_of(at_ref[1 + i], 16), rows)
        for b in range(blocks):
            here = pl.ds(pl.multiple_of(b * width + core * span, LANES), span)
            cols = slice((first + b) * span, (first + b + 1) * span)
            copy = pltpu.make_async_copy(ref.at[:, here], w_ref.at[to, cols], sems.at[len(made)])
            copy.start()
            made.append(copy)
    row = lambda c, o, r: vec_ref[c, o, r : r + 1, :].astype(F32)
    for b in range(4):
        pair = [jnp.where(core == 0, row(b % 2, b // 2, i), row(b % 2, b // 2, 2 + i)) for i in range(2)]
        bias_s[:, b * span : (b + 1) * span] = jnp.concatenate(pair, axis=1)
    bias_s[:, 4 * span : 5 * span] = jnp.zeros((1, span), F32)
    bias_s[:, 5 * span :] = jnp.concatenate([row(i, core, 4) for i in range(2)], axis=1)
    chunks, wide = types_ref.shape
    part = wide // 2
    kinds_s[:, :chunks] = jnp.where(types_ref[...] > 0, 1.0, 0.0).T
    for side in range(2):
        kind = core if side == 0 else 1 - core
        column = kinds_s[pl.ds(pl.multiple_of(kind * part, part), part), :]
        for chunk in range(chunks):
            at = side * half + chunk * part
            ent_ref[at : at + part, :] = jnp.broadcast_to(column[:, chunk : chunk + 1], (part, LANES)).astype(BF)
            place = chunk * wide + kind * part + lax.broadcasted_iota(jnp.int32, (part, LANES), 0)
            lanes = lax.broadcasted_iota(jnp.int32, (part, LANES), 1)
            seg = sum((place >= ends_ref[d]).astype(jnp.int32) for d in range(ends_ref.shape[0]))
            same = lanes == seg
            qseg_ref[at : at + part, :] = jnp.where(same, 1.0, 0.0).astype(BF)
            kseg_ref[at : at + part, :] = jnp.where(same | (lanes >= ends_ref.shape[0]), 0.0, BLOCKED).astype(BF)
    lane = lax.broadcasted_iota(jnp.int32, (block, LANES - hd), 1)
    tail = jnp.where(lane < 2, -1.0, jnp.where(lane == 2, 1.0, 0.0)).astype(BF)
    for copy in made:
        copy.wait()
    for side, rows_ref in enumerate((own_ref, other_ref)):

        def project(piece, carry, side=side, rows_ref=rows_ref):
            rows = rows_ref[pl.ds(pl.multiple_of(piece * block, block), block), :]
            at = pl.ds(pl.multiple_of(side * half + piece * block, block), block)
            ent = ent_ref[at, :hd]
            wide = ent_ref[at, :1] > 0
            word = (1 - ent).astype(BF)

            def part(index):
                cols = slice(index * span, (index + 1) * span)
                return jnp.dot(rows, w_ref[:, cols], preferred_element_type=F32) + bias_s[:, cols]

            q_word = (jnp.where(wide, part(2), part(0))).astype(BF) * BF(scale)
            q_ent = (jnp.where(wide, part(3), part(1))).astype(BF) * BF(scale)
            keys = part(4).astype(BF)
            vals = part(5).astype(BF)
            for h in range(heads):
                cut = slice(h * hd, (h + 1) * hd)
                qcat_ref[h, at, :] = jnp.concatenate([q_word[:, cut], q_ent[:, cut]], axis=1)
                kcat_ref[h, at, :] = jnp.concatenate([keys[:, cut] * word, keys[:, cut] * ent], axis=1)
                vaug_ref[h, at, :] = jnp.concatenate([vals[:, cut], tail], axis=1)
            return carry

        lax.fori_loop(0, half // block, project, 0)


def row_project(at, ends, own, other, vec, types, query_pieces, kv_pieces, heads, hd):
    half, width = own.shape
    full = 2 * half
    span = heads * hd
    vmem = pl.BlockSpec(memory_space=pltpu.VMEM)
    smem = pl.BlockSpec(memory_space=pltpu.SMEM)
    anywhere = pl.BlockSpec(memory_space=pl.ANY)
    query_rows = tuple(p.shape[0] for p in query_pieces)
    kv_rows = tuple(p.shape[0] for p in kv_pieces)
    shapes = [
        (heads, full, 2 * hd), (heads, full, 2 * hd), (heads, full, LANES), (width, 6 * span),
        (full, LANES), (full, LANES), (full, LANES),
    ]
    return pl.pallas_call(
        functools.partial(project_kernel, heads, hd, query_rows, kv_rows),
        in_specs=[smem, smem] + [vmem] * 4 + [anywhere] * (len(query_pieces) + len(kv_pieces)),
        out_specs=[vmem] * len(shapes),
        out_shape=[jax.ShapeDtypeStruct(s, BF) for s in shapes],
        scratch_shapes=[
            pltpu.VMEM((types.shape[1], LANES), F32),
            pltpu.VMEM((1, 6 * span), F32),
            pltpu.SemaphoreType.DMA((4 * len(query_pieces) + 2 * len(kv_pieces),)),
        ],
        compiler_params=pltpu.CompilerParams(vmem_limit_bytes=60 << 20),
        cost_estimate=pl.CostEstimate(
            flops=2 * full * width * 6 * span, bytes_accessed=18 * full * width, transcendentals=0
        ),
        name="row_project",
    )(at, ends, own, other, vec, types, *query_pieces, *kv_pieces)


def attend_kernel(
    heads, hd, qcat_ref, qseg_ref, kcat_ref, kseg_ref, vaug_ref, keep_ref, send_ref, wts_ref, inv_ref, score_s
):
    step = pl.program_id(0)
    block = keep_ref.shape[0]
    q_seg = qseg_ref[...]
    lane = lax.broadcasted_iota(jnp.int32, (block, LANES), 1)
    inv_all = jnp.zeros((block, LANES), F32)
    mixed = []
    for h in range(heads):
        q_aug = jnp.concatenate([qcat_ref[h], q_seg], axis=1)
        k_aug = jnp.concatenate([kcat_ref[h], kseg_ref[...]], axis=1)
        score_s[h % 2] = lax.dot_general(
            q_aug, k_aug, (((1,), (1,)), ((), ())), preferred_element_type=F32
        )
        for r in range(0, block, CHUNK):
            s = score_s[h % 2, r : r + CHUNK, :]
            top = jnp.max(s, axis=1, keepdims=True)
            wts_ref[h, r : r + CHUNK, :] = jnp.exp(s - top).astype(BF)
        out = jnp.dot(wts_ref[h], vaug_ref[h], preferred_element_type=F32)
        inv = 1.0 / out[:, hd + 2 : hd + 3]
        inv_all = jnp.where(lane == h, inv, inv_all)
        mixed.append((out[:, :hd] * inv).astype(BF))
    mixed = jnp.concatenate(mixed, axis=1)
    inv_ref[...] = inv_all
    late = pl.num_programs(0) // 2

    @pl.when(step < late)
    def _():
        send_ref[...] = mixed

    @pl.when(step >= late)
    def _():
        keep_ref[...] = mixed


def row_attend(qcat, kcat, vaug, qseg, kseg, heads, hd):
    full = qcat.shape[1]
    half = full // 2
    block = min(256, half)
    span = heads * hd
    first = half // block
    whole = lambda *dims: pl.BlockSpec(dims, lambda i: (0,) * len(dims))
    turn = lambda i: jnp.where(i < first, i + first, i - first)
    return pl.pallas_call(
        functools.partial(attend_kernel, heads, hd),
        grid=(full // block,),
        in_specs=[
            pl.BlockSpec((heads, block, 2 * hd), lambda i: (0, turn(i), 0)),
            pl.BlockSpec((block, LANES), lambda i: (turn(i), 0)),
            whole(heads, full, 2 * hd),
            whole(full, LANES),
            whole(heads, full, LANES),
        ],
        out_specs=[
            pl.BlockSpec((block, span), lambda i: (jnp.maximum(i - first, 0), 0)),
            pl.BlockSpec((block, span), lambda i: (jnp.minimum(i, first - 1), 0)),
            pl.BlockSpec((heads, block, full), lambda i: (0, turn(i), 0)),
            pl.BlockSpec((block, LANES), lambda i: (turn(i), 0)),
        ],
        out_shape=[
            jax.ShapeDtypeStruct((half, span), BF),
            jax.ShapeDtypeStruct((half, span), BF),
            jax.ShapeDtypeStruct((heads, full, full), BF),
            jax.ShapeDtypeStruct((full, LANES), F32),
        ],
        scratch_shapes=[pltpu.VMEM((2, block, full), F32)],
        compiler_params=pltpu.CompilerParams(vmem_limit_bytes=60 << 20),
        cost_estimate=pl.CostEstimate(
            flops=8 * heads * full * full * LANES,
            bytes_accessed=2 * heads * full * full + 4 * full * LANES * heads,
            transcendentals=heads * full * full,
        ),
        name="row_attend",
    )(qcat, qseg, kcat, kseg, vaug)


def token_kernel(
    out_rows, up_rows, down_rows, at_ref, own_ref, mine_ref, theirs_ref, cot_ref, vec_ref, *refs
):
    groups = (out_rows, up_rows, down_rows)
    sets, at = [], 0
    for rows in groups:
        sets.append(refs[at : at + len(rows)])
        at += len(rows)
    (
        result_ref, gy1_ref, gmine_ref, gtheirs_ref, act_out, hlow_out, gffn_out, gup_out, gattn_ref,
        small_ref, act_ref, hlow_ref, gffn_ref, gup_ref, leave, wout_s, wup_s, wdown_s, acc_s, hid_s, norm_s, inv_s, slope_s, gy2_s, tmp_s, sum_s, vec_s, sems,
    ) = refs[at:]
    total, width = own_ref.shape
    ff = wup_s.shape[1]
    parts = ff // width
    span = mine_ref.shape[1]
    core = at_ref[0]
    made, slot = [], 0
    for rows, piece_refs, dst in zip(groups, sets, (wout_s, wup_s, wdown_s)):
        batch = []
        for n, ref in zip(rows, piece_refs):
            to = pl.ds(pl.multiple_of(at_ref[1 + slot], 16), n)
            copy = pltpu.make_async_copy(ref, dst.at[to, :], sems.at[slot])
            copy.start()
            batch.append(copy)
            slot += 1
        made.append(batch)

    def wait(index):
        for copy in made[index]:
            copy.wait()

    leaving = []

    def send_out(src, dst):
        copy = pltpu.make_async_copy(src, dst, leave.at[len(leaving)])
        copy.start()
        leaving.append(copy)

    def whole_vector(r):
        return jnp.concatenate([vec_ref[f % 2, f // 2, r : r + 1, :] for f in range(4)], axis=1).astype(F32)

    for c in range(parts):
        up_bias = [vec_ref[c % 2, c // 2, 6 + i : 7 + i, :] for i in range(4)]
        vec_s[c : c + 1, :] = jnp.concatenate(up_bias, axis=1).astype(F32)
    for i, r in enumerate((5, 10, 11, 12, 13, 14)):
        vec_s[4 + i : 5 + i, :] = whole_vector(r)

    def row(index):
        return vec_s[index : index + 1, :]

    rows_at = lambda i, n: pl.ds(pl.multiple_of(i * n, n), n)
    chunk = 16
    mine_rows = pl.ds(pl.multiple_of(core * span, LANES), span)
    other_rows = pl.ds(pl.multiple_of((1 - core) * span, LANES), span)
    sum_s[...] = jnp.zeros_like(sum_s)
    wait(0)
    acc_s[...] = jnp.dot(mine_ref[...], wout_s[mine_rows, :], preferred_element_type=F32)
    acc_s[...] += jnp.dot(theirs_ref[...], wout_s[other_rows, :], preferred_element_type=F32)

    def first_norm(i, carry):
        at = rows_at(i, chunk)
        y = own_ref[at, :].astype(F32) + (acc_s[at, :] + row(4))
        center = y - jnp.mean(y, axis=1, keepdims=True)
        inv = lax.rsqrt(jnp.mean(center * center, axis=1, keepdims=True) + EPSILON)
        normed = center * inv
        hidden = normed * row(6) + row(7)
        norm_s[at, :] = normed
        inv_s[at, :] = jnp.broadcast_to(inv, (chunk, LANES))
        hid_s[at, :] = hidden
        hlow_ref[at, :] = hidden.astype(BF)
        return carry

    lax.fori_loop(0, total // chunk, first_norm, 0, unroll=4)
    send_out(hlow_ref, hlow_out)
    wait(1)
    for c in range(parts):
        cols = slice(c * width, (c + 1) * width)
        tmp_s[c % 2] = jnp.dot(hlow_ref[...], wup_s[:, cols], preferred_element_type=F32)
        for r in range(0, total, chunk):
            x = tmp_s[c % 2, r : r + chunk, :] + row(c)
            cdf = 0.5 + 0.5 * lax.erf(x * (0.5**0.5))
            act_ref[r : r + chunk, cols] = (x * cdf).astype(BF)
            slope_s[r : r + chunk, cols] = cdf + x * (jnp.exp(-0.5 * x * x) * (0.15915494309189535**0.5))
    send_out(act_ref, act_out)
    wait(2)
    acc_s[...] = jnp.dot(act_ref[...], wdown_s[...], preferred_element_type=F32)

    def second_norm(i, carry):
        at = rows_at(i, chunk)
        y = hid_s[at, :] + (acc_s[at, :] + row(5))
        center = y - jnp.mean(y, axis=1, keepdims=True)
        inv = lax.rsqrt(jnp.mean(center * center, axis=1, keepdims=True) + EPSILON)
        normed = center * inv
        result_ref[at, :] = (normed * row(8) + row(9)).astype(BF)
        cot = cot_ref[at, :].astype(F32)
        sum_s[2] += cot * normed
        sum_s[3] += cot
        scaled = cot * row(8)
        g = inv * (
            scaled
            - jnp.mean(scaled, axis=1, keepdims=True)
            - normed * jnp.mean(scaled * normed, axis=1, keepdims=True)
        )
        gy2_s[at, :] = g
        gffn_ref[at, :] = g.astype(BF)
        return carry

    lax.fori_loop(0, total // chunk, second_norm, 0, unroll=2)
    send_out(gffn_ref, gffn_out)
    ones = jnp.ones((8, total), BF)
    ups = []
    for c in range(parts):
        cols = slice(c * width, (c + 1) * width)
        tmp_s[c % 2] = lax.dot_general(
            gffn_ref[...], wdown_s[cols, :], (((1,), (1,)), ((), ())), preferred_element_type=F32
        )
        for r in range(0, total, chunk):
            gup_ref[r : r + chunk, cols] = (
                tmp_s[c % 2, r : r + chunk, :] * slope_s[r : r + chunk, cols]
            ).astype(BF)
        ups.append(jnp.dot(ones, gup_ref[:, cols], preferred_element_type=F32)[:1])
    send_out(gup_ref, gup_out)
    acc_s[...] = lax.dot_general(
        gup_ref[...], wup_s[...], (((1,), (1,)), ((), ())), preferred_element_type=F32
    )

    def first_back(i, carry):
        at = rows_at(i, chunk)
        g_in = gy2_s[at, :] + acc_s[at, :]
        normed = norm_s[at, :]
        sum_s[0] += g_in * normed
        sum_s[1] += g_in
        scaled = g_in * row(6)
        g = inv_s[at, :1] * (
            scaled
            - jnp.mean(scaled, axis=1, keepdims=True)
            - normed * jnp.mean(scaled * normed, axis=1, keepdims=True)
        )
        gy1_ref[at, :] = g
        gattn_ref[at, :] = g.astype(BF)
        return carry

    lax.fori_loop(0, total // chunk, first_back, 0, unroll=2)
    gmine_ref[...] = lax.dot_general(
        gattn_ref[...], wout_s[mine_rows, :], (((1,), (1,)), ((), ())), preferred_element_type=F32
    ).astype(BF)
    gtheirs_ref[...] = lax.dot_general(
        gattn_ref[...], wout_s[other_rows, :], (((1,), (1,)), ((), ())), preferred_element_type=F32
    ).astype(BF)
    sums = [jnp.dot(ones, ref[...], preferred_element_type=F32)[:1] for ref in (gattn_ref, gffn_ref)]
    sums += [jnp.sum(sum_s[i], axis=0, keepdims=True) for i in range(4)]
    n = width // 4
    half = width // 2
    for shard in range(4):
        at = 8 * shard
        cut = slice(shard * n, (shard + 1) * n)
        for i in range(2):
            small_ref[at + i : at + i + 1, :] = ups[shard][:, i * half : (i + 1) * half]
        for i in range(3):
            small_ref[at + 2 + i : at + 3 + i, :] = jnp.concatenate(
                [sums[2 * i][:, cut], sums[2 * i + 1][:, cut]], axis=1
            )
        small_ref[at + 5 : at + 8, :] = jnp.zeros((3, half), F32)
    for copy in leaving:
        copy.wait()


def token_block(at, own, mine, theirs, cot, vec, out_pieces, up_pieces, down_pieces):
    total, width = own.shape
    span = mine.shape[1]
    ff = up_pieces[0].shape[1]
    vmem = pl.BlockSpec(memory_space=pltpu.VMEM)
    pieces = [*out_pieces, *up_pieces, *down_pieces]
    shapes = [
        ((total, width), BF), ((total, width), F32), ((total, span), BF), ((total, span), BF),
        ((total, ff), BF), ((total, width), BF), ((total, width), BF), ((total, ff), BF),
        ((total, width), BF), ((32, width // 2), F32),
    ]
    rows = lambda group: tuple(p.shape[0] for p in group)
    return pl.pallas_call(
        functools.partial(token_kernel, rows(out_pieces), rows(up_pieces), rows(down_pieces)),
        in_specs=[pl.BlockSpec(memory_space=pltpu.SMEM)]
        + [vmem] * 5
        + [pl.BlockSpec(memory_space=pl.ANY)] * len(pieces),
        out_specs=[pl.BlockSpec(memory_space=pl.ANY) if 4 <= i < 8 else vmem for i in range(len(shapes))],
        out_shape=[jax.ShapeDtypeStruct(s, d) for s, d in shapes],
        scratch_shapes=[
            *[pltpu.VMEM(shape, BF) for shape, _ in shapes[4:8]],
            pltpu.SemaphoreType.DMA((4,)),
            pltpu.VMEM((width, width), BF),
            pltpu.VMEM((width, ff), BF),
            pltpu.VMEM((ff, width), BF),
            pltpu.VMEM((total, width), F32),
            pltpu.VMEM((total, width), F32),
            pltpu.VMEM((total, width), F32),
            pltpu.VMEM((total, LANES), F32),
            pltpu.VMEM((total, ff), F32),
            pltpu.VMEM((total, width), F32),
            pltpu.VMEM((2, total, width), F32),
            pltpu.VMEM((4, 16, width), F32),
            pltpu.VMEM((16, width), F32),
            pltpu.SemaphoreType.DMA((len(pieces),)),
        ],
        compiler_params=pltpu.CompilerParams(vmem_limit_bytes=60 << 20),
        cost_estimate=pl.CostEstimate(
            flops=2 * total * width * (4 * ff + 2 * width),
            bytes_accessed=4 * width * ff + 6 * total * ff,
            transcendentals=2 * total * ff,
        ),
        name="token_block",
    )(at, own, mine, theirs, cot, vec, *pieces)


def turned(core, outer, near, z):
    pick = lambda a, b: jnp.where(core == 0, a, b)
    return pick(outer, near), pick(z, outer), pick(near, z)


def place_of(owner, index, relative, b, c):
    first = index if relative else 1 - index
    return (first, c, b) if owner == 0 else (b, first, c)


def up_pieces(owner, index, n, span, hid_t, gup_ref, emit):
    for relative in range(2):
        for b in range(2):
            for c in range(2):
                outer, near, z = place_of(owner, index, relative, b, c)
                left = hid_t[pl.ds(pl.multiple_of((2 * outer + owner) * n, 16), n), :]
                for far in range(2):
                    cols = pl.ds(pl.multiple_of((near * 4 + z * 2 + far) * span, LANES), span)
                    emit((relative, b, c, far), jnp.dot(left, gup_ref[:, cols], preferred_element_type=F32))


def rest_pieces(owner, index, n, wide, span, att_t, act_ref, gffn_ref, gattn_ref, small_ref, emit):
    half = wide // 2
    for relative in range(2):
        for b in range(2):
            outer = place_of(owner, index, relative, b, 0)[0]
            shard = 2 * outer + owner
            small = small_ref[pl.ds(pl.multiple_of(shard * 8, 8), 8), :]
            for c in range(2):
                _, near, z = place_of(owner, index, relative, b, c)
                cols = pl.ds(pl.multiple_of(shard * wide + near * half, LANES), half)
                if owner == 0:
                    if b:
                        continue
                    rows, marks = act_ref[:, cols], [((relative, zz, c), zz) for zz in range(2)]
                else:
                    if c:
                        continue
                    rows, marks = act_ref[:, cols], [((relative, b, zz), zz) for zz in range(2)]
                down = lax.dot_general(rows, gffn_ref[...], (((0,), (0,)), ((), ())), preferred_element_type=F32)
                for mark, zz in marks:
                    at = pl.ds(pl.multiple_of(shard * n + (near * 2 + zz) * (n // 4), 16), n // 4)
                    out = jnp.dot(att_t[at, :], gattn_ref[...], preferred_element_type=F32)
                    for far in range(2):
                        cut = slice(far * span, (far + 1) * span)
                        head = (near == 0) if zz == 0 and far == 0 else False
                        emit(
                            (*mark, far),
                            down[zz * half // 2 : (zz + 1) * half // 2, cut],
                            out[:, cut],
                            jnp.where(head, small, 0.0),
                        )


def fetch(sems, *pairs):
    made = [pltpu.make_async_copy(src, dst, sems.at[i]) for i, (src, dst) in enumerate(pairs)]
    for copy in made:
        copy.start()
    return made


def up_send_kernel(at_ref, hlow_ref, gup_ref, send_ref, hid_t):
    width = hlow_ref.shape[1]
    n, span = width // 4, gup_ref.shape[1] // 8
    hid_t[...] = hlow_ref[...].T

    def emit(at, value):
        send_ref[at] = value.astype(BF)

    for owner in range(2):

        @pl.when(at_ref[0] == 1 - owner)
        def _(owner=owner):
            up_pieces(owner, at_ref[1 + owner], n, span, hid_t, gup_ref, emit)


def fill_att(at_ref, mine_ref, theirs_ref, att_t):
    span = mine_ref.shape[1]
    core = at_ref[0]
    att_t[pl.ds(pl.multiple_of(core * span, LANES), span), :] = mine_ref[...].T
    att_t[pl.ds(pl.multiple_of((1 - core) * span, LANES), span), :] = theirs_ref[...].T


def rest_send_kernel(at_ref, mine_ref, theirs_ref, act_ref, gffn_ref, gattn_ref, small_ref, send_ref, att_t):
    width = gffn_ref.shape[1]
    n, wide, span = width // 4, act_ref.shape[1] // 4, mine_ref.shape[1]
    fill_att(at_ref, mine_ref, theirs_ref, att_t)

    def emit(at, down, out, small):
        send_ref[(*at, slice(0, wide // 4))] = down.astype(BF)
        send_ref[(*at, slice(wide // 4, wide // 4 + n // 4))] = out.astype(BF)
        send_ref[(*at, slice(wide // 4 + n // 4, None))] = small.astype(BF)

    for owner in range(2):

        @pl.when(at_ref[0] == 1 - owner)
        def _(owner=owner):
            rest_pieces(
                owner, at_ref[1 + owner], n, wide, span, att_t, act_ref, gffn_ref, gattn_ref, small_ref, emit
            )


def keep_kernel(
    at_ref, mine_ref, theirs_ref, hlow_ref, gffn_ref, gattn_ref, small_ref, gup_hbm, up_hbm, act_hbm, rest_hbm,
    away_ref, kept_ref, hid_t, att_t, gup_ref, up_ref, act_ref, rest_ref, sems,
):
    width = gffn_ref.shape[1]
    n, wide, span = width // 4, act_ref.shape[1] // 4, mine_ref.shape[1]
    m = n + wide // 4
    come = fetch(sems, (gup_hbm, gup_ref), (up_hbm, up_ref), (act_hbm, act_ref), (rest_hbm, rest_ref))
    hid_t[...] = hlow_ref[...].T
    fill_att(at_ref, mine_ref, theirs_ref, att_t)
    for copy in come[:2]:
        copy.wait()

    def put(at, rows, value, got_ref, got):
        out_ref = kept_ref if at[0] else away_ref
        out_ref[(*at[1:], rows)] = (value + got_ref[(*at, got)].astype(F32)).astype(BF)

    def emit_up(at, value):
        put(at, slice(0, n), value, up_ref, slice(None))

    def emit(at, down, out, small):
        put(at, slice(n, m), down, rest_ref, slice(0, wide // 4))
        put(at, slice(m, m + n // 4), out, rest_ref, slice(wide // 4, wide // 4 + n // 4))
        put(at, slice(m + n // 4, None), small, rest_ref, slice(wide // 4 + n // 4, None))

    for owner in range(2):

        @pl.when(at_ref[0] == owner)
        def _(owner=owner):
            index = at_ref[1 + owner]
            up_pieces(owner, index, n, span, hid_t, gup_ref, emit_up)

    for copy in come[2:]:
        copy.wait()
    for owner in range(2):

        @pl.when(at_ref[0] == owner)
        def _(owner=owner):
            index = at_ref[1 + owner]
            rest_pieces(owner, index, n, wide, span, att_t, act_ref, gffn_ref, gattn_ref, small_ref, emit)


def grads_call(kernel, name, at, arrays, fetched, shapes, transposed, flops):
    vmem = pl.BlockSpec(memory_space=pltpu.VMEM)
    anywhere = pl.BlockSpec(memory_space=pl.ANY)
    return pl.pallas_call(
        kernel,
        in_specs=[pl.BlockSpec(memory_space=pltpu.SMEM)] + [vmem] * len(arrays) + [anywhere] * len(fetched),
        out_specs=[vmem] * len(shapes),
        out_shape=[jax.ShapeDtypeStruct(s, BF) for s in shapes],
        scratch_shapes=[pltpu.VMEM(t, BF) for t in transposed]
        + [pltpu.VMEM(f.shape, BF) for f in fetched]
        + [pltpu.SemaphoreType.DMA((len(fetched),))] * bool(fetched),
        compiler_params=pltpu.CompilerParams(vmem_limit_bytes=60 << 20),
        cost_estimate=pl.CostEstimate(
            flops=flops, bytes_accessed=2 * sum(a.size for a in (*arrays, *fetched)), transcendentals=0
        ),
        name=name,
    )(at, *arrays, *fetched)


def row_backward_kernel(
    heads, hd, first_head, gmine_ref, gother_ref, keep_ref, send_ref, inv_ref, wts_ref, qcat_ref, kcat_ref,
    vaug_ref, ent_ref, entb_ref, *refs,
):
    gq_ref, gkv_ref, gscore_s, low_s, gk_s, gv_s = refs[-6:]
    step = pl.program_id(0)
    block = gmine_ref.shape[0]
    full = kcat_ref.shape[1]
    scale = hd ** (-0.5)
    lane = lax.broadcasted_iota(jnp.int32, (block, LANES - hd), 1)
    is_ent = entb_ref[:, :1] > 0
    early = step < pl.num_programs(0) // 2
    g_all = jnp.where(early, gmine_ref[...], gother_ref[...])
    att_all = jnp.where(early, keep_ref[...], send_ref[...])
    g_word, g_ent = [], []
    for h in range(heads):
        cut = slice(h * hd, (h + 1) * hd)
        g_low = (g_all[:, cut].astype(F32) * inv_ref[:, first_head + h : first_head + h + 1]).astype(BF)
        delta = jnp.sum(g_low.astype(F32) * att_all[:, cut].astype(F32), axis=1, keepdims=True)
        d_hi = delta.astype(BF)
        d_lo = (delta - d_hi.astype(F32)).astype(BF)
        extra = jnp.where(
            lane == 0, d_hi.astype(F32), jnp.where(lane == 1, d_lo.astype(F32), 0.0)
        ).astype(BF)
        g_aug = jnp.concatenate([g_low, extra], axis=1)
        gscore_s[h % 2] = lax.dot_general(
            g_aug, vaug_ref[h], (((1,), (1,)), ((), ())), preferred_element_type=F32
        )
        for r in range(0, block, CHUNK):
            low_s[h % 2, r : r + CHUNK, :] = (
                wts_ref[h, r : r + CHUNK, :].astype(F32) * gscore_s[h % 2, r : r + CHUNK, :]
            ).astype(BF)
        g_q = jnp.dot(low_s[h % 2], kcat_ref[h], preferred_element_type=F32) * scale
        g_word.append(g_q[:, :hd])
        g_ent.append(g_q[:, hd:])
        g_k = lax.dot_general(
            qcat_ref[h], low_s[h % 2], (((0,), (0,)), ((), ())), preferred_element_type=F32
        )
        g_v = lax.dot_general(
            g_low, wts_ref[h], (((0,), (0,)), ((), ())), preferred_element_type=F32
        )

        @pl.when(step == 0)
        def _(h=h, g_k=g_k, g_v=g_v):
            gk_s[h] = g_k
            gv_s[h] = g_v

        @pl.when(step > 0)
        def _(h=h, g_k=g_k, g_v=g_v):
            gk_s[h] += g_k
            gv_s[h] += g_v

    g_word = jnp.concatenate(g_word, axis=1)
    g_ent = jnp.concatenate(g_ent, axis=1)
    gq_ref[0] = jnp.where(is_ent, 0.0, g_word).astype(BF)
    gq_ref[1] = jnp.where(is_ent, 0.0, g_ent).astype(BF)
    gq_ref[2] = jnp.where(is_ent, g_word, 0.0).astype(BF)
    gq_ref[3] = jnp.where(is_ent, g_ent, 0.0).astype(BF)

    @pl.when(step == pl.num_programs(0) - 1)
    def _():
        def close(piece, carry):
            at = pl.ds(pl.multiple_of(piece * block, block), block)
            pick = ent_ref[at, :1] > 0
            g_keys, g_vals = [], []
            for h in range(heads):
                both = gk_s[h, :, at].T
                g_keys.append(jnp.where(pick, both[:, hd:], both[:, :hd]))
                g_vals.append(gv_s[h, :, at].T)
            gkv_ref[0, at, :] = jnp.concatenate(g_keys, axis=1).astype(BF)
            gkv_ref[1, at, :] = jnp.concatenate(g_vals, axis=1).astype(BF)
            return carry

        lax.fori_loop(0, full // block, close, 0)


def row_backward(first_head, heads, grads, gmine, gother, keep, send, inv, wts, qcat, kcat, vaug, ent, hd):
    half, all_cols = keep.shape
    full = 2 * half
    block = min(256, half)
    first = half // block
    cols = heads * hd
    g, c = first_head // heads, first_head * hd // cols
    by_rows = pl.BlockSpec((block, LANES), lambda i: (i, 0))
    by_head = lambda width: pl.BlockSpec((heads, block, width), lambda i: (g, i, 0))
    of_head = lambda width: pl.BlockSpec((heads, full, width), lambda i: (g, 0, 0))
    low = pl.BlockSpec((block, cols), lambda i: (jnp.minimum(i, first - 1), c))
    high = pl.BlockSpec((block, cols), lambda i: (jnp.maximum(i - first, 0), c))
    given = [] if grads is None else list(grads)
    return pl.pallas_call(
        functools.partial(row_backward_kernel, heads, hd, first_head),
        grid=(full // block,),
        in_specs=[
            low, high, low, high,
            by_rows,
            by_head(full),
            by_head(2 * hd),
            of_head(2 * hd),
            of_head(LANES),
            pl.BlockSpec((full, LANES), lambda i: (0, 0)),
            by_rows,
        ]
        + [pl.BlockSpec(memory_space=pl.ANY)] * len(given),
        out_specs=[
            pl.BlockSpec((4, block, cols), lambda i: (0, i, c)),
            pl.BlockSpec((2, full, cols), lambda i: (0, 0, c)),
        ],
        out_shape=[
            jax.ShapeDtypeStruct((4, full, all_cols), BF),
            jax.ShapeDtypeStruct((2, full, all_cols), BF),
        ],
        scratch_shapes=[
            pltpu.VMEM((2, block, full), F32),
            pltpu.VMEM((2, block, full), BF),
            pltpu.VMEM((heads, 2 * hd, full), F32),
            pltpu.VMEM((heads, hd, full), F32),
        ],
        input_output_aliases={11 + i: i for i in range(len(given))},
        compiler_params=pltpu.CompilerParams(vmem_limit_bytes=60 << 20),
        cost_estimate=pl.CostEstimate(
            flops=16 * heads * full * full * LANES,
            bytes_accessed=2 * heads * full * full + 20 * full * cols,
            transcendentals=0,
        ),
        name="row_backward",
    )(gmine, gother, keep, send, inv, wts, qcat, kcat, vaug, ent, ent, *given)


def qkv_grad_kernel(
    at_ref, own_ref, other_ref, gq_hbm, gkv_hbm, send_ref, keep_ref, rows_t, gq_ref, gkv_ref, sems
):
    half, width = own_ref.shape
    n = width // 16
    span = gq_ref.shape[2]
    core, index = at_ref[0], at_ref[1]
    come = fetch(sems, (gq_hbm, gq_ref), (gkv_hbm, gkv_ref))
    rows_t[:, :half] = own_ref[...].T
    rows_t[:, half:] = other_ref[...].T
    for copy in come:
        copy.wait()

    def write(out_ref, at, start, count):
        left = rows_t[pl.ds(pl.multiple_of(start, 16), count * n), :]
        for b in range(6):
            right = gq_ref[b] if b < 4 else gkv_ref[b - 4]
            piece = jnp.dot(left, right, preferred_element_type=F32).astype(BF)
            for p in range(count):
                out_ref[(*at(p), slice(b * n, (b + 1) * n))] = piece[p * n : (p + 1) * n, :]

    ones = jnp.ones((8, 2 * half), BF)
    sums = [
        jnp.dot(ones, gq_ref[b] if b < 4 else gkv_ref[b - 4], preferred_element_type=F32)[:1] for b in range(6)
    ]

    def write_sums(out_ref, at, outer, near, on_core):
        query = jnp.where(outer == 0, jnp.where(near == 0, sums[0], sums[1]), jnp.where(near == 0, sums[2], sums[3]))
        value = jnp.where(outer == on_core, sums[5], 0.0)
        rows = jnp.concatenate([query, value, jnp.zeros((6, span), F32)], axis=0)
        out_ref[(*at, slice(6 * n, None))] = rows.astype(BF)

    for which, out_ref in ((1 - index, send_ref), (index, keep_ref)):

        @pl.when(core == 0)
        def _(which=which, out_ref=out_ref):
            write(out_ref, lambda p: (p // 2 % 2, p // 4, p % 2), which * 8 * n, 8)
            for p in range(8):
                at = (p // 2 % 2, p // 4, p % 2)
                write_sums(out_ref, at, which, p // 4, 0)

        @pl.when(core == 1)
        def _(which=which, out_ref=out_ref):
            for o in range(2):
                write(out_ref, lambda p, o=o: (o, p // 2, p % 2), o * 8 * n + which * 4 * n, 4)
                for p in range(4):
                    write_sums(out_ref, (o, p // 2, p % 2), o, which, 1)


def qkv_grad(at, own, other, gq, gkv):
    half, width = own.shape
    span = gkv.shape[2]
    n = width // 16
    vmem = pl.BlockSpec(memory_space=pltpu.VMEM)
    return pl.pallas_call(
        qkv_grad_kernel,
        in_specs=[pl.BlockSpec(memory_space=pltpu.SMEM)]
        + [vmem] * 2
        + [pl.BlockSpec(memory_space=pl.ANY)] * 2,
        out_specs=[vmem] * 2,
        out_shape=[jax.ShapeDtypeStruct((2, 2, 2, 6 * n + 8, span), BF)] * 2,
        scratch_shapes=[
            pltpu.VMEM((width, 2 * half), BF),
            pltpu.VMEM(gq.shape, BF),
            pltpu.VMEM(gkv.shape, BF),
            pltpu.SemaphoreType.DMA((2,)),
        ],
        compiler_params=pltpu.CompilerParams(vmem_limit_bytes=60 << 20),
        cost_estimate=pl.CostEstimate(
            flops=24 * half * width * span, bytes_accessed=32 * half * span, transcendentals=0
        ),
        name="qkv_grad",
    )(at, own, other, gq, gkv)


def input_grad_kernel(gq_ref, gkv_ref, w_ref, gy1_ref, mine_ref, away_ref):
    span = gkv_ref.shape[2]
    total = None
    for b in range(6):
        left = gq_ref[b] if b < 4 else gkv_ref[b - 4]
        part = lax.dot_general(
            left, w_ref[:, b * span : (b + 1) * span], (((1,), (1,)), ((), ())), preferred_element_type=F32
        )
        total = part if total is None else total + part
    early = pl.program_id(0) < pl.num_programs(0) // 2

    @pl.when(early)
    def _():
        away_ref[...] = total.astype(BF)

    @pl.when(jnp.logical_not(early))
    def _():
        mine_ref[...] = gy1_ref[...] + total


def row_input_grad(gq, gkv, w, gy1):
    half, width = gy1.shape
    span = gkv.shape[2]
    block = min(256, half)
    first = half // block
    turn = lambda i: jnp.where(i < first, i + first, i - first)
    late = pl.BlockSpec((block, width), lambda i: (jnp.maximum(i - first, 0), 0))
    return pl.pallas_call(
        input_grad_kernel,
        grid=(2 * first,),
        in_specs=[
            pl.BlockSpec((4, block, span), lambda i: (0, turn(i), 0)),
            pl.BlockSpec((2, block, span), lambda i: (0, turn(i), 0)),
            pl.BlockSpec((width, 6 * span), lambda i: (0, 0)),
            late,
        ],
        out_specs=[late, pl.BlockSpec((block, width), lambda i: (jnp.minimum(i, first - 1), 0))],
        out_shape=[jax.ShapeDtypeStruct((half, width), F32), jax.ShapeDtypeStruct((half, width), BF)],
        compiler_params=pltpu.CompilerParams(vmem_limit_bytes=60 << 20),
        cost_estimate=pl.CostEstimate(
            flops=4 * half * width * 6 * span, bytes_accessed=20 * half * width, transcendentals=0
        ),
        name="row_input_grad",
    )(gq, gkv, w, gy1)


def lay_rest_kernel(at_ref, mine_ref, other_ref, up_ref, down_ref, out_ref, small_ref):
    span = mine_ref.shape[2]
    k, n, m = up_ref.shape[0], down_ref.shape[0] // 4, out_ref.shape[0] // 4
    core, index = at_ref[0], at_ref[1]
    last = slice(k + n + m, None)
    small_ref[...] = jnp.where(index == 0, mine_ref[0, last, :].astype(F32), other_ref[0, last, :].astype(F32))
    for a, ref in ((index, mine_ref), (1 - index, other_ref)):
        for b in range(2):
            pair = jnp.where(core == 0, b * 2 + a, a * 2 + b)
            for far in range(2):
                j = b * 2 + far
                cols = pl.ds(pl.multiple_of((pair * 2 + far) * span, LANES), span)
                up_ref[:, cols] = ref[j, :k, :].astype(F32)
                cols = slice(far * span, (far + 1) * span)
                down_ref[pl.ds(pl.multiple_of(pair * n, 8), n), cols] = ref[j, k : k + n, :].astype(F32)
                out_ref[pl.ds(pl.multiple_of(pair * m, 8), m), cols] = ref[j, k + n : k + n + m, :].astype(F32)


def lay_qkv_kernel(at_ref, keep_ref, got_ref, query_ref, kv_ref, small_ref):
    span = keep_ref.shape[2]
    n = (keep_ref.shape[1] - 8) // 6
    last = slice(6 * n, None)
    for half, src in ((at_ref[0], keep_ref), (1 - at_ref[0], got_ref)):
        small_ref[half] = src[0, last, :].astype(F32)
        for b in range(6):
            ref, i = (query_ref, b) if b < 4 else (kv_ref, b - 4)
            cols = pl.ds(pl.multiple_of(i * 2 * span + half * span, LANES), span)
            for j in range(4):
                ref[j * n : (j + 1) * n, cols] = src[j, b * n : (b + 1) * n, :].astype(F32)


def lay(kernel, name, at, arrays, shapes):
    vmem = pl.BlockSpec(memory_space=pltpu.VMEM)
    return pl.pallas_call(
        kernel,
        in_specs=[pl.BlockSpec(memory_space=pltpu.SMEM)] + [vmem] * len(arrays),
        out_specs=[vmem] * len(shapes),
        out_shape=[jax.ShapeDtypeStruct(s, F32) for s in shapes],
        compiler_params=pltpu.CompilerParams(vmem_limit_bytes=60 << 20),
        cost_estimate=pl.CostEstimate(
            flops=0, bytes_accessed=6 * sum(a.size for a in arrays), transcendentals=0
        ),
        name=name,
    )(at, *arrays)


def row_layer(
    inputs, query_weight, kv_weight, out_weight, up_weight, down_weight,
    query_bias, value_bias, out_bias, up_bias, down_bias,
    norm1_gain, norm1_shift, norm2_gain, norm2_shift, types, lengths, cotangent,
):
    rows_here, span, width = inputs.shape
    hd = width // HEADS
    full = types.shape[1]
    heads = HEADS // 2
    cols = heads * hd
    row_count = lax.axis_size("row")
    core, outer, row_id = (lax.axis_index(n) for n in ("core", "outer", "row"))
    place = [row_id // bit % 2 for bit in (1, 2, 4)]
    near = place[0]
    own_count = full // 2
    both_ways = [(0, 1), (1, 0)]

    def after(values, *others):
        return lax.optimization_barrier((values, *others))[0]

    def swap(values):
        return lax.ppermute(values, "core", both_ways)

    def cross(values):
        return lax.ppermute(values, "outer", both_ways)

    def pair_up(values, bit):
        return lax.ppermute(values, "row", [(i, i ^ bit) for i in range(row_count)])

    def in_order(index, mine, other, axis=0):
        first, second = jnp.where(index == 0, mine, other), jnp.where(index == 0, other, mine)
        return jnp.stack([first, second], axis=axis)

    def take(values, index, axis=0):
        return lax.dynamic_index_in_dim(values, index, axis, keepdims=False)

    def halves_of_rows(values):
        pieces = values.reshape(rows_here, 2, span // 2, width)
        other = swap(take(pieces, 1 - core, 1))
        return in_order(core, take(pieces, core, 1), other).reshape(row_count, span // 2, width)

    def over_rows(values):
        return lax.all_to_all(values, "row", 0, 0, tiled=True)

    def rows_whole(back):
        back = back.reshape(2, rows_here, span // 2, width)
        other = swap(take(back, 1 - core))
        both = in_order(core, take(back, core), other)
        return both.transpose(1, 0, 2, 3).reshape(rows_here, span, width)

    shard = query_weight.shape[0]
    wide = down_weight.shape[0]

    def near_half(values):
        return take(values.reshape(2, values.shape[0] // 2, values.shape[1]), near)

    f_own, f_core = 2 * outer + core, 2 * outer + 1 - core
    f_cross, f_both = 2 * (1 - outer) + core, 2 * (1 - outer) + 1 - core

    q_got = cross(near_half(query_weight))
    to_rows = halves_of_rows(inputs)
    own_rows = over_rows(to_rows).reshape(own_count, width)
    query_own, kv_own, types, lengths, query_bias = lax.optimization_barrier(
        (query_weight, kv_weight, types, lengths, query_bias, to_rows)
    )[:5]
    q_core, kv_core = swap(query_own), swap(kv_own)
    q_passed, kv_got = pair_up(q_got, 1), cross(after(kv_weight, q_got))
    q_got2 = swap(after(q_got, q_core, kv_core))
    own_rows, q_passed = lax.optimization_barrier((own_rows, q_passed))
    other_rows = swap(own_rows)
    q_passed2, kv_got2 = swap(q_passed), swap(kv_got)
    cot_halves = halves_of_rows(after(cotangent, own_rows))
    query_pieces = [query_weight, q_core, q_got, q_passed, q_got2, q_passed2]
    kv_pieces = [kv_weight, kv_core, kv_got, kv_got2]
    part = shard // 2
    query_at = [
        f_own * shard, f_core * shard,
        f_cross * shard + near * part, f_cross * shard + (1 - near) * part,
        f_both * shard + near * part, f_both * shard + (1 - near) * part,
    ]
    kv_at = [f_own * shard, f_core * shard, f_cross * shard, f_both * shard]
    at_qkv = jnp.stack([core, *query_at, *kv_at]).astype(jnp.int32)

    tags = jnp.concatenate([types, lengths], axis=1)
    tags_other = after(swap(tags), q_got2)
    tags = take(in_order(core, tags, tags_other).reshape(row_count, -1), row_id)
    types_row, lengths_row = tags[:full].reshape(row_count, span), tags[full:]
    docs = lengths_row.shape[0]
    ends = jnp.sum(jnp.where(jnp.arange(docs)[:, None] >= jnp.arange(docs)[None], lengths_row[None], 0), axis=1)

    vectors = (
        query_bias, value_bias, out_bias, up_bias, down_bias,
        norm1_gain, norm1_shift, norm2_gain, norm2_shift,
    )
    packed = jnp.concatenate(vectors)
    packed = in_order(outer, packed, cross(packed))
    vec = in_order(core, packed, swap(packed)).reshape(2, 2, -1, shard)

    qcat, kcat, vaug, w_sel, ent, qseg, kseg = row_project(
        at_qkv, ends, own_rows, other_rows, vec, types_row, query_pieces, kv_pieces, heads, hd
    )

    low_rows = down_weight[: wide // 2]
    u_got = cross(after(near_half(up_weight), kv_got))
    d_got = cross(after(near_half(low_rows), kv_got))
    late_out, late_up, late_down = lax.optimization_barrier((out_weight, up_weight, down_weight, kv_got2))[:3]
    o_core, u_core, d_core = swap(late_out), swap(late_up), swap(late_down)
    u_mid, d_mid, m_out, m_down, o_core, u_core, d_core = lax.optimization_barrier(
        (u_got, d_got, out_weight, down_weight, o_core, u_core, d_core, kcat)
    )[:7]
    u_passed, d_passed = pair_up(u_mid, 1), pair_up(d_mid, 1)
    o_got, t_got = cross(m_out), cross(m_down[wide // 2 :])
    u_got2, d_got2 = swap(u_mid), swap(d_mid)
    cot = over_rows(after(cot_halves, other_rows)).reshape(own_count, width)
    keep, send, wts, inv = row_attend(qcat, kcat, vaug, qseg, kseg, heads, hd)
    theirs = swap(send)
    u_passed2, d_passed2, o_got2, t_got2 = (
        swap(v) for v in lax.optimization_barrier((u_passed, d_passed, o_got, t_got, keep))[:4]
    )
    out_pieces = [out_weight, o_core, o_got, o_got2]
    out_at = [f * shard for f in (f_own, f_core, f_cross, f_both)]
    up_pieces = [up_weight, u_core, u_got, u_passed, u_got2, u_passed2]
    down_pieces = [down_weight, d_core, d_got, d_passed, t_got, d_got2, d_passed2, t_got2]
    quarter = wide // 4
    down_at = [
        f_own * wide, f_core * wide,
        f_cross * wide + near * quarter, f_cross * wide + (1 - near) * quarter, f_cross * wide + 2 * quarter,
        f_both * wide + near * quarter, f_both * wide + (1 - near) * quarter, f_both * wide + 2 * quarter,
    ]
    at_rest = jnp.stack([core, *out_at, *query_at, *down_at]).astype(jnp.int32)

    (
        result, gy1, gmine, gtheirs, act, hlow, gffn, gup, gattn, small
    ) = token_block(at_rest, own_rows, keep, theirs, cot, vec, out_pieces, up_pieces, down_pieces)
    gother = swap(gtheirs)
    at_core = core.astype(jnp.int32).reshape(1)
    at_near = near.astype(jnp.int32).reshape(1)
    at_grads = jnp.stack([core, outer, near]).astype(jnp.int32)
    m, ff = width // 16, up_weight.shape[1]
    bits = (2, 2, 2)
    tall = (2, *bits, ff // 16 + m + 8, cols)
    (rest_send,) = grads_call(
        rest_send_kernel, "rest_send", at_grads, [keep, theirs, act, gffn, gattn, small], [], [tall],
        [(width, own_count)], own_count * width * (ff + width),
    )
    hlow, gup, gother, rest_send = lax.optimization_barrier((hlow, gup, gother, rest_send))
    (up_send,) = grads_call(
        up_send_kernel, "up_send", at_grads, [hlow, gup], [], [(2, *bits, shard, cols)],
        [(width, own_count)], own_count * width * ff,
    )

    def add(*arrays):
        return functools.reduce(jnp.add, [v.astype(F32) for v in arrays]).astype(BF)

    def by_core(a, b):
        return jnp.where(core == 0, a, b)

    stages = {
        "s1": ("outer", "y"), "s2": ("z", "outer"), "s3": ("y", "z"), "far": ("far", "far"), "g1": ("z", "y"),
        "t1": ("z", "y"), "t2": ("y", "z"), "t3": ("far", "far"),
    }
    index_on = {"outer": outer, "y": near, "z": place[1], "far": place[2]}
    index_of = {name: by_core(index_on[a], index_on[b]) for name, (a, b) in stages.items()}
    every = ("row", "outer", "core")

    def pairs_of(stage):
        found = []
        for r in range(row_count):
            for o in range(2):
                for c in range(2):
                    axis = stages[stage][c]
                    to = (r, 1 - o) if axis == "outer" else (r ^ {"y": 1, "z": 2, "far": 4}[axis], o)
                    found.append(((r * 2 + o) * 2 + c, (to[0] * 2 + to[1]) * 2 + c))
        return found

    def send_over(values, stage):
        return lax.ppermute(values, every, pairs_of(stage))

    axis_at = {"far": 0, "z": 1, "y": 2}

    def trade(values, stage):
        away, mine = (
            by_core(*(take(values, i, axis_at[axis]) for axis in stages[stage]))
            for i in (1 - index_of[stage], index_of[stage])
        )
        token[0] = away
        return mine, send_over(away, stage)

    def traded(state, stage):
        mine, other = in_turn(*state)
        token[0] = other
        return by_core(*(in_order(index_of[stage], mine, other, axis_at[axis]) for axis in stages[stage]))

    def by_rows(values):
        return values.reshape(2, 2, 2, span // 2, width)

    token = [gother]

    def in_turn(*arrays):
        return lax.optimization_barrier((*arrays, token[0]))[: len(arrays)]

    def halve(state, axis):
        mine, other = in_turn(*state)
        away, mine = (
            add(take(mine, i), take(other, i)) for i in (1 - index_of[axis], index_of[axis])
        )
        token[0] = away
        return mine, send_over(away, axis)

    def start_spread(state, axis):
        total = add(*in_turn(*state))
        token[0] = total
        return total, send_over(total, axis)

    def spread(state, have, axis):
        total = in_order(index_of[have], *in_turn(*state))
        token[0] = total
        return total, send_over(total, axis)

    out_rows = trade(by_rows(result), "t1")
    away, mine = grads_call(
        keep_kernel, "keep_grads", at_grads,
        [keep, theirs, hlow, gffn, gattn, small], [gup, swap(up_send), act, swap(rest_send)],
        [(*bits, shard + tall[-2], cols)] * 2, [(width, own_count)] * 2, own_count * width * (2 * ff + width),
    )
    rest = (mine, send_over(away, "s1"))
    token[0] = away
    out_rows = trade(traded(out_rows, "t1"), "t2")
    gmine, _ = lax.optimization_barrier((gmine, token[0]))
    gq, gkv = row_backward(
        0, heads, None, gmine, gother, keep, send, inv, wts, qcat, kcat, vaug, ent, hd
    )
    n = width // 16
    token[0] = gkv
    out_rows = trade(traded(out_rows, "t2"), "t3")
    rest = halve(rest, "s2")
    at_first = jnp.stack([core, index_of["s1"]]).astype(jnp.int32)
    q_send, q_keep = qkv_grad(at_first, own_rows, after(other_rows, token[0]), gq, gkv)
    six = (q_keep, send_over(q_send, "s1"))
    token[0] = q_send
    out_rows = traded(out_rows, "t3")
    in_mine, in_away = row_input_grad(gq, gkv, after(w_sel, token[0]), gy1)
    in_other = swap(in_away)
    token[0] = in_away
    rest = halve(rest, "s3")
    in_mine, in_other = in_turn(in_mine, in_other)
    grad_in = (in_mine + in_other.astype(F32)).astype(BF)
    in_rows = trade(by_rows(grad_in), "t1")
    six = halve(six, "s2")
    rest = halve(rest, "far")
    in_rows = trade(traded(in_rows, "t1"), "t2")
    six = halve(six, "s3")
    rest = start_spread(rest, "far")
    six = halve(six, "far")
    rest = spread(rest, "far", "s3")
    six = start_spread(six, "far")
    in_rows = trade(traded(in_rows, "t2"), "t3")
    rest = spread(rest, "s3", "g1")
    six = spread(six, "far", "s3")
    in_rows = traded(in_rows, "t3")
    output, input_grad = rows_whole(out_rows), rows_whole(in_rows)
    six = spread(six, "s3", "g1")
    at_last = jnp.stack([core, index_of["g1"]]).astype(jnp.int32)
    g_up, g_down, g_out, small = lay(
        lay_rest_kernel, "lay_rest", at_last, [v.reshape(4, *v.shape[2:]) for v in in_turn(*rest)],
        [up_weight.shape, down_weight.shape, out_weight.shape, (8, cols)],
    )
    token[0] = g_out
    six = in_order(index_of["g1"], *in_turn(*six))
    away, kept = by_core(six[:, 1], six[0]), by_core(six[:, 0], six[1])
    parts = [v.reshape(4, *v.shape[2:]) for v in (kept, swap(away))]
    g_query, g_kv, halves = lay(
        lay_qkv_kernel, "lay_qkv", at_core, parts, [query_weight.shape, kv_weight.shape, (2, 8, cols)]
    )
    pairs = small[2:5].reshape(6, shard)
    value = take(halves[:, 1].sum(axis=0).reshape(2, shard), core)
    return (
        output, input_grad, g_query, g_kv, g_out, g_up, g_down,
        halves[:, 0].reshape(-1), value, pairs[0], small[:2].reshape(-1), *(pairs[i] for i in range(1, 6)),
    )


def solution(mesh):
    def step(*args):
        ctx, fsdp = mesh.shape["ctx"], mesh.shape["fsdp"]
        row_count = args[0].shape[0] // (fsdp // 2)
        per_row = ctx // row_count
        fine = Mesh(
            mesh.devices.reshape(row_count, per_row, fsdp // 2, 2), ("row", "group", "outer", "core")
        )
        tokens = P(("outer", "core"), ("row", "group"), None)
        mat, vec = P(("outer", "core"), None), P(("outer", "core"))
        in_specs = (tokens, *[mat] * 5, *[vec] * 9, mat, mat, tokens)
        out_specs = (tokens, tokens, *[mat] * 5, *[vec] * 9)
        quarter = args[0].shape[2] // 4
        fits = per_row == 1 and fsdp == 4 and row_count == 8 and args[0].shape[2] % (2 * LANES) == 0 and quarter % 32 == 0
        body = row_layer if fits else functools.partial(layer, None, per_row)
        return jax.shard_map(
            body, mesh=fine, in_specs=in_specs, out_specs=out_specs, check_vma=False
        )(*args)

    return step
```

```python
import functools

import jax
import jax.numpy as jnp
from jax import lax
from jax.experimental import pallas as pl
from jax.experimental.pallas import tpu as pltpu
from jax.sharding import Mesh
from jax.sharding import PartitionSpec as P

HEADS = 12
EPSILON = 1e-05
BLOCKED = -1e30
BF = jnp.bfloat16
F32 = jnp.float32
LANES = 128
CHUNK = 16


def matmul(left_mat, right_mat):
    return jnp.dot(left_mat, right_mat, preferred_element_type=F32)


def rows_inner(left_mat, right_mat):
    return lax.dot_general(left_mat, right_mat, (((0,), (0,)), ((), ())), preferred_element_type=F32)


def times_transposed(left_mat, right_mat):
    return lax.dot_general(left_mat, right_mat, (((1,), (1,)), ((), ())), preferred_element_type=F32)


def normalize(values, gain_vec, shift_vec):
    center = values - jnp.mean(values, axis=-1, keepdims=True)
    scale_inv = lax.rsqrt(jnp.mean(center * center, axis=-1, keepdims=True) + EPSILON)
    normed = center * scale_inv
    return (normed * gain_vec + shift_vec, normed, scale_inv)


def normalize_back(grad_in, normed, scale_inv, gain_vec):
    scaled = grad_in * gain_vec
    inner_part = (
        scaled
        - jnp.mean(scaled, axis=-1, keepdims=True)
        - normed * jnp.mean(scaled * normed, axis=-1, keepdims=True)
    )
    return (inner_part * scale_inv, jnp.sum(grad_in * normed, axis=0), jnp.sum(grad_in, axis=0))


def column_sum(values):
    return jnp.sum(values.astype(F32), axis=0)


def forward_kernel(
    heads, hd, rows_ref, w_ref, bias_ref, ent_ref, qseg_ref, kseg_ref,
    att_ref, wts_ref, inv_ref, qcat_ref, kcat_ref, vneg_ref,
    kaug_s, vaug_s, score_s,
):
    step = pl.program_id(0)
    span = heads * hd
    full = rows_ref.shape[0]
    block = att_ref.shape[0]
    scale = hd ** (-0.5)

    @pl.when(step == 0)
    def _():
        kaug_s[:, :, LANES:] = jnp.broadcast_to(kseg_ref[...][None], (heads, full, LANES))
        lane = lax.broadcasted_iota(jnp.int32, (block, LANES - hd), 1)
        one_col = jnp.where(lane == 0, 1.0, 0.0).astype(BF)
        neg_col = jnp.where(lane < 2, -1.0, 0.0).astype(BF)

        def project(piece, carry):
            at = pl.ds(pl.multiple_of(piece * block, block), block)
            rows = rows_ref[at, :]
            ent = ent_ref[at, :hd]
            wide = ent_ref[at, :1] > 0
            word = (1 - ent).astype(BF)

            def part(index):
                cols = slice(index * span, (index + 1) * span)
                return jnp.dot(rows, w_ref[:, cols], preferred_element_type=F32) + bias_ref[:, cols]

            q_word = (jnp.where(wide, part(2), part(0))).astype(BF) * BF(scale)
            q_ent = (jnp.where(wide, part(3), part(1))).astype(BF) * BF(scale)
            keys = part(4).astype(BF)
            vals = part(5).astype(BF)
            for h in range(heads):
                cut = slice(h * hd, (h + 1) * hd)
                qcat_ref[h, at, :] = jnp.concatenate([q_word[:, cut], q_ent[:, cut]], axis=1)
                k_pair = jnp.concatenate([keys[:, cut] * word, keys[:, cut] * ent], axis=1)
                kcat_ref[h, at, :] = k_pair
                kaug_s[h, at, :LANES] = k_pair
                vneg_ref[h, at, :] = jnp.concatenate([vals[:, cut], neg_col], axis=1)
                vaug_s[h, at, :] = jnp.concatenate([vals[:, cut], one_col], axis=1)
            return carry

        lax.fori_loop(0, full // block, project, 0)

    here = pl.ds(pl.multiple_of(step * block, block), block)
    q_seg = qseg_ref[here, :]
    lane = lax.broadcasted_iota(jnp.int32, (block, LANES), 1)
    inv_all = jnp.zeros((block, LANES), F32)
    mixed = []
    for h in range(heads):
        q_aug = jnp.concatenate([qcat_ref[h, here, :], q_seg], axis=1)
        score_s[h % 2] = lax.dot_general(
            q_aug, kaug_s[h], (((1,), (1,)), ((), ())), preferred_element_type=F32
        )
        for r in range(0, block, CHUNK):
            s = score_s[h % 2, r : r + CHUNK, :]
            top = jnp.max(s, axis=1, keepdims=True)
            wts_ref[h, r : r + CHUNK, :] = jnp.exp(s - top).astype(BF)
        out = jnp.dot(wts_ref[h], vaug_s[h], preferred_element_type=F32)
        inv = 1.0 / out[:, hd : hd + 1]
        inv_all = jnp.where(lane == h, inv, inv_all)
        mixed.append((out[:, :hd] * inv).astype(BF))
    att_ref[...] = jnp.concatenate(mixed, axis=1)
    inv_ref[...] = inv_all


def attention_forward(rows, w_sel, bias_sel, ent, qseg, kseg, heads, hd):
    full, width = rows.shape
    block = min(256, full)
    span = heads * hd
    steps = full // block
    whole = lambda *dims: pl.BlockSpec(dims, lambda i: (0,) * len(dims))
    return pl.pallas_call(
        functools.partial(forward_kernel, heads, hd),
        grid=(steps,),
        in_specs=[
            whole(full, width),
            whole(width, 6 * span),
            whole(1, 6 * span),
            whole(full, LANES),
            whole(full, LANES),
            whole(full, LANES),
        ],
        out_specs=[
            pl.BlockSpec((block, span), lambda i: (i, 0)),
            pl.BlockSpec((heads, block, full), lambda i: (0, i, 0)),
            pl.BlockSpec((block, LANES), lambda i: (i, 0)),
            whole(heads, full, 2 * hd),
            whole(heads, full, 2 * hd),
            whole(heads, full, LANES),
        ],
        out_shape=[
            jax.ShapeDtypeStruct((full, span), BF),
            jax.ShapeDtypeStruct((heads, full, full), BF),
            jax.ShapeDtypeStruct((full, LANES), F32),
            jax.ShapeDtypeStruct((heads, full, 2 * hd), BF),
            jax.ShapeDtypeStruct((heads, full, 2 * hd), BF),
            jax.ShapeDtypeStruct((heads, full, LANES), BF),
        ],
        scratch_shapes=[
            pltpu.VMEM((heads, full, 2 * LANES), BF),
            pltpu.VMEM((heads, full, LANES), BF),
            pltpu.VMEM((2, block, full), F32),
        ],
        compiler_params=pltpu.CompilerParams(vmem_limit_bytes=60 << 20),
        cost_estimate=pl.CostEstimate(
            flops=2 * full * width * 6 * span + 8 * heads * full * full * LANES,
            bytes_accessed=2 * heads * full * full + 10 * full * width,
            transcendentals=heads * full * full,
        ),
        name="attention_forward",
    )(rows, w_sel, bias_sel, ent, qseg, kseg)


def backward_kernel(
    heads, hd, go_ref, att_ref, inv_ref, wts_ref, qcat_ref, kcat_ref, vneg_ref, ent_ref, entb_ref,
    gq_ref, gkv_ref, gscore_s, low_s, gk_s, gv_s,
):
    step = pl.program_id(0)
    span = heads * hd
    block = go_ref.shape[0]
    full = kcat_ref.shape[1]
    scale = hd ** (-0.5)
    lane = lax.broadcasted_iota(jnp.int32, (block, LANES - hd), 1)
    is_ent = entb_ref[:, :1] > 0
    g_word, g_ent = [], []
    for h in range(heads):
        cut = slice(h * hd, (h + 1) * hd)
        g_low = (go_ref[:, cut].astype(F32) * inv_ref[:, h : h + 1]).astype(BF)
        delta = jnp.sum(g_low.astype(F32) * att_ref[:, cut].astype(F32), axis=1, keepdims=True)
        d_hi = delta.astype(BF)
        d_lo = (delta - d_hi.astype(F32)).astype(BF)
        extra = jnp.where(
            lane == 0, d_hi.astype(F32), jnp.where(lane == 1, d_lo.astype(F32), 0.0)
        ).astype(BF)
        g_aug = jnp.concatenate([g_low, extra], axis=1)
        gscore_s[h % 2] = lax.dot_general(
            g_aug, vneg_ref[h], (((1,), (1,)), ((), ())), preferred_element_type=F32
        )
        for r in range(0, block, CHUNK):
            low_s[h % 2, r : r + CHUNK, :] = (
                wts_ref[h, r : r + CHUNK, :].astype(F32) * gscore_s[h % 2, r : r + CHUNK, :]
            ).astype(BF)
        g_q = jnp.dot(low_s[h % 2], kcat_ref[h], preferred_element_type=F32) * scale
        g_word.append(g_q[:, :hd])
        g_ent.append(g_q[:, hd:])
        g_k = lax.dot_general(
            qcat_ref[h], low_s[h % 2], (((0,), (0,)), ((), ())), preferred_element_type=F32
        )
        g_v = lax.dot_general(
            g_low, wts_ref[h], (((0,), (0,)), ((), ())), preferred_element_type=F32
        )

        @pl.when(step == 0)
        def _(h=h, g_k=g_k, g_v=g_v):
            gk_s[h] = g_k
            gv_s[h] = g_v

        @pl.when(step > 0)
        def _(h=h, g_k=g_k, g_v=g_v):
            gk_s[h] += g_k
            gv_s[h] += g_v

    g_word = jnp.concatenate(g_word, axis=1)
    g_ent = jnp.concatenate(g_ent, axis=1)
    gq_ref[:, :span] = jnp.where(is_ent, 0.0, g_word).astype(BF)
    gq_ref[:, span : 2 * span] = jnp.where(is_ent, 0.0, g_ent).astype(BF)
    gq_ref[:, 2 * span : 3 * span] = jnp.where(is_ent, g_word, 0.0).astype(BF)
    gq_ref[:, 3 * span :] = jnp.where(is_ent, g_ent, 0.0).astype(BF)

    @pl.when(step == pl.num_programs(0) - 1)
    def _():
        def close(piece, carry):
            at = pl.ds(pl.multiple_of(piece * block, block), block)
            pick = ent_ref[at, :1] > 0
            g_keys, g_vals = [], []
            for h in range(heads):
                both = gk_s[h, :, at].T
                g_keys.append(jnp.where(pick, both[:, hd:], both[:, :hd]))
                g_vals.append(gv_s[h, :, at].T)
            gkv_ref[at, :span] = jnp.concatenate(g_keys, axis=1).astype(BF)
            gkv_ref[at, span:] = jnp.concatenate(g_vals, axis=1).astype(BF)
            return carry

        lax.fori_loop(0, full // block, close, 0)


def attention_backward(g_out, att, inv, wts, qcat, kcat, vneg, ent, heads, hd):
    full, span = att.shape
    block = min(256, full)
    whole = lambda *dims: pl.BlockSpec(dims, lambda i: (0,) * len(dims))
    by_rows = lambda width: pl.BlockSpec((block, width), lambda i: (i, 0))
    by_head = lambda width: pl.BlockSpec((heads, block, width), lambda i: (0, i, 0))
    return pl.pallas_call(
        functools.partial(backward_kernel, heads, hd),
        grid=(full // block,),
        in_specs=[
            by_rows(span),
            by_rows(span),
            by_rows(LANES),
            by_head(full),
            by_head(2 * hd),
            whole(heads, full, 2 * hd),
            whole(heads, full, LANES),
            whole(full, LANES),
            by_rows(LANES),
        ],
        out_specs=[by_rows(4 * span), whole(full, 2 * span)],
        out_shape=[
            jax.ShapeDtypeStruct((full, 4 * span), BF),
            jax.ShapeDtypeStruct((full, 2 * span), BF),
        ],
        scratch_shapes=[
            pltpu.VMEM((2, block, full), F32),
            pltpu.VMEM((2, block, full), BF),
            pltpu.VMEM((heads, 2 * hd, full), F32),
            pltpu.VMEM((heads, hd, full), F32),
        ],
        compiler_params=pltpu.CompilerParams(vmem_limit_bytes=60 << 20),
        cost_estimate=pl.CostEstimate(
            flops=16 * heads * full * full * LANES,
            bytes_accessed=2 * heads * full * full + 20 * full * span,
            transcendentals=0,
        ),
        name="attention_backward",
    )(g_out, att, inv, wts, qcat, kcat, vneg, ent, ent)


def layer(
    half, per_row, inputs, query_weight, kv_weight, out_weight, up_weight, down_weight,
    query_bias, value_bias, out_bias, up_bias, down_bias,
    norm1_gain, norm1_shift, norm2_gain, norm2_shift, types, lengths, cotangent,
):
    rows_here, span, width = inputs.shape
    head_dim = width // HEADS
    full = types.shape[1]
    members = 2 * per_row
    heads = HEADS // members
    cols = heads * head_dim
    row_count = lax.axis_size("row")
    outer = lax.axis_size("outer")
    core = lax.axis_index("core")
    group = lax.axis_index("group")
    member = group * 2 + core
    row_id = lax.axis_index("row")
    own = row_count * (span // 2)

    def swap(values):
        return lax.ppermute(values, "core", [(0, 1), (1, 0)])

    def in_order(index, mine, other):
        return jnp.stack([jnp.where(index == 0, mine, other), jnp.where(index == 0, other, mine)])

    def gather_outer(values):
        if outer == 2:
            other = lax.ppermute(values, "outer", [(0, 1), (1, 0)])
            return in_order(lax.axis_index("outer"), values, other)
        return lax.all_gather(values, "outer", axis=0, tiled=False)

    def gather_members(values):
        pair = in_order(core, values, swap(values))
        if per_row == 1:
            return pair
        spread = lax.all_gather(pair, "group", axis=0, tiled=False)
        return spread.reshape((members,) + values.shape)

    def exchange_members(values):
        if per_row == 1:
            mine = lax.dynamic_index_in_dim(values, core, 0, keepdims=False)
            away = lax.dynamic_index_in_dim(values, 1 - core, 0, keepdims=False)
            return in_order(core, mine, swap(away))
        return lax.all_to_all(values, ("group", "core"), 0, 0, tiled=True)

    def take(values, index, axis):
        return lax.dynamic_index_in_dim(values, index, axis, keepdims=False)

    def to_row(values):
        pieces = values.reshape(rows_here, 2, span // 2, width)
        other = swap(take(pieces, 1 - core, 1))
        both = in_order(core, take(pieces, core, 1), other).reshape(row_count, span // 2, width)
        return lax.all_to_all(both, "row", 0, 0, tiled=True).reshape(own, width)

    def from_row(values):
        back = lax.all_to_all(values.reshape(row_count, span // 2, width), "row", 0, 0, tiled=True)
        back = back.reshape(2, rows_here, span // 2, width)
        other = swap(take(back, 1 - core, 0))
        both = in_order(core, take(back, core, 0), other)
        return both.transpose(1, 0, 2, 3).reshape(rows_here, span, width)

    own_rows = to_row(inputs)
    all_rows = gather_members(own_rows).reshape(full, width)

    tags = jnp.concatenate([types, lengths], axis=1)
    tags = in_order(core, tags, swap(tags)).reshape(row_count, -1)
    tags = take(tags, row_id, 0)
    types_row, lengths_row = tags[:full], tags[full:]

    def by_member(values):
        return values.reshape(row_count, per_row, 2, span // 2).transpose(1, 2, 0, 3).reshape(full)

    entity = by_member(types_row) > 0
    positions = by_member(lax.iota(jnp.int32, full))
    docs = lengths_row.shape[0]
    ends = [jnp.sum(lengths_row[: d + 1]) for d in range(docs)]
    seg = sum((positions >= end).astype(jnp.int32) for end in ends)
    lanes = lax.broadcasted_iota(jnp.int32, (full, LANES), 1)
    same = lanes == seg[:, None]
    qseg = jnp.where(same, 1.0, 0.0).astype(BF)
    kseg = jnp.where(same | (lanes >= docs), 0.0, BLOCKED).astype(BF)
    ent = jnp.broadcast_to(jnp.where(entity, 1.0, 0.0).astype(BF)[:, None], (full, LANES))

    shard = query_weight.shape[0]
    cut = jnp.concatenate([query_weight, kv_weight], axis=1).reshape(shard, 6, members, cols)
    away = take(cut, group * 2 + 1 - core, 2).reshape(shard, 6 * cols)
    mine = take(cut, member, 2).reshape(shard, 6 * cols)
    w_sel = gather_outer(in_order(core, mine, swap(away))).reshape(width, 6 * cols)

    vectors = (
        query_bias, value_bias, out_bias, up_bias, down_bias,
        norm1_gain, norm1_shift, norm2_gain, norm2_shift,
    )
    sizes = [v.shape[0] for v in vectors]
    packed = jnp.concatenate(vectors)
    packed = lax.all_gather(packed, ("outer", "core"), axis=0, tiled=False)
    offsets = [sum(sizes[:i]) for i in range(len(sizes) + 1)]
    (b_query, b_value, b_out, b_up, b_down, g_one, s_one, g_two, s_two) = (
        packed[:, a:b].reshape(-1).astype(F32) for a, b in zip(offsets[:-1], offsets[1:])
    )
    b_six = jnp.concatenate([b_query, jnp.zeros((width,), F32), b_value])
    b_sel = take(b_six.reshape(6, members, cols), member, 1).reshape(1, 6 * cols)

    att, inv_stored, wts = None, None, None
    att, wts, inv_stored, qcat, kcat, vneg = attention_forward(
        all_rows, w_sel, b_sel, ent, qseg, kseg, heads, head_dim
    )

    def fetch(values):
        return gather_outer(in_order(core, values, swap(values))).reshape(-1, values.shape[1])

    w_out, w_up, w_down = fetch(out_weight), fetch(up_weight), fetch(down_weight)

    def heads_to_tokens(values):
        got = exchange_members(values.reshape(members, own, cols))
        return got.transpose(1, 0, 2).reshape(own, width)

    def tokens_to_heads(values):
        parts = values.reshape(own, members, cols).transpose(1, 0, 2)
        return exchange_members(parts).reshape(full, cols)

    attended = heads_to_tokens(att)
    attn_out = matmul(attended, w_out) + b_out
    hidden, normed_one, inv_one = normalize(own_rows.astype(F32) + attn_out, g_one, s_one)
    hidden_low = hidden.astype(BF)
    up_proj = matmul(hidden_low, w_up) + b_up
    gelu_out, gelu_pull = jax.vjp(lambda v: jax.nn.gelu(v, approximate=False), up_proj)
    act_low = gelu_out.astype(BF)
    ffn_out = matmul(act_low, w_down) + b_down
    result, normed_two, inv_two = normalize(hidden + ffn_out, g_two, s_two)
    output = from_row(result.astype(BF))

    cot = to_row(cotangent).astype(F32)
    grad_y2, grad_g2, grad_s2 = normalize_back(cot, normed_two, inv_two, g_two)
    grad_ffn = grad_y2.astype(BF)
    grad_act = times_transposed(grad_ffn, w_down)
    grad_up = gelu_pull(grad_act)[0].astype(BF)
    grad_hidden = grad_y2 + times_transposed(grad_up, w_up)
    grad_y1, grad_g1, grad_s1 = normalize_back(grad_hidden, normed_one, inv_one, g_one)
    grad_attn = grad_y1.astype(BF)
    grad_attended = times_transposed(grad_attn, w_out).astype(BF)

    def pick_rows(left, core_index, outer_index):
        parts = left.reshape(left.shape[0], outer, 2, -1)
        if outer_index is None:
            return take(parts, core_index, 2).reshape(left.shape[0], -1)
        return take(take(parts, core_index, 2), outer_index, 1)

    def reduce_outer(partial):
        if outer == 2:
            me = lax.axis_index("outer")
            other = lax.ppermute(take(partial, 1 - me, 0).astype(BF), "outer", [(0, 1), (1, 0)])
            return take(partial, me, 0).astype(F32) + other.astype(F32)
        return lax.psum_scatter(partial.astype(BF), "outer", scatter_dimension=0, tiled=False).astype(F32)

    def shard_grad(left, right):
        away = rows_inner(pick_rows(left, 1 - core, None), right).astype(BF)
        mine = rows_inner(pick_rows(left, core, None), right)
        pair = mine + swap(away).astype(F32)
        part = reduce_outer(pair.reshape(outer, -1, right.shape[1]))
        return lax.psum(part.astype(BF), ("row", "group")).astype(F32)

    g_w_down = shard_grad(act_low, grad_ffn)
    g_w_up = shard_grad(hidden_low, grad_up)
    g_w_out = shard_grad(attended, grad_attn)

    gq, gkv = attention_backward(
        tokens_to_heads(grad_attended), att, inv_stored, wts, qcat, kcat, vneg, ent, heads, head_dim
    )
    g_six = jnp.concatenate([gq, gkv], axis=1)
    g_sel = reduce_outer(rows_inner(all_rows, g_six).reshape(outer, -1, 6 * cols))
    g_sel = lax.psum(g_sel.astype(BF), "row").reshape(2, shard, 6, cols)
    got = in_order(core, take(g_sel, core, 0), swap(take(g_sel, 1 - core, 0)))
    if per_row > 1:
        got = lax.all_gather(got, "group", axis=0, tiled=False)
    got = got.reshape(members, shard, 6, cols).transpose(1, 2, 0, 3).reshape(shard, 6 * width)
    g_w_query = got[:, : 4 * width].astype(F32)
    g_w_kv = got[:, 4 * width :].astype(F32)

    part_in = times_transposed(g_six, w_sel)
    got_in = exchange_members(part_in.astype(BF).reshape(members, own, width))
    grad_in = grad_y1 + jnp.sum(got_in.astype(F32), axis=0)
    input_grad = from_row(grad_in.astype(BF))

    six_sum = column_sum(g_six).reshape(6, 1, cols)
    spot = lax.broadcasted_iota(jnp.int32, (1, members, 1), 1) == member
    six_sum = jnp.where(spot, six_sum, 0.0).reshape(6, width)
    small = [
        six_sum[:4].reshape(-1), six_sum[5], column_sum(grad_attn), column_sum(grad_up),
        column_sum(grad_ffn), grad_g1, grad_s1, grad_g2, grad_s2,
    ]
    total = lax.psum(jnp.concatenate(small), ("row", "group", "outer", "core"))
    me = lax.axis_index("outer") * 2 + core
    pieces, at = [], 0
    for size in sizes:
        whole_size = size * outer * 2
        pieces.append(lax.dynamic_slice_in_dim(total[at : at + whole_size], me * size, size))
        at += whole_size
    return (output, input_grad, g_w_query, g_w_kv, g_w_out, g_w_up, g_w_down, *pieces)


def project_kernel(
    heads, hd, query_rows, kv_rows, at_ref, ends_ref, own_ref, other_ref, vec_ref, types_ref, *refs
):
    n_query, n_kv = len(query_rows), len(kv_rows)
    query_refs, kv_refs = refs[:n_query], refs[n_query : n_query + n_kv]
    qcat_ref, kcat_ref, vaug_ref, w_ref, ent_ref, qseg_ref, kseg_ref, kinds_s, bias_s, sems = refs[n_query + n_kv :]
    span = heads * hd
    half, width = own_ref.shape
    block = min(256, half)
    scale = hd ** (-0.5)
    core = at_ref[0]
    made = []
    for i, (ref, rows) in enumerate(zip(query_refs + kv_refs, query_rows + kv_rows)):
        first, blocks = (0, 4) if i < n_query else (4, 2)
        to = pl.ds(pl.multiple_of(at_ref[1 + i], 16), rows)
        for b in range(blocks):
            here = pl.ds(pl.multiple_of(b * width + core * span, LANES), span)
            cols = slice((first + b) * span, (first + b + 1) * span)
            copy = pltpu.make_async_copy(ref.at[:, here], w_ref.at[to, cols], sems.at[len(made)])
            copy.start()
            made.append(copy)
    row = lambda c, o, r: vec_ref[c, o, r : r + 1, :].astype(F32)
    for b in range(4):
        pair = [jnp.where(core == 0, row(b % 2, b // 2, i), row(b % 2, b // 2, 2 + i)) for i in range(2)]
        bias_s[:, b * span : (b + 1) * span] = jnp.concatenate(pair, axis=1)
    bias_s[:, 4 * span : 5 * span] = jnp.zeros((1, span), F32)
    bias_s[:, 5 * span :] = jnp.concatenate([row(i, core, 4) for i in range(2)], axis=1)
    chunks, wide = types_ref.shape
    part = wide // 2
    kinds_s[:, :chunks] = jnp.where(types_ref[...] > 0, 1.0, 0.0).T
    for side in range(2):
        kind = core if side == 0 else 1 - core
        column = kinds_s[pl.ds(pl.multiple_of(kind * part, part), part), :]
        for chunk in range(chunks):
            at = side * half + chunk * part
            ent_ref[at : at + part, :] = jnp.broadcast_to(column[:, chunk : chunk + 1], (part, LANES)).astype(BF)
            place = chunk * wide + kind * part + lax.broadcasted_iota(jnp.int32, (part, LANES), 0)
            lanes = lax.broadcasted_iota(jnp.int32, (part, LANES), 1)
            seg = sum((place >= ends_ref[d]).astype(jnp.int32) for d in range(ends_ref.shape[0]))
            same = lanes == seg
            qseg_ref[at : at + part, :] = jnp.where(same, 1.0, 0.0).astype(BF)
            kseg_ref[at : at + part, :] = jnp.where(same | (lanes >= ends_ref.shape[0]), 0.0, BLOCKED).astype(BF)
    lane = lax.broadcasted_iota(jnp.int32, (block, LANES - hd), 1)
    tail = jnp.where(lane < 2, -1.0, jnp.where(lane == 2, 1.0, 0.0)).astype(BF)
    for copy in made:
        copy.wait()
    for side, rows_ref in enumerate((own_ref, other_ref)):

        def project(piece, carry, side=side, rows_ref=rows_ref):
            rows = rows_ref[pl.ds(pl.multiple_of(piece * block, block), block), :]
            at = pl.ds(pl.multiple_of(side * half + piece * block, block), block)
            ent = ent_ref[at, :hd]
            wide = ent_ref[at, :1] > 0
            word = (1 - ent).astype(BF)

            def part(index):
                cols = slice(index * span, (index + 1) * span)
                return jnp.dot(rows, w_ref[:, cols], preferred_element_type=F32) + bias_s[:, cols]

            q_word = (jnp.where(wide, part(2), part(0))).astype(BF) * BF(scale)
            q_ent = (jnp.where(wide, part(3), part(1))).astype(BF) * BF(scale)
            keys = part(4).astype(BF)
            vals = part(5).astype(BF)
            for h in range(heads):
                cut = slice(h * hd, (h + 1) * hd)
                qcat_ref[h, at, :] = jnp.concatenate([q_word[:, cut], q_ent[:, cut]], axis=1)
                kcat_ref[h, at, :] = jnp.concatenate([keys[:, cut] * word, keys[:, cut] * ent], axis=1)
                vaug_ref[h, at, :] = jnp.concatenate([vals[:, cut], tail], axis=1)
            return carry

        lax.fori_loop(0, half // block, project, 0)


def row_project(at, ends, own, other, vec, types, query_pieces, kv_pieces, heads, hd):
    half, width = own.shape
    full = 2 * half
    span = heads * hd
    vmem = pl.BlockSpec(memory_space=pltpu.VMEM)
    smem = pl.BlockSpec(memory_space=pltpu.SMEM)
    anywhere = pl.BlockSpec(memory_space=pl.ANY)
    query_rows = tuple(p.shape[0] for p in query_pieces)
    kv_rows = tuple(p.shape[0] for p in kv_pieces)
    shapes = [
        (heads, full, 2 * hd), (heads, full, 2 * hd), (heads, full, LANES), (width, 6 * span),
        (full, LANES), (full, LANES), (full, LANES),
    ]
    return pl.pallas_call(
        functools.partial(project_kernel, heads, hd, query_rows, kv_rows),
        in_specs=[smem, smem] + [vmem] * 4 + [anywhere] * (len(query_pieces) + len(kv_pieces)),
        out_specs=[vmem] * len(shapes),
        out_shape=[jax.ShapeDtypeStruct(s, BF) for s in shapes],
        scratch_shapes=[
            pltpu.VMEM((types.shape[1], LANES), F32),
            pltpu.VMEM((1, 6 * span), F32),
            pltpu.SemaphoreType.DMA((4 * len(query_pieces) + 2 * len(kv_pieces),)),
        ],
        compiler_params=pltpu.CompilerParams(vmem_limit_bytes=60 << 20),
        cost_estimate=pl.CostEstimate(
            flops=2 * full * width * 6 * span, bytes_accessed=18 * full * width, transcendentals=0
        ),
        name="row_project",
    )(at, ends, own, other, vec, types, *query_pieces, *kv_pieces)


def attend_kernel(
    heads, hd, qcat_ref, qseg_ref, kcat_ref, kseg_ref, vaug_ref, keep_ref, send_ref, wts_ref, inv_ref, score_s
):
    step = pl.program_id(0)
    block = keep_ref.shape[0]
    q_seg = qseg_ref[...]
    lane = lax.broadcasted_iota(jnp.int32, (block, LANES), 1)
    inv_all = jnp.zeros((block, LANES), F32)
    mixed = []
    for h in range(heads):
        q_aug = jnp.concatenate([qcat_ref[h], q_seg], axis=1)
        k_aug = jnp.concatenate([kcat_ref[h], kseg_ref[...]], axis=1)
        score_s[h % 2] = lax.dot_general(
            q_aug, k_aug, (((1,), (1,)), ((), ())), preferred_element_type=F32
        )
        for r in range(0, block, CHUNK):
            s = score_s[h % 2, r : r + CHUNK, :]
            top = jnp.max(s, axis=1, keepdims=True)
            wts_ref[h, r : r + CHUNK, :] = jnp.exp(s - top).astype(BF)
        out = jnp.dot(wts_ref[h], vaug_ref[h], preferred_element_type=F32)
        inv = 1.0 / out[:, hd + 2 : hd + 3]
        inv_all = jnp.where(lane == h, inv, inv_all)
        mixed.append((out[:, :hd] * inv).astype(BF))
    mixed = jnp.concatenate(mixed, axis=1)
    inv_ref[...] = inv_all
    late = pl.num_programs(0) // 2

    @pl.when(step < late)
    def _():
        send_ref[...] = mixed

    @pl.when(step >= late)
    def _():
        keep_ref[...] = mixed


def row_attend(qcat, kcat, vaug, qseg, kseg, heads, hd):
    full = qcat.shape[1]
    half = full // 2
    block = min(256, half)
    span = heads * hd
    first = half // block
    whole = lambda *dims: pl.BlockSpec(dims, lambda i: (0,) * len(dims))
    turn = lambda i: jnp.where(i < first, i + first, i - first)
    return pl.pallas_call(
        functools.partial(attend_kernel, heads, hd),
        grid=(full // block,),
        in_specs=[
            pl.BlockSpec((heads, block, 2 * hd), lambda i: (0, turn(i), 0)),
            pl.BlockSpec((block, LANES), lambda i: (turn(i), 0)),
            whole(heads, full, 2 * hd),
            whole(full, LANES),
            whole(heads, full, LANES),
        ],
        out_specs=[
            pl.BlockSpec((block, span), lambda i: (jnp.maximum(i - first, 0), 0)),
            pl.BlockSpec((block, span), lambda i: (jnp.minimum(i, first - 1), 0)),
            pl.BlockSpec((heads, block, full), lambda i: (0, turn(i), 0)),
            pl.BlockSpec((block, LANES), lambda i: (turn(i), 0)),
        ],
        out_shape=[
            jax.ShapeDtypeStruct((half, span), BF),
            jax.ShapeDtypeStruct((half, span), BF),
            jax.ShapeDtypeStruct((heads, full, full), BF),
            jax.ShapeDtypeStruct((full, LANES), F32),
        ],
        scratch_shapes=[pltpu.VMEM((2, block, full), F32)],
        compiler_params=pltpu.CompilerParams(vmem_limit_bytes=60 << 20),
        cost_estimate=pl.CostEstimate(
            flops=8 * heads * full * full * LANES,
            bytes_accessed=2 * heads * full * full + 4 * full * LANES * heads,
            transcendentals=heads * full * full,
        ),
        name="row_attend",
    )(qcat, qseg, kcat, kseg, vaug)


def token_kernel(
    out_rows, up_rows, down_rows, at_ref, own_ref, mine_ref, theirs_ref, cot_ref, vec_ref, *refs
):
    groups = (out_rows, up_rows, down_rows)
    sets, at = [], 0
    for rows in groups:
        sets.append(refs[at : at + len(rows)])
        at += len(rows)
    (
        result_ref, gy1_ref, gmine_ref, gtheirs_ref, act_out, hlow_out, gffn_out, gup_out, gattn_ref,
        small_ref, act_ref, hlow_ref, gffn_ref, gup_ref, leave, wout_s, wup_s, wdown_s, acc_s, hid_s, norm_s, inv_s, slope_s, gy2_s, tmp_s, sum_s, vec_s, sems,
    ) = refs[at:]
    total, width = own_ref.shape
    ff = wup_s.shape[1]
    parts = ff // width
    span = mine_ref.shape[1]
    core = at_ref[0]
    made, slot = [], 0
    for rows, piece_refs, dst in zip(groups, sets, (wout_s, wup_s, wdown_s)):
        batch = []
        for n, ref in zip(rows, piece_refs):
            to = pl.ds(pl.multiple_of(at_ref[1 + slot], 16), n)
            copy = pltpu.make_async_copy(ref, dst.at[to, :], sems.at[slot])
            copy.start()
            batch.append(copy)
            slot += 1
        made.append(batch)

    def wait(index):
        for copy in made[index]:
            copy.wait()

    leaving = []

    def send_out(src, dst):
        copy = pltpu.make_async_copy(src, dst, leave.at[len(leaving)])
        copy.start()
        leaving.append(copy)

    def whole_vector(r):
        return jnp.concatenate([vec_ref[f % 2, f // 2, r : r + 1, :] for f in range(4)], axis=1).astype(F32)

    for c in range(parts):
        up_bias = [vec_ref[c % 2, c // 2, 6 + i : 7 + i, :] for i in range(4)]
        vec_s[c : c + 1, :] = jnp.concatenate(up_bias, axis=1).astype(F32)
    for i, r in enumerate((5, 10, 11, 12, 13, 14)):
        vec_s[4 + i : 5 + i, :] = whole_vector(r)

    def row(index):
        return vec_s[index : index + 1, :]

    rows_at = lambda i, n: pl.ds(pl.multiple_of(i * n, n), n)
    chunk = 16
    mine_rows = pl.ds(pl.multiple_of(core * span, LANES), span)
    other_rows = pl.ds(pl.multiple_of((1 - core) * span, LANES), span)
    sum_s[...] = jnp.zeros_like(sum_s)
    wait(0)
    acc_s[...] = jnp.dot(mine_ref[...], wout_s[mine_rows, :], preferred_element_type=F32)
    acc_s[...] += jnp.dot(theirs_ref[...], wout_s[other_rows, :], preferred_element_type=F32)

    def first_norm(i, carry):
        at = rows_at(i, chunk)
        y = own_ref[at, :].astype(F32) + (acc_s[at, :] + row(4))
        center = y - jnp.mean(y, axis=1, keepdims=True)
        inv = lax.rsqrt(jnp.mean(center * center, axis=1, keepdims=True) + EPSILON)
        normed = center * inv
        hidden = normed * row(6) + row(7)
        norm_s[at, :] = normed
        inv_s[at, :] = jnp.broadcast_to(inv, (chunk, LANES))
        hid_s[at, :] = hidden
        hlow_ref[at, :] = hidden.astype(BF)
        return carry

    lax.fori_loop(0, total // chunk, first_norm, 0, unroll=8)
    send_out(hlow_ref, hlow_out)
    wait(1)
    for c in range(parts):
        cols = slice(c * width, (c + 1) * width)
        tmp_s[c % 2] = jnp.dot(hlow_ref[...], wup_s[:, cols], preferred_element_type=F32)
        for r in range(0, total, chunk):
            x = tmp_s[c % 2, r : r + chunk, :] + row(c)
            cdf = 0.5 + 0.5 * lax.erf(x * (0.5**0.5))
            act_ref[r : r + chunk, cols] = (x * cdf).astype(BF)
            slope_s[r : r + chunk, cols] = cdf + x * (jnp.exp(-0.5 * x * x) * (0.15915494309189535**0.5))
    send_out(act_ref, act_out)
    wait(2)
    acc_s[...] = jnp.dot(act_ref[...], wdown_s[...], preferred_element_type=F32)

    def second_norm(i, carry):
        at = rows_at(i, chunk)
        y = hid_s[at, :] + (acc_s[at, :] + row(5))
        center = y - jnp.mean(y, axis=1, keepdims=True)
        inv = lax.rsqrt(jnp.mean(center * center, axis=1, keepdims=True) + EPSILON)
        normed = center * inv
        result_ref[at, :] = (normed * row(8) + row(9)).astype(BF)
        cot = cot_ref[at, :].astype(F32)
        sum_s[2] += cot * normed
        sum_s[3] += cot
        scaled = cot * row(8)
        g = inv * (
            scaled
            - jnp.mean(scaled, axis=1, keepdims=True)
            - normed * jnp.mean(scaled * normed, axis=1, keepdims=True)
        )
        gy2_s[at, :] = g
        gffn_ref[at, :] = g.astype(BF)
        return carry

    lax.fori_loop(0, total // chunk, second_norm, 0, unroll=4)
    send_out(gffn_ref, gffn_out)
    ones = jnp.ones((8, total), BF)
    ups = []
    for c in range(parts):
        cols = slice(c * width, (c + 1) * width)
        tmp_s[c % 2] = lax.dot_general(
            gffn_ref[...], wdown_s[cols, :], (((1,), (1,)), ((), ())), preferred_element_type=F32
        )
        for r in range(0, total, chunk):
            gup_ref[r : r + chunk, cols] = (
                tmp_s[c % 2, r : r + chunk, :] * slope_s[r : r + chunk, cols]
            ).astype(BF)
        ups.append(jnp.dot(ones, gup_ref[:, cols], preferred_element_type=F32)[:1])
    send_out(gup_ref, gup_out)
    acc_s[...] = lax.dot_general(
        gup_ref[...], wup_s[...], (((1,), (1,)), ((), ())), preferred_element_type=F32
    )

    def first_back(i, carry):
        at = rows_at(i, chunk)
        g_in = gy2_s[at, :] + acc_s[at, :]
        normed = norm_s[at, :]
        sum_s[0] += g_in * normed
        sum_s[1] += g_in
        scaled = g_in * row(6)
        g = inv_s[at, :1] * (
            scaled
            - jnp.mean(scaled, axis=1, keepdims=True)
            - normed * jnp.mean(scaled * normed, axis=1, keepdims=True)
        )
        gy1_ref[at, :] = g
        gattn_ref[at, :] = g.astype(BF)
        return carry

    lax.fori_loop(0, total // chunk, first_back, 0, unroll=4)
    gmine_ref[...] = lax.dot_general(
        gattn_ref[...], wout_s[mine_rows, :], (((1,), (1,)), ((), ())), preferred_element_type=F32
    ).astype(BF)
    gtheirs_ref[...] = lax.dot_general(
        gattn_ref[...], wout_s[other_rows, :], (((1,), (1,)), ((), ())), preferred_element_type=F32
    ).astype(BF)
    sums = [jnp.dot(ones, ref[...], preferred_element_type=F32)[:1] for ref in (gattn_ref, gffn_ref)]
    sums += [jnp.sum(sum_s[i], axis=0, keepdims=True) for i in range(4)]
    n = width // 4
    half = width // 2
    for shard in range(4):
        at = 8 * shard
        cut = slice(shard * n, (shard + 1) * n)
        for i in range(2):
            small_ref[at + i : at + i + 1, :] = ups[shard][:, i * half : (i + 1) * half]
        for i in range(3):
            small_ref[at + 2 + i : at + 3 + i, :] = jnp.concatenate(
                [sums[2 * i][:, cut], sums[2 * i + 1][:, cut]], axis=1
            )
        small_ref[at + 5 : at + 8, :] = jnp.zeros((3, half), F32)
    for copy in leaving:
        copy.wait()


def token_block(at, own, mine, theirs, cot, vec, out_pieces, up_pieces, down_pieces):
    total, width = own.shape
    span = mine.shape[1]
    ff = up_pieces[0].shape[1]
    vmem = pl.BlockSpec(memory_space=pltpu.VMEM)
    pieces = [*out_pieces, *up_pieces, *down_pieces]
    shapes = [
        ((total, width), BF), ((total, width), F32), ((total, span), BF), ((total, span), BF),
        ((total, ff), BF), ((total, width), BF), ((total, width), BF), ((total, ff), BF),
        ((total, width), BF), ((32, width // 2), F32),
    ]
    rows = lambda group: tuple(p.shape[0] for p in group)
    return pl.pallas_call(
        functools.partial(token_kernel, rows(out_pieces), rows(up_pieces), rows(down_pieces)),
        in_specs=[pl.BlockSpec(memory_space=pltpu.SMEM)]
        + [vmem] * 5
        + [pl.BlockSpec(memory_space=pl.ANY)] * len(pieces),
        out_specs=[pl.BlockSpec(memory_space=pl.ANY) if 4 <= i < 8 else vmem for i in range(len(shapes))],
        out_shape=[jax.ShapeDtypeStruct(s, d) for s, d in shapes],
        scratch_shapes=[
            *[pltpu.VMEM(shape, BF) for shape, _ in shapes[4:8]],
            pltpu.SemaphoreType.DMA((4,)),
            pltpu.VMEM((width, width), BF),
            pltpu.VMEM((width, ff), BF),
            pltpu.VMEM((ff, width), BF),
            pltpu.VMEM((total, width), F32),
            pltpu.VMEM((total, width), F32),
            pltpu.VMEM((total, width), F32),
            pltpu.VMEM((total, LANES), F32),
            pltpu.VMEM((total, ff), F32),
            pltpu.VMEM((total, width), F32),
            pltpu.VMEM((2, total, width), F32),
            pltpu.VMEM((4, 16, width), F32),
            pltpu.VMEM((16, width), F32),
            pltpu.SemaphoreType.DMA((len(pieces),)),
        ],
        compiler_params=pltpu.CompilerParams(vmem_limit_bytes=60 << 20),
        cost_estimate=pl.CostEstimate(
            flops=2 * total * width * (4 * ff + 2 * width),
            bytes_accessed=4 * width * ff + 6 * total * ff,
            transcendentals=2 * total * ff,
        ),
        name="token_block",
    )(at, own, mine, theirs, cot, vec, *pieces)


def turned(core, outer, near, z):
    pick = lambda a, b: jnp.where(core == 0, a, b)
    return pick(outer, near), pick(z, outer), pick(near, z)


def place_of(owner, index, relative, b, c):
    first = index if relative else 1 - index
    return (first, c, b) if owner == 0 else (b, first, c)


def up_pieces(owner, index, n, span, hid_t, gup_ref, emit):
    for relative in range(2):
        for b in range(2):
            for c in range(2):
                outer, near, z = place_of(owner, index, relative, b, c)
                left = hid_t[pl.ds(pl.multiple_of((2 * outer + owner) * n, 16), n), :]
                for far in range(2):
                    cols = pl.ds(pl.multiple_of((near * 4 + z * 2 + far) * span, LANES), span)
                    emit((relative, b, c, far), jnp.dot(left, gup_ref[:, cols], preferred_element_type=F32))


def rest_pieces(owner, index, n, wide, span, att_t, act_ref, gffn_ref, gattn_ref, small_ref, emit):
    half = wide // 2
    for relative in range(2):
        for b in range(2):
            outer = place_of(owner, index, relative, b, 0)[0]
            shard = 2 * outer + owner
            small = small_ref[pl.ds(pl.multiple_of(shard * 8, 8), 8), :]
            for c in range(2):
                _, near, z = place_of(owner, index, relative, b, c)
                cols = pl.ds(pl.multiple_of(shard * wide + near * half, LANES), half)
                if owner == 0:
                    if b:
                        continue
                    rows, marks = act_ref[:, cols], [((relative, zz, c), zz) for zz in range(2)]
                else:
                    if c:
                        continue
                    rows, marks = act_ref[:, cols], [((relative, b, zz), zz) for zz in range(2)]
                down = lax.dot_general(rows, gffn_ref[...], (((0,), (0,)), ((), ())), preferred_element_type=F32)
                for mark, zz in marks:
                    at = pl.ds(pl.multiple_of(shard * n + (near * 2 + zz) * (n // 4), 16), n // 4)
                    out = jnp.dot(att_t[at, :], gattn_ref[...], preferred_element_type=F32)
                    for far in range(2):
                        cut = slice(far * span, (far + 1) * span)
                        head = (near == 0) if zz == 0 and far == 0 else False
                        emit(
                            (*mark, far),
                            down[zz * half // 2 : (zz + 1) * half // 2, cut],
                            out[:, cut],
                            jnp.where(head, small, 0.0),
                        )


def fetch(sems, *pairs):
    made = [pltpu.make_async_copy(src, dst, sems.at[i]) for i, (src, dst) in enumerate(pairs)]
    for copy in made:
        copy.start()
    return made


def up_send_kernel(at_ref, hlow_ref, gup_ref, send_ref, hid_t):
    width = hlow_ref.shape[1]
    n, span = width // 4, gup_ref.shape[1] // 8
    hid_t[...] = hlow_ref[...].T

    def emit(at, value):
        send_ref[at] = value.astype(BF)

    for owner in range(2):

        @pl.when(at_ref[0] == 1 - owner)
        def _(owner=owner):
            up_pieces(owner, at_ref[1 + owner], n, span, hid_t, gup_ref, emit)


def fill_att(at_ref, mine_ref, theirs_ref, att_t):
    span = mine_ref.shape[1]
    core = at_ref[0]
    att_t[pl.ds(pl.multiple_of(core * span, LANES), span), :] = mine_ref[...].T
    att_t[pl.ds(pl.multiple_of((1 - core) * span, LANES), span), :] = theirs_ref[...].T


def rest_send_kernel(at_ref, mine_ref, theirs_ref, act_ref, gffn_ref, gattn_ref, small_ref, send_ref, att_t):
    width = gffn_ref.shape[1]
    n, wide, span = width // 4, act_ref.shape[1] // 4, mine_ref.shape[1]
    fill_att(at_ref, mine_ref, theirs_ref, att_t)

    def emit(at, down, out, small):
        send_ref[(*at, slice(0, wide // 4))] = down.astype(BF)
        send_ref[(*at, slice(wide // 4, wide // 4 + n // 4))] = out.astype(BF)
        send_ref[(*at, slice(wide // 4 + n // 4, None))] = small.astype(BF)

    for owner in range(2):

        @pl.when(at_ref[0] == 1 - owner)
        def _(owner=owner):
            rest_pieces(
                owner, at_ref[1 + owner], n, wide, span, att_t, act_ref, gffn_ref, gattn_ref, small_ref, emit
            )


def keep_kernel(
    at_ref, mine_ref, theirs_ref, hlow_ref, gffn_ref, gattn_ref, small_ref, gup_hbm, up_hbm, act_hbm, rest_hbm,
    away_ref, kept_ref, hid_t, att_t, gup_ref, up_ref, act_ref, rest_ref, sems,
):
    width = gffn_ref.shape[1]
    n, wide, span = width // 4, act_ref.shape[1] // 4, mine_ref.shape[1]
    m = n + wide // 4
    come = fetch(sems, (gup_hbm, gup_ref), (up_hbm, up_ref), (act_hbm, act_ref), (rest_hbm, rest_ref))
    hid_t[...] = hlow_ref[...].T
    fill_att(at_ref, mine_ref, theirs_ref, att_t)
    for copy in come[:2]:
        copy.wait()

    def put(at, rows, value, got_ref, got):
        out_ref = kept_ref if at[0] else away_ref
        out_ref[(*at[1:], rows)] = (value + got_ref[(*at, got)].astype(F32)).astype(BF)

    def emit_up(at, value):
        put(at, slice(0, n), value, up_ref, slice(None))

    def emit(at, down, out, small):
        put(at, slice(n, m), down, rest_ref, slice(0, wide // 4))
        put(at, slice(m, m + n // 4), out, rest_ref, slice(wide // 4, wide // 4 + n // 4))
        put(at, slice(m + n // 4, None), small, rest_ref, slice(wide // 4 + n // 4, None))

    for owner in range(2):

        @pl.when(at_ref[0] == owner)
        def _(owner=owner):
            index = at_ref[1 + owner]
            up_pieces(owner, index, n, span, hid_t, gup_ref, emit_up)

    for copy in come[2:]:
        copy.wait()
    for owner in range(2):

        @pl.when(at_ref[0] == owner)
        def _(owner=owner):
            index = at_ref[1 + owner]
            rest_pieces(owner, index, n, wide, span, att_t, act_ref, gffn_ref, gattn_ref, small_ref, emit)


def grads_call(kernel, name, at, arrays, fetched, shapes, transposed, flops):
    vmem = pl.BlockSpec(memory_space=pltpu.VMEM)
    anywhere = pl.BlockSpec(memory_space=pl.ANY)
    return pl.pallas_call(
        kernel,
        in_specs=[pl.BlockSpec(memory_space=pltpu.SMEM)] + [vmem] * len(arrays) + [anywhere] * len(fetched),
        out_specs=[vmem] * len(shapes),
        out_shape=[jax.ShapeDtypeStruct(s, BF) for s in shapes],
        scratch_shapes=[pltpu.VMEM(t, BF) for t in transposed]
        + [pltpu.VMEM(f.shape, BF) for f in fetched]
        + [pltpu.SemaphoreType.DMA((len(fetched),))] * bool(fetched),
        compiler_params=pltpu.CompilerParams(vmem_limit_bytes=60 << 20),
        cost_estimate=pl.CostEstimate(
            flops=flops, bytes_accessed=2 * sum(a.size for a in (*arrays, *fetched)), transcendentals=0
        ),
        name=name,
    )(at, *arrays, *fetched)


def row_backward_kernel(
    heads, hd, first_head, gmine_ref, gother_ref, keep_ref, send_ref, inv_ref, wts_ref, qcat_ref, kcat_ref,
    vaug_ref, ent_ref, entb_ref, *refs,
):
    gq_ref, gkv_ref, gscore_s, low_s, gk_s, gv_s = refs[-6:]
    step = pl.program_id(0)
    block = gmine_ref.shape[0]
    full = kcat_ref.shape[1]
    scale = hd ** (-0.5)
    lane = lax.broadcasted_iota(jnp.int32, (block, LANES - hd), 1)
    is_ent = entb_ref[:, :1] > 0
    early = step < pl.num_programs(0) // 2
    g_all = jnp.where(early, gmine_ref[...], gother_ref[...])
    att_all = jnp.where(early, keep_ref[...], send_ref[...])
    g_word, g_ent = [], []
    for h in range(heads):
        cut = slice(h * hd, (h + 1) * hd)
        g_low = (g_all[:, cut].astype(F32) * inv_ref[:, first_head + h : first_head + h + 1]).astype(BF)
        delta = jnp.sum(g_low.astype(F32) * att_all[:, cut].astype(F32), axis=1, keepdims=True)
        d_hi = delta.astype(BF)
        d_lo = (delta - d_hi.astype(F32)).astype(BF)
        extra = jnp.where(
            lane == 0, d_hi.astype(F32), jnp.where(lane == 1, d_lo.astype(F32), 0.0)
        ).astype(BF)
        g_aug = jnp.concatenate([g_low, extra], axis=1)
        gscore_s[h % 2] = lax.dot_general(
            g_aug, vaug_ref[h], (((1,), (1,)), ((), ())), preferred_element_type=F32
        )
        for r in range(0, block, CHUNK):
            low_s[h % 2, r : r + CHUNK, :] = (
                wts_ref[h, r : r + CHUNK, :].astype(F32) * gscore_s[h % 2, r : r + CHUNK, :]
            ).astype(BF)
        g_q = jnp.dot(low_s[h % 2], kcat_ref[h], preferred_element_type=F32) * scale
        g_word.append(g_q[:, :hd])
        g_ent.append(g_q[:, hd:])
        g_k = lax.dot_general(
            qcat_ref[h], low_s[h % 2], (((0,), (0,)), ((), ())), preferred_element_type=F32
        )
        g_v = lax.dot_general(
            g_low, wts_ref[h], (((0,), (0,)), ((), ())), preferred_element_type=F32
        )

        @pl.when(step == 0)
        def _(h=h, g_k=g_k, g_v=g_v):
            gk_s[h] = g_k
            gv_s[h] = g_v

        @pl.when(step > 0)
        def _(h=h, g_k=g_k, g_v=g_v):
            gk_s[h] += g_k
            gv_s[h] += g_v

    g_word = jnp.concatenate(g_word, axis=1)
    g_ent = jnp.concatenate(g_ent, axis=1)
    gq_ref[0] = jnp.where(is_ent, 0.0, g_word).astype(BF)
    gq_ref[1] = jnp.where(is_ent, 0.0, g_ent).astype(BF)
    gq_ref[2] = jnp.where(is_ent, g_word, 0.0).astype(BF)
    gq_ref[3] = jnp.where(is_ent, g_ent, 0.0).astype(BF)

    @pl.when(step == pl.num_programs(0) - 1)
    def _():
        def close(piece, carry):
            at = pl.ds(pl.multiple_of(piece * block, block), block)
            pick = ent_ref[at, :1] > 0
            g_keys, g_vals = [], []
            for h in range(heads):
                both = gk_s[h, :, at].T
                g_keys.append(jnp.where(pick, both[:, hd:], both[:, :hd]))
                g_vals.append(gv_s[h, :, at].T)
            gkv_ref[0, at, :] = jnp.concatenate(g_keys, axis=1).astype(BF)
            gkv_ref[1, at, :] = jnp.concatenate(g_vals, axis=1).astype(BF)
            return carry

        lax.fori_loop(0, full // block, close, 0)


def row_backward(first_head, heads, grads, gmine, gother, keep, send, inv, wts, qcat, kcat, vaug, ent, hd):
    half, all_cols = keep.shape
    full = 2 * half
    block = min(256, half)
    first = half // block
    cols = heads * hd
    g, c = first_head // heads, first_head * hd // cols
    by_rows = pl.BlockSpec((block, LANES), lambda i: (i, 0))
    by_head = lambda width: pl.BlockSpec((heads, block, width), lambda i: (g, i, 0))
    of_head = lambda width: pl.BlockSpec((heads, full, width), lambda i: (g, 0, 0))
    low = pl.BlockSpec((block, cols), lambda i: (jnp.minimum(i, first - 1), c))
    high = pl.BlockSpec((block, cols), lambda i: (jnp.maximum(i - first, 0), c))
    given = [] if grads is None else list(grads)
    return pl.pallas_call(
        functools.partial(row_backward_kernel, heads, hd, first_head),
        grid=(full // block,),
        in_specs=[
            low, high, low, high,
            by_rows,
            by_head(full),
            by_head(2 * hd),
            of_head(2 * hd),
            of_head(LANES),
            pl.BlockSpec((full, LANES), lambda i: (0, 0)),
            by_rows,
        ]
        + [pl.BlockSpec(memory_space=pl.ANY)] * len(given),
        out_specs=[
            pl.BlockSpec((4, block, cols), lambda i: (0, i, c)),
            pl.BlockSpec((2, full, cols), lambda i: (0, 0, c)),
        ],
        out_shape=[
            jax.ShapeDtypeStruct((4, full, all_cols), BF),
            jax.ShapeDtypeStruct((2, full, all_cols), BF),
        ],
        scratch_shapes=[
            pltpu.VMEM((2, block, full), F32),
            pltpu.VMEM((2, block, full), BF),
            pltpu.VMEM((heads, 2 * hd, full), F32),
            pltpu.VMEM((heads, hd, full), F32),
        ],
        input_output_aliases={11 + i: i for i in range(len(given))},
        compiler_params=pltpu.CompilerParams(vmem_limit_bytes=60 << 20),
        cost_estimate=pl.CostEstimate(
            flops=16 * heads * full * full * LANES,
            bytes_accessed=2 * heads * full * full + 20 * full * cols,
            transcendentals=0,
        ),
        name="row_backward",
    )(gmine, gother, keep, send, inv, wts, qcat, kcat, vaug, ent, ent, *given)


def qkv_grad_kernel(
    at_ref, own_ref, other_ref, gq_hbm, gkv_hbm, send_ref, keep_ref, rows_t, gq_ref, gkv_ref, sems
):
    half, width = own_ref.shape
    n = width // 16
    span = gq_ref.shape[2]
    core, index = at_ref[0], at_ref[1]
    come = fetch(sems, (gq_hbm, gq_ref), (gkv_hbm, gkv_ref))
    rows_t[:, :half] = own_ref[...].T
    rows_t[:, half:] = other_ref[...].T
    for copy in come:
        copy.wait()

    def write(out_ref, at, start, count):
        left = rows_t[pl.ds(pl.multiple_of(start, 16), count * n), :]
        for b in range(6):
            right = gq_ref[b] if b < 4 else gkv_ref[b - 4]
            piece = jnp.dot(left, right, preferred_element_type=F32).astype(BF)
            for p in range(count):
                out_ref[(*at(p), slice(b * n, (b + 1) * n))] = piece[p * n : (p + 1) * n, :]

    ones = jnp.ones((8, 2 * half), BF)
    sums = [
        jnp.dot(ones, gq_ref[b] if b < 4 else gkv_ref[b - 4], preferred_element_type=F32)[:1] for b in range(6)
    ]

    def write_sums(out_ref, at, outer, near, on_core):
        query = jnp.where(outer == 0, jnp.where(near == 0, sums[0], sums[1]), jnp.where(near == 0, sums[2], sums[3]))
        value = jnp.where(outer == on_core, sums[5], 0.0)
        rows = jnp.concatenate([query, value, jnp.zeros((6, span), F32)], axis=0)
        out_ref[(*at, slice(6 * n, None))] = rows.astype(BF)

    for which, out_ref in ((1 - index, send_ref), (index, keep_ref)):

        @pl.when(core == 0)
        def _(which=which, out_ref=out_ref):
            write(out_ref, lambda p: (p // 2 % 2, p // 4, p % 2), which * 8 * n, 8)
            for p in range(8):
                at = (p // 2 % 2, p // 4, p % 2)
                write_sums(out_ref, at, which, p // 4, 0)

        @pl.when(core == 1)
        def _(which=which, out_ref=out_ref):
            for o in range(2):
                write(out_ref, lambda p, o=o: (o, p // 2, p % 2), o * 8 * n + which * 4 * n, 4)
                for p in range(4):
                    write_sums(out_ref, (o, p // 2, p % 2), o, which, 1)


def qkv_grad(at, own, other, gq, gkv):
    half, width = own.shape
    span = gkv.shape[2]
    n = width // 16
    vmem = pl.BlockSpec(memory_space=pltpu.VMEM)
    return pl.pallas_call(
        qkv_grad_kernel,
        in_specs=[pl.BlockSpec(memory_space=pltpu.SMEM)]
        + [vmem] * 2
        + [pl.BlockSpec(memory_space=pl.ANY)] * 2,
        out_specs=[vmem] * 2,
        out_shape=[jax.ShapeDtypeStruct((2, 2, 2, 6 * n + 8, span), BF)] * 2,
        scratch_shapes=[
            pltpu.VMEM((width, 2 * half), BF),
            pltpu.VMEM(gq.shape, BF),
            pltpu.VMEM(gkv.shape, BF),
            pltpu.SemaphoreType.DMA((2,)),
        ],
        compiler_params=pltpu.CompilerParams(vmem_limit_bytes=60 << 20),
        cost_estimate=pl.CostEstimate(
            flops=24 * half * width * span, bytes_accessed=32 * half * span, transcendentals=0
        ),
        name="qkv_grad",
    )(at, own, other, gq, gkv)


def input_grad_kernel(gq_ref, gkv_ref, w_ref, gy1_ref, mine_ref, away_ref):
    span = gkv_ref.shape[2]
    total = None
    for b in range(6):
        left = gq_ref[b] if b < 4 else gkv_ref[b - 4]
        part = lax.dot_general(
            left, w_ref[:, b * span : (b + 1) * span], (((1,), (1,)), ((), ())), preferred_element_type=F32
        )
        total = part if total is None else total + part
    early = pl.program_id(0) < pl.num_programs(0) // 2

    @pl.when(early)
    def _():
        away_ref[...] = total.astype(BF)

    @pl.when(jnp.logical_not(early))
    def _():
        mine_ref[...] = gy1_ref[...] + total


def row_input_grad(gq, gkv, w, gy1):
    half, width = gy1.shape
    span = gkv.shape[2]
    block = min(256, half)
    first = half // block
    turn = lambda i: jnp.where(i < first, i + first, i - first)
    late = pl.BlockSpec((block, width), lambda i: (jnp.maximum(i - first, 0), 0))
    return pl.pallas_call(
        input_grad_kernel,
        grid=(2 * first,),
        in_specs=[
            pl.BlockSpec((4, block, span), lambda i: (0, turn(i), 0)),
            pl.BlockSpec((2, block, span), lambda i: (0, turn(i), 0)),
            pl.BlockSpec((width, 6 * span), lambda i: (0, 0)),
            late,
        ],
        out_specs=[late, pl.BlockSpec((block, width), lambda i: (jnp.minimum(i, first - 1), 0))],
        out_shape=[jax.ShapeDtypeStruct((half, width), F32), jax.ShapeDtypeStruct((half, width), BF)],
        compiler_params=pltpu.CompilerParams(vmem_limit_bytes=60 << 20),
        cost_estimate=pl.CostEstimate(
            flops=4 * half * width * 6 * span, bytes_accessed=20 * half * width, transcendentals=0
        ),
        name="row_input_grad",
    )(gq, gkv, w, gy1)


def lay_rest_kernel(at_ref, mine_ref, other_ref, up_ref, down_ref, out_ref, small_ref):
    span = mine_ref.shape[2]
    k, n, m = up_ref.shape[0], down_ref.shape[0] // 4, out_ref.shape[0] // 4
    core, index = at_ref[0], at_ref[1]
    last = slice(k + n + m, None)
    small_ref[...] = jnp.where(index == 0, mine_ref[0, last, :].astype(F32), other_ref[0, last, :].astype(F32))
    for a, ref in ((index, mine_ref), (1 - index, other_ref)):
        for b in range(2):
            pair = jnp.where(core == 0, b * 2 + a, a * 2 + b)
            for far in range(2):
                j = b * 2 + far
                cols = pl.ds(pl.multiple_of((pair * 2 + far) * span, LANES), span)
                up_ref[:, cols] = ref[j, :k, :].astype(F32)
                cols = slice(far * span, (far + 1) * span)
                down_ref[pl.ds(pl.multiple_of(pair * n, 8), n), cols] = ref[j, k : k + n, :].astype(F32)
                out_ref[pl.ds(pl.multiple_of(pair * m, 8), m), cols] = ref[j, k + n : k + n + m, :].astype(F32)


def lay_qkv_kernel(at_ref, keep_ref, got_ref, query_ref, kv_ref, small_ref):
    span = keep_ref.shape[2]
    n = (keep_ref.shape[1] - 8) // 6
    last = slice(6 * n, None)
    for half, src in ((at_ref[0], keep_ref), (1 - at_ref[0], got_ref)):
        small_ref[half] = src[0, last, :].astype(F32)
        for b in range(6):
            ref, i = (query_ref, b) if b < 4 else (kv_ref, b - 4)
            cols = pl.ds(pl.multiple_of(i * 2 * span + half * span, LANES), span)
            for j in range(4):
                ref[j * n : (j + 1) * n, cols] = src[j, b * n : (b + 1) * n, :].astype(F32)


def lay(kernel, name, at, arrays, shapes):
    vmem = pl.BlockSpec(memory_space=pltpu.VMEM)
    return pl.pallas_call(
        kernel,
        in_specs=[pl.BlockSpec(memory_space=pltpu.SMEM)] + [vmem] * len(arrays),
        out_specs=[vmem] * len(shapes),
        out_shape=[jax.ShapeDtypeStruct(s, F32) for s in shapes],
        compiler_params=pltpu.CompilerParams(vmem_limit_bytes=60 << 20),
        cost_estimate=pl.CostEstimate(
            flops=0, bytes_accessed=6 * sum(a.size for a in arrays), transcendentals=0
        ),
        name=name,
    )(at, *arrays)


def row_layer(
    inputs, query_weight, kv_weight, out_weight, up_weight, down_weight,
    query_bias, value_bias, out_bias, up_bias, down_bias,
    norm1_gain, norm1_shift, norm2_gain, norm2_shift, types, lengths, cotangent,
):
    rows_here, span, width = inputs.shape
    hd = width // HEADS
    full = types.shape[1]
    heads = HEADS // 2
    cols = heads * hd
    row_count = lax.axis_size("row")
    core, outer, row_id = (lax.axis_index(n) for n in ("core", "outer", "row"))
    place = [row_id // bit % 2 for bit in (1, 2, 4)]
    near = place[0]
    own_count = full // 2
    both_ways = [(0, 1), (1, 0)]

    def after(values, *others):
        return lax.optimization_barrier((values, *others))[0]

    def swap(values):
        return lax.ppermute(values, "core", both_ways)

    def cross(values):
        return lax.ppermute(values, "outer", both_ways)

    def pair_up(values, bit):
        return lax.ppermute(values, "row", [(i, i ^ bit) for i in range(row_count)])

    def in_order(index, mine, other, axis=0):
        first, second = jnp.where(index == 0, mine, other), jnp.where(index == 0, other, mine)
        return jnp.stack([first, second], axis=axis)

    def take(values, index, axis=0):
        return lax.dynamic_index_in_dim(values, index, axis, keepdims=False)

    def halves_of_rows(values):
        pieces = values.reshape(rows_here, 2, span // 2, width)
        other = swap(take(pieces, 1 - core, 1))
        return in_order(core, take(pieces, core, 1), other).reshape(row_count, span // 2, width)

    def over_rows(values):
        return lax.all_to_all(values, "row", 0, 0, tiled=True)

    def rows_whole(back):
        back = back.reshape(2, rows_here, span // 2, width)
        other = swap(take(back, 1 - core))
        both = in_order(core, take(back, core), other)
        return both.transpose(1, 0, 2, 3).reshape(rows_here, span, width)

    shard = query_weight.shape[0]
    wide = down_weight.shape[0]

    def near_half(values):
        return take(values.reshape(2, values.shape[0] // 2, values.shape[1]), near)

    f_own, f_core = 2 * outer + core, 2 * outer + 1 - core
    f_cross, f_both = 2 * (1 - outer) + core, 2 * (1 - outer) + 1 - core

    q_got = cross(near_half(query_weight))
    to_rows = halves_of_rows(inputs)
    own_rows = over_rows(to_rows).reshape(own_count, width)
    query_own, kv_own, types, lengths, query_bias = lax.optimization_barrier(
        (query_weight, kv_weight, types, lengths, query_bias, to_rows)
    )[:5]
    q_core, kv_core = swap(query_own), swap(kv_own)
    q_passed, kv_got = pair_up(q_got, 1), cross(after(kv_weight, q_got))
    q_got2 = swap(after(q_got, q_core, kv_core))
    own_rows, q_passed = lax.optimization_barrier((own_rows, q_passed))
    other_rows = swap(own_rows)
    q_passed2, kv_got2 = swap(q_passed), swap(kv_got)
    cot_halves = halves_of_rows(after(cotangent, own_rows))
    query_pieces = [query_weight, q_core, q_got, q_passed, q_got2, q_passed2]
    kv_pieces = [kv_weight, kv_core, kv_got, kv_got2]
    part = shard // 2
    query_at = [
        f_own * shard, f_core * shard,
        f_cross * shard + near * part, f_cross * shard + (1 - near) * part,
        f_both * shard + near * part, f_both * shard + (1 - near) * part,
    ]
    kv_at = [f_own * shard, f_core * shard, f_cross * shard, f_both * shard]
    at_qkv = jnp.stack([core, *query_at, *kv_at]).astype(jnp.int32)

    tags = jnp.concatenate([types, lengths], axis=1)
    tags_other = after(swap(tags), q_got2)
    tags = take(in_order(core, tags, tags_other).reshape(row_count, -1), row_id)
    types_row, lengths_row = tags[:full].reshape(row_count, span), tags[full:]
    docs = lengths_row.shape[0]
    ends = jnp.sum(jnp.where(jnp.arange(docs)[:, None] >= jnp.arange(docs)[None], lengths_row[None], 0), axis=1)

    vectors = (
        query_bias, value_bias, out_bias, up_bias, down_bias,
        norm1_gain, norm1_shift, norm2_gain, norm2_shift,
    )
    packed = jnp.concatenate(vectors)
    packed = in_order(outer, packed, cross(packed))
    vec = in_order(core, packed, swap(packed)).reshape(2, 2, -1, shard)

    qcat, kcat, vaug, w_sel, ent, qseg, kseg = row_project(
        at_qkv, ends, own_rows, other_rows, vec, types_row, query_pieces, kv_pieces, heads, hd
    )

    low_rows = down_weight[: wide // 2]
    u_got = cross(after(near_half(up_weight), kv_got))
    d_got = cross(after(near_half(low_rows), kv_got))
    late_out, late_up, late_down = lax.optimization_barrier((out_weight, up_weight, down_weight, kv_got2))[:3]
    o_core, u_core, d_core = swap(late_out), swap(late_up), swap(late_down)
    u_mid, d_mid, m_out, m_down, o_core, u_core, d_core = lax.optimization_barrier(
        (u_got, d_got, out_weight, down_weight, o_core, u_core, d_core, kcat)
    )[:7]
    u_passed, d_passed = pair_up(u_mid, 1), pair_up(d_mid, 1)
    o_got, t_got = cross(m_out), cross(m_down[wide // 2 :])
    u_got2, d_got2 = swap(u_mid), swap(d_mid)
    cot = over_rows(after(cot_halves, other_rows)).reshape(own_count, width)
    keep, send, wts, inv = row_attend(qcat, kcat, vaug, qseg, kseg, heads, hd)
    theirs = swap(send)
    u_passed2, d_passed2, o_got2, t_got2 = (
        swap(v) for v in lax.optimization_barrier((u_passed, d_passed, o_got, t_got, keep))[:4]
    )
    out_pieces = [out_weight, o_core, o_got, o_got2]
    out_at = [f * shard for f in (f_own, f_core, f_cross, f_both)]
    up_pieces = [up_weight, u_core, u_got, u_passed, u_got2, u_passed2]
    down_pieces = [down_weight, d_core, d_got, d_passed, t_got, d_got2, d_passed2, t_got2]
    quarter = wide // 4
    down_at = [
        f_own * wide, f_core * wide,
        f_cross * wide + near * quarter, f_cross * wide + (1 - near) * quarter, f_cross * wide + 2 * quarter,
        f_both * wide + near * quarter, f_both * wide + (1 - near) * quarter, f_both * wide + 2 * quarter,
    ]
    at_rest = jnp.stack([core, *out_at, *query_at, *down_at]).astype(jnp.int32)

    (
        result, gy1, gmine, gtheirs, act, hlow, gffn, gup, gattn, small
    ) = token_block(at_rest, own_rows, keep, theirs, cot, vec, out_pieces, up_pieces, down_pieces)
    gother = swap(gtheirs)
    at_core = core.astype(jnp.int32).reshape(1)
    at_near = near.astype(jnp.int32).reshape(1)
    at_grads = jnp.stack([core, outer, near]).astype(jnp.int32)
    m, ff = width // 16, up_weight.shape[1]
    bits = (2, 2, 2)
    tall = (2, *bits, ff // 16 + m + 8, cols)
    (rest_send,) = grads_call(
        rest_send_kernel, "rest_send", at_grads, [keep, theirs, act, gffn, gattn, small], [], [tall],
        [(width, own_count)], own_count * width * (ff + width),
    )
    hlow, gup, gother, rest_send = lax.optimization_barrier((hlow, gup, gother, rest_send))
    (up_send,) = grads_call(
        up_send_kernel, "up_send", at_grads, [hlow, gup], [], [(2, *bits, shard, cols)],
        [(width, own_count)], own_count * width * ff,
    )

    def add(*arrays):
        return functools.reduce(jnp.add, [v.astype(F32) for v in arrays]).astype(BF)

    def by_core(a, b):
        return jnp.where(core == 0, a, b)

    stages = {
        "s1": ("outer", "y"), "s2": ("z", "outer"), "s3": ("y", "z"), "far": ("far", "far"), "g1": ("z", "y"),
        "t1": ("z", "y"), "t2": ("y", "z"), "t3": ("far", "far"),
    }
    index_on = {"outer": outer, "y": near, "z": place[1], "far": place[2]}
    index_of = {name: by_core(index_on[a], index_on[b]) for name, (a, b) in stages.items()}
    every = ("row", "outer", "core")

    def pairs_of(stage):
        found = []
        for r in range(row_count):
            for o in range(2):
                for c in range(2):
                    axis = stages[stage][c]
                    to = (r, 1 - o) if axis == "outer" else (r ^ {"y": 1, "z": 2, "far": 4}[axis], o)
                    found.append(((r * 2 + o) * 2 + c, (to[0] * 2 + to[1]) * 2 + c))
        return found

    def send_over(values, stage):
        return lax.ppermute(values, every, pairs_of(stage))

    axis_at = {"far": 0, "z": 1, "y": 2}

    def trade(values, stage):
        away, mine = (
            by_core(*(take(values, i, axis_at[axis]) for axis in stages[stage]))
            for i in (1 - index_of[stage], index_of[stage])
        )
        token[0] = away
        return mine, send_over(away, stage)

    def traded(state, stage):
        mine, other = in_turn(*state)
        token[0] = other
        return by_core(*(in_order(index_of[stage], mine, other, axis_at[axis]) for axis in stages[stage]))

    def by_rows(values):
        return values.reshape(2, 2, 2, span // 2, width)

    token = [gother]

    def in_turn(*arrays):
        return lax.optimization_barrier((*arrays, token[0]))[: len(arrays)]

    def halve(state, axis):
        mine, other = in_turn(*state)
        away, mine = (
            add(take(mine, i), take(other, i)) for i in (1 - index_of[axis], index_of[axis])
        )
        token[0] = away
        return mine, send_over(away, axis)

    def start_spread(state, axis):
        total = add(*in_turn(*state))
        token[0] = total
        return total, send_over(total, axis)

    def spread(state, have, axis):
        total = in_order(index_of[have], *in_turn(*state))
        token[0] = total
        return total, send_over(total, axis)

    out_rows = trade(by_rows(result), "t1")
    away, mine = grads_call(
        keep_kernel, "keep_grads", at_grads,
        [keep, theirs, hlow, gffn, gattn, small], [gup, swap(up_send), act, swap(rest_send)],
        [(*bits, shard + tall[-2], cols)] * 2, [(width, own_count)] * 2, own_count * width * (2 * ff + width),
    )
    rest = (mine, send_over(away, "s1"))
    token[0] = away
    out_rows = trade(traded(out_rows, "t1"), "t2")
    gmine, _ = lax.optimization_barrier((gmine, token[0]))
    gq, gkv = row_backward(
        0, heads, None, gmine, gother, keep, send, inv, wts, qcat, kcat, vaug, ent, hd
    )
    n = width // 16
    token[0] = gkv
    out_rows = trade(traded(out_rows, "t2"), "t3")
    rest = halve(rest, "s2")
    at_first = jnp.stack([core, index_of["s1"]]).astype(jnp.int32)
    q_send, q_keep = qkv_grad(at_first, own_rows, after(other_rows, token[0]), gq, gkv)
    six = (q_keep, send_over(q_send, "s1"))
    token[0] = q_send
    out_rows = traded(out_rows, "t3")
    in_mine, in_away = row_input_grad(gq, gkv, after(w_sel, token[0]), gy1)
    in_other = swap(in_away)
    token[0] = in_away
    rest = halve(rest, "s3")
    in_mine, in_other = in_turn(in_mine, in_other)
    grad_in = (in_mine + in_other.astype(F32)).astype(BF)
    in_rows = trade(by_rows(grad_in), "t1")
    six = halve(six, "s2")
    rest = halve(rest, "far")
    in_rows = trade(traded(in_rows, "t1"), "t2")
    six = halve(six, "s3")
    rest = start_spread(rest, "far")
    six = halve(six, "far")
    rest = spread(rest, "far", "s3")
    six = start_spread(six, "far")
    in_rows = trade(traded(in_rows, "t2"), "t3")
    rest = spread(rest, "s3", "g1")
    six = spread(six, "far", "s3")
    in_rows = traded(in_rows, "t3")
    output, input_grad = rows_whole(out_rows), rows_whole(in_rows)
    six = spread(six, "s3", "g1")
    at_last = jnp.stack([core, index_of["g1"]]).astype(jnp.int32)
    g_up, g_down, g_out, small = lay(
        lay_rest_kernel, "lay_rest", at_last, [v.reshape(4, *v.shape[2:]) for v in in_turn(*rest)],
        [up_weight.shape, down_weight.shape, out_weight.shape, (8, cols)],
    )
    token[0] = g_out
    six = in_order(index_of["g1"], *in_turn(*six))
    away, kept = by_core(six[:, 1], six[0]), by_core(six[:, 0], six[1])
    parts = [v.reshape(4, *v.shape[2:]) for v in (kept, swap(away))]
    g_query, g_kv, halves = lay(
        lay_qkv_kernel, "lay_qkv", at_core, parts, [query_weight.shape, kv_weight.shape, (2, 8, cols)]
    )
    pairs = small[2:5].reshape(6, shard)
    value = take(halves[:, 1].sum(axis=0).reshape(2, shard), core)
    return (
        output, input_grad, g_query, g_kv, g_out, g_up, g_down,
        halves[:, 0].reshape(-1), value, pairs[0], small[:2].reshape(-1), *(pairs[i] for i in range(1, 6)),
    )


def solution(mesh):
    def step(*args):
        ctx, fsdp = mesh.shape["ctx"], mesh.shape["fsdp"]
        row_count = args[0].shape[0] // (fsdp // 2)
        per_row = ctx // row_count
        fine = Mesh(
            mesh.devices.reshape(row_count, per_row, fsdp // 2, 2), ("row", "group", "outer", "core")
        )
        tokens = P(("outer", "core"), ("row", "group"), None)
        mat, vec = P(("outer", "core"), None), P(("outer", "core"))
        in_specs = (tokens, *[mat] * 5, *[vec] * 9, mat, mat, tokens)
        out_specs = (tokens, tokens, *[mat] * 5, *[vec] * 9)
        quarter = args[0].shape[2] // 4
        fits = per_row == 1 and fsdp == 4 and row_count == 8 and args[0].shape[2] % (2 * LANES) == 0 and quarter % 32 == 0
        body = row_layer if fits else functools.partial(layer, None, per_row)
        return jax.shard_map(
            body, mesh=fine, in_specs=in_specs, out_specs=out_specs, check_vma=False
        )(*args)

    return step
```

```python
import functools

import jax
import jax.numpy as jnp
from jax import lax
from jax.experimental import pallas as pl
from jax.experimental.pallas import tpu as pltpu
from jax.sharding import Mesh
from jax.sharding import PartitionSpec as P

HEADS = 12
EPSILON = 1e-05
BLOCKED = -1e30
BF = jnp.bfloat16
F32 = jnp.float32
LANES = 128
CHUNK = 16


def matmul(left_mat, right_mat):
    return jnp.dot(left_mat, right_mat, preferred_element_type=F32)


def rows_inner(left_mat, right_mat):
    return lax.dot_general(left_mat, right_mat, (((0,), (0,)), ((), ())), preferred_element_type=F32)


def times_transposed(left_mat, right_mat):
    return lax.dot_general(left_mat, right_mat, (((1,), (1,)), ((), ())), preferred_element_type=F32)


def normalize(values, gain_vec, shift_vec):
    center = values - jnp.mean(values, axis=-1, keepdims=True)
    scale_inv = lax.rsqrt(jnp.mean(center * center, axis=-1, keepdims=True) + EPSILON)
    normed = center * scale_inv
    return (normed * gain_vec + shift_vec, normed, scale_inv)


def normalize_back(grad_in, normed, scale_inv, gain_vec):
    scaled = grad_in * gain_vec
    inner_part = (
        scaled
        - jnp.mean(scaled, axis=-1, keepdims=True)
        - normed * jnp.mean(scaled * normed, axis=-1, keepdims=True)
    )
    return (inner_part * scale_inv, jnp.sum(grad_in * normed, axis=0), jnp.sum(grad_in, axis=0))


def column_sum(values):
    return jnp.sum(values.astype(F32), axis=0)


def forward_kernel(
    heads, hd, rows_ref, w_ref, bias_ref, ent_ref, qseg_ref, kseg_ref,
    att_ref, wts_ref, inv_ref, qcat_ref, kcat_ref, vneg_ref,
    kaug_s, vaug_s, score_s,
):
    step = pl.program_id(0)
    span = heads * hd
    full = rows_ref.shape[0]
    block = att_ref.shape[0]
    scale = hd ** (-0.5)

    @pl.when(step == 0)
    def _():
        kaug_s[:, :, LANES:] = jnp.broadcast_to(kseg_ref[...][None], (heads, full, LANES))
        lane = lax.broadcasted_iota(jnp.int32, (block, LANES - hd), 1)
        one_col = jnp.where(lane == 0, 1.0, 0.0).astype(BF)
        neg_col = jnp.where(lane < 2, -1.0, 0.0).astype(BF)

        def project(piece, carry):
            at = pl.ds(pl.multiple_of(piece * block, block), block)
            rows = rows_ref[at, :]
            ent = ent_ref[at, :hd]
            wide = ent_ref[at, :1] > 0
            word = (1 - ent).astype(BF)

            def part(index):
                cols = slice(index * span, (index + 1) * span)
                return jnp.dot(rows, w_ref[:, cols], preferred_element_type=F32) + bias_ref[:, cols]

            q_word = (jnp.where(wide, part(2), part(0))).astype(BF) * BF(scale)
            q_ent = (jnp.where(wide, part(3), part(1))).astype(BF) * BF(scale)
            keys = part(4).astype(BF)
            vals = part(5).astype(BF)
            for h in range(heads):
                cut = slice(h * hd, (h + 1) * hd)
                qcat_ref[h, at, :] = jnp.concatenate([q_word[:, cut], q_ent[:, cut]], axis=1)
                k_pair = jnp.concatenate([keys[:, cut] * word, keys[:, cut] * ent], axis=1)
                kcat_ref[h, at, :] = k_pair
                kaug_s[h, at, :LANES] = k_pair
                vneg_ref[h, at, :] = jnp.concatenate([vals[:, cut], neg_col], axis=1)
                vaug_s[h, at, :] = jnp.concatenate([vals[:, cut], one_col], axis=1)
            return carry

        lax.fori_loop(0, full // block, project, 0)

    here = pl.ds(pl.multiple_of(step * block, block), block)
    q_seg = qseg_ref[here, :]
    lane = lax.broadcasted_iota(jnp.int32, (block, LANES), 1)
    inv_all = jnp.zeros((block, LANES), F32)
    mixed = []
    for h in range(heads):
        q_aug = jnp.concatenate([qcat_ref[h, here, :], q_seg], axis=1)
        score_s[h % 2] = lax.dot_general(
            q_aug, kaug_s[h], (((1,), (1,)), ((), ())), preferred_element_type=F32
        )
        for r in range(0, block, CHUNK):
            s = score_s[h % 2, r : r + CHUNK, :]
            top = jnp.max(s, axis=1, keepdims=True)
            wts_ref[h, r : r + CHUNK, :] = jnp.exp(s - top).astype(BF)
        out = jnp.dot(wts_ref[h], vaug_s[h], preferred_element_type=F32)
        inv = 1.0 / out[:, hd : hd + 1]
        inv_all = jnp.where(lane == h, inv, inv_all)
        mixed.append((out[:, :hd] * inv).astype(BF))
    att_ref[...] = jnp.concatenate(mixed, axis=1)
    inv_ref[...] = inv_all


def attention_forward(rows, w_sel, bias_sel, ent, qseg, kseg, heads, hd):
    full, width = rows.shape
    block = min(256, full)
    span = heads * hd
    steps = full // block
    whole = lambda *dims: pl.BlockSpec(dims, lambda i: (0,) * len(dims))
    return pl.pallas_call(
        functools.partial(forward_kernel, heads, hd),
        grid=(steps,),
        in_specs=[
            whole(full, width),
            whole(width, 6 * span),
            whole(1, 6 * span),
            whole(full, LANES),
            whole(full, LANES),
            whole(full, LANES),
        ],
        out_specs=[
            pl.BlockSpec((block, span), lambda i: (i, 0)),
            pl.BlockSpec((heads, block, full), lambda i: (0, i, 0)),
            pl.BlockSpec((block, LANES), lambda i: (i, 0)),
            whole(heads, full, 2 * hd),
            whole(heads, full, 2 * hd),
            whole(heads, full, LANES),
        ],
        out_shape=[
            jax.ShapeDtypeStruct((full, span), BF),
            jax.ShapeDtypeStruct((heads, full, full), BF),
            jax.ShapeDtypeStruct((full, LANES), F32),
            jax.ShapeDtypeStruct((heads, full, 2 * hd), BF),
            jax.ShapeDtypeStruct((heads, full, 2 * hd), BF),
            jax.ShapeDtypeStruct((heads, full, LANES), BF),
        ],
        scratch_shapes=[
            pltpu.VMEM((heads, full, 2 * LANES), BF),
            pltpu.VMEM((heads, full, LANES), BF),
            pltpu.VMEM((2, block, full), F32),
        ],
        compiler_params=pltpu.CompilerParams(vmem_limit_bytes=60 << 20),
        cost_estimate=pl.CostEstimate(
            flops=2 * full * width * 6 * span + 8 * heads * full * full * LANES,
            bytes_accessed=2 * heads * full * full + 10 * full * width,
            transcendentals=heads * full * full,
        ),
        name="attention_forward",
    )(rows, w_sel, bias_sel, ent, qseg, kseg)


def backward_kernel(
    heads, hd, go_ref, att_ref, inv_ref, wts_ref, qcat_ref, kcat_ref, vneg_ref, ent_ref, entb_ref,
    gq_ref, gkv_ref, gscore_s, low_s, gk_s, gv_s,
):
    step = pl.program_id(0)
    span = heads * hd
    block = go_ref.shape[0]
    full = kcat_ref.shape[1]
    scale = hd ** (-0.5)
    lane = lax.broadcasted_iota(jnp.int32, (block, LANES - hd), 1)
    is_ent = entb_ref[:, :1] > 0
    g_word, g_ent = [], []
    for h in range(heads):
        cut = slice(h * hd, (h + 1) * hd)
        g_low = (go_ref[:, cut].astype(F32) * inv_ref[:, h : h + 1]).astype(BF)
        delta = jnp.sum(g_low.astype(F32) * att_ref[:, cut].astype(F32), axis=1, keepdims=True)
        d_hi = delta.astype(BF)
        d_lo = (delta - d_hi.astype(F32)).astype(BF)
        extra = jnp.where(
            lane == 0, d_hi.astype(F32), jnp.where(lane == 1, d_lo.astype(F32), 0.0)
        ).astype(BF)
        g_aug = jnp.concatenate([g_low, extra], axis=1)
        gscore_s[h % 2] = lax.dot_general(
            g_aug, vneg_ref[h], (((1,), (1,)), ((), ())), preferred_element_type=F32
        )
        for r in range(0, block, CHUNK):
            low_s[h % 2, r : r + CHUNK, :] = (
                wts_ref[h, r : r + CHUNK, :].astype(F32) * gscore_s[h % 2, r : r + CHUNK, :]
            ).astype(BF)
        g_q = jnp.dot(low_s[h % 2], kcat_ref[h], preferred_element_type=F32) * scale
        g_word.append(g_q[:, :hd])
        g_ent.append(g_q[:, hd:])
        g_k = lax.dot_general(
            qcat_ref[h], low_s[h % 2], (((0,), (0,)), ((), ())), preferred_element_type=F32
        )
        g_v = lax.dot_general(
            g_low, wts_ref[h], (((0,), (0,)), ((), ())), preferred_element_type=F32
        )

        @pl.when(step == 0)
        def _(h=h, g_k=g_k, g_v=g_v):
            gk_s[h] = g_k
            gv_s[h] = g_v

        @pl.when(step > 0)
        def _(h=h, g_k=g_k, g_v=g_v):
            gk_s[h] += g_k
            gv_s[h] += g_v

    g_word = jnp.concatenate(g_word, axis=1)
    g_ent = jnp.concatenate(g_ent, axis=1)
    gq_ref[:, :span] = jnp.where(is_ent, 0.0, g_word).astype(BF)
    gq_ref[:, span : 2 * span] = jnp.where(is_ent, 0.0, g_ent).astype(BF)
    gq_ref[:, 2 * span : 3 * span] = jnp.where(is_ent, g_word, 0.0).astype(BF)
    gq_ref[:, 3 * span :] = jnp.where(is_ent, g_ent, 0.0).astype(BF)

    @pl.when(step == pl.num_programs(0) - 1)
    def _():
        def close(piece, carry):
            at = pl.ds(pl.multiple_of(piece * block, block), block)
            pick = ent_ref[at, :1] > 0
            g_keys, g_vals = [], []
            for h in range(heads):
                both = gk_s[h, :, at].T
                g_keys.append(jnp.where(pick, both[:, hd:], both[:, :hd]))
                g_vals.append(gv_s[h, :, at].T)
            gkv_ref[at, :span] = jnp.concatenate(g_keys, axis=1).astype(BF)
            gkv_ref[at, span:] = jnp.concatenate(g_vals, axis=1).astype(BF)
            return carry

        lax.fori_loop(0, full // block, close, 0)


def attention_backward(g_out, att, inv, wts, qcat, kcat, vneg, ent, heads, hd):
    full, span = att.shape
    block = min(256, full)
    whole = lambda *dims: pl.BlockSpec(dims, lambda i: (0,) * len(dims))
    by_rows = lambda width: pl.BlockSpec((block, width), lambda i: (i, 0))
    by_head = lambda width: pl.BlockSpec((heads, block, width), lambda i: (0, i, 0))
    return pl.pallas_call(
        functools.partial(backward_kernel, heads, hd),
        grid=(full // block,),
        in_specs=[
            by_rows(span),
            by_rows(span),
            by_rows(LANES),
            by_head(full),
            by_head(2 * hd),
            whole(heads, full, 2 * hd),
            whole(heads, full, LANES),
            whole(full, LANES),
            by_rows(LANES),
        ],
        out_specs=[by_rows(4 * span), whole(full, 2 * span)],
        out_shape=[
            jax.ShapeDtypeStruct((full, 4 * span), BF),
            jax.ShapeDtypeStruct((full, 2 * span), BF),
        ],
        scratch_shapes=[
            pltpu.VMEM((2, block, full), F32),
            pltpu.VMEM((2, block, full), BF),
            pltpu.VMEM((heads, 2 * hd, full), F32),
            pltpu.VMEM((heads, hd, full), F32),
        ],
        compiler_params=pltpu.CompilerParams(vmem_limit_bytes=60 << 20),
        cost_estimate=pl.CostEstimate(
            flops=16 * heads * full * full * LANES,
            bytes_accessed=2 * heads * full * full + 20 * full * span,
            transcendentals=0,
        ),
        name="attention_backward",
    )(g_out, att, inv, wts, qcat, kcat, vneg, ent, ent)


def layer(
    half, per_row, inputs, query_weight, kv_weight, out_weight, up_weight, down_weight,
    query_bias, value_bias, out_bias, up_bias, down_bias,
    norm1_gain, norm1_shift, norm2_gain, norm2_shift, types, lengths, cotangent,
):
    rows_here, span, width = inputs.shape
    head_dim = width // HEADS
    full = types.shape[1]
    members = 2 * per_row
    heads = HEADS // members
    cols = heads * head_dim
    row_count = lax.axis_size("row")
    outer = lax.axis_size("outer")
    core = lax.axis_index("core")
    group = lax.axis_index("group")
    member = group * 2 + core
    row_id = lax.axis_index("row")
    own = row_count * (span // 2)

    def swap(values):
        return lax.ppermute(values, "core", [(0, 1), (1, 0)])

    def in_order(index, mine, other):
        return jnp.stack([jnp.where(index == 0, mine, other), jnp.where(index == 0, other, mine)])

    def gather_outer(values):
        if outer == 2:
            other = lax.ppermute(values, "outer", [(0, 1), (1, 0)])
            return in_order(lax.axis_index("outer"), values, other)
        return lax.all_gather(values, "outer", axis=0, tiled=False)

    def gather_members(values):
        pair = in_order(core, values, swap(values))
        if per_row == 1:
            return pair
        spread = lax.all_gather(pair, "group", axis=0, tiled=False)
        return spread.reshape((members,) + values.shape)

    def exchange_members(values):
        if per_row == 1:
            mine = lax.dynamic_index_in_dim(values, core, 0, keepdims=False)
            away = lax.dynamic_index_in_dim(values, 1 - core, 0, keepdims=False)
            return in_order(core, mine, swap(away))
        return lax.all_to_all(values, ("group", "core"), 0, 0, tiled=True)

    def take(values, index, axis):
        return lax.dynamic_index_in_dim(values, index, axis, keepdims=False)

    def to_row(values):
        pieces = values.reshape(rows_here, 2, span // 2, width)
        other = swap(take(pieces, 1 - core, 1))
        both = in_order(core, take(pieces, core, 1), other).reshape(row_count, span // 2, width)
        return lax.all_to_all(both, "row", 0, 0, tiled=True).reshape(own, width)

    def from_row(values):
        back = lax.all_to_all(values.reshape(row_count, span // 2, width), "row", 0, 0, tiled=True)
        back = back.reshape(2, rows_here, span // 2, width)
        other = swap(take(back, 1 - core, 0))
        both = in_order(core, take(back, core, 0), other)
        return both.transpose(1, 0, 2, 3).reshape(rows_here, span, width)

    own_rows = to_row(inputs)
    all_rows = gather_members(own_rows).reshape(full, width)

    tags = jnp.concatenate([types, lengths], axis=1)
    tags = in_order(core, tags, swap(tags)).reshape(row_count, -1)
    tags = take(tags, row_id, 0)
    types_row, lengths_row = tags[:full], tags[full:]

    def by_member(values):
        return values.reshape(row_count, per_row, 2, span // 2).transpose(1, 2, 0, 3).reshape(full)

    entity = by_member(types_row) > 0
    positions = by_member(lax.iota(jnp.int32, full))
    docs = lengths_row.shape[0]
    ends = [jnp.sum(lengths_row[: d + 1]) for d in range(docs)]
    seg = sum((positions >= end).astype(jnp.int32) for end in ends)
    lanes = lax.broadcasted_iota(jnp.int32, (full, LANES), 1)
    same = lanes == seg[:, None]
    qseg = jnp.where(same, 1.0, 0.0).astype(BF)
    kseg = jnp.where(same | (lanes >= docs), 0.0, BLOCKED).astype(BF)
    ent = jnp.broadcast_to(jnp.where(entity, 1.0, 0.0).astype(BF)[:, None], (full, LANES))

    shard = query_weight.shape[0]
    cut = jnp.concatenate([query_weight, kv_weight], axis=1).reshape(shard, 6, members, cols)
    away = take(cut, group * 2 + 1 - core, 2).reshape(shard, 6 * cols)
    mine = take(cut, member, 2).reshape(shard, 6 * cols)
    w_sel = gather_outer(in_order(core, mine, swap(away))).reshape(width, 6 * cols)

    vectors = (
        query_bias, value_bias, out_bias, up_bias, down_bias,
        norm1_gain, norm1_shift, norm2_gain, norm2_shift,
    )
    sizes = [v.shape[0] for v in vectors]
    packed = jnp.concatenate(vectors)
    packed = lax.all_gather(packed, ("outer", "core"), axis=0, tiled=False)
    offsets = [sum(sizes[:i]) for i in range(len(sizes) + 1)]
    (b_query, b_value, b_out, b_up, b_down, g_one, s_one, g_two, s_two) = (
        packed[:, a:b].reshape(-1).astype(F32) for a, b in zip(offsets[:-1], offsets[1:])
    )
    b_six = jnp.concatenate([b_query, jnp.zeros((width,), F32), b_value])
    b_sel = take(b_six.reshape(6, members, cols), member, 1).reshape(1, 6 * cols)

    att, inv_stored, wts = None, None, None
    att, wts, inv_stored, qcat, kcat, vneg = attention_forward(
        all_rows, w_sel, b_sel, ent, qseg, kseg, heads, head_dim
    )

    def fetch(values):
        return gather_outer(in_order(core, values, swap(values))).reshape(-1, values.shape[1])

    w_out, w_up, w_down = fetch(out_weight), fetch(up_weight), fetch(down_weight)

    def heads_to_tokens(values):
        got = exchange_members(values.reshape(members, own, cols))
        return got.transpose(1, 0, 2).reshape(own, width)

    def tokens_to_heads(values):
        parts = values.reshape(own, members, cols).transpose(1, 0, 2)
        return exchange_members(parts).reshape(full, cols)

    attended = heads_to_tokens(att)
    attn_out = matmul(attended, w_out) + b_out
    hidden, normed_one, inv_one = normalize(own_rows.astype(F32) + attn_out, g_one, s_one)
    hidden_low = hidden.astype(BF)
    up_proj = matmul(hidden_low, w_up) + b_up
    gelu_out, gelu_pull = jax.vjp(lambda v: jax.nn.gelu(v, approximate=False), up_proj)
    act_low = gelu_out.astype(BF)
    ffn_out = matmul(act_low, w_down) + b_down
    result, normed_two, inv_two = normalize(hidden + ffn_out, g_two, s_two)
    output = from_row(result.astype(BF))

    cot = to_row(cotangent).astype(F32)
    grad_y2, grad_g2, grad_s2 = normalize_back(cot, normed_two, inv_two, g_two)
    grad_ffn = grad_y2.astype(BF)
    grad_act = times_transposed(grad_ffn, w_down)
    grad_up = gelu_pull(grad_act)[0].astype(BF)
    grad_hidden = grad_y2 + times_transposed(grad_up, w_up)
    grad_y1, grad_g1, grad_s1 = normalize_back(grad_hidden, normed_one, inv_one, g_one)
    grad_attn = grad_y1.astype(BF)
    grad_attended = times_transposed(grad_attn, w_out).astype(BF)

    def pick_rows(left, core_index, outer_index):
        parts = left.reshape(left.shape[0], outer, 2, -1)
        if outer_index is None:
            return take(parts, core_index, 2).reshape(left.shape[0], -1)
        return take(take(parts, core_index, 2), outer_index, 1)

    def reduce_outer(partial):
        if outer == 2:
            me = lax.axis_index("outer")
            other = lax.ppermute(take(partial, 1 - me, 0).astype(BF), "outer", [(0, 1), (1, 0)])
            return take(partial, me, 0).astype(F32) + other.astype(F32)
        return lax.psum_scatter(partial.astype(BF), "outer", scatter_dimension=0, tiled=False).astype(F32)

    def shard_grad(left, right):
        away = rows_inner(pick_rows(left, 1 - core, None), right).astype(BF)
        mine = rows_inner(pick_rows(left, core, None), right)
        pair = mine + swap(away).astype(F32)
        part = reduce_outer(pair.reshape(outer, -1, right.shape[1]))
        return lax.psum(part.astype(BF), ("row", "group")).astype(F32)

    g_w_down = shard_grad(act_low, grad_ffn)
    g_w_up = shard_grad(hidden_low, grad_up)
    g_w_out = shard_grad(attended, grad_attn)

    gq, gkv = attention_backward(
        tokens_to_heads(grad_attended), att, inv_stored, wts, qcat, kcat, vneg, ent, heads, head_dim
    )
    g_six = jnp.concatenate([gq, gkv], axis=1)
    g_sel = reduce_outer(rows_inner(all_rows, g_six).reshape(outer, -1, 6 * cols))
    g_sel = lax.psum(g_sel.astype(BF), "row").reshape(2, shard, 6, cols)
    got = in_order(core, take(g_sel, core, 0), swap(take(g_sel, 1 - core, 0)))
    if per_row > 1:
        got = lax.all_gather(got, "group", axis=0, tiled=False)
    got = got.reshape(members, shard, 6, cols).transpose(1, 2, 0, 3).reshape(shard, 6 * width)
    g_w_query = got[:, : 4 * width].astype(F32)
    g_w_kv = got[:, 4 * width :].astype(F32)

    part_in = times_transposed(g_six, w_sel)
    got_in = exchange_members(part_in.astype(BF).reshape(members, own, width))
    grad_in = grad_y1 + jnp.sum(got_in.astype(F32), axis=0)
    input_grad = from_row(grad_in.astype(BF))

    six_sum = column_sum(g_six).reshape(6, 1, cols)
    spot = lax.broadcasted_iota(jnp.int32, (1, members, 1), 1) == member
    six_sum = jnp.where(spot, six_sum, 0.0).reshape(6, width)
    small = [
        six_sum[:4].reshape(-1), six_sum[5], column_sum(grad_attn), column_sum(grad_up),
        column_sum(grad_ffn), grad_g1, grad_s1, grad_g2, grad_s2,
    ]
    total = lax.psum(jnp.concatenate(small), ("row", "group", "outer", "core"))
    me = lax.axis_index("outer") * 2 + core
    pieces, at = [], 0
    for size in sizes:
        whole_size = size * outer * 2
        pieces.append(lax.dynamic_slice_in_dim(total[at : at + whole_size], me * size, size))
        at += whole_size
    return (output, input_grad, g_w_query, g_w_kv, g_w_out, g_w_up, g_w_down, *pieces)


def project_kernel(
    heads, hd, query_rows, kv_rows, at_ref, ends_ref, own_ref, other_ref, vec_ref, types_ref, *refs
):
    n_query, n_kv = len(query_rows), len(kv_rows)
    query_refs, kv_refs = refs[:n_query], refs[n_query : n_query + n_kv]
    qcat_ref, kcat_ref, vaug_ref, w_ref, ent_ref, qseg_ref, kseg_ref, kinds_s, bias_s, sems = refs[n_query + n_kv :]
    span = heads * hd
    half, width = own_ref.shape
    block = min(256, half)
    scale = hd ** (-0.5)
    core = at_ref[0]
    made = []
    for i, (ref, rows) in enumerate(zip(query_refs + kv_refs, query_rows + kv_rows)):
        first, blocks = (0, 4) if i < n_query else (4, 2)
        to = pl.ds(pl.multiple_of(at_ref[1 + i], 16), rows)
        for b in range(blocks):
            here = pl.ds(pl.multiple_of(b * width + core * span, LANES), span)
            cols = slice((first + b) * span, (first + b + 1) * span)
            copy = pltpu.make_async_copy(ref.at[:, here], w_ref.at[to, cols], sems.at[len(made)])
            copy.start()
            made.append(copy)
    row = lambda c, o, r: vec_ref[c, o, r : r + 1, :].astype(F32)
    for b in range(4):
        pair = [jnp.where(core == 0, row(b % 2, b // 2, i), row(b % 2, b // 2, 2 + i)) for i in range(2)]
        bias_s[:, b * span : (b + 1) * span] = jnp.concatenate(pair, axis=1)
    bias_s[:, 4 * span : 5 * span] = jnp.zeros((1, span), F32)
    bias_s[:, 5 * span :] = jnp.concatenate([row(i, core, 4) for i in range(2)], axis=1)
    chunks, wide = types_ref.shape
    part = wide // 2
    kinds_s[:, :chunks] = jnp.where(types_ref[...] > 0, 1.0, 0.0).T
    for side in range(2):
        kind = core if side == 0 else 1 - core
        column = kinds_s[pl.ds(pl.multiple_of(kind * part, part), part), :]
        for chunk in range(chunks):
            at = side * half + chunk * part
            ent_ref[at : at + part, :] = jnp.broadcast_to(column[:, chunk : chunk + 1], (part, LANES)).astype(BF)
            place = chunk * wide + kind * part + lax.broadcasted_iota(jnp.int32, (part, LANES), 0)
            lanes = lax.broadcasted_iota(jnp.int32, (part, LANES), 1)
            seg = sum((place >= ends_ref[d]).astype(jnp.int32) for d in range(ends_ref.shape[0]))
            same = lanes == seg
            qseg_ref[at : at + part, :] = jnp.where(same, 1.0, 0.0).astype(BF)
            kseg_ref[at : at + part, :] = jnp.where(same | (lanes >= ends_ref.shape[0]), 0.0, BLOCKED).astype(BF)
    lane = lax.broadcasted_iota(jnp.int32, (block, LANES - hd), 1)
    tail = jnp.where(lane < 2, -1.0, jnp.where(lane == 2, 1.0, 0.0)).astype(BF)
    for copy in made:
        copy.wait()
    for side, rows_ref in enumerate((own_ref, other_ref)):

        def project(piece, carry, side=side, rows_ref=rows_ref):
            rows = rows_ref[pl.ds(pl.multiple_of(piece * block, block), block), :]
            at = pl.ds(pl.multiple_of(side * half + piece * block, block), block)
            ent = ent_ref[at, :hd]
            wide = ent_ref[at, :1] > 0
            word = (1 - ent).astype(BF)

            def part(index):
                cols = slice(index * span, (index + 1) * span)
                return jnp.dot(rows, w_ref[:, cols], preferred_element_type=F32) + bias_s[:, cols]

            q_word = (jnp.where(wide, part(2), part(0))).astype(BF) * BF(scale)
            q_ent = (jnp.where(wide, part(3), part(1))).astype(BF) * BF(scale)
            keys = part(4).astype(BF)
            vals = part(5).astype(BF)
            for h in range(heads):
                cut = slice(h * hd, (h + 1) * hd)
                qcat_ref[h, at, :] = jnp.concatenate([q_word[:, cut], q_ent[:, cut]], axis=1)
                kcat_ref[h, at, :] = jnp.concatenate([keys[:, cut] * word, keys[:, cut] * ent], axis=1)
                vaug_ref[h, at, :] = jnp.concatenate([vals[:, cut], tail], axis=1)
            return carry

        lax.fori_loop(0, half // block, project, 0)


def row_project(at, ends, own, other, vec, types, query_pieces, kv_pieces, heads, hd):
    half, width = own.shape
    full = 2 * half
    span = heads * hd
    vmem = pl.BlockSpec(memory_space=pltpu.VMEM)
    smem = pl.BlockSpec(memory_space=pltpu.SMEM)
    anywhere = pl.BlockSpec(memory_space=pl.ANY)
    query_rows = tuple(p.shape[0] for p in query_pieces)
    kv_rows = tuple(p.shape[0] for p in kv_pieces)
    shapes = [
        (heads, full, 2 * hd), (heads, full, 2 * hd), (heads, full, LANES), (width, 6 * span),
        (full, LANES), (full, LANES), (full, LANES),
    ]
    return pl.pallas_call(
        functools.partial(project_kernel, heads, hd, query_rows, kv_rows),
        in_specs=[smem, smem] + [vmem] * 4 + [anywhere] * (len(query_pieces) + len(kv_pieces)),
        out_specs=[vmem] * len(shapes),
        out_shape=[jax.ShapeDtypeStruct(s, BF) for s in shapes],
        scratch_shapes=[
            pltpu.VMEM((types.shape[1], LANES), F32),
            pltpu.VMEM((1, 6 * span), F32),
            pltpu.SemaphoreType.DMA((4 * len(query_pieces) + 2 * len(kv_pieces),)),
        ],
        compiler_params=pltpu.CompilerParams(vmem_limit_bytes=60 << 20),
        cost_estimate=pl.CostEstimate(
            flops=2 * full * width * 6 * span, bytes_accessed=18 * full * width, transcendentals=0
        ),
        name="row_project",
    )(at, ends, own, other, vec, types, *query_pieces, *kv_pieces)


def attend_kernel(
    heads, hd, qcat_ref, qseg_ref, kcat_ref, kseg_ref, vaug_ref, keep_ref, send_ref, wts_ref, inv_ref, score_s
):
    step = pl.program_id(0)
    block = keep_ref.shape[0]
    q_seg = qseg_ref[...]
    lane = lax.broadcasted_iota(jnp.int32, (block, LANES), 1)
    inv_all = jnp.zeros((block, LANES), F32)
    mixed = []
    for h in range(heads):
        q_aug = jnp.concatenate([qcat_ref[h], q_seg], axis=1)
        k_aug = jnp.concatenate([kcat_ref[h], kseg_ref[...]], axis=1)
        score_s[h % 2] = lax.dot_general(
            q_aug, k_aug, (((1,), (1,)), ((), ())), preferred_element_type=F32
        )
        for r in range(0, block, CHUNK):
            s = score_s[h % 2, r : r + CHUNK, :]
            top = jnp.max(s, axis=1, keepdims=True)
            wts_ref[h, r : r + CHUNK, :] = jnp.exp(s - top).astype(BF)
        out = jnp.dot(wts_ref[h], vaug_ref[h], preferred_element_type=F32)
        inv = 1.0 / out[:, hd + 2 : hd + 3]
        inv_all = jnp.where(lane == h, inv, inv_all)
        mixed.append((out[:, :hd] * inv).astype(BF))
    mixed = jnp.concatenate(mixed, axis=1)
    inv_ref[...] = inv_all
    late = pl.num_programs(0) // 2

    @pl.when(step < late)
    def _():
        send_ref[...] = mixed

    @pl.when(step >= late)
    def _():
        keep_ref[...] = mixed


def row_attend(qcat, kcat, vaug, qseg, kseg, heads, hd):
    full = qcat.shape[1]
    half = full // 2
    block = min(256, half)
    span = heads * hd
    first = half // block
    whole = lambda *dims: pl.BlockSpec(dims, lambda i: (0,) * len(dims))
    turn = lambda i: jnp.where(i < first, i + first, i - first)
    return pl.pallas_call(
        functools.partial(attend_kernel, heads, hd),
        grid=(full // block,),
        in_specs=[
            pl.BlockSpec((heads, block, 2 * hd), lambda i: (0, turn(i), 0)),
            pl.BlockSpec((block, LANES), lambda i: (turn(i), 0)),
            whole(heads, full, 2 * hd),
            whole(full, LANES),
            whole(heads, full, LANES),
        ],
        out_specs=[
            pl.BlockSpec((block, span), lambda i: (jnp.maximum(i - first, 0), 0)),
            pl.BlockSpec((block, span), lambda i: (jnp.minimum(i, first - 1), 0)),
            pl.BlockSpec((heads, block, full), lambda i: (0, turn(i), 0)),
            pl.BlockSpec((block, LANES), lambda i: (turn(i), 0)),
        ],
        out_shape=[
            jax.ShapeDtypeStruct((half, span), BF),
            jax.ShapeDtypeStruct((half, span), BF),
            jax.ShapeDtypeStruct((heads, full, full), BF),
            jax.ShapeDtypeStruct((full, LANES), F32),
        ],
        scratch_shapes=[pltpu.VMEM((2, block, full), F32)],
        compiler_params=pltpu.CompilerParams(vmem_limit_bytes=60 << 20),
        cost_estimate=pl.CostEstimate(
            flops=8 * heads * full * full * LANES,
            bytes_accessed=2 * heads * full * full + 4 * full * LANES * heads,
            transcendentals=heads * full * full,
        ),
        name="row_attend",
    )(qcat, qseg, kcat, kseg, vaug)


def token_kernel(
    out_rows, up_rows, down_rows, at_ref, own_ref, mine_ref, theirs_ref, cot_ref, vec_ref, *refs
):
    groups = (out_rows, up_rows, down_rows)
    sets, at = [], 0
    for rows in groups:
        sets.append(refs[at : at + len(rows)])
        at += len(rows)
    (
        result_ref, gy1_ref, gmine_ref, gtheirs_ref, act_out, hlow_out, gffn_out, gup_out, gattn_ref,
        small_ref, act_ref, hlow_ref, gffn_ref, gup_ref, leave, wout_s, wup_s, wdown_s, acc_s, hid_s, norm_s, inv_s, slope_s, gy2_s, tmp_s, sum_s, vec_s, sems,
    ) = refs[at:]
    total, width = own_ref.shape
    ff = wup_s.shape[1]
    parts = ff // width
    span = mine_ref.shape[1]
    core = at_ref[0]
    made, slot = [], 0
    for rows, piece_refs, dst in zip(groups, sets, (wout_s, wup_s, wdown_s)):
        batch = []
        for n, ref in zip(rows, piece_refs):
            to = pl.ds(pl.multiple_of(at_ref[1 + slot], 16), n)
            copy = pltpu.make_async_copy(ref, dst.at[to, :], sems.at[slot])
            copy.start()
            batch.append(copy)
            slot += 1
        made.append(batch)

    def wait(index):
        for copy in made[index]:
            copy.wait()

    leaving = []

    def send_out(src, dst):
        copy = pltpu.make_async_copy(src, dst, leave.at[len(leaving)])
        copy.start()
        leaving.append(copy)

    def whole_vector(r):
        return jnp.concatenate([vec_ref[f % 2, f // 2, r : r + 1, :] for f in range(4)], axis=1).astype(F32)

    for c in range(parts):
        up_bias = [vec_ref[c % 2, c // 2, 6 + i : 7 + i, :] for i in range(4)]
        vec_s[c : c + 1, :] = jnp.concatenate(up_bias, axis=1).astype(F32)
    for i, r in enumerate((5, 10, 11, 12, 13, 14)):
        vec_s[4 + i : 5 + i, :] = whole_vector(r)

    def row(index):
        return vec_s[index : index + 1, :]

    rows_at = lambda i, n: pl.ds(pl.multiple_of(i * n, n), n)
    chunk = 16
    mine_rows = pl.ds(pl.multiple_of(core * span, LANES), span)
    other_rows = pl.ds(pl.multiple_of((1 - core) * span, LANES), span)
    sum_s[...] = jnp.zeros_like(sum_s)
    wait(0)
    acc_s[...] = jnp.dot(mine_ref[...], wout_s[mine_rows, :], preferred_element_type=F32)
    acc_s[...] += jnp.dot(theirs_ref[...], wout_s[other_rows, :], preferred_element_type=F32)

    def first_norm(i, carry):
        at = rows_at(i, chunk)
        y = own_ref[at, :].astype(F32) + (acc_s[at, :] + row(4))
        center = y - jnp.mean(y, axis=1, keepdims=True)
        inv = lax.rsqrt(jnp.mean(center * center, axis=1, keepdims=True) + EPSILON)
        normed = center * inv
        hidden = normed * row(6) + row(7)
        norm_s[at, :] = normed
        inv_s[at, :] = jnp.broadcast_to(inv, (chunk, LANES))
        hid_s[at, :] = hidden
        hlow_ref[at, :] = hidden.astype(BF)
        return carry

    lax.fori_loop(0, total // chunk, first_norm, 0, unroll=16)
    send_out(hlow_ref, hlow_out)
    wait(1)
    for c in range(parts):
        cols = slice(c * width, (c + 1) * width)
        tmp_s[c % 2] = jnp.dot(hlow_ref[...], wup_s[:, cols], preferred_element_type=F32)
        for r in range(0, total, chunk):
            x = tmp_s[c % 2, r : r + chunk, :] + row(c)
            cdf = 0.5 + 0.5 * lax.erf(x * (0.5**0.5))
            act_ref[r : r + chunk, cols] = (x * cdf).astype(BF)
            slope_s[r : r + chunk, cols] = cdf + x * (jnp.exp(-0.5 * x * x) * (0.15915494309189535**0.5))
    send_out(act_ref, act_out)
    wait(2)
    acc_s[...] = jnp.dot(act_ref[...], wdown_s[...], preferred_element_type=F32)

    def second_norm(i, carry):
        at = rows_at(i, chunk)
        y = hid_s[at, :] + (acc_s[at, :] + row(5))
        center = y - jnp.mean(y, axis=1, keepdims=True)
        inv = lax.rsqrt(jnp.mean(center * center, axis=1, keepdims=True) + EPSILON)
        normed = center * inv
        result_ref[at, :] = (normed * row(8) + row(9)).astype(BF)
        cot = cot_ref[at, :].astype(F32)
        sum_s[2] += cot * normed
        sum_s[3] += cot
        scaled = cot * row(8)
        g = inv * (
            scaled
            - jnp.mean(scaled, axis=1, keepdims=True)
            - normed * jnp.mean(scaled * normed, axis=1, keepdims=True)
        )
        gy2_s[at, :] = g
        gffn_ref[at, :] = g.astype(BF)
        return carry

    lax.fori_loop(0, total // chunk, second_norm, 0, unroll=8)
    send_out(gffn_ref, gffn_out)
    ones = jnp.ones((8, total), BF)
    ups = []
    for c in range(parts):
        cols = slice(c * width, (c + 1) * width)
        tmp_s[c % 2] = lax.dot_general(
            gffn_ref[...], wdown_s[cols, :], (((1,), (1,)), ((), ())), preferred_element_type=F32
        )
        for r in range(0, total, chunk):
            gup_ref[r : r + chunk, cols] = (
                tmp_s[c % 2, r : r + chunk, :] * slope_s[r : r + chunk, cols]
            ).astype(BF)
        ups.append(jnp.dot(ones, gup_ref[:, cols], preferred_element_type=F32)[:1])
    send_out(gup_ref, gup_out)
    acc_s[...] = lax.dot_general(
        gup_ref[...], wup_s[...], (((1,), (1,)), ((), ())), preferred_element_type=F32
    )

    def first_back(i, carry):
        at = rows_at(i, chunk)
        g_in = gy2_s[at, :] + acc_s[at, :]
        normed = norm_s[at, :]
        sum_s[0] += g_in * normed
        sum_s[1] += g_in
        scaled = g_in * row(6)
        g = inv_s[at, :1] * (
            scaled
            - jnp.mean(scaled, axis=1, keepdims=True)
            - normed * jnp.mean(scaled * normed, axis=1, keepdims=True)
        )
        gy1_ref[at, :] = g
        gattn_ref[at, :] = g.astype(BF)
        return carry

    lax.fori_loop(0, total // chunk, first_back, 0, unroll=8)
    gmine_ref[...] = lax.dot_general(
        gattn_ref[...], wout_s[mine_rows, :], (((1,), (1,)), ((), ())), preferred_element_type=F32
    ).astype(BF)
    gtheirs_ref[...] = lax.dot_general(
        gattn_ref[...], wout_s[other_rows, :], (((1,), (1,)), ((), ())), preferred_element_type=F32
    ).astype(BF)
    sums = [jnp.dot(ones, ref[...], preferred_element_type=F32)[:1] for ref in (gattn_ref, gffn_ref)]
    sums += [jnp.sum(sum_s[i], axis=0, keepdims=True) for i in range(4)]
    n = width // 4
    half = width // 2
    for shard in range(4):
        at = 8 * shard
        cut = slice(shard * n, (shard + 1) * n)
        for i in range(2):
            small_ref[at + i : at + i + 1, :] = ups[shard][:, i * half : (i + 1) * half]
        for i in range(3):
            small_ref[at + 2 + i : at + 3 + i, :] = jnp.concatenate(
                [sums[2 * i][:, cut], sums[2 * i + 1][:, cut]], axis=1
            )
        small_ref[at + 5 : at + 8, :] = jnp.zeros((3, half), F32)
    for copy in leaving:
        copy.wait()


def token_block(at, own, mine, theirs, cot, vec, out_pieces, up_pieces, down_pieces):
    total, width = own.shape
    span = mine.shape[1]
    ff = up_pieces[0].shape[1]
    vmem = pl.BlockSpec(memory_space=pltpu.VMEM)
    pieces = [*out_pieces, *up_pieces, *down_pieces]
    shapes = [
        ((total, width), BF), ((total, width), F32), ((total, span), BF), ((total, span), BF),
        ((total, ff), BF), ((total, width), BF), ((total, width), BF), ((total, ff), BF),
        ((total, width), BF), ((32, width // 2), F32),
    ]
    rows = lambda group: tuple(p.shape[0] for p in group)
    return pl.pallas_call(
        functools.partial(token_kernel, rows(out_pieces), rows(up_pieces), rows(down_pieces)),
        in_specs=[pl.BlockSpec(memory_space=pltpu.SMEM)]
        + [vmem] * 5
        + [pl.BlockSpec(memory_space=pl.ANY)] * len(pieces),
        out_specs=[pl.BlockSpec(memory_space=pl.ANY) if 4 <= i < 8 else vmem for i in range(len(shapes))],
        out_shape=[jax.ShapeDtypeStruct(s, d) for s, d in shapes],
        scratch_shapes=[
            *[pltpu.VMEM(shape, BF) for shape, _ in shapes[4:8]],
            pltpu.SemaphoreType.DMA((4,)),
            pltpu.VMEM((width, width), BF),
            pltpu.VMEM((width, ff), BF),
            pltpu.VMEM((ff, width), BF),
            pltpu.VMEM((total, width), F32),
            pltpu.VMEM((total, width), F32),
            pltpu.VMEM((total, width), F32),
            pltpu.VMEM((total, LANES), F32),
            pltpu.VMEM((total, ff), F32),
            pltpu.VMEM((total, width), F32),
            pltpu.VMEM((2, total, width), F32),
            pltpu.VMEM((4, 16, width), F32),
            pltpu.VMEM((16, width), F32),
            pltpu.SemaphoreType.DMA((len(pieces),)),
        ],
        compiler_params=pltpu.CompilerParams(vmem_limit_bytes=60 << 20),
        cost_estimate=pl.CostEstimate(
            flops=2 * total * width * (4 * ff + 2 * width),
            bytes_accessed=4 * width * ff + 6 * total * ff,
            transcendentals=2 * total * ff,
        ),
        name="token_block",
    )(at, own, mine, theirs, cot, vec, *pieces)


def turned(core, outer, near, z):
    pick = lambda a, b: jnp.where(core == 0, a, b)
    return pick(outer, near), pick(z, outer), pick(near, z)


def place_of(owner, index, relative, b, c):
    first = index if relative else 1 - index
    return (first, c, b) if owner == 0 else (b, first, c)


def up_pieces(owner, index, n, span, hid_t, gup_ref, emit):
    for relative in range(2):
        for b in range(2):
            for c in range(2):
                outer, near, z = place_of(owner, index, relative, b, c)
                left = hid_t[pl.ds(pl.multiple_of((2 * outer + owner) * n, 16), n), :]
                for far in range(2):
                    cols = pl.ds(pl.multiple_of((near * 4 + z * 2 + far) * span, LANES), span)
                    emit((relative, b, c, far), jnp.dot(left, gup_ref[:, cols], preferred_element_type=F32))


def rest_pieces(owner, index, n, wide, span, att_t, act_ref, gffn_ref, gattn_ref, small_ref, emit):
    half = wide // 2
    for relative in range(2):
        for b in range(2):
            outer = place_of(owner, index, relative, b, 0)[0]
            shard = 2 * outer + owner
            small = small_ref[pl.ds(pl.multiple_of(shard * 8, 8), 8), :]
            for c in range(2):
                _, near, z = place_of(owner, index, relative, b, c)
                cols = pl.ds(pl.multiple_of(shard * wide + near * half, LANES), half)
                if owner == 0:
                    if b:
                        continue
                    rows, marks = act_ref[:, cols], [((relative, zz, c), zz) for zz in range(2)]
                else:
                    if c:
                        continue
                    rows, marks = act_ref[:, cols], [((relative, b, zz), zz) for zz in range(2)]
                down = lax.dot_general(rows, gffn_ref[...], (((0,), (0,)), ((), ())), preferred_element_type=F32)
                for mark, zz in marks:
                    at = pl.ds(pl.multiple_of(shard * n + (near * 2 + zz) * (n // 4), 16), n // 4)
                    out = jnp.dot(att_t[at, :], gattn_ref[...], preferred_element_type=F32)
                    for far in range(2):
                        cut = slice(far * span, (far + 1) * span)
                        head = (near == 0) if zz == 0 and far == 0 else False
                        emit(
                            (*mark, far),
                            down[zz * half // 2 : (zz + 1) * half // 2, cut],
                            out[:, cut],
                            jnp.where(head, small, 0.0),
                        )


def fetch(sems, *pairs):
    made = [pltpu.make_async_copy(src, dst, sems.at[i]) for i, (src, dst) in enumerate(pairs)]
    for copy in made:
        copy.start()
    return made


def up_send_kernel(at_ref, hlow_ref, gup_ref, send_ref, hid_t):
    width = hlow_ref.shape[1]
    n, span = width // 4, gup_ref.shape[1] // 8
    hid_t[...] = hlow_ref[...].T

    def emit(at, value):
        send_ref[at] = value.astype(BF)

    for owner in range(2):

        @pl.when(at_ref[0] == 1 - owner)
        def _(owner=owner):
            up_pieces(owner, at_ref[1 + owner], n, span, hid_t, gup_ref, emit)


def fill_att(at_ref, mine_ref, theirs_ref, att_t):
    span = mine_ref.shape[1]
    core = at_ref[0]
    att_t[pl.ds(pl.multiple_of(core * span, LANES), span), :] = mine_ref[...].T
    att_t[pl.ds(pl.multiple_of((1 - core) * span, LANES), span), :] = theirs_ref[...].T


def rest_send_kernel(at_ref, mine_ref, theirs_ref, act_ref, gffn_ref, gattn_ref, small_ref, send_ref, att_t):
    width = gffn_ref.shape[1]
    n, wide, span = width // 4, act_ref.shape[1] // 4, mine_ref.shape[1]
    fill_att(at_ref, mine_ref, theirs_ref, att_t)

    def emit(at, down, out, small):
        send_ref[(*at, slice(0, wide // 4))] = down.astype(BF)
        send_ref[(*at, slice(wide // 4, wide // 4 + n // 4))] = out.astype(BF)
        send_ref[(*at, slice(wide // 4 + n // 4, None))] = small.astype(BF)

    for owner in range(2):

        @pl.when(at_ref[0] == 1 - owner)
        def _(owner=owner):
            rest_pieces(
                owner, at_ref[1 + owner], n, wide, span, att_t, act_ref, gffn_ref, gattn_ref, small_ref, emit
            )


def keep_kernel(
    at_ref, mine_ref, theirs_ref, hlow_ref, gffn_ref, gattn_ref, small_ref, gup_hbm, up_hbm, act_hbm, rest_hbm,
    away_ref, kept_ref, hid_t, att_t, gup_ref, up_ref, act_ref, rest_ref, sems,
):
    width = gffn_ref.shape[1]
    n, wide, span = width // 4, act_ref.shape[1] // 4, mine_ref.shape[1]
    m = n + wide // 4
    come = fetch(sems, (gup_hbm, gup_ref), (up_hbm, up_ref), (act_hbm, act_ref), (rest_hbm, rest_ref))
    hid_t[...] = hlow_ref[...].T
    fill_att(at_ref, mine_ref, theirs_ref, att_t)
    for copy in come[:2]:
        copy.wait()

    def put(at, rows, value, got_ref, got):
        out_ref = kept_ref if at[0] else away_ref
        out_ref[(*at[1:], rows)] = (value + got_ref[(*at, got)].astype(F32)).astype(BF)

    def emit_up(at, value):
        put(at, slice(0, n), value, up_ref, slice(None))

    def emit(at, down, out, small):
        put(at, slice(n, m), down, rest_ref, slice(0, wide // 4))
        put(at, slice(m, m + n // 4), out, rest_ref, slice(wide // 4, wide // 4 + n // 4))
        put(at, slice(m + n // 4, None), small, rest_ref, slice(wide // 4 + n // 4, None))

    for owner in range(2):

        @pl.when(at_ref[0] == owner)
        def _(owner=owner):
            index = at_ref[1 + owner]
            up_pieces(owner, index, n, span, hid_t, gup_ref, emit_up)

    for copy in come[2:]:
        copy.wait()
    for owner in range(2):

        @pl.when(at_ref[0] == owner)
        def _(owner=owner):
            index = at_ref[1 + owner]
            rest_pieces(owner, index, n, wide, span, att_t, act_ref, gffn_ref, gattn_ref, small_ref, emit)


def grads_call(kernel, name, at, arrays, fetched, shapes, transposed, flops):
    vmem = pl.BlockSpec(memory_space=pltpu.VMEM)
    anywhere = pl.BlockSpec(memory_space=pl.ANY)
    return pl.pallas_call(
        kernel,
        in_specs=[pl.BlockSpec(memory_space=pltpu.SMEM)] + [vmem] * len(arrays) + [anywhere] * len(fetched),
        out_specs=[vmem] * len(shapes),
        out_shape=[jax.ShapeDtypeStruct(s, BF) for s in shapes],
        scratch_shapes=[pltpu.VMEM(t, BF) for t in transposed]
        + [pltpu.VMEM(f.shape, BF) for f in fetched]
        + [pltpu.SemaphoreType.DMA((len(fetched),))] * bool(fetched),
        compiler_params=pltpu.CompilerParams(vmem_limit_bytes=60 << 20),
        cost_estimate=pl.CostEstimate(
            flops=flops, bytes_accessed=2 * sum(a.size for a in (*arrays, *fetched)), transcendentals=0
        ),
        name=name,
    )(at, *arrays, *fetched)


def row_backward_kernel(
    heads, hd, first_head, gmine_ref, gother_ref, keep_ref, send_ref, inv_ref, wts_ref, qcat_ref, kcat_ref,
    vaug_ref, ent_ref, entb_ref, *refs,
):
    gq_ref, gkv_ref, gscore_s, low_s, gk_s, gv_s = refs[-6:]
    step = pl.program_id(0)
    block = gmine_ref.shape[0]
    full = kcat_ref.shape[1]
    scale = hd ** (-0.5)
    lane = lax.broadcasted_iota(jnp.int32, (block, LANES - hd), 1)
    is_ent = entb_ref[:, :1] > 0
    early = step < pl.num_programs(0) // 2
    g_all = jnp.where(early, gmine_ref[...], gother_ref[...])
    att_all = jnp.where(early, keep_ref[...], send_ref[...])
    g_word, g_ent = [], []
    for h in range(heads):
        cut = slice(h * hd, (h + 1) * hd)
        g_low = (g_all[:, cut].astype(F32) * inv_ref[:, first_head + h : first_head + h + 1]).astype(BF)
        delta = jnp.sum(g_low.astype(F32) * att_all[:, cut].astype(F32), axis=1, keepdims=True)
        d_hi = delta.astype(BF)
        d_lo = (delta - d_hi.astype(F32)).astype(BF)
        extra = jnp.where(
            lane == 0, d_hi.astype(F32), jnp.where(lane == 1, d_lo.astype(F32), 0.0)
        ).astype(BF)
        g_aug = jnp.concatenate([g_low, extra], axis=1)
        gscore_s[h % 2] = lax.dot_general(
            g_aug, vaug_ref[h], (((1,), (1,)), ((), ())), preferred_element_type=F32
        )
        for r in range(0, block, CHUNK):
            low_s[h % 2, r : r + CHUNK, :] = (
                wts_ref[h, r : r + CHUNK, :].astype(F32) * gscore_s[h % 2, r : r + CHUNK, :]
            ).astype(BF)
        g_q = jnp.dot(low_s[h % 2], kcat_ref[h], preferred_element_type=F32) * scale
        g_word.append(g_q[:, :hd])
        g_ent.append(g_q[:, hd:])
        g_k = lax.dot_general(
            qcat_ref[h], low_s[h % 2], (((0,), (0,)), ((), ())), preferred_element_type=F32
        )
        g_v = lax.dot_general(
            g_low, wts_ref[h], (((0,), (0,)), ((), ())), preferred_element_type=F32
        )

        @pl.when(step == 0)
        def _(h=h, g_k=g_k, g_v=g_v):
            gk_s[h] = g_k
            gv_s[h] = g_v

        @pl.when(step > 0)
        def _(h=h, g_k=g_k, g_v=g_v):
            gk_s[h] += g_k
            gv_s[h] += g_v

    g_word = jnp.concatenate(g_word, axis=1)
    g_ent = jnp.concatenate(g_ent, axis=1)
    gq_ref[0] = jnp.where(is_ent, 0.0, g_word).astype(BF)
    gq_ref[1] = jnp.where(is_ent, 0.0, g_ent).astype(BF)
    gq_ref[2] = jnp.where(is_ent, g_word, 0.0).astype(BF)
    gq_ref[3] = jnp.where(is_ent, g_ent, 0.0).astype(BF)

    @pl.when(step == pl.num_programs(0) - 1)
    def _():
        def close(piece, carry):
            at = pl.ds(pl.multiple_of(piece * block, block), block)
            pick = ent_ref[at, :1] > 0
            g_keys, g_vals = [], []
            for h in range(heads):
                both = gk_s[h, :, at].T
                g_keys.append(jnp.where(pick, both[:, hd:], both[:, :hd]))
                g_vals.append(gv_s[h, :, at].T)
            gkv_ref[0, at, :] = jnp.concatenate(g_keys, axis=1).astype(BF)
            gkv_ref[1, at, :] = jnp.concatenate(g_vals, axis=1).astype(BF)
            return carry

        lax.fori_loop(0, full // block, close, 0)


def row_backward(first_head, heads, grads, gmine, gother, keep, send, inv, wts, qcat, kcat, vaug, ent, hd):
    half, all_cols = keep.shape
    full = 2 * half
    block = min(256, half)
    first = half // block
    cols = heads * hd
    g, c = first_head // heads, first_head * hd // cols
    by_rows = pl.BlockSpec((block, LANES), lambda i: (i, 0))
    by_head = lambda width: pl.BlockSpec((heads, block, width), lambda i: (g, i, 0))
    of_head = lambda width: pl.BlockSpec((heads, full, width), lambda i: (g, 0, 0))
    low = pl.BlockSpec((block, cols), lambda i: (jnp.minimum(i, first - 1), c))
    high = pl.BlockSpec((block, cols), lambda i: (jnp.maximum(i - first, 0), c))
    given = [] if grads is None else list(grads)
    return pl.pallas_call(
        functools.partial(row_backward_kernel, heads, hd, first_head),
        grid=(full // block,),
        in_specs=[
            low, high, low, high,
            by_rows,
            by_head(full),
            by_head(2 * hd),
            of_head(2 * hd),
            of_head(LANES),
            pl.BlockSpec((full, LANES), lambda i: (0, 0)),
            by_rows,
        ]
        + [pl.BlockSpec(memory_space=pl.ANY)] * len(given),
        out_specs=[
            pl.BlockSpec((4, block, cols), lambda i: (0, i, c)),
            pl.BlockSpec((2, full, cols), lambda i: (0, 0, c)),
        ],
        out_shape=[
            jax.ShapeDtypeStruct((4, full, all_cols), BF),
            jax.ShapeDtypeStruct((2, full, all_cols), BF),
        ],
        scratch_shapes=[
            pltpu.VMEM((2, block, full), F32),
            pltpu.VMEM((2, block, full), BF),
            pltpu.VMEM((heads, 2 * hd, full), F32),
            pltpu.VMEM((heads, hd, full), F32),
        ],
        input_output_aliases={11 + i: i for i in range(len(given))},
        compiler_params=pltpu.CompilerParams(vmem_limit_bytes=60 << 20),
        cost_estimate=pl.CostEstimate(
            flops=16 * heads * full * full * LANES,
            bytes_accessed=2 * heads * full * full + 20 * full * cols,
            transcendentals=0,
        ),
        name="row_backward",
    )(gmine, gother, keep, send, inv, wts, qcat, kcat, vaug, ent, ent, *given)


def qkv_grad_kernel(
    at_ref, own_ref, other_ref, gq_hbm, gkv_hbm, send_ref, keep_ref, rows_t, gq_ref, gkv_ref, sems
):
    half, width = own_ref.shape
    n = width // 16
    span = gq_ref.shape[2]
    core, index = at_ref[0], at_ref[1]
    come = fetch(sems, (gq_hbm, gq_ref), (gkv_hbm, gkv_ref))
    rows_t[:, :half] = own_ref[...].T
    rows_t[:, half:] = other_ref[...].T
    for copy in come:
        copy.wait()

    def write(out_ref, at, start, count):
        left = rows_t[pl.ds(pl.multiple_of(start, 16), count * n), :]
        for b in range(6):
            right = gq_ref[b] if b < 4 else gkv_ref[b - 4]
            piece = jnp.dot(left, right, preferred_element_type=F32).astype(BF)
            for p in range(count):
                out_ref[(*at(p), slice(b * n, (b + 1) * n))] = piece[p * n : (p + 1) * n, :]

    ones = jnp.ones((8, 2 * half), BF)
    sums = [
        jnp.dot(ones, gq_ref[b] if b < 4 else gkv_ref[b - 4], preferred_element_type=F32)[:1] for b in range(6)
    ]

    def write_sums(out_ref, at, outer, near, on_core):
        query = jnp.where(outer == 0, jnp.where(near == 0, sums[0], sums[1]), jnp.where(near == 0, sums[2], sums[3]))
        value = jnp.where(outer == on_core, sums[5], 0.0)
        rows = jnp.concatenate([query, value, jnp.zeros((6, span), F32)], axis=0)
        out_ref[(*at, slice(6 * n, None))] = rows.astype(BF)

    for which, out_ref in ((1 - index, send_ref), (index, keep_ref)):

        @pl.when(core == 0)
        def _(which=which, out_ref=out_ref):
            write(out_ref, lambda p: (p // 2 % 2, p // 4, p % 2), which * 8 * n, 8)
            for p in range(8):
                at = (p // 2 % 2, p // 4, p % 2)
                write_sums(out_ref, at, which, p // 4, 0)

        @pl.when(core == 1)
        def _(which=which, out_ref=out_ref):
            for o in range(2):
                write(out_ref, lambda p, o=o: (o, p // 2, p % 2), o * 8 * n + which * 4 * n, 4)
                for p in range(4):
                    write_sums(out_ref, (o, p // 2, p % 2), o, which, 1)


def qkv_grad(at, own, other, gq, gkv):
    half, width = own.shape
    span = gkv.shape[2]
    n = width // 16
    vmem = pl.BlockSpec(memory_space=pltpu.VMEM)
    return pl.pallas_call(
        qkv_grad_kernel,
        in_specs=[pl.BlockSpec(memory_space=pltpu.SMEM)]
        + [vmem] * 2
        + [pl.BlockSpec(memory_space=pl.ANY)] * 2,
        out_specs=[vmem] * 2,
        out_shape=[jax.ShapeDtypeStruct((2, 2, 2, 6 * n + 8, span), BF)] * 2,
        scratch_shapes=[
            pltpu.VMEM((width, 2 * half), BF),
            pltpu.VMEM(gq.shape, BF),
            pltpu.VMEM(gkv.shape, BF),
            pltpu.SemaphoreType.DMA((2,)),
        ],
        compiler_params=pltpu.CompilerParams(vmem_limit_bytes=60 << 20),
        cost_estimate=pl.CostEstimate(
            flops=24 * half * width * span, bytes_accessed=32 * half * span, transcendentals=0
        ),
        name="qkv_grad",
    )(at, own, other, gq, gkv)


def input_grad_kernel(gq_ref, gkv_ref, w_ref, gy1_ref, mine_ref, away_ref):
    span = gkv_ref.shape[2]
    total = None
    for b in range(6):
        left = gq_ref[b] if b < 4 else gkv_ref[b - 4]
        part = lax.dot_general(
            left, w_ref[:, b * span : (b + 1) * span], (((1,), (1,)), ((), ())), preferred_element_type=F32
        )
        total = part if total is None else total + part
    early = pl.program_id(0) < pl.num_programs(0) // 2

    @pl.when(early)
    def _():
        away_ref[...] = total.astype(BF)

    @pl.when(jnp.logical_not(early))
    def _():
        mine_ref[...] = gy1_ref[...] + total


def row_input_grad(gq, gkv, w, gy1):
    half, width = gy1.shape
    span = gkv.shape[2]
    block = min(256, half)
    first = half // block
    turn = lambda i: jnp.where(i < first, i + first, i - first)
    late = pl.BlockSpec((block, width), lambda i: (jnp.maximum(i - first, 0), 0))
    return pl.pallas_call(
        input_grad_kernel,
        grid=(2 * first,),
        in_specs=[
            pl.BlockSpec((4, block, span), lambda i: (0, turn(i), 0)),
            pl.BlockSpec((2, block, span), lambda i: (0, turn(i), 0)),
            pl.BlockSpec((width, 6 * span), lambda i: (0, 0)),
            late,
        ],
        out_specs=[late, pl.BlockSpec((block, width), lambda i: (jnp.minimum(i, first - 1), 0))],
        out_shape=[jax.ShapeDtypeStruct((half, width), F32), jax.ShapeDtypeStruct((half, width), BF)],
        compiler_params=pltpu.CompilerParams(vmem_limit_bytes=60 << 20),
        cost_estimate=pl.CostEstimate(
            flops=4 * half * width * 6 * span, bytes_accessed=20 * half * width, transcendentals=0
        ),
        name="row_input_grad",
    )(gq, gkv, w, gy1)


def lay_rest_kernel(at_ref, mine_ref, other_ref, up_ref, down_ref, out_ref, small_ref):
    span = mine_ref.shape[2]
    k, n, m = up_ref.shape[0], down_ref.shape[0] // 4, out_ref.shape[0] // 4
    core, index = at_ref[0], at_ref[1]
    last = slice(k + n + m, None)
    small_ref[...] = jnp.where(index == 0, mine_ref[0, last, :].astype(F32), other_ref[0, last, :].astype(F32))
    for a, ref in ((index, mine_ref), (1 - index, other_ref)):
        for b in range(2):
            pair = jnp.where(core == 0, b * 2 + a, a * 2 + b)
            for far in range(2):
                j = b * 2 + far
                cols = pl.ds(pl.multiple_of((pair * 2 + far) * span, LANES), span)
                up_ref[:, cols] = ref[j, :k, :].astype(F32)
                cols = slice(far * span, (far + 1) * span)
                down_ref[pl.ds(pl.multiple_of(pair * n, 8), n), cols] = ref[j, k : k + n, :].astype(F32)
                out_ref[pl.ds(pl.multiple_of(pair * m, 8), m), cols] = ref[j, k + n : k + n + m, :].astype(F32)


def lay_qkv_kernel(at_ref, keep_ref, got_ref, query_ref, kv_ref, small_ref):
    span = keep_ref.shape[2]
    n = (keep_ref.shape[1] - 8) // 6
    last = slice(6 * n, None)
    for half, src in ((at_ref[0], keep_ref), (1 - at_ref[0], got_ref)):
        small_ref[half] = src[0, last, :].astype(F32)
        for b in range(6):
            ref, i = (query_ref, b) if b < 4 else (kv_ref, b - 4)
            cols = pl.ds(pl.multiple_of(i * 2 * span + half * span, LANES), span)
            for j in range(4):
                ref[j * n : (j + 1) * n, cols] = src[j, b * n : (b + 1) * n, :].astype(F32)


def lay(kernel, name, at, arrays, shapes):
    vmem = pl.BlockSpec(memory_space=pltpu.VMEM)
    return pl.pallas_call(
        kernel,
        in_specs=[pl.BlockSpec(memory_space=pltpu.SMEM)] + [vmem] * len(arrays),
        out_specs=[vmem] * len(shapes),
        out_shape=[jax.ShapeDtypeStruct(s, F32) for s in shapes],
        compiler_params=pltpu.CompilerParams(vmem_limit_bytes=60 << 20),
        cost_estimate=pl.CostEstimate(
            flops=0, bytes_accessed=6 * sum(a.size for a in arrays), transcendentals=0
        ),
        name=name,
    )(at, *arrays)


def row_layer(
    inputs, query_weight, kv_weight, out_weight, up_weight, down_weight,
    query_bias, value_bias, out_bias, up_bias, down_bias,
    norm1_gain, norm1_shift, norm2_gain, norm2_shift, types, lengths, cotangent,
):
    rows_here, span, width = inputs.shape
    hd = width // HEADS
    full = types.shape[1]
    heads = HEADS // 2
    cols = heads * hd
    row_count = lax.axis_size("row")
    core, outer, row_id = (lax.axis_index(n) for n in ("core", "outer", "row"))
    place = [row_id // bit % 2 for bit in (1, 2, 4)]
    near = place[0]
    own_count = full // 2
    both_ways = [(0, 1), (1, 0)]

    def after(values, *others):
        return lax.optimization_barrier((values, *others))[0]

    def swap(values):
        return lax.ppermute(values, "core", both_ways)

    def cross(values):
        return lax.ppermute(values, "outer", both_ways)

    def pair_up(values, bit):
        return lax.ppermute(values, "row", [(i, i ^ bit) for i in range(row_count)])

    def in_order(index, mine, other, axis=0):
        first, second = jnp.where(index == 0, mine, other), jnp.where(index == 0, other, mine)
        return jnp.stack([first, second], axis=axis)

    def take(values, index, axis=0):
        return lax.dynamic_index_in_dim(values, index, axis, keepdims=False)

    def halves_of_rows(values):
        pieces = values.reshape(rows_here, 2, span // 2, width)
        other = swap(take(pieces, 1 - core, 1))
        return in_order(core, take(pieces, core, 1), other).reshape(row_count, span // 2, width)

    def over_rows(values):
        return lax.all_to_all(values, "row", 0, 0, tiled=True)

    def rows_whole(back):
        back = back.reshape(2, rows_here, span // 2, width)
        other = swap(take(back, 1 - core))
        both = in_order(core, take(back, core), other)
        return both.transpose(1, 0, 2, 3).reshape(rows_here, span, width)

    shard = query_weight.shape[0]
    wide = down_weight.shape[0]

    def near_half(values):
        return take(values.reshape(2, values.shape[0] // 2, values.shape[1]), near)

    f_own, f_core = 2 * outer + core, 2 * outer + 1 - core
    f_cross, f_both = 2 * (1 - outer) + core, 2 * (1 - outer) + 1 - core

    q_got = cross(near_half(query_weight))
    to_rows = halves_of_rows(inputs)
    own_rows = over_rows(to_rows).reshape(own_count, width)
    query_own, kv_own, types, lengths, query_bias = lax.optimization_barrier(
        (query_weight, kv_weight, types, lengths, query_bias, to_rows)
    )[:5]
    q_core, kv_core = swap(query_own), swap(kv_own)
    q_passed, kv_got = pair_up(q_got, 1), cross(after(kv_weight, q_got))
    q_got2 = swap(after(q_got, q_core, kv_core))
    own_rows, q_passed = lax.optimization_barrier((own_rows, q_passed))
    other_rows = swap(own_rows)
    q_passed2, kv_got2 = swap(q_passed), swap(kv_got)
    cot_halves = halves_of_rows(after(cotangent, own_rows))
    query_pieces = [query_weight, q_core, q_got, q_passed, q_got2, q_passed2]
    kv_pieces = [kv_weight, kv_core, kv_got, kv_got2]
    part = shard // 2
    query_at = [
        f_own * shard, f_core * shard,
        f_cross * shard + near * part, f_cross * shard + (1 - near) * part,
        f_both * shard + near * part, f_both * shard + (1 - near) * part,
    ]
    kv_at = [f_own * shard, f_core * shard, f_cross * shard, f_both * shard]
    at_qkv = jnp.stack([core, *query_at, *kv_at]).astype(jnp.int32)

    tags = jnp.concatenate([types, lengths], axis=1)
    tags_other = after(swap(tags), q_got2)
    tags = take(in_order(core, tags, tags_other).reshape(row_count, -1), row_id)
    types_row, lengths_row = tags[:full].reshape(row_count, span), tags[full:]
    docs = lengths_row.shape[0]
    ends = jnp.sum(jnp.where(jnp.arange(docs)[:, None] >= jnp.arange(docs)[None], lengths_row[None], 0), axis=1)

    vectors = (
        query_bias, value_bias, out_bias, up_bias, down_bias,
        norm1_gain, norm1_shift, norm2_gain, norm2_shift,
    )
    packed = jnp.concatenate(vectors)
    packed = in_order(outer, packed, cross(packed))
    vec = in_order(core, packed, swap(packed)).reshape(2, 2, -1, shard)

    qcat, kcat, vaug, w_sel, ent, qseg, kseg = row_project(
        at_qkv, ends, own_rows, other_rows, vec, types_row, query_pieces, kv_pieces, heads, hd
    )

    low_rows = down_weight[: wide // 2]
    u_got = cross(after(near_half(up_weight), kv_got))
    d_got = cross(after(near_half(low_rows), kv_got))
    late_out, late_up, late_down = lax.optimization_barrier((out_weight, up_weight, down_weight, kv_got2))[:3]
    o_core, u_core, d_core = swap(late_out), swap(late_up), swap(late_down)
    u_mid, d_mid, m_out, m_down, o_core, u_core, d_core = lax.optimization_barrier(
        (u_got, d_got, out_weight, down_weight, o_core, u_core, d_core, kcat)
    )[:7]
    u_passed, d_passed = pair_up(u_mid, 1), pair_up(d_mid, 1)
    o_got, t_got = cross(m_out), cross(m_down[wide // 2 :])
    u_got2, d_got2 = swap(u_mid), swap(d_mid)
    cot = over_rows(after(cot_halves, other_rows)).reshape(own_count, width)
    keep, send, wts, inv = row_attend(qcat, kcat, vaug, qseg, kseg, heads, hd)
    theirs = swap(send)
    u_passed2, d_passed2, o_got2, t_got2 = (
        swap(v) for v in lax.optimization_barrier((u_passed, d_passed, o_got, t_got, keep))[:4]
    )
    out_pieces = [out_weight, o_core, o_got, o_got2]
    out_at = [f * shard for f in (f_own, f_core, f_cross, f_both)]
    up_pieces = [up_weight, u_core, u_got, u_passed, u_got2, u_passed2]
    down_pieces = [down_weight, d_core, d_got, d_passed, t_got, d_got2, d_passed2, t_got2]
    quarter = wide // 4
    down_at = [
        f_own * wide, f_core * wide,
        f_cross * wide + near * quarter, f_cross * wide + (1 - near) * quarter, f_cross * wide + 2 * quarter,
        f_both * wide + near * quarter, f_both * wide + (1 - near) * quarter, f_both * wide + 2 * quarter,
    ]
    at_rest = jnp.stack([core, *out_at, *query_at, *down_at]).astype(jnp.int32)

    (
        result, gy1, gmine, gtheirs, act, hlow, gffn, gup, gattn, small
    ) = token_block(at_rest, own_rows, keep, theirs, cot, vec, out_pieces, up_pieces, down_pieces)
    gother = swap(gtheirs)
    at_core = core.astype(jnp.int32).reshape(1)
    at_near = near.astype(jnp.int32).reshape(1)
    at_grads = jnp.stack([core, outer, near]).astype(jnp.int32)
    m, ff = width // 16, up_weight.shape[1]
    bits = (2, 2, 2)
    tall = (2, *bits, ff // 16 + m + 8, cols)
    (rest_send,) = grads_call(
        rest_send_kernel, "rest_send", at_grads, [keep, theirs, act, gffn, gattn, small], [], [tall],
        [(width, own_count)], own_count * width * (ff + width),
    )
    hlow, gup, gother, rest_send = lax.optimization_barrier((hlow, gup, gother, rest_send))
    (up_send,) = grads_call(
        up_send_kernel, "up_send", at_grads, [hlow, gup], [], [(2, *bits, shard, cols)],
        [(width, own_count)], own_count * width * ff,
    )

    def add(*arrays):
        return functools.reduce(jnp.add, [v.astype(F32) for v in arrays]).astype(BF)

    def by_core(a, b):
        return jnp.where(core == 0, a, b)

    stages = {
        "s1": ("outer", "y"), "s2": ("z", "outer"), "s3": ("y", "z"), "far": ("far", "far"), "g1": ("z", "y"),
        "t1": ("z", "y"), "t2": ("y", "z"), "t3": ("far", "far"),
    }
    index_on = {"outer": outer, "y": near, "z": place[1], "far": place[2]}
    index_of = {name: by_core(index_on[a], index_on[b]) for name, (a, b) in stages.items()}
    every = ("row", "outer", "core")

    def pairs_of(stage):
        found = []
        for r in range(row_count):
            for o in range(2):
                for c in range(2):
                    axis = stages[stage][c]
                    to = (r, 1 - o) if axis == "outer" else (r ^ {"y": 1, "z": 2, "far": 4}[axis], o)
                    found.append(((r * 2 + o) * 2 + c, (to[0] * 2 + to[1]) * 2 + c))
        return found

    def send_over(values, stage):
        return lax.ppermute(values, every, pairs_of(stage))

    axis_at = {"far": 0, "z": 1, "y": 2}

    def trade(values, stage):
        away, mine = (
            by_core(*(take(values, i, axis_at[axis]) for axis in stages[stage]))
            for i in (1 - index_of[stage], index_of[stage])
        )
        token[0] = away
        return mine, send_over(away, stage)

    def traded(state, stage):
        mine, other = in_turn(*state)
        token[0] = other
        return by_core(*(in_order(index_of[stage], mine, other, axis_at[axis]) for axis in stages[stage]))

    def by_rows(values):
        return values.reshape(2, 2, 2, span // 2, width)

    token = [gother]

    def in_turn(*arrays):
        return lax.optimization_barrier((*arrays, token[0]))[: len(arrays)]

    def halve(state, axis):
        mine, other = in_turn(*state)
        away, mine = (
            add(take(mine, i), take(other, i)) for i in (1 - index_of[axis], index_of[axis])
        )
        token[0] = away
        return mine, send_over(away, axis)

    def start_spread(state, axis):
        total = add(*in_turn(*state))
        token[0] = total
        return total, send_over(total, axis)

    def spread(state, have, axis):
        total = in_order(index_of[have], *in_turn(*state))
        token[0] = total
        return total, send_over(total, axis)

    out_rows = trade(by_rows(result), "t1")
    away, mine = grads_call(
        keep_kernel, "keep_grads", at_grads,
        [keep, theirs, hlow, gffn, gattn, small], [gup, swap(up_send), act, swap(rest_send)],
        [(*bits, shard + tall[-2], cols)] * 2, [(width, own_count)] * 2, own_count * width * (2 * ff + width),
    )
    rest = (mine, send_over(away, "s1"))
    token[0] = away
    out_rows = trade(traded(out_rows, "t1"), "t2")
    gmine, _ = lax.optimization_barrier((gmine, token[0]))
    gq, gkv = row_backward(
        0, heads, None, gmine, gother, keep, send, inv, wts, qcat, kcat, vaug, ent, hd
    )
    n = width // 16
    token[0] = gkv
    out_rows = trade(traded(out_rows, "t2"), "t3")
    rest = halve(rest, "s2")
    at_first = jnp.stack([core, index_of["s1"]]).astype(jnp.int32)
    q_send, q_keep = qkv_grad(at_first, own_rows, after(other_rows, token[0]), gq, gkv)
    six = (q_keep, send_over(q_send, "s1"))
    token[0] = q_send
    out_rows = traded(out_rows, "t3")
    in_mine, in_away = row_input_grad(gq, gkv, after(w_sel, token[0]), gy1)
    in_other = swap(in_away)
    token[0] = in_away
    rest = halve(rest, "s3")
    in_mine, in_other = in_turn(in_mine, in_other)
    grad_in = (in_mine + in_other.astype(F32)).astype(BF)
    in_rows = trade(by_rows(grad_in), "t1")
    six = halve(six, "s2")
    rest = halve(rest, "far")
    in_rows = trade(traded(in_rows, "t1"), "t2")
    six = halve(six, "s3")
    rest = start_spread(rest, "far")
    six = halve(six, "far")
    rest = spread(rest, "far", "s3")
    six = start_spread(six, "far")
    in_rows = trade(traded(in_rows, "t2"), "t3")
    rest = spread(rest, "s3", "g1")
    six = spread(six, "far", "s3")
    in_rows = traded(in_rows, "t3")
    output, input_grad = rows_whole(out_rows), rows_whole(in_rows)
    six = spread(six, "s3", "g1")
    at_last = jnp.stack([core, index_of["g1"]]).astype(jnp.int32)
    g_up, g_down, g_out, small = lay(
        lay_rest_kernel, "lay_rest", at_last, [v.reshape(4, *v.shape[2:]) for v in in_turn(*rest)],
        [up_weight.shape, down_weight.shape, out_weight.shape, (8, cols)],
    )
    token[0] = g_out
    six = in_order(index_of["g1"], *in_turn(*six))
    away, kept = by_core(six[:, 1], six[0]), by_core(six[:, 0], six[1])
    parts = [v.reshape(4, *v.shape[2:]) for v in (kept, swap(away))]
    g_query, g_kv, halves = lay(
        lay_qkv_kernel, "lay_qkv", at_core, parts, [query_weight.shape, kv_weight.shape, (2, 8, cols)]
    )
    pairs = small[2:5].reshape(6, shard)
    value = take(halves[:, 1].sum(axis=0).reshape(2, shard), core)
    return (
        output, input_grad, g_query, g_kv, g_out, g_up, g_down,
        halves[:, 0].reshape(-1), value, pairs[0], small[:2].reshape(-1), *(pairs[i] for i in range(1, 6)),
    )


def solution(mesh):
    def step(*args):
        ctx, fsdp = mesh.shape["ctx"], mesh.shape["fsdp"]
        row_count = args[0].shape[0] // (fsdp // 2)
        per_row = ctx // row_count
        fine = Mesh(
            mesh.devices.reshape(row_count, per_row, fsdp // 2, 2), ("row", "group", "outer", "core")
        )
        tokens = P(("outer", "core"), ("row", "group"), None)
        mat, vec = P(("outer", "core"), None), P(("outer", "core"))
        in_specs = (tokens, *[mat] * 5, *[vec] * 9, mat, mat, tokens)
        out_specs = (tokens, tokens, *[mat] * 5, *[vec] * 9)
        quarter = args[0].shape[2] // 4
        fits = per_row == 1 and fsdp == 4 and row_count == 8 and args[0].shape[2] % (2 * LANES) == 0 and quarter % 32 == 0
        body = row_layer if fits else functools.partial(layer, None, per_row)
        return jax.shard_map(
            body, mesh=fine, in_specs=in_specs, out_specs=out_specs, check_vma=False
        )(*args)

    return step
```
